32 devices in a mesh: fsdp: 4 (over y, x), seq: 8 (over z, core).
Axes of the slice: x: 2, y: 2, z: 4, core: 2. Of those that a mesh axis runs over, the one named last changes fastest.
Arguments:
- tokens: bfloat16 [4, 1024, 2048], P('fsdp', 'seq'), may hold values from -6 to 6
- doc_lengths: int32 [4, 4], P('fsdp'), may hold values from 1 to 512, 1024 in all within a row
- attn_gain: bfloat16 [2048], P('fsdp'), may hold values from 0.5 to 1.5
- attn_shift: bfloat16 [2048], P('fsdp'), may hold values from -1.5 to 1.5
- qkv_weight: bfloat16 [2048, 2304], P('fsdp'), may hold values from -0.125 to 0.125
- query_bias: bfloat16 [2048], P('fsdp'), may hold values from -1.5 to 1.5
- value_bias: bfloat16 [128], P('fsdp'), may hold values from -0.3125 to 0.3125
- out_weight: bfloat16 [2048, 2048], P('fsdp'), may hold values from -1 to 1
- out_bias: bfloat16 [2048], P('fsdp'), may hold values from -1.5 to 1.5
- mlp_gain: bfloat16 [2048], P('fsdp'), may hold values from 0.5 to 1.5
- mlp_shift: bfloat16 [2048], P('fsdp'), may hold values from -1.5 to 1.5
- up_weight: bfloat16 [2048, 8192], P('fsdp'), may hold values from -0.125 to 0.125
- up_bias: bfloat16 [8192], P('fsdp'), may hold values from -1.5 to 1.5
- down_weight: bfloat16 [8192, 2048], P('fsdp'), may hold values from -0.0625 to 0.0625
- down_bias: bfloat16 [2048], P('fsdp'), may hold values from -1.5 to 1.5
- cotangent: bfloat16 [4, 1024, 2048], P('fsdp', 'seq'), may hold values from -6 to 6
Outputs:
- layer_out: bfloat16 [4, 1024, 2048], P('fsdp', 'seq')
- grad_tokens: bfloat16 [4, 1024, 2048], P('fsdp', 'seq')
- grad_attn_gain: float32 [2048], P('fsdp')
- grad_attn_shift: float32 [2048], P('fsdp')
- grad_qkv_weight: float32 [2048, 2304], P('fsdp')
- grad_query_bias: float32 [2048], P('fsdp')
- grad_value_bias: float32 [128], P('fsdp')
- grad_out_weight: float32 [2048, 2048], P('fsdp')
- grad_out_bias: float32 [2048], P('fsdp')
- grad_mlp_gain: float32 [2048], P('fsdp')
- grad_mlp_shift: float32 [2048], P('fsdp')
- grad_up_weight: float32 [2048, 8192], P('fsdp')
- grad_up_bias: float32 [8192], P('fsdp')
- grad_down_weight: float32 [8192, 2048], P('fsdp')
- grad_down_bias: float32 [2048], P('fsdp')
The draws below stay inside these ranges and needn't reach their ends.
Inputs may be any that keep to these rules, and one draw needn't show every extreme that they name: Each row of doc_lengths holds the lengths of the 4 documents that fill its stream of 1024 tokens, in order; the longest is exactly 512.
All inputs are finite; a program needn't handle non-finite values.
Results may differ from the reference program's by a relative error of at most 0.013.
Values may be sent and summed in bfloat16 or wider, within the bound.
A program may use at most 448 MiB of HBM per device.

```python
import math
import jax
import jax.numpy as jnp
import numpy as np
from jax import lax

D = 2048
HD = 128
FF = 8192
DOCS = 4
STREAM = 1024
DOC_MOST = 512
N_FSDP = 4


def block_levels(stream_key, extent, split, smallest, high):
    loudness = 1.0
    for axis_at, parts in split:
        draws = jax.random.uniform(jax.random.fold_in(jax.random.fold_in(stream_key, 6), axis_at), (parts,), jnp.float32, smallest / len(split), high / len(split))
        loudness = loudness * jnp.repeat(jnp.exp(draws), extent[axis_at] // parts).reshape((-1,) + (1,) * (len(extent) - 1 - axis_at))
    return loudness


def length_profile(count, total, bound, skew):
    loads = [(1 << 20) // math.isqrt(standing ** skew) + 1 for standing in range(2, count + 1)]
    spare, counts = total - bound - (count - 1), [1] * (count - 1)
    while spare > 0:
        free = [i for i in range(count - 1) if counts[i] < bound]
        pool, budget = sum([loads[i] for i in free]), spare
        for i in free:
            extra = min(bound - counts[i], max(1, budget * loads[i] // pool), spare)
            counts[i] = counts[i] + extra
            spare = spare - extra
    return np.array([bound] + counts)


def uneven_parts(stream_key, amount, total, bound, slope):
    if amount == 2:
        one = jax.random.randint(stream_key, (), max(1, total - bound), min(bound, total - 1) + 1)
        return jnp.stack([one, total - one])
    sizes = jnp.asarray(length_profile(amount, total, bound, slope), jnp.int32)
    couples = (amount - 1) // 2
    giver, receiver = sizes[1:1 + 2 * couples:2], sizes[2:2 + 2 * couples:2]
    margin = jnp.minimum(giver - 1, bound - receiver)
    shifted = jax.random.randint(jax.random.fold_in(stream_key, 1), (couples,), 0, 1 << 20) % (margin + 1)
    sizes = sizes.at[1:1 + 2 * couples:2].set(giver - shifted).at[2:2 + 2 * couples:2].set(receiver + shifted)
    return sizes[jax.random.permutation(jax.random.fold_in(stream_key, 2), amount)]


def noise(rng, shape, deviation, reach, shards=(), kind=jnp.bfloat16):
    level = block_levels(rng, shape, shards, -0.22, 0.18) if shards else 1.0
    values = jax.random.normal(rng, shape, jnp.float32) * deviation * level
    return jnp.minimum(jnp.maximum(values, -reach), reach).astype(kind)


def setup_inputs(seed: int = 0) -> dict:
    arg_keys = jax.random.split(jax.random.key(seed), 17)
    return {
        "tokens": noise(arg_keys[0], (N_FSDP, STREAM, D), 1.0, 6.0, ((0, 4), (1, 8))),
        "doc_lengths": jax.vmap(lambda own: uneven_parts(own, DOCS, STREAM, DOC_MOST, 2))(jax.random.split(arg_keys[1], N_FSDP)).reshape((N_FSDP, DOCS)).astype(jnp.int32),
        "attn_gain": jnp.clip(1.0 + 0.1 * jax.random.normal(arg_keys[2], (D,), jnp.float32), 0.5, 1.5).astype(jnp.bfloat16),
        "attn_shift": noise(arg_keys[3], (D,), 0.1, 1.5, ((0, 4),)),
        "qkv_weight": noise(arg_keys[4], (D, D + 2 * HD), D ** -0.5, 0.125, ((0, 4),)),
        "query_bias": noise(arg_keys[5], (D,), 0.1, 1.5, ((0, 4),)),
        "value_bias": noise(arg_keys[6], (HD,), 0.02, 0.3125, ((0, 4),)),
        "out_weight": noise(arg_keys[7], (D, D), (D // 64) ** -0.5, 1.0, ((0, 4),)),
        "out_bias": noise(arg_keys[8], (D,), 0.1, 1.5, ((0, 4),)),
        "mlp_gain": jnp.clip(1.0 + 0.1 * jax.random.normal(arg_keys[9], (D,), jnp.float32), 0.5, 1.5).astype(jnp.bfloat16),
        "mlp_shift": noise(arg_keys[10], (D,), 0.1, 1.5, ((0, 4),)),
        "up_weight": noise(arg_keys[11], (D, FF), D ** -0.5, 0.125, ((0, 4),)),
        "up_bias": noise(arg_keys[12], (FF,), 0.1, 1.5, ((0, 4),)),
        "down_weight": noise(arg_keys[13], (FF, D), FF ** -0.5, 0.0625, ((0, 4),)),
        "down_bias": noise(arg_keys[14], (D,), 0.1, 1.5, ((0, 4),)),
        "cotangent": noise(arg_keys[15], (N_FSDP, STREAM, D), 1.0, 6.0, ((0, 4), (1, 8))),
    }


EPSILON = 1e-05

@jax.custom_vjp
def low(v):
    return lax.optimization_barrier(v.astype(jnp.bfloat16)).astype(jnp.float32)

@jax.custom_vjp
def low_back(v):
    return v

def low_keep(v):
    return (low(v), None)

def low_pass(kept, grad):
    return (grad,)

def back_keep(v):
    return (v, None)

def back_low(kept, grad):
    return (low(grad),)
low.defvjp(low_keep, low_pass)
low_back.defvjp(back_keep, back_low)

def norm_rows(values_in, norm_gain, norm_shift):
    row_mean = lax.optimization_barrier(jnp.mean(values_in, axis=-1, keepdims=True))
    centered = values_in - row_mean
    variance = lax.optimization_barrier(jnp.mean(centered * centered, axis=-1, keepdims=True))
    return centered * lax.rsqrt(variance + EPSILON) * norm_gain + norm_shift

def product(left, right):
    return jnp.dot(left, right, precision=lax.Precision.HIGHEST)

def row_docs(positions, lengths):
    doc_ends = jnp.cumsum(lengths).astype(jnp.int32)
    return lax.optimization_barrier(jnp.sum((positions[:, None] >= doc_ends[None, :]).astype(jnp.int32), axis=1)).astype(jnp.int32)

def attend_rows(query_rows, key_rows, value_rows, lengths, head_count):
    row_count = query_rows.shape[0]
    head_size = query_rows.shape[1]
    block_rows = min(512, row_count)
    score_scale = 1.0 / math.sqrt(head_size)
    key_pos = jnp.arange(key_rows.shape[0], dtype=jnp.int32)
    key_doc = row_docs(key_pos, lengths)

    def one_block(inputs):
        block_query, first_row = inputs
        positions = (first_row + jnp.arange(block_rows, dtype=jnp.int32)) // head_count
        query_doc = row_docs(positions, lengths)
        scores = low_back(product(block_query, key_rows.T) * score_scale)
        allowed = (query_doc[:, None] == key_doc[None, :]) & (positions[:, None] >= key_pos[None, :])
        scores = jnp.where(allowed, scores, -1e+30)
        row_peak = lax.optimization_barrier(jnp.max(scores, axis=-1, keepdims=True))
        weights = jnp.exp(scores - row_peak)
        probs = weights / lax.optimization_barrier(jnp.sum(weights, axis=-1, keepdims=True))
        return product(low(probs), value_rows)
    blocked = query_rows.reshape(row_count // block_rows, block_rows, head_size)
    firsts = jnp.arange(row_count // block_rows, dtype=jnp.int32) * block_rows
    outputs = lax.map(jax.checkpoint(one_block), (blocked, firsts))
    return outputs.reshape(row_count, head_size)

def layer(tokens_in, attn_gain, attn_shift, qkv_weight, query_bias, value_bias, out_weight, out_bias, mlp_gain, mlp_shift, up_weight, up_bias, down_weight, down_bias, lengths):
    model_width = tokens_in.shape[1]
    head_size = value_bias.shape[0]
    head_count = model_width // head_size
    normed = low(norm_rows(tokens_in, attn_gain, attn_shift))
    projected = product(normed, qkv_weight)
    query_low = low(low_back(projected[:, :model_width] + query_bias))
    key_rows = low(low_back(projected[:, model_width:model_width + head_size]))
    value_rows = low(low_back(projected[:, model_width + head_size:] + value_bias))
    attended = attend_rows(query_low.reshape(-1, head_size), key_rows, value_rows, lengths, head_count)
    mixed_out = low(low_back(attended.reshape(tokens_in.shape[0], model_width)))
    branch = low_back(product(mixed_out, out_weight) + out_bias)
    residual = tokens_in + branch
    normed_mlp = low(norm_rows(residual, mlp_gain, mlp_shift))
    inner_pre = low_back(product(normed_mlp, up_weight) + up_bias)
    activated = low(jax.nn.gelu(inner_pre, approximate=True))
    return residual + product(activated, down_weight) + down_bias

def reference(tokens, doc_lengths, attn_gain, attn_shift, qkv_weight, query_bias, value_bias, out_weight, out_bias, mlp_gain, mlp_shift, up_weight, up_bias, down_weight, down_bias, cotangent):
    params = tuple((item.astype(jnp.float32) for item in (attn_gain, attn_shift, qkv_weight, query_bias, value_bias, out_weight, out_bias, mlp_gain, mlp_shift, up_weight, up_bias, down_weight, down_bias)))

    def per_stream(running, inputs):
        stream_tokens, lengths, stream_cot = inputs

        def forward(tokens_in, *weights_in):
            return layer(tokens_in, *weights_in, lengths)
        outputs, pullback = jax.vjp(forward, stream_tokens.astype(jnp.float32), *params)
        gradients = pullback(stream_cot.astype(jnp.float32))
        running = tuple((summed + grad_in for summed, grad_in in zip(running, gradients[1:])))
        return (running, (outputs.astype(jnp.bfloat16), gradients[0].astype(jnp.bfloat16)))
    zeros_all = tuple((jnp.zeros(item.shape, jnp.float32) for item in params))
    totals, (layer_out, grad_tokens) = lax.scan(per_stream, zeros_all, (tokens, doc_lengths, cotangent))
    return (layer_out, grad_tokens, totals[0], totals[1], totals[2], totals[3], totals[4], totals[5], totals[6], totals[7], totals[8], totals[9], totals[10], totals[11], totals[12])
```

```python
import math

import jax
import jax.numpy as jnp
from jax import lax
from jax.sharding import Mesh
from jax.sharding import PartitionSpec as P

EPSILON = 1e-05
F32 = jnp.float32
BF16 = jnp.bfloat16
PLANE = ("fsdp", "core")
COLUMN = ("zz", "core")


def norm_parts(values_in):
    row_mean = jnp.mean(values_in, axis=-1, keepdims=True)
    centered = values_in - row_mean
    variance = jnp.mean(centered * centered, axis=-1, keepdims=True)
    inverse = lax.rsqrt(variance + EPSILON)
    return centered * inverse, inverse


def norm_back(grad, normal, inverse, gain):
    scaled = grad * gain
    first = jnp.mean(scaled, axis=-1, keepdims=True)
    second = jnp.mean(scaled * normal, axis=-1, keepdims=True)
    return inverse * (scaled - first - normal * second)


def row_docs(positions, lengths):
    doc_ends = jnp.cumsum(lengths)
    return jnp.sum((positions[:, None] >= doc_ends[None, :]).astype(jnp.int32), axis=1)


def dot(left, right):
    return jnp.dot(left, right, preferred_element_type=F32)


def dot_tn(left, right):
    return lax.dot_general(left, right, (((0,), (0,)), ((), ())), preferred_element_type=F32)


def dot_nt(left, right):
    return lax.dot_general(left, right, (((1,), (1,)), ((), ())), preferred_element_type=F32)


def shards(
    tokens,
    doc_lengths,
    attn_gain,
    attn_shift,
    qkv_weight,
    query_bias,
    value_bias,
    out_weight,
    out_bias,
    mlp_gain,
    mlp_shift,
    up_weight,
    up_bias,
    down_weight,
    down_bias,
    cotangent,
):
    n_f, n_z, n_c = lax.axis_size("fsdp"), lax.axis_size("zz"), lax.axis_size("core")
    f, z, c = lax.axis_index("fsdp"), lax.axis_index("zz"), lax.axis_index("core")
    n_p = n_f * n_c
    tokens_in = tokens[0].astype(F32)
    lengths = doc_lengths[0]
    grad_out = cotangent[0]
    rows, width = tokens_in.shape
    head = value_bias.shape[0] * n_f
    hidden = up_weight.shape[1]
    own_q = width // n_p
    own_h = hidden // n_p
    scale = 1.0 / math.sqrt(head)

    smalls = (attn_gain, attn_shift, query_bias, out_bias, mlp_gain, mlp_shift, down_bias, up_bias, value_bias)
    packed = lax.all_gather(jnp.concatenate(smalls), "fsdp")
    wide, at = [], 0
    for item in smalls:
        size = item.shape[0]
        wide.append(packed[:, at : at + size].reshape(-1).astype(F32))
        at += size
    gain_one, shift_one, bias_q, bias_out, gain_two, shift_two, bias_down, bias_up, bias_v = wide
    plane_at = f * n_c + c
    bias_q_own = lax.dynamic_slice_in_dim(bias_q, plane_at * own_q, own_q)
    bias_up_own = lax.dynamic_slice_in_dim(bias_up, plane_at * own_h, own_h)

    def own_columns(weight, size):
        local = weight.reshape(weight.shape[0], n_f, n_c, size)
        local = lax.dynamic_index_in_dim(local, c, axis=2, keepdims=False)
        swapped = lax.all_to_all(local, "fsdp", split_axis=1, concat_axis=0, tiled=True)
        return swapped.reshape(width, size)

    w_q = own_columns(qkv_weight[:, :width], own_q)
    w_kv = lax.all_gather(qkv_weight[:, width:], "fsdp", axis=0, tiled=True)
    w_up = own_columns(up_weight, own_h)
    w_out = lax.dynamic_slice_in_dim(out_weight, c * own_q, own_q, axis=0)
    w_down = lax.dynamic_slice_in_dim(down_weight, c * own_h, own_h, axis=0)

    def plane_gather(block):
        return lax.all_gather(block, PLANE, axis=0, tiled=True)

    def plane_scatter(partial):
        return lax.psum_scatter(
            partial.astype(BF16), PLANE, scatter_dimension=0, tiled=True
        ).astype(F32)

    def to_rows(block):
        return lax.all_to_all(block, PLANE, split_axis=0, concat_axis=1, tiled=True)

    def to_heads(block):
        return lax.all_to_all(block, PLANE, split_axis=1, concat_axis=0, tiled=True)

    normal_one, inverse_one = norm_parts(tokens_in)
    normed = (normal_one * gain_one + shift_one).astype(BF16)
    normed_pl = plane_gather(normed)
    grad_pl = plane_gather(grad_out)
    query_own = (dot(normed_pl, w_q) + bias_q_own).astype(BF16)
    keyval = dot(normed, w_kv)
    keyval = jnp.concatenate([keyval[:, :head], keyval[:, head:] + bias_v], axis=1).astype(BF16)
    keyval_all = lax.all_gather(keyval, COLUMN, axis=0, tiled=True)
    keys, values = keyval_all[:, :head], keyval_all[:, head:]
    query = to_rows(query_own)
    n_heads = width // head
    query_h = query.reshape(rows, n_heads, head).transpose(1, 0, 2)
    key_pos = jnp.arange(keys.shape[0], dtype=jnp.int32)
    positions = (z * n_c + c) * rows + jnp.arange(rows, dtype=jnp.int32)
    allowed = (row_docs(positions, lengths)[:, None] == row_docs(key_pos, lengths)[None, :]) & (
        positions[:, None] >= key_pos[None, :]
    )
    scores = jnp.einsum("hqd,kd->hqk", query_h, keys, preferred_element_type=F32) * scale
    scores = jnp.where(allowed[None], scores, -1e30)
    weights = jnp.exp(scores - jnp.max(scores, axis=-1, keepdims=True))
    probs = weights / jnp.sum(weights, axis=-1, keepdims=True)
    probs_low = probs.astype(BF16)
    mixed_h = jnp.einsum("hqk,kd->hqd", probs_low, values, preferred_element_type=F32).astype(BF16)
    mixed_own = to_heads(mixed_h.transpose(1, 0, 2).reshape(rows, width))
    branch = plane_scatter(dot(mixed_own, w_out)) + bias_out
    residual = tokens_in + branch

    normal_two, inverse_two = norm_parts(residual)
    normed_mlp = (normal_two * gain_two + shift_two).astype(BF16)
    normed_mlp_pl = plane_gather(normed_mlp)
    inner = dot(normed_mlp_pl, w_up) + bias_up_own
    activated, gelu_back = jax.vjp(lambda v: jax.nn.gelu(v, approximate=True), inner)
    activated = activated.astype(BF16)
    layer_out = residual + plane_scatter(dot(activated, w_down)) + bias_down
    d_act = dot_nt(grad_pl, w_down)
    d_inner = gelu_back(d_act)[0].astype(BF16)
    e_two = plane_scatter(dot_nt(d_inner, w_up))
    g_down = dot_tn(activated, grad_pl)
    g_up = dot_tn(normed_mlp_pl, d_inner)
    d_residual = grad_out.astype(F32) + norm_back(e_two, normal_two, inverse_two, gain_two)

    d_branch = d_residual.astype(BF16)
    d_branch_pl = plane_gather(d_branch)
    d_mixed = to_rows(dot_nt(d_branch_pl, w_out).astype(BF16))
    g_out = dot_tn(mixed_own, d_branch_pl)
    d_mixed_h = d_mixed.reshape(rows, n_heads, head).transpose(1, 0, 2)
    d_probs = jnp.einsum("hqd,kd->hqk", d_mixed_h, values, preferred_element_type=F32)
    delta = jnp.sum(probs * d_probs, axis=-1, keepdims=True)
    d_scores = (probs * (d_probs - delta)).astype(BF16)
    d_query_h = (
        jnp.einsum("hqk,kd->hqd", d_scores, keys, preferred_element_type=F32) * scale
    ).astype(BF16)
    d_keys = jnp.einsum("hqk,hqd->kd", d_scores, query_h, preferred_element_type=F32) * scale
    d_values = jnp.einsum("hqk,hqd->kd", probs_low, d_mixed_h, preferred_element_type=F32)
    d_kv = lax.psum_scatter(
        jnp.concatenate([d_keys, d_values], axis=1), COLUMN, scatter_dimension=0, tiled=True
    ).astype(BF16)
    d_query = d_query_h.transpose(1, 0, 2).reshape(rows, width)
    d_query_own = to_heads(d_query)
    d_kv_pl = plane_gather(d_kv)
    g_q = dot_tn(normed_pl, d_query_own)
    normed_cols = lax.dynamic_slice_in_dim(normed_pl, plane_at * own_q, own_q, axis=1)
    g_kv = dot_tn(normed_cols, d_kv_pl)
    e_one = plane_scatter(dot_nt(d_query_own, w_q)) + dot_nt(d_kv, w_kv)
    grad_tokens = d_residual + norm_back(e_one, normal_one, inverse_one, gain_one)

    def reduce_z(block):
        return lax.psum(block.astype(BF16), "zz")

    def rows_home(block):
        pieces = lax.all_gather(reduce_z(block), "core", axis=0, tiled=True)
        return pieces.astype(F32)

    def columns_home(block):
        moved = lax.all_to_all(
            reduce_z(block), "fsdp", split_axis=0, concat_axis=0, tiled=True
        ).reshape(n_f, width // n_f, block.shape[1])
        both = lax.all_gather(moved, "core", axis=0)
        return both.transpose(2, 1, 0, 3).reshape(width // n_f, n_p * block.shape[1]).astype(F32)

    grad_down = rows_home(g_down)
    grad_up = columns_home(g_up)
    grad_out_w = rows_home(g_out)
    grad_qkv = jnp.concatenate([columns_home(g_q), rows_home(g_kv)], axis=1)

    d_inner_f = d_inner.astype(F32)
    up_sum = lax.dynamic_update_slice_in_dim(
        jnp.zeros((hidden,), F32), jnp.sum(d_inner_f, axis=0), plane_at * own_h, axis=0
    )
    vectors = (
        jnp.sum(e_one * normal_one, axis=0),
        jnp.sum(e_one, axis=0),
        jnp.sum(d_query.astype(F32), axis=0),
        jnp.sum(d_kv[:, head:].astype(F32), axis=0),
        jnp.sum(d_branch.astype(F32), axis=0),
        jnp.sum(e_two * normal_two, axis=0),
        jnp.sum(e_two, axis=0),
        up_sum,
        jnp.sum(grad_out.astype(F32), axis=0),
    )
    total = lax.psum(jnp.concatenate(vectors), ("fsdp", "zz", "core"))
    small, at = [], 0
    for item in vectors:
        size = item.shape[0] // n_f
        small.append(lax.dynamic_slice_in_dim(total, at + f * size, size))
        at += item.shape[0]
    return (
        layer_out.astype(BF16)[None],
        grad_tokens.astype(BF16)[None],
        small[0],
        small[1],
        grad_qkv,
        small[2],
        small[3],
        grad_out_w,
        small[4],
        small[5],
        small[6],
        grad_up,
        small[7],
        grad_down,
        small[8],
    )


def solution(mesh):
    n_f, n_s = mesh.shape["fsdp"], mesh.shape["seq"]
    split = Mesh(mesh.devices.reshape(n_f, n_s // 2, 2), ("fsdp", "zz", "core"))
    act = P("fsdp", ("zz", "core"), None)
    vec = P("fsdp")
    mat = P("fsdp", None)
    return jax.shard_map(
        shards,
        mesh=split,
        in_specs=(act, mat, vec, vec, mat, vec, vec, mat, vec, vec, vec, mat, vec, mat, vec, act),
        out_specs=(act, act, vec, vec, mat, vec, vec, mat, vec, vec, vec, mat, vec, mat, vec),
        check_vma=False,
    )
```

```python
import functools
import math

import jax
import jax.numpy as jnp
from jax import lax
from jax.experimental import pallas as pl
from jax.experimental.pallas import tpu as pltpu
from jax.sharding import Mesh
from jax.sharding import PartitionSpec as P

EPSILON = 1e-05
F32 = jnp.float32
BF16 = jnp.bfloat16
MESH = pl.DeviceIdType.MESH
VMEM = pltpu.VMEM
DMA = pltpu.SemaphoreType.DMA
ON_CHIP = pl.BlockSpec(memory_space=pltpu.VMEM)
ANYWHERE = pl.BlockSpec(memory_space=pl.ANY)
LANES = 128


def flip(index, offset, bits):
    for bit in range(bits):
        if offset >> bit & 1:
            index = index + (1 << bit) * (1 - 2 * ((index // (1 << bit)) % 2))
    return index


def bit_orders(n_f):
    bits = n_f.bit_length() - 1
    assert 1 << bits == n_f
    turns = min(bits, 2)
    return bits, [[(turn + at) % bits for at in range(bits)] for turn in range(turns)]


def greet(targets):
    barrier = pltpu.get_barrier_semaphore()
    for target in targets:
        pl.semaphore_signal(barrier, inc=1, device_id=target, device_id_type=MESH)
    pl.semaphore_wait(barrier, len(targets))


def plane_peers(n_f, f, c):
    bits = n_f.bit_length() - 1
    peers = []
    for offset in range(n_f):
        for other in range(2):
            if offset or other:
                peers.append(
                    (offset * 2 + other, {"fsdp": flip(f, offset, bits), "core": c + other * (1 - 2 * c)})
                )
    return peers


def column_peers(n_z, z, c):
    peers = []
    for offset in range(n_z):
        for other in range(2):
            if offset or other:
                peers.append(
                    (offset * 2 + other, {"zz": (z + offset) % n_z, "core": c + other * (1 - 2 * c)})
                )
    return peers


def remote(source, target, send, recv, device):
    return pltpu.make_async_remote_copy(
        src_ref=source,
        dst_ref=target,
        send_sem=send,
        recv_sem=recv,
        device_id=device,
        device_id_type=MESH,
    )


def gather_body(n_f, x_ref, out_ref, send, recv, core_send, core_recv, local_sem):
    f, c = lax.axis_index("fsdp"), lax.axis_index("core")
    rows = x_ref.shape[0]
    bits, orders = bit_orders(n_f)
    part = rows // len(orders)
    greet([{"fsdp": flip(f, 1 << bit, bits)} for bit in range(bits)] + [{"core": 1 - c}])

    def slot(offset):
        return flip(f, offset, bits) * 2 + c

    def piece(turn, offset):
        return out_ref.at[slot(offset), pl.ds(turn * part, part)]

    def link(turn, offset, bit):
        source = x_ref.at[pl.ds(turn * part, part)] if offset == 0 else piece(turn, offset)
        sem = turn * n_f + (offset ^ (1 << bit))
        return remote(
            source,
            piece(turn, offset),
            send.at[sem],
            recv.at[sem],
            {"fsdp": flip(f, 1 << bit, bits)},
        )

    def arrival(turn, offset):
        sem = turn * n_f + offset
        return remote(
            piece(turn, offset), piece(turn, offset), send.at[sem], recv.at[sem], {"core": 1 - c}
        )

    def across(turn, offset):
        source = x_ref.at[pl.ds(turn * part, part)] if offset == 0 else piece(turn, offset)
        sem = turn * n_f + offset
        return remote(
            source, piece(turn, offset), core_send.at[sem], core_recv.at[sem], {"core": 1 - c}
        )

    def crossing(turn, offset):
        where = out_ref.at[flip(f, offset, bits) * 2 + 1 - c, pl.ds(turn * part, part)]
        sem = turn * n_f + offset
        return remote(where, where, core_send.at[sem], core_recv.at[sem], {"core": 1 - c})

    started = []

    def go(copy):
        copy.start()
        started.append(copy)

    for step in range(bits):
        for turn, order in enumerate(orders):
            go(link(turn, 0, order[step]))
    for turn in range(len(orders)):
        go(across(turn, 0))
    own = pltpu.make_async_copy(x_ref, out_ref.at[slot(0)], local_sem)
    own.start()
    have = [[0] for _ in orders]
    for step in range(bits):
        for at in range(1 << step):
            for turn, order in enumerate(orders):
                offset = have[turn][at] ^ (1 << order[step])
                arrival(turn, offset).wait_recv()
                for later in range(step + 1, bits):
                    go(link(turn, offset, order[later]))
                go(across(turn, offset))
                have[turn].append(offset)
    for copy in started:
        copy.wait_send()
    for turn in range(len(orders)):
        for offset in have[turn]:
            crossing(turn, offset).wait_recv()
    own.wait()


def plane_gather(x, n_f, ident):
    rows, width = x.shape
    count = len(bit_orders(n_f)[1]) * n_f
    out = pl.pallas_call(
        functools.partial(gather_body, n_f),
        out_shape=jax.ShapeDtypeStruct((n_f * 2, rows, width), x.dtype),
        in_specs=[ON_CHIP],
        out_specs=ON_CHIP,
        scratch_shapes=[DMA((count,))] * 4 + [DMA],
        compiler_params=pltpu.CompilerParams(
            collective_id=ident, has_side_effects=True, vmem_limit_bytes=40 << 20
        ),
        name="plane_gather",
    )(x)
    return out.reshape(n_f * 2 * rows, width)


def scatter_body(n_f, part_ref, out_ref, acc, core_in, link_in, send, recv, core_send, core_recv):
    f, c = lax.axis_index("fsdp"), lax.axis_index("core")
    rows = out_ref.shape[0]
    bits, orders = bit_orders(n_f)
    part = rows // len(orders)
    greet([{"fsdp": flip(f, 1 << bit, bits)} for bit in range(bits)] + [{"core": 1 - c}])
    started = []

    def go(copy):
        copy.start()
        started.append(copy)

    def across(turn, offset):
        where = pl.ds(turn * part, part)
        sem = turn * n_f + offset
        return remote(
            part_ref.at[flip(f, offset, bits) * 2 + 1 - c, where],
            core_in.at[offset, where],
            core_send.at[sem],
            core_recv.at[sem],
            {"core": 1 - c},
        )

    def link(turn, offset, bit):
        where = pl.ds(turn * part, part)
        sem = turn * n_f + offset
        return remote(
            acc.at[offset, where],
            link_in.at[offset, where],
            send.at[sem],
            recv.at[sem],
            {"fsdp": flip(f, 1 << bit, bits)},
        )

    plan = [[] for _ in range(bits)] + [[(turn, 0) for turn in range(len(orders))]]
    for step in range(bits):
        for offset in range(n_f):
            for turn, order in enumerate(orders):
                if offset >> order[step] & 1 and not any(offset >> b & 1 for b in order[:step]):
                    plan[step].append((turn, offset))
    for todo in plan:
        for turn, offset in todo:
            go(across(turn, offset))
    for step, todo in enumerate(plan):
        for turn, offset in todo:
            where = pl.ds(turn * part, part)
            across(turn, offset).wait_recv()
            total = part_ref[flip(f, offset, bits) * 2 + c, where].astype(F32)
            total = total + core_in[offset, where].astype(F32)
            for bit in orders[turn][:step]:
                link(turn, offset | (1 << bit), bit).wait_recv()
                total = total + link_in[offset | (1 << bit), where].astype(F32)
            if offset:
                acc[offset, where] = total.astype(BF16)
                go(link(turn, offset, orders[turn][step]))
            else:
                out_ref[where] = total
    for copy in started:
        copy.wait_send()


def plane_scatter(partial, n_f, ident):
    width = partial.shape[1]
    rows = partial.shape[0] // (n_f * 2)
    count = len(bit_orders(n_f)[1]) * n_f
    return pl.pallas_call(
        functools.partial(scatter_body, n_f),
        out_shape=jax.ShapeDtypeStruct((rows, width), F32),
        in_specs=[ON_CHIP],
        out_specs=ON_CHIP,
        scratch_shapes=[VMEM((n_f, rows, width), BF16)] * 3 + [DMA((count,))] * 4,
        compiler_params=pltpu.CompilerParams(
            collective_id=ident, has_side_effects=True, vmem_limit_bytes=40 << 20
        ),
        name="plane_scatter",
    )(partial.astype(BF16).reshape(n_f * 2, rows, width))


def exchange_body(n_f, n_z, plane_in, column_in, plane_out, column_out, sems, whole):
    f, z, c = lax.axis_index("fsdp"), lax.axis_index("zz"), lax.axis_index("core")
    peers = plane_peers(n_f, f, c)
    others = column_peers(n_z, z, c) if column_in is not None else []
    greet([device for _, device in peers] + [device for _, device in others])
    copies = []
    local = []
    if column_in is not None:
        mine = z * 2 + c
        for sem, device in others:
            to = device["zz"] * 2 + device["core"]
            source = column_in if whole else column_in.at[to]
            copies.append(
                remote(source, column_out.at[mine], sems[2].at[sem], sems[3].at[sem], device)
            )
        source = column_in if whole else column_in.at[mine]
        local.append(pltpu.make_async_copy(source, column_out.at[mine], sems[5]))
    mine = f * 2 + c
    for sem, device in peers:
        to = device["fsdp"] * 2 + device["core"]
        copies.append(
            remote(plane_in.at[to], plane_out.at[mine], sems[0].at[sem], sems[1].at[sem], device)
        )
    local.append(pltpu.make_async_copy(plane_in.at[mine], plane_out.at[mine], sems[4]))
    for copy in copies + local:
        copy.start()
    for copy in copies:
        copy.wait_send()
    for sem, device in peers:
        frm = device["fsdp"] * 2 + device["core"]
        remote(
            plane_out.at[frm], plane_out.at[frm], sems[0].at[sem], sems[1].at[sem], device
        ).wait_recv()
    if column_in is not None:
        for offset in range(n_z):
            for other in range(2):
                if offset or other:
                    frm = ((z + n_z - offset) % n_z) * 2 + c + other * (1 - 2 * c)
                    sem = offset * 2 + other
                    remote(
                        column_out.at[frm],
                        column_out.at[frm],
                        sems[2].at[sem],
                        sems[3].at[sem],
                        {"core": 1 - c},
                    ).wait_recv()
    for copy in local:
        copy.wait()


def exchange(plane_in, column_in, n_f, n_z, ident, whole=False):
    outs = [jax.ShapeDtypeStruct(plane_in.shape, plane_in.dtype)]
    ins = [plane_in]
    if column_in is not None:
        block = column_in.shape if whole else column_in.shape[1:]
        outs.append(jax.ShapeDtypeStruct((n_z * 2,) + block, column_in.dtype))
        ins.append(column_in)

    def body(*refs):
        if column_in is None:
            plane_ref, plane_out = refs[:2]
            exchange_body(n_f, n_z, plane_ref, None, plane_out, None, refs[2:], whole)
        else:
            plane_ref, column_ref, plane_out, column_out = refs[:4]
            exchange_body(
                n_f, n_z, plane_ref, column_ref, plane_out, column_out, refs[4:], whole
            )

    result = pl.pallas_call(
        body,
        out_shape=outs,
        in_specs=[ON_CHIP] * len(ins),
        out_specs=[ON_CHIP] * len(outs),
        scratch_shapes=[DMA((n_f * 2,))] * 2 + [DMA((n_z * 2,))] * 2 + [DMA] * 2,
        compiler_params=pltpu.CompilerParams(
            collective_id=ident, has_side_effects=True, vmem_limit_bytes=24 << 20
        ),
        name="exchange",
    )(*ins)
    return result if column_in is not None else result[0]


def line_body(n_z, count, refs):
    grads, finals, ups, downs = (refs[at * count : (at + 1) * count] for at in range(4))
    sems = refs[4 * count :]
    red_send, up_recv, down_recv, fin_send, fin_recv, more_send = sems
    z = lax.axis_index("zz")
    root = (n_z - 1) // 2
    barrier = pltpu.get_barrier_semaphore()
    for step in (1, -1):

        @pl.when((z + step >= 0) & (z + step < n_z))
        def _():
            pl.semaphore_signal(
                barrier, inc=1, device_id={"zz": z + step}, device_id_type=MESH
            )

    @pl.when((z == 0) | (z == n_z - 1))
    def _():
        pl.semaphore_wait(barrier, 1)

    @pl.when((z > 0) & (z < n_z - 1))
    def _():
        pl.semaphore_wait(barrier, 2)

    base = [0]
    for ref in grads:
        base.append(base[-1] + ref.shape[0])

    def up(tensor, k, source):
        sem = base[tensor] + k
        return remote(
            source, ups[tensor].at[k], red_send.at[sem], up_recv.at[sem], {"zz": z + 1}
        )

    def down(tensor, k, source):
        sem = base[tensor] + k
        return remote(
            source, downs[tensor].at[k], red_send.at[sem], down_recv.at[sem], {"zz": z - 1}
        )

    def spread(tensor, k, step, sends):
        sem = base[tensor] + k
        return remote(
            finals[tensor].at[k],
            finals[tensor].at[k],
            sends.at[sem],
            fin_recv.at[sem],
            {"zz": z + step},
        )

    def reduce_step(tensor, k):
        own = grads[tensor].at[k]

        @pl.when(z < root)
        def _():
            @pl.when(z == 0)
            def _():
                up(tensor, k, own).start()

            @pl.when(z > 0)
            def _():
                up(tensor, k, own).wait_recv()
                ups[tensor][k] = (
                    grads[tensor][k].astype(F32) + ups[tensor][k].astype(F32)
                ).astype(BF16)
                up(tensor, k, ups[tensor].at[k]).start()

        @pl.when(z > root)
        def _():
            @pl.when(z == n_z - 1)
            def _():
                down(tensor, k, own).start()

            @pl.when(z < n_z - 1)
            def _():
                down(tensor, k, own).wait_recv()
                downs[tensor][k] = (
                    grads[tensor][k].astype(F32) + downs[tensor][k].astype(F32)
                ).astype(BF16)
                down(tensor, k, downs[tensor].at[k]).start()

        @pl.when(z == root)
        def _():
            total = grads[tensor][k].astype(F32)
            if root > 0:
                up(tensor, k, own).wait_recv()
                total = total + ups[tensor][k].astype(F32)
            if root < n_z - 1:
                down(tensor, k, own).wait_recv()
                total = total + downs[tensor][k].astype(F32)
            finals[tensor][k] = total.astype(BF16)
            if root > 0:
                spread(tensor, k, -1, fin_send).start()
            if root < n_z - 1:
                spread(tensor, k, 1, more_send).start()

    def spread_step(tensor, k):
        @pl.when(z != root)
        def _():
            spread(tensor, k, 0, fin_send).wait_recv()

        @pl.when((z < root) & (z > 0))
        def _():
            spread(tensor, k, -1, fin_send).start()

        @pl.when((z > root) & (z < n_z - 1))
        def _():
            spread(tensor, k, 1, more_send).start()

    def finish(tensor, k):
        @pl.when(z < root)
        def _():
            up(tensor, k, grads[tensor].at[k]).wait_send()

        @pl.when(z > root)
        def _():
            down(tensor, k, grads[tensor].at[k]).wait_send()

        if root > 0:

            @pl.when((z <= root) & (z > 0))
            def _():
                spread(tensor, k, -1, fin_send).wait_send()

        if root < n_z - 1:

            @pl.when((z >= root) & (z < n_z - 1))
            def _():
                spread(tensor, k, 1, more_send).wait_send()

    lag = 4
    for tensor in range(count):
        chunks = grads[tensor].shape[0]

        @pl.loop(0, chunks)
        def _(k):
            reduce_step(tensor, k)
            if chunks > lag:

                @pl.when(k >= lag)
                def _():
                    spread_step(tensor, k - lag)

        @pl.loop(max(chunks - lag, 0), chunks)
        def _(k):
            spread_step(tensor, k)

    for tensor in range(count):

        @pl.loop(0, grads[tensor].shape[0])
        def _(k):
            finish(tensor, k)


def line_sum(grads, n_z, ident):
    count = len(grads)
    chunks = sum(item.shape[0] for item in grads)

    def body(*refs):
        line_body(n_z, count, refs)

    return pl.pallas_call(
        body,
        out_shape=[jax.ShapeDtypeStruct(item.shape, BF16) for item in grads],
        in_specs=[ON_CHIP] * count,
        out_specs=[ON_CHIP] * count,
        scratch_shapes=[VMEM(item.shape, BF16) for item in grads] * 2 + [DMA((chunks,))] * 6,
        compiler_params=pltpu.CompilerParams(
            collective_id=ident, has_side_effects=True, vmem_limit_bytes=60 << 20
        ),
        name="line_sum",
    )(*grads)


def home_body(n_f, down, up, outw, query, kv, down_o, up_o, out_o, query_o, kv_o, *sems):
    f, c = lax.axis_index("fsdp"), lax.axis_index("core")
    bits = n_f.bit_length() - 1
    send, recv, core_send, core_recv, local_sem = sems
    greet([{"fsdp": flip(f, offset, bits)} for offset in range(1, n_f)] + [{"core": 1 - c}])
    pair = [(down, down_o), (outw, out_o), (kv, kv_o)]
    split = [(up, up_o), (query, query_o)]
    started, local = [], []

    def go(copy):
        copy.start()
        started.append(copy)

    def cols(ref, source, tensor):
        width = split[tensor][0].shape[1]
        return ref.at[:, pl.ds(pl.multiple_of(source * width, LANES), width)]

    def rows(tensor, to):
        source = split[tensor][0]
        height = source.shape[0] // n_f
        return source.at[pl.ds(to * height, height)]

    def link(tensor, offset):
        to = flip(f, offset, bits)
        sem = tensor * n_f + offset
        return remote(
            rows(tensor, to),
            cols(split[tensor][1], f * 2 + c, tensor),
            send.at[sem],
            recv.at[sem],
            {"fsdp": to},
        )

    def arrival(tensor, offset):
        where = cols(split[tensor][1], flip(f, offset, bits) * 2 + c, tensor)
        sem = tensor * n_f + offset
        return remote(where, where, send.at[sem], recv.at[sem], {"core": 1 - c})

    def across(tensor, offset, side):
        where = cols(split[tensor][1], flip(f, offset, bits) * 2 + side, tensor)
        sem = tensor * n_f + offset
        source = rows(tensor, f) if offset == 0 else where
        return remote(source, where, core_send.at[sem], core_recv.at[sem], {"core": 1 - c})

    def swap(at, side):
        sem = 2 * n_f + at
        return remote(
            pair[at][0], pair[at][1].at[side], core_send.at[sem], core_recv.at[sem], {"core": 1 - c}
        )

    for tensor in range(2):
        for offset in range(1, n_f):
            go(link(tensor, offset))
    for at, (source, target) in enumerate(pair):
        go(swap(at, c))
        local.append(pltpu.make_async_copy(source, target.at[c], local_sem.at[at]))
    for tensor in range(2):
        go(across(tensor, 0, c))
        local.append(
            pltpu.make_async_copy(
                rows(tensor, f), cols(split[tensor][1], f * 2 + c, tensor), local_sem.at[3 + tensor]
            )
        )
    for copy in local:
        copy.start()
    for offset in range(1, n_f):
        for tensor in range(2):
            arrival(tensor, offset).wait_recv()
            go(across(tensor, offset, c))
    for copy in started:
        copy.wait_send()
    for at in range(3):
        swap(at, 1 - c).wait_recv()
    for tensor in range(2):
        for offset in range(n_f):
            across(tensor, offset, 1 - c).wait_recv()
    for copy in local:
        copy.wait()


def home(down, up, outw, query, kv, n_f, ident):
    shapes = [
        (2,) + down.shape,
        (up.shape[0] // n_f, up.shape[1] * n_f * 2),
        (2,) + outw.shape,
        (query.shape[0] // n_f, query.shape[1] * n_f * 2),
        (2,) + kv.shape,
    ]
    return pl.pallas_call(
        functools.partial(home_body, n_f),
        out_shape=[jax.ShapeDtypeStruct(shape, BF16) for shape in shapes],
        in_specs=[ON_CHIP] * 5,
        out_specs=[ON_CHIP] * 5,
        scratch_shapes=[DMA((2 * n_f,))] * 2 + [DMA((2 * n_f + 3,))] * 2 + [DMA((5,))],
        compiler_params=pltpu.CompilerParams(
            collective_id=ident, has_side_effects=True, vmem_limit_bytes=48 << 20
        ),
        name="grads_home",
    )(down, up, outw, query, kv)


def heads_side_by_side(block, head):
    count = block.shape[1] // head
    return jnp.concatenate([block[:, at * head : (at + 1) * head] for at in range(count)], axis=0)


def heads_apart(block, count):
    rows = block.shape[0] // count
    return jnp.concatenate([block[at * rows : (at + 1) * rows] for at in range(count)], axis=1)


def attend_body(head, scale, query_ref, kv_ref, mask_ref, mixed_ref, lse_ref):
    query = heads_side_by_side(query_ref[0], head)
    count = query_ref.shape[2] // head
    keys, values = kv_ref[:, :head], kv_ref[:, head:]
    mask = jnp.concatenate([mask_ref[...]] * count, axis=1)
    scores = dot_nt(keys, query) * scale + mask
    peak = jnp.max(scores, axis=0, keepdims=True)
    weights = jnp.exp(scores - peak)
    total = jnp.sum(weights, axis=0, keepdims=True)
    probs = (weights / total).astype(BF16)
    mixed_ref[0] = heads_apart(dot_tn(probs, values).astype(BF16), count)
    lse_ref[0] = peak + jnp.log(total)


def attend(query, kv, mask, head):
    n_p, rows, width = query.shape
    span = kv.shape[0]
    count = width // head
    return pl.pallas_call(
        functools.partial(attend_body, head, 1.0 / math.sqrt(head)),
        out_shape=[
            jax.ShapeDtypeStruct(query.shape, BF16),
            jax.ShapeDtypeStruct((n_p, 1, count * rows), F32),
        ],
        grid=(n_p,),
        in_specs=[
            pl.BlockSpec((1, rows, width), lambda p: (p, 0, 0)),
            pl.BlockSpec((span, 2 * head), lambda p: (0, 0)),
            pl.BlockSpec((span, rows), lambda p: (0, 0)),
        ],
        out_specs=[
            pl.BlockSpec((1, rows, width), lambda p: (p, 0, 0)),
            pl.BlockSpec((1, 1, count * rows), lambda p: (p, 0, 0)),
        ],
        name="attend",
    )(query, kv, mask)


def attend_back_body(head, scale, query_ref, grad_ref, kv_ref, mask_ref, lse_ref, dq_ref, dkv_ref):
    query = heads_side_by_side(query_ref[0], head)
    grad = heads_side_by_side(grad_ref[0], head)
    count = query_ref.shape[2] // head
    keys, values = kv_ref[:, :head], kv_ref[:, head:]
    mask = jnp.concatenate([mask_ref[...]] * count, axis=1)
    scores = dot_nt(keys, query) * scale + mask
    probs = jnp.exp(scores - lse_ref[0])
    d_probs = dot_nt(values, grad)
    delta = jnp.sum(probs * d_probs, axis=0, keepdims=True)
    d_scores = (probs * (d_probs - delta)).astype(BF16)
    dq_ref[0] = heads_apart((dot_tn(d_scores, keys) * scale).astype(BF16), count)
    d_keys = dot(d_scores, query) * scale
    d_values = dot(probs.astype(BF16), grad)

    @pl.when(pl.program_id(0) == 0)
    def _():
        dkv_ref[:, :head] = d_keys
        dkv_ref[:, head:] = d_values

    @pl.when(pl.program_id(0) > 0)
    def _():
        dkv_ref[:, :head] += d_keys
        dkv_ref[:, head:] += d_values


def attend_back(query, grad, kv, mask, lse, head):
    n_p, rows, width = query.shape
    span = kv.shape[0]
    count = width // head
    block = pl.BlockSpec((1, rows, width), lambda p: (p, 0, 0))
    return pl.pallas_call(
        functools.partial(attend_back_body, head, 1.0 / math.sqrt(head)),
        out_shape=[
            jax.ShapeDtypeStruct(query.shape, BF16),
            jax.ShapeDtypeStruct((span, 2 * head), F32),
        ],
        grid=(n_p,),
        in_specs=[
            block,
            block,
            pl.BlockSpec((span, 2 * head), lambda p: (0, 0)),
            pl.BlockSpec((span, rows), lambda p: (0, 0)),
            pl.BlockSpec((1, 1, count * rows), lambda p: (p, 0, 0)),
        ],
        out_specs=[block, pl.BlockSpec((span, 2 * head), lambda p: (0, 0))],
        name="attend_back",
    )(query, grad, kv, mask, lse)


def norm_parts(values_in):
    row_mean = jnp.mean(values_in, axis=-1, keepdims=True)
    centered = values_in - row_mean
    variance = jnp.mean(centered * centered, axis=-1, keepdims=True)
    inverse = lax.rsqrt(variance + EPSILON)
    return centered * inverse, inverse


def norm_back(grad, normal, inverse, gain):
    scaled = grad * gain
    first = jnp.mean(scaled, axis=-1, keepdims=True)
    second = jnp.mean(scaled * normal, axis=-1, keepdims=True)
    return inverse * (scaled - first - normal * second)


def row_docs(positions, lengths):
    doc_ends = jnp.cumsum(lengths)
    return jnp.sum((positions[:, None] >= doc_ends[None, :]).astype(jnp.int32), axis=1)


def dot(left, right):
    return jnp.dot(left, right, preferred_element_type=F32)


def dot_tn(left, right):
    return lax.dot_general(left, right, (((0,), (0,)), ((), ())), preferred_element_type=F32)


def dot_nt(left, right):
    return lax.dot_general(left, right, (((1,), (1,)), ((), ())), preferred_element_type=F32)


def shards(
    tokens,
    doc_lengths,
    attn_gain,
    attn_shift,
    qkv_weight,
    query_bias,
    value_bias,
    out_weight,
    out_bias,
    mlp_gain,
    mlp_shift,
    up_weight,
    up_bias,
    down_weight,
    down_bias,
    cotangent,
):
    n_f, n_z, n_c = lax.axis_size("fsdp"), lax.axis_size("zz"), lax.axis_size("core")
    f, z, c = lax.axis_index("fsdp"), lax.axis_index("zz"), lax.axis_index("core")
    n_p = n_f * n_c
    tokens_in = tokens[0].astype(F32)
    lengths = doc_lengths[0]
    grad_out = cotangent[0]
    rows, width = tokens_in.shape
    head = value_bias.shape[0] * n_f
    hidden = up_weight.shape[1]
    own_q = width // n_p
    own_h = hidden // n_p

    smalls = (attn_gain, attn_shift, query_bias, out_bias, mlp_gain, mlp_shift, down_bias, up_bias, value_bias)
    packed = lax.all_gather(jnp.concatenate(smalls), "fsdp")
    wide, at = [], 0
    for item in smalls:
        size = item.shape[0]
        wide.append(packed[:, at : at + size].reshape(-1).astype(F32))
        at += size
    gain_one, shift_one, bias_q, bias_out, gain_two, shift_two, bias_down, bias_up, bias_v = wide
    plane_at = f * n_c + c
    bias_q_own = lax.dynamic_slice_in_dim(bias_q, plane_at * own_q, own_q)
    bias_up_own = lax.dynamic_slice_in_dim(bias_up, plane_at * own_h, own_h)

    def own_columns(weight, size):
        pieces = []
        for offset in range(n_f):
            to = flip(f, offset, n_f.bit_length() - 1)
            block = lax.dynamic_slice_in_dim(weight, (to * n_c + c) * size, size, axis=1)
            if offset:
                block = lax.ppermute(block, "fsdp", [(i, i ^ offset) for i in range(n_f)])
            pieces.append(block)
        stacked = jnp.zeros((n_f, weight.shape[0], size), BF16)
        for offset in range(n_f):
            stacked = lax.dynamic_update_slice_in_dim(
                stacked, pieces[offset][None], flip(f, offset, n_f.bit_length() - 1), axis=0
            )
        return stacked.reshape(width, size)

    w_q = own_columns(qkv_weight[:, :width], own_q)
    w_kv = lax.all_gather(qkv_weight[:, width:], "fsdp", axis=0, tiled=True)
    w_up = own_columns(up_weight, own_h)
    w_out = lax.dynamic_slice_in_dim(out_weight, c * own_q, own_q, axis=0)
    w_down = lax.dynamic_slice_in_dim(down_weight, c * own_h, own_h, axis=0)

    normal_one, inverse_one = norm_parts(tokens_in)
    normed = (normal_one * gain_one + shift_one).astype(BF16)
    normed_pl = plane_gather(normed, n_f, 0)
    query_own = (dot(normed_pl, w_q) + bias_q_own).astype(BF16)
    keyval = dot(normed, w_kv)
    keyval = jnp.concatenate([keyval[:, :head], keyval[:, head:] + bias_v], axis=1).astype(BF16)
    query, keyval_all = exchange(
        query_own.reshape(n_p, rows, own_q), keyval, n_f, n_z, 1, whole=True
    )
    stream = n_z * n_c * rows
    span = min(stream, stream // 2 + rows)
    key_first = jnp.clip((z * n_c + c + 1) * rows - span, 0, stream - span)
    kv = lax.dynamic_slice_in_dim(keyval_all.reshape(stream, 2 * head), key_first, span, axis=0)
    key_pos = key_first + jnp.arange(span, dtype=jnp.int32)
    positions = (z * n_c + c) * rows + jnp.arange(rows, dtype=jnp.int32)
    allowed = (row_docs(key_pos, lengths)[:, None] == row_docs(positions, lengths)[None, :]) & (
        positions[None, :] >= key_pos[:, None]
    )
    mask = jnp.where(allowed, 0.0, -1e30).astype(F32)
    mixed, lse = attend(query, kv, mask, head)
    mixed_own = exchange(mixed, None, n_f, n_z, 2).reshape(n_p * rows, own_q)
    branch = plane_scatter(dot(mixed_own, w_out), n_f, 3) + bias_out
    residual = tokens_in + branch

    normal_two, inverse_two = norm_parts(residual)
    normed_mlp = (normal_two * gain_two + shift_two).astype(BF16)
    normed_mlp_pl = plane_gather(normed_mlp, n_f, 4)
    grad_pl = plane_gather(grad_out, n_f, 5)
    inner = dot(normed_mlp_pl, w_up) + bias_up_own
    activated, gelu_back = jax.vjp(lambda v: jax.nn.gelu(v, approximate=True), inner)
    activated = activated.astype(BF16)
    layer_out = residual + plane_scatter(dot(activated, w_down), n_f, 6) + bias_down
    d_act = dot_nt(grad_pl, w_down)
    d_inner = gelu_back(d_act)[0].astype(BF16)
    e_two = plane_scatter(dot_nt(d_inner, w_up), n_f, 7)
    g_down = dot_tn(activated, grad_pl).astype(BF16)
    g_up = dot_tn(normed_mlp_pl, d_inner).astype(BF16)
    d_residual = grad_out.astype(F32) + norm_back(e_two, normal_two, inverse_two, gain_two)

    d_branch = d_residual.astype(BF16)
    d_branch_pl = plane_gather(d_branch, n_f, 8)
    d_mixed = exchange(
        dot_nt(d_branch_pl, w_out).astype(BF16).reshape(n_p, rows, own_q), None, n_f, n_z, 9
    )
    g_out = dot_tn(mixed_own, d_branch_pl).astype(BF16)
    d_query, d_kv_span = attend_back(query, d_mixed, kv, mask, lse, head)
    d_kv_part = lax.dynamic_update_slice_in_dim(
        jnp.zeros((stream, 2 * head), BF16), d_kv_span.astype(BF16), key_first, axis=0
    )
    d_query_own, d_kv_parts = exchange(
        d_query, d_kv_part.reshape(n_z * n_c, rows, 2 * head), n_f, n_z, 10
    )
    d_query_own = d_query_own.reshape(n_p * rows, own_q)
    d_kv = jnp.sum(d_kv_parts.astype(F32), axis=0).astype(BF16)
    e_one = plane_scatter(dot_nt(d_query_own, w_q), n_f, 11) + dot_nt(d_kv, w_kv)
    d_kv_pl = plane_gather(d_kv, n_f, 12)
    g_q = dot_tn(normed_pl, d_query_own).astype(BF16)
    normed_cols = lax.dynamic_slice_in_dim(normed_pl, plane_at * own_q, own_q, axis=1)
    g_kv = dot_tn(normed_cols, d_kv_pl).astype(BF16)
    grad_tokens = d_residual + norm_back(e_one, normal_one, inverse_one, gain_one)

    def chunked(block):
        height = max(16, (1 << 17) // block.shape[1])
        height = min(height, block.shape[0])
        return block.reshape(block.shape[0] // height, height, block.shape[1])

    pieces = (g_down, g_up, g_out, g_q, g_kv)
    summed = line_sum([chunked(item) for item in pieces], n_z, 13)
    summed = [item.reshape(like.shape) for item, like in zip(summed, pieces)]
    h_down, h_up, h_out, h_q, h_kv = home(*summed, n_f, 14)
    grad_down = h_down.reshape(n_c * own_h, width).astype(F32)
    grad_out_w = h_out.reshape(n_c * own_q, width).astype(F32)
    grad_qkv = jnp.concatenate([h_q, h_kv.reshape(n_c * own_q, 2 * head)], axis=1).astype(F32)

    up_sum = lax.dynamic_update_slice_in_dim(
        jnp.zeros((hidden,), F32), jnp.sum(d_inner.astype(F32), axis=0), plane_at * own_h, axis=0
    )
    vectors = (
        jnp.sum(e_one * normal_one, axis=0),
        jnp.sum(e_one, axis=0),
        jnp.sum(d_query.astype(F32), axis=1).reshape(-1),
        jnp.sum(d_kv[:, head:].astype(F32), axis=0),
        jnp.sum(d_branch.astype(F32), axis=0),
        jnp.sum(e_two * normal_two, axis=0),
        jnp.sum(e_two, axis=0),
        up_sum,
        jnp.sum(grad_out.astype(F32), axis=0),
    )
    total = lax.psum(jnp.concatenate(vectors), ("fsdp", "zz", "core"))
    small, at = [], 0
    for item in vectors:
        size = item.shape[0] // n_f
        small.append(lax.dynamic_slice_in_dim(total, at + f * size, size))
        at += item.shape[0]
    return (
        layer_out.astype(BF16)[None],
        grad_tokens.astype(BF16)[None],
        small[0],
        small[1],
        grad_qkv,
        small[2],
        small[3],
        grad_out_w,
        small[4],
        small[5],
        small[6],
        h_up.astype(F32),
        small[7],
        grad_down,
        small[8],
    )


def solution(mesh):
    n_f, n_s = mesh.shape["fsdp"], mesh.shape["seq"]
    split = Mesh(mesh.devices.reshape(n_f, n_s // 2, 2), ("fsdp", "zz", "core"))
    act = P("fsdp", ("zz", "core"), None)
    vec = P("fsdp")
    mat = P("fsdp", None)
    return jax.shard_map(
        shards,
        mesh=split,
        in_specs=(act, mat, vec, vec, mat, vec, vec, mat, vec, vec, vec, mat, vec, mat, vec, act),
        out_specs=(act, act, vec, vec, mat, vec, vec, mat, vec, vec, vec, mat, vec, mat, vec),
        check_vma=False,
    )
```

```python
import functools
import math

import jax
import jax.numpy as jnp
from jax import lax
from jax.experimental import pallas as pl
from jax.experimental.pallas import tpu as pltpu
from jax.sharding import Mesh
from jax.sharding import PartitionSpec as P

EPSILON = 1e-05
F32 = jnp.float32
BF16 = jnp.bfloat16
MESH = pl.DeviceIdType.MESH
VMEM = pltpu.VMEM
DMA = pltpu.SemaphoreType.DMA
ON_CHIP = pl.BlockSpec(memory_space=pltpu.VMEM)
ANYWHERE = pl.BlockSpec(memory_space=pl.ANY)
LANES = 128


def flip(index, offset, bits):
    for bit in range(bits):
        if offset >> bit & 1:
            index = index + (1 << bit) * (1 - 2 * ((index // (1 << bit)) % 2))
    return index


def bit_orders(n_f):
    bits = n_f.bit_length() - 1
    assert 1 << bits == n_f
    turns = min(bits, 2)
    return bits, [[(turn + at) % bits for at in range(bits)] for turn in range(turns)]


def greet(targets):
    barrier = pltpu.get_barrier_semaphore()
    for target in targets:
        pl.semaphore_signal(barrier, inc=1, device_id=target, device_id_type=MESH)
    pl.semaphore_wait(barrier, len(targets))


def plane_peers(n_f, f, c):
    bits = n_f.bit_length() - 1
    peers = []
    for offset in range(n_f):
        for other in range(2):
            if offset or other:
                peers.append(
                    (offset * 2 + other, {"fsdp": flip(f, offset, bits), "core": c + other * (1 - 2 * c)})
                )
    return peers


def column_peers(n_z, z, c):
    peers = []
    for offset in range(n_z):
        for other in range(2):
            if offset or other:
                peers.append(
                    (offset * 2 + other, {"zz": (z + offset) % n_z, "core": c + other * (1 - 2 * c)})
                )
    return peers


def remote(source, target, send, recv, device):
    return pltpu.make_async_remote_copy(
        src_ref=source,
        dst_ref=target,
        send_sem=send,
        recv_sem=recv,
        device_id=device,
        device_id_type=MESH,
    )


def gather_body(n_f, x_ref, out_ref, send, recv, core_send, core_recv, local_sem):
    f, c = lax.axis_index("fsdp"), lax.axis_index("core")
    rows = x_ref.shape[0]
    bits, orders = bit_orders(n_f)
    part = rows // len(orders)
    greet([{"fsdp": flip(f, 1 << bit, bits)} for bit in range(bits)] + [{"core": 1 - c}])

    def slot(offset):
        return flip(f, offset, bits) * 2 + c

    def piece(turn, offset):
        return out_ref.at[slot(offset), pl.ds(turn * part, part)]

    def link(turn, offset, bit):
        source = x_ref.at[pl.ds(turn * part, part)] if offset == 0 else piece(turn, offset)
        sem = turn * n_f + (offset ^ (1 << bit))
        return remote(
            source,
            piece(turn, offset),
            send.at[sem],
            recv.at[sem],
            {"fsdp": flip(f, 1 << bit, bits)},
        )

    def arrival(turn, offset):
        sem = turn * n_f + offset
        return remote(
            piece(turn, offset), piece(turn, offset), send.at[sem], recv.at[sem], {"core": 1 - c}
        )

    def across(turn, offset):
        source = x_ref.at[pl.ds(turn * part, part)] if offset == 0 else piece(turn, offset)
        sem = turn * n_f + offset
        return remote(
            source, piece(turn, offset), core_send.at[sem], core_recv.at[sem], {"core": 1 - c}
        )

    def crossing(turn, offset):
        where = out_ref.at[flip(f, offset, bits) * 2 + 1 - c, pl.ds(turn * part, part)]
        sem = turn * n_f + offset
        return remote(where, where, core_send.at[sem], core_recv.at[sem], {"core": 1 - c})

    started = []

    def go(copy):
        copy.start()
        started.append(copy)

    for step in range(bits):
        for turn, order in enumerate(orders):
            go(link(turn, 0, order[step]))
    for turn in range(len(orders)):
        go(across(turn, 0))
    own = pltpu.make_async_copy(x_ref, out_ref.at[slot(0)], local_sem)
    own.start()
    have = [[0] for _ in orders]
    for step in range(bits):
        for at in range(1 << step):
            for turn, order in enumerate(orders):
                offset = have[turn][at] ^ (1 << order[step])
                arrival(turn, offset).wait_recv()
                for later in range(step + 1, bits):
                    go(link(turn, offset, order[later]))
                go(across(turn, offset))
                have[turn].append(offset)
    for copy in started:
        copy.wait_send()
    for turn in range(len(orders)):
        for offset in have[turn]:
            crossing(turn, offset).wait_recv()
    own.wait()


def plane_gather(x, n_f, ident):
    rows, width = x.shape
    count = len(bit_orders(n_f)[1]) * n_f
    out = pl.pallas_call(
        functools.partial(gather_body, n_f),
        out_shape=jax.ShapeDtypeStruct((n_f * 2, rows, width), x.dtype),
        in_specs=[ON_CHIP],
        out_specs=ON_CHIP,
        scratch_shapes=[DMA((count,))] * 4 + [DMA],
        compiler_params=pltpu.CompilerParams(
            collective_id=ident, has_side_effects=True, vmem_limit_bytes=40 << 20
        ),
        name="plane_gather",
    )(x)
    return out.reshape(n_f * 2 * rows, width)


def scatter_body(n_f, part_ref, out_ref, acc, core_in, link_in, send, recv, core_send, core_recv):
    f, c = lax.axis_index("fsdp"), lax.axis_index("core")
    rows = out_ref.shape[0]
    bits, orders = bit_orders(n_f)
    part = rows // len(orders)
    greet([{"fsdp": flip(f, 1 << bit, bits)} for bit in range(bits)] + [{"core": 1 - c}])
    started = []

    def go(copy):
        copy.start()
        started.append(copy)

    def across(turn, offset):
        where = pl.ds(turn * part, part)
        sem = turn * n_f + offset
        return remote(
            part_ref.at[flip(f, offset, bits) * 2 + 1 - c, where],
            core_in.at[offset, where],
            core_send.at[sem],
            core_recv.at[sem],
            {"core": 1 - c},
        )

    def link(turn, offset, bit):
        where = pl.ds(turn * part, part)
        sem = turn * n_f + offset
        return remote(
            acc.at[offset, where],
            link_in.at[offset, where],
            send.at[sem],
            recv.at[sem],
            {"fsdp": flip(f, 1 << bit, bits)},
        )

    plan = [[] for _ in range(bits)] + [[(turn, 0) for turn in range(len(orders))]]
    for step in range(bits):
        for offset in range(n_f):
            for turn, order in enumerate(orders):
                if offset >> order[step] & 1 and not any(offset >> b & 1 for b in order[:step]):
                    plan[step].append((turn, offset))
    for todo in plan:
        for turn, offset in todo:
            go(across(turn, offset))
    for step, todo in enumerate(plan):
        for turn, offset in todo:
            where = pl.ds(turn * part, part)
            across(turn, offset).wait_recv()
            total = part_ref[flip(f, offset, bits) * 2 + c, where].astype(F32)
            total = total + core_in[offset, where].astype(F32)
            for bit in orders[turn][:step]:
                link(turn, offset | (1 << bit), bit).wait_recv()
                total = total + link_in[offset | (1 << bit), where].astype(F32)
            if offset:
                acc[offset, where] = total.astype(BF16)
                go(link(turn, offset, orders[turn][step]))
            else:
                out_ref[where] = total
    for copy in started:
        copy.wait_send()


def plane_scatter(partial, n_f, ident):
    width = partial.shape[1]
    rows = partial.shape[0] // (n_f * 2)
    count = len(bit_orders(n_f)[1]) * n_f
    return pl.pallas_call(
        functools.partial(scatter_body, n_f),
        out_shape=jax.ShapeDtypeStruct((rows, width), F32),
        in_specs=[ON_CHIP],
        out_specs=ON_CHIP,
        scratch_shapes=[VMEM((n_f, rows, width), BF16)] * 3 + [DMA((count,))] * 4,
        compiler_params=pltpu.CompilerParams(
            collective_id=ident, has_side_effects=True, vmem_limit_bytes=40 << 20
        ),
        name="plane_scatter",
    )(partial.astype(BF16).reshape(n_f * 2, rows, width))


def exchange_body(n_f, n_z, plane_in, column_in, plane_out, column_out, sems, whole):
    f, z, c = lax.axis_index("fsdp"), lax.axis_index("zz"), lax.axis_index("core")
    peers = plane_peers(n_f, f, c)
    others = column_peers(n_z, z, c) if column_in is not None else []
    greet([device for _, device in peers] + [device for _, device in others])
    copies = []
    local = []
    if column_in is not None:
        mine = z * 2 + c
        for sem, device in others:
            to = device["zz"] * 2 + device["core"]
            source = column_in if whole else column_in.at[to]
            copies.append(
                remote(source, column_out.at[mine], sems[2].at[sem], sems[3].at[sem], device)
            )
        source = column_in if whole else column_in.at[mine]
        local.append(pltpu.make_async_copy(source, column_out.at[mine], sems[5]))
    mine = f * 2 + c
    for sem, device in peers:
        to = device["fsdp"] * 2 + device["core"]
        copies.append(
            remote(plane_in.at[to], plane_out.at[mine], sems[0].at[sem], sems[1].at[sem], device)
        )
    local.append(pltpu.make_async_copy(plane_in.at[mine], plane_out.at[mine], sems[4]))
    for copy in copies + local:
        copy.start()
    for copy in copies:
        copy.wait_send()
    for sem, device in peers:
        frm = device["fsdp"] * 2 + device["core"]
        remote(
            plane_out.at[frm], plane_out.at[frm], sems[0].at[sem], sems[1].at[sem], device
        ).wait_recv()
    if column_in is not None:
        for offset in range(n_z):
            for other in range(2):
                if offset or other:
                    frm = ((z + n_z - offset) % n_z) * 2 + c + other * (1 - 2 * c)
                    sem = offset * 2 + other
                    remote(
                        column_out.at[frm],
                        column_out.at[frm],
                        sems[2].at[sem],
                        sems[3].at[sem],
                        {"core": 1 - c},
                    ).wait_recv()
    for copy in local:
        copy.wait()


def exchange(plane_in, column_in, n_f, n_z, ident, whole=False):
    outs = [jax.ShapeDtypeStruct(plane_in.shape, plane_in.dtype)]
    ins = [plane_in]
    if column_in is not None:
        block = column_in.shape if whole else column_in.shape[1:]
        outs.append(jax.ShapeDtypeStruct((n_z * 2,) + block, column_in.dtype))
        ins.append(column_in)

    def body(*refs):
        if column_in is None:
            plane_ref, plane_out = refs[:2]
            exchange_body(n_f, n_z, plane_ref, None, plane_out, None, refs[2:], whole)
        else:
            plane_ref, column_ref, plane_out, column_out = refs[:4]
            exchange_body(
                n_f, n_z, plane_ref, column_ref, plane_out, column_out, refs[4:], whole
            )

    result = pl.pallas_call(
        body,
        out_shape=outs,
        in_specs=[ON_CHIP] * len(ins),
        out_specs=[ON_CHIP] * len(outs),
        scratch_shapes=[DMA((n_f * 2,))] * 2 + [DMA((n_z * 2,))] * 2 + [DMA] * 2,
        compiler_params=pltpu.CompilerParams(
            collective_id=ident, has_side_effects=True, vmem_limit_bytes=24 << 20
        ),
        name="exchange",
    )(*ins)
    return result if column_in is not None else result[0]


class Line:
    def __init__(self, n_z, chunks, sems):
        self.n_z, self.chunks = n_z, chunks
        self.red_send, self.red_recv, self.fin_send, self.fin_recv, self.own_sem = sems
        self.z = lax.axis_index("zz")
        self.done = 0

    def toward(self, k, source):
        return remote(
            source,
            self.chunks[k][1],
            self.red_send.at[k],
            self.red_recv.at[k],
            {"zz": jnp.maximum(self.z - 1, 0)},
        )

    def outward(self, k, source):
        return remote(
            source,
            self.chunks[k][2],
            self.fin_send.at[k],
            self.fin_recv.at[k],
            {"zz": jnp.minimum(self.z + 1, self.n_z - 1)},
        )

    def keep(self, k):
        return pltpu.make_async_copy(self.chunks[k][1], self.chunks[k][2], self.own_sem.at[k])

    def reduce(self, k):
        own, landing, _ = self.chunks[k]

        @pl.when(self.z == self.n_z - 1)
        def _():
            self.toward(k, own).start()

        @pl.when(self.z < self.n_z - 1)
        def _():
            self.toward(k, own).wait_recv()
            height = min(16, own.shape[0])

            @pl.loop(0, own.shape[0] // height)
            def _(at):
                where = pl.ds(pl.multiple_of(at * height, height), height)
                landing[where] = (own[where].astype(F32) + landing[where].astype(F32)).astype(BF16)

        @pl.when((self.z < self.n_z - 1) & (self.z > 0))
        def _():
            self.toward(k, landing).start()

        @pl.when(self.z == 0)
        def _():
            self.outward(k, landing).start()
            self.keep(k).start()

    def spread(self, k):
        @pl.when(self.z > 0)
        def _():
            self.outward(k, self.chunks[k][2]).wait_recv()

        @pl.when((self.z > 0) & (self.z < self.n_z - 1))
        def _():
            self.outward(k, self.chunks[k][2]).start()

        @pl.when(self.z == 0)
        def _():
            self.keep(k).wait()

    def tick(self, then=None):
        t = self.done
        self.done += 1
        total = len(self.chunks)
        if t < total:
            self.reduce(t)
        for z in range(self.n_z):
            k = t - 2 - 4 * z
            if 0 <= k < total:

                @pl.when(self.z == z)
                def _():
                    self.spread(k)
                    if then is not None:
                        then(k)

    def ticks(self):
        return len(self.chunks) + 2 + 4 * (self.n_z - 1)

    def finish(self):
        for k in range(len(self.chunks)):

            @pl.when(self.z > 0)
            def _():
                self.toward(k, self.chunks[k][0]).wait_send()

            @pl.when(self.z < self.n_z - 1)
            def _():
                self.outward(k, self.chunks[k][2]).wait_send()


def line_greet(n_z):
    z = lax.axis_index("zz")
    barrier = pltpu.get_barrier_semaphore()
    for step in (1, -1):

        @pl.when((z + step >= 0) & (z + step < n_z))
        def _():
            pl.semaphore_signal(barrier, inc=1, device_id={"zz": z + step}, device_id_type=MESH)

    @pl.when((z == 0) | (z == n_z - 1))
    def _():
        pl.semaphore_wait(barrier, 1)

    @pl.when((z > 0) & (z < n_z - 1))
    def _():
        pl.semaphore_wait(barrier, 2)


def line_body(n_z, count, refs):
    grads, finals, landings = (refs[at * count : (at + 1) * count] for at in range(3))
    line_greet(n_z)
    chunks = [
        (own.at[k], landing.at[k], final.at[k])
        for own, landing, final in zip(grads, landings, finals)
        for k in range(own.shape[0])
    ]
    line = Line(n_z, chunks, refs[3 * count :])
    for _ in range(line.ticks()):
        line.tick()
    line.finish()


def line_sum(grads, n_z, ident):
    count = len(grads)
    chunks = sum(item.shape[0] for item in grads)

    def body(*refs):
        line_body(n_z, count, refs)

    return pl.pallas_call(
        body,
        out_shape=[jax.ShapeDtypeStruct(item.shape, BF16) for item in grads],
        in_specs=[ON_CHIP] * count,
        out_specs=[ANYWHERE] * count,
        scratch_shapes=[VMEM(item.shape, BF16) for item in grads] + [DMA((chunks,))] * 5,
        compiler_params=pltpu.CompilerParams(
            collective_id=ident, has_side_effects=True, vmem_limit_bytes=60 << 20
        ),
        name="line_sum",
    )(*grads)


def vector_body(n_f, n_z, in_ref, out_ref, plane_in, part, line_in, sems):
    f, z, c = lax.axis_index("fsdp"), lax.axis_index("zz"), lax.axis_index("core")
    send, recv, line_send, line_recv, local = sems
    peers = plane_peers(n_f, f, c)
    others = [(offset, {"zz": (z + offset) % n_z}) for offset in range(1, n_z)]
    greet([device for _, device in peers] + [device for _, device in others])
    mine = f * 2 + c
    copies = [
        remote(in_ref.at[device["fsdp"]], plane_in.at[mine], send.at[sem], recv.at[sem], device)
        for sem, device in peers
    ]
    for copy in copies:
        copy.start()
    own = pltpu.make_async_copy(in_ref.at[f], plane_in.at[mine], local)
    own.start()
    own.wait()
    for sem, device in peers:
        where = plane_in.at[device["fsdp"] * 2 + device["core"]]
        remote(where, where, send.at[sem], recv.at[sem], device).wait_recv()
    total = plane_in[0]
    for at in range(1, n_f * 2):
        total = total + plane_in[at]
    part[...] = total
    line = [
        remote(part, line_in.at[z], line_send.at[sem], line_recv.at[sem], device)
        for sem, device in others
    ]
    for copy in line:
        copy.start()
    for offset in range(1, n_z):
        where = line_in.at[(z + n_z - offset) % n_z]
        remote(
            where, where, line_send.at[offset], line_recv.at[offset], {"core": 1 - c}
        ).wait_recv()
    line_in[z] = total
    total = line_in[0]
    for at in range(1, n_z):
        total = total + line_in[at]
    out_ref[...] = total
    for copy in copies + line:
        copy.wait_send()


def vector_sum(parts, n_f, n_z, ident):
    block = parts.shape[1:]

    def body(in_ref, out_ref, plane_in, part, line_in, *sems):
        vector_body(n_f, n_z, in_ref, out_ref, plane_in, part, line_in, sems)

    return pl.pallas_call(
        body,
        out_shape=jax.ShapeDtypeStruct(block, F32),
        in_specs=[ON_CHIP],
        out_specs=ON_CHIP,
        scratch_shapes=[VMEM((n_f * 2,) + block, F32), VMEM(block, F32), VMEM((n_z,) + block, F32)]
        + [DMA((n_f * 2,))] * 2
        + [DMA((n_z,))] * 2
        + [DMA],
        compiler_params=pltpu.CompilerParams(
            collective_id=ident, has_side_effects=True, vmem_limit_bytes=24 << 20
        ),
        name="vector_sum",
    )(parts)


def front_body(n_f, small, w_query, w_kv, small_o, query_o, kv_o, sems):
    f, c = lax.axis_index("fsdp"), lax.axis_index("core")
    bits = n_f.bit_length() - 1
    send, recv, local = sems
    greet([{"fsdp": flip(f, offset, bits)} for offset in range(1, n_f)])
    size = query_o.shape[2]

    def block(to):
        return w_query.at[:, pl.ds(pl.multiple_of((to * 2 + c) * size, LANES), size)]

    copies, locals_ = [], []
    for at, (source, target) in enumerate(((small, small_o), (None, query_o), (w_kv, kv_o))):
        for offset in range(1, n_f):
            to = flip(f, offset, bits)
            sem = at * n_f + offset
            copies.append(
                remote(
                    block(to) if source is None else source,
                    target.at[f],
                    send.at[sem],
                    recv.at[sem],
                    {"fsdp": to},
                )
            )
        locals_.append(
            pltpu.make_async_copy(
                block(f) if source is None else source, target.at[f], local.at[at]
            )
        )
    for copy in copies + locals_:
        copy.start()
    for copy in copies:
        copy.wait_send()
    for at, target in enumerate((small_o, query_o, kv_o)):
        for offset in range(1, n_f):
            where = target.at[flip(f, offset, bits)]
            sem = at * n_f + offset
            remote(where, where, send.at[sem], recv.at[sem], {"core": 1 - c}).wait_recv()
    for copy in locals_:
        copy.wait()


def front(small, w_query, w_kv, own_q, n_f, ident):
    def body(*refs):
        front_body(n_f, *refs[:6], refs[6:])

    return pl.pallas_call(
        body,
        out_shape=[
            jax.ShapeDtypeStruct((n_f,) + small.shape, BF16),
            jax.ShapeDtypeStruct((n_f, w_query.shape[0], own_q), BF16),
            jax.ShapeDtypeStruct((n_f,) + w_kv.shape, BF16),
        ],
        in_specs=[ON_CHIP, ANYWHERE, ON_CHIP],
        out_specs=[ON_CHIP] * 3,
        scratch_shapes=[DMA((3 * n_f,))] * 2 + [DMA((3,))],
        compiler_params=pltpu.CompilerParams(
            collective_id=ident, has_side_effects=True, vmem_limit_bytes=24 << 20
        ),
        name="front",
    )(small, w_query, w_kv)


def home_body(n_f, down, up, outw, query, kv, down_o, up_o, out_o, query_o, kv_o, *sems):
    f, c = lax.axis_index("fsdp"), lax.axis_index("core")
    bits = n_f.bit_length() - 1
    send, recv, core_send, core_recv, local_sem = sems
    greet([{"fsdp": flip(f, offset, bits)} for offset in range(1, n_f)] + [{"core": 1 - c}])
    pair = [(down, down_o), (outw, out_o), (kv, kv_o)]
    split = [(up, up_o), (query, query_o)]
    started, local = [], []

    def go(copy):
        copy.start()
        started.append(copy)

    def cols(ref, source, tensor):
        width = split[tensor][0].shape[1]
        return ref.at[:, pl.ds(pl.multiple_of(source * width, LANES), width)]

    def rows(tensor, to):
        source = split[tensor][0]
        height = source.shape[0] // n_f
        return source.at[pl.ds(to * height, height)]

    def link(tensor, offset):
        to = flip(f, offset, bits)
        sem = tensor * n_f + offset
        return remote(
            rows(tensor, to),
            cols(split[tensor][1], f * 2 + c, tensor),
            send.at[sem],
            recv.at[sem],
            {"fsdp": to},
        )

    def arrival(tensor, offset):
        where = cols(split[tensor][1], flip(f, offset, bits) * 2 + c, tensor)
        sem = tensor * n_f + offset
        return remote(where, where, send.at[sem], recv.at[sem], {"core": 1 - c})

    def across(tensor, offset, side):
        where = cols(split[tensor][1], flip(f, offset, bits) * 2 + side, tensor)
        sem = tensor * n_f + offset
        source = rows(tensor, f) if offset == 0 else where
        return remote(source, where, core_send.at[sem], core_recv.at[sem], {"core": 1 - c})

    def swap(at, side):
        sem = 2 * n_f + at
        return remote(
            pair[at][0], pair[at][1].at[side], core_send.at[sem], core_recv.at[sem], {"core": 1 - c}
        )

    for tensor in range(2):
        for offset in range(1, n_f):
            go(link(tensor, offset))
    for at, (source, target) in enumerate(pair):
        go(swap(at, c))
        local.append(pltpu.make_async_copy(source, target.at[c], local_sem.at[at]))
    for tensor in range(2):
        go(across(tensor, 0, c))
        local.append(
            pltpu.make_async_copy(
                rows(tensor, f), cols(split[tensor][1], f * 2 + c, tensor), local_sem.at[3 + tensor]
            )
        )
    for copy in local:
        copy.start()
    for offset in range(1, n_f):
        for tensor in range(2):
            arrival(tensor, offset).wait_recv()
            go(across(tensor, offset, c))
    for copy in started:
        copy.wait_send()
    for at in range(3):
        swap(at, 1 - c).wait_recv()
    for tensor in range(2):
        for offset in range(n_f):
            across(tensor, offset, 1 - c).wait_recv()
    for copy in local:
        copy.wait()


def home(down, up, outw, query, kv, n_f, ident):
    shapes = [
        (2,) + down.shape,
        (up.shape[0] // n_f, up.shape[1] * n_f * 2),
        (2,) + outw.shape,
        (query.shape[0] // n_f, query.shape[1] * n_f * 2),
        (2,) + kv.shape,
    ]
    return pl.pallas_call(
        functools.partial(home_body, n_f),
        out_shape=[jax.ShapeDtypeStruct(shape, BF16) for shape in shapes],
        in_specs=[ON_CHIP] * 5,
        out_specs=[ON_CHIP] * 5,
        scratch_shapes=[DMA((2 * n_f,))] * 2 + [DMA((2 * n_f + 3,))] * 2 + [DMA((5,))],
        compiler_params=pltpu.CompilerParams(
            collective_id=ident, has_side_effects=True, vmem_limit_bytes=48 << 20
        ),
        name="grads_home",
    )(down, up, outw, query, kv)


def heads_side_by_side(block, head):
    count = block.shape[1] // head
    return jnp.concatenate([block[:, at * head : (at + 1) * head] for at in range(count)], axis=0)


def heads_apart(block, count):
    rows = block.shape[0] // count
    return jnp.concatenate([block[at * rows : (at + 1) * rows] for at in range(count)], axis=1)


def attend_body(head, scale, query_ref, kv_ref, mask_ref, mixed_ref, lse_ref):
    query = heads_side_by_side(query_ref[0], head)
    count = query_ref.shape[2] // head
    keys, values = kv_ref[:, :head], kv_ref[:, head:]
    mask = jnp.concatenate([mask_ref[...]] * count, axis=1)
    scores = dot_nt(keys, query) * scale + mask
    peak = jnp.max(scores, axis=0, keepdims=True)
    weights = jnp.exp(scores - peak)
    total = jnp.sum(weights, axis=0, keepdims=True)
    probs = (weights / total).astype(BF16)
    mixed_ref[0] = heads_apart(dot_tn(probs, values).astype(BF16), count)
    lse_ref[0] = peak + jnp.log(total)


def attend(query, kv, mask, head):
    n_p, rows, width = query.shape
    span = kv.shape[0]
    count = width // head
    return pl.pallas_call(
        functools.partial(attend_body, head, 1.0 / math.sqrt(head)),
        out_shape=[
            jax.ShapeDtypeStruct(query.shape, BF16),
            jax.ShapeDtypeStruct((n_p, 1, count * rows), F32),
        ],
        grid=(n_p,),
        in_specs=[
            pl.BlockSpec((1, rows, width), lambda p: (p, 0, 0)),
            pl.BlockSpec((span, 2 * head), lambda p: (0, 0)),
            pl.BlockSpec((span, rows), lambda p: (0, 0)),
        ],
        out_specs=[
            pl.BlockSpec((1, rows, width), lambda p: (p, 0, 0)),
            pl.BlockSpec((1, 1, count * rows), lambda p: (p, 0, 0)),
        ],
        name="attend",
    )(query, kv, mask)


def attend_back_body(head, scale, query_ref, grad_ref, kv_ref, mask_ref, lse_ref, dq_ref, dkv_ref):
    query = heads_side_by_side(query_ref[0], head)
    grad = heads_side_by_side(grad_ref[0], head)
    count = query_ref.shape[2] // head
    keys, values = kv_ref[:, :head], kv_ref[:, head:]
    mask = jnp.concatenate([mask_ref[...]] * count, axis=1)
    scores = dot_nt(keys, query) * scale + mask
    probs = jnp.exp(scores - lse_ref[0])
    d_probs = dot_nt(values, grad)
    delta = jnp.sum(probs * d_probs, axis=0, keepdims=True)
    d_scores = (probs * (d_probs - delta)).astype(BF16)
    dq_ref[0] = heads_apart((dot_tn(d_scores, keys) * scale).astype(BF16), count)
    d_keys = dot(d_scores, query) * scale
    d_values = dot(probs.astype(BF16), grad)

    @pl.when(pl.program_id(0) == 0)
    def _():
        dkv_ref[:, :head] = d_keys
        dkv_ref[:, head:] = d_values

    @pl.when(pl.program_id(0) > 0)
    def _():
        dkv_ref[:, :head] += d_keys
        dkv_ref[:, head:] += d_values


def attend_back(query, grad, kv, mask, lse, head):
    n_p, rows, width = query.shape
    span = kv.shape[0]
    count = width // head
    block = pl.BlockSpec((1, rows, width), lambda p: (p, 0, 0))
    return pl.pallas_call(
        functools.partial(attend_back_body, head, 1.0 / math.sqrt(head)),
        out_shape=[
            jax.ShapeDtypeStruct(query.shape, BF16),
            jax.ShapeDtypeStruct((span, 2 * head), F32),
        ],
        grid=(n_p,),
        in_specs=[
            block,
            block,
            pl.BlockSpec((span, 2 * head), lambda p: (0, 0)),
            pl.BlockSpec((span, rows), lambda p: (0, 0)),
            pl.BlockSpec((1, 1, count * rows), lambda p: (p, 0, 0)),
        ],
        out_specs=[block, pl.BlockSpec((span, 2 * head), lambda p: (0, 0))],
        name="attend_back",
    )(query, grad, kv, mask, lse)


def norm_parts(values_in):
    row_mean = jnp.mean(values_in, axis=-1, keepdims=True)
    centered = values_in - row_mean
    variance = jnp.mean(centered * centered, axis=-1, keepdims=True)
    inverse = lax.rsqrt(variance + EPSILON)
    return centered * inverse, inverse


def norm_back(grad, normal, inverse, gain):
    scaled = grad * gain
    first = jnp.mean(scaled, axis=-1, keepdims=True)
    second = jnp.mean(scaled * normal, axis=-1, keepdims=True)
    return inverse * (scaled - first - normal * second)


def row_docs(positions, lengths):
    doc_ends = jnp.cumsum(lengths)
    return jnp.sum((positions[:, None] >= doc_ends[None, :]).astype(jnp.int32), axis=1)


def dot(left, right):
    return jnp.dot(left, right, preferred_element_type=F32)


def dot_tn(left, right):
    return lax.dot_general(left, right, (((0,), (0,)), ((), ())), preferred_element_type=F32)


def dot_nt(left, right):
    return lax.dot_general(left, right, (((1,), (1,)), ((), ())), preferred_element_type=F32)


def shards(
    tokens,
    doc_lengths,
    attn_gain,
    attn_shift,
    qkv_weight,
    query_bias,
    value_bias,
    out_weight,
    out_bias,
    mlp_gain,
    mlp_shift,
    up_weight,
    up_bias,
    down_weight,
    down_bias,
    cotangent,
):
    n_f, n_z, n_c = lax.axis_size("fsdp"), lax.axis_size("zz"), lax.axis_size("core")
    f, z, c = lax.axis_index("fsdp"), lax.axis_index("zz"), lax.axis_index("core")
    n_p = n_f * n_c
    tokens_in = tokens[0].astype(F32)
    lengths = doc_lengths[0]
    grad_out = cotangent[0]
    rows, width = tokens_in.shape
    head = value_bias.shape[0] * n_f
    hidden = up_weight.shape[1]
    own_q = width // n_p
    own_h = hidden // n_p

    smalls = (attn_gain, attn_shift, query_bias, out_bias, mlp_gain, mlp_shift, down_bias, up_bias, value_bias)
    packed = jnp.concatenate(smalls)
    length = packed.shape[0]
    packed = jnp.pad(packed, (0, -length % (16 * LANES))).reshape(-1, LANES)
    packed, w_q, w_kv = front(packed, qkv_weight, qkv_weight[:, width:], own_q, n_f, 15)
    w_q = w_q.reshape(width, own_q)
    w_kv = w_kv.reshape(width, 2 * head)
    packed = packed.reshape(n_f, -1)
    wide, at = [], 0
    for item in smalls:
        size = item.shape[0]
        wide.append(packed[:, at : at + size].reshape(-1).astype(F32))
        at += size
    gain_one, shift_one, bias_q, bias_out, gain_two, shift_two, bias_down, bias_up, bias_v = wide
    plane_at = f * n_c + c
    bias_q_own = lax.dynamic_slice_in_dim(bias_q, plane_at * own_q, own_q)
    bias_up_own = lax.dynamic_slice_in_dim(bias_up, plane_at * own_h, own_h)

    def own_columns(weight, size):
        pieces = []
        for offset in range(n_f):
            to = flip(f, offset, n_f.bit_length() - 1)
            block = lax.dynamic_slice_in_dim(weight, (to * n_c + c) * size, size, axis=1)
            if offset:
                block = lax.ppermute(block, "fsdp", [(i, i ^ offset) for i in range(n_f)])
            pieces.append(block)
        stacked = jnp.zeros((n_f, weight.shape[0], size), BF16)
        for offset in range(n_f):
            stacked = lax.dynamic_update_slice_in_dim(
                stacked, pieces[offset][None], flip(f, offset, n_f.bit_length() - 1), axis=0
            )
        return stacked.reshape(width, size)

    w_up = own_columns(up_weight, own_h)
    w_out = lax.dynamic_slice_in_dim(out_weight, c * own_q, own_q, axis=0)
    w_down = lax.dynamic_slice_in_dim(down_weight, c * own_h, own_h, axis=0)

    normal_one, inverse_one = norm_parts(tokens_in)
    normed = (normal_one * gain_one + shift_one).astype(BF16)
    normed_pl = plane_gather(normed, n_f, 0)
    query_own = (dot(normed_pl, w_q) + bias_q_own).astype(BF16)
    keyval = dot(normed, w_kv)
    keyval = jnp.concatenate([keyval[:, :head], keyval[:, head:] + bias_v], axis=1).astype(BF16)
    query, keyval_all = exchange(
        query_own.reshape(n_p, rows, own_q), keyval, n_f, n_z, 1, whole=True
    )
    stream = n_z * n_c * rows
    span = min(stream, stream // 2 + rows)
    key_first = jnp.clip((z * n_c + c + 1) * rows - span, 0, stream - span)
    kv = lax.dynamic_slice_in_dim(keyval_all.reshape(stream, 2 * head), key_first, span, axis=0)
    key_pos = key_first + jnp.arange(span, dtype=jnp.int32)
    positions = (z * n_c + c) * rows + jnp.arange(rows, dtype=jnp.int32)
    allowed = (row_docs(key_pos, lengths)[:, None] == row_docs(positions, lengths)[None, :]) & (
        positions[None, :] >= key_pos[:, None]
    )
    mask = jnp.where(allowed, 0.0, -1e30).astype(F32)
    mixed, lse = attend(query, kv, mask, head)
    mixed_own = exchange(mixed, None, n_f, n_z, 2).reshape(n_p * rows, own_q)
    branch = plane_scatter(dot(mixed_own, w_out), n_f, 3) + bias_out
    residual = tokens_in + branch

    normal_two, inverse_two = norm_parts(residual)
    normed_mlp = (normal_two * gain_two + shift_two).astype(BF16)
    normed_mlp_pl = plane_gather(normed_mlp, n_f, 4)
    grad_pl = plane_gather(grad_out, n_f, 5)
    inner = dot(normed_mlp_pl, w_up) + bias_up_own
    activated, gelu_back = jax.vjp(lambda v: jax.nn.gelu(v, approximate=True), inner)
    activated = activated.astype(BF16)
    layer_out = residual + plane_scatter(dot(activated, w_down), n_f, 6) + bias_down
    d_act = dot_nt(grad_pl, w_down)
    d_inner = gelu_back(d_act)[0].astype(BF16)
    e_two = plane_scatter(dot_nt(d_inner, w_up), n_f, 7)
    g_down = dot_tn(activated, grad_pl).astype(BF16)
    g_up = dot_tn(normed_mlp_pl, d_inner).astype(BF16)
    d_residual = grad_out.astype(F32) + norm_back(e_two, normal_two, inverse_two, gain_two)

    d_branch = d_residual.astype(BF16)
    d_branch_pl = plane_gather(d_branch, n_f, 8)
    d_mixed = exchange(
        dot_nt(d_branch_pl, w_out).astype(BF16).reshape(n_p, rows, own_q), None, n_f, n_z, 9
    )
    g_out = dot_tn(mixed_own, d_branch_pl).astype(BF16)
    d_query, d_kv_span = attend_back(query, d_mixed, kv, mask, lse, head)
    d_kv_part = lax.dynamic_update_slice_in_dim(
        jnp.zeros((stream, 2 * head), BF16), d_kv_span.astype(BF16), key_first, axis=0
    )
    d_query_own, d_kv_parts = exchange(
        d_query, d_kv_part.reshape(n_z * n_c, rows, 2 * head), n_f, n_z, 10
    )
    d_query_own = d_query_own.reshape(n_p * rows, own_q)
    d_kv = jnp.sum(d_kv_parts.astype(F32), axis=0).astype(BF16)
    e_one = plane_scatter(dot_nt(d_query_own, w_q), n_f, 11) + dot_nt(d_kv, w_kv)
    d_kv_pl = plane_gather(d_kv, n_f, 12)
    g_q = dot_tn(normed_pl, d_query_own).astype(BF16)
    normed_cols = lax.dynamic_slice_in_dim(normed_pl, plane_at * own_q, own_q, axis=1)
    g_kv = dot_tn(normed_cols, d_kv_pl).astype(BF16)
    grad_tokens = d_residual + norm_back(e_one, normal_one, inverse_one, gain_one)

    def chunked(block):
        height = max(16, (1 << 17) // block.shape[1])
        height = min(height, block.shape[0])
        return block.reshape(block.shape[0] // height, height, block.shape[1])

    pieces = (g_down, g_up, g_out, g_q, g_kv)
    summed = line_sum([chunked(item) for item in pieces], n_z, 13)
    summed = [item.reshape(like.shape) for item, like in zip(summed, pieces)]
    h_down, h_up, h_out, h_q, h_kv = home(*summed, n_f, 14)
    grad_down = h_down.reshape(n_c * own_h, width).astype(F32)
    grad_out_w = h_out.reshape(n_c * own_q, width).astype(F32)
    grad_qkv = jnp.concatenate([h_q, h_kv.reshape(n_c * own_q, 2 * head)], axis=1).astype(F32)

    up_sum = lax.dynamic_update_slice_in_dim(
        jnp.zeros((hidden,), F32), jnp.sum(d_inner.astype(F32), axis=0), plane_at * own_h, axis=0
    )
    vectors = (
        jnp.sum(e_one * normal_one, axis=0),
        jnp.sum(e_one, axis=0),
        jnp.sum(d_query.astype(F32), axis=1).reshape(-1),
        jnp.sum(d_kv[:, head:].astype(F32), axis=0),
        jnp.sum(d_branch.astype(F32), axis=0),
        jnp.sum(e_two * normal_two, axis=0),
        jnp.sum(e_two, axis=0),
        up_sum,
        jnp.sum(grad_out.astype(F32), axis=0),
    )
    owned = jnp.concatenate([item.reshape(n_f, -1) for item in vectors], axis=1)
    owned = jnp.pad(owned, ((0, 0), (0, -owned.shape[1] % (8 * LANES))))
    total = vector_sum(owned.reshape(n_f, -1, LANES), n_f, n_z, 16).reshape(-1)
    small, at = [], 0
    for item in vectors:
        size = item.shape[0] // n_f
        small.append(total[at : at + size])
        at += size
    return (
        layer_out.astype(BF16)[None],
        grad_tokens.astype(BF16)[None],
        small[0],
        small[1],
        grad_qkv,
        small[2],
        small[3],
        grad_out_w,
        small[4],
        small[5],
        small[6],
        h_up.astype(F32),
        small[7],
        grad_down,
        small[8],
    )


def solution(mesh):
    n_f, n_s = mesh.shape["fsdp"], mesh.shape["seq"]
    split = Mesh(mesh.devices.reshape(n_f, n_s // 2, 2), ("fsdp", "zz", "core"))
    act = P("fsdp", ("zz", "core"), None)
    vec = P("fsdp")
    mat = P("fsdp", None)
    return jax.shard_map(
        shards,
        mesh=split,
        in_specs=(act, mat, vec, vec, mat, vec, vec, mat, vec, vec, vec, mat, vec, mat, vec, act),
        out_specs=(act, act, vec, vec, mat, vec, vec, mat, vec, vec, vec, mat, vec, mat, vec),
        check_vma=False,
    )
```

```python
import functools
import math

import jax
import jax.numpy as jnp
from jax import lax
from jax.experimental import pallas as pl
from jax.experimental.pallas import tpu as pltpu
from jax.sharding import Mesh
from jax.sharding import PartitionSpec as P

EPSILON = 1e-05
F32 = jnp.float32
BF16 = jnp.bfloat16
MESH = pl.DeviceIdType.MESH
VMEM = pltpu.VMEM
DMA = pltpu.SemaphoreType.DMA
ON_CHIP = pl.BlockSpec(memory_space=pltpu.VMEM)
ANYWHERE = pl.BlockSpec(memory_space=pl.ANY)
LANES = 128


def flip(index, offset, bits):
    for bit in range(bits):
        if offset >> bit & 1:
            index = index + (1 << bit) * (1 - 2 * ((index // (1 << bit)) % 2))
    return index


def bit_orders(n_f):
    bits = n_f.bit_length() - 1
    assert 1 << bits == n_f
    turns = min(bits, 2)
    return bits, [[(turn + at) % bits for at in range(bits)] for turn in range(turns)]


def greet(targets):
    barrier = pltpu.get_barrier_semaphore()
    for target in targets:
        pl.semaphore_signal(barrier, inc=1, device_id=target, device_id_type=MESH)
    pl.semaphore_wait(barrier, len(targets))


def plane_peers(n_f, f, c):
    bits = n_f.bit_length() - 1
    peers = []
    for offset in range(n_f):
        for other in range(2):
            if offset or other:
                peers.append(
                    (offset * 2 + other, {"fsdp": flip(f, offset, bits), "core": c + other * (1 - 2 * c)})
                )
    return peers


def column_peers(n_z, z, c):
    peers = []
    for offset in range(n_z):
        for other in range(2):
            if offset or other:
                peers.append(
                    (offset * 2 + other, {"zz": (z + offset) % n_z, "core": c + other * (1 - 2 * c)})
                )
    return peers


def remote(source, target, send, recv, device):
    return pltpu.make_async_remote_copy(
        src_ref=source,
        dst_ref=target,
        send_sem=send,
        recv_sem=recv,
        device_id=device,
        device_id_type=MESH,
    )


def no_pause(count):
    pass


def near(n_f, f, c):
    bits = n_f.bit_length() - 1
    return [{"fsdp": flip(f, 1 << bit, bits)} for bit in range(bits)] + [{"core": 1 - c}]


def gather_stage(n_f, x_ref, out_ref, send, recv, core_send, core_recv, local_sem, pause):
    f, c = lax.axis_index("fsdp"), lax.axis_index("core")
    rows = x_ref.shape[0]
    bits, orders = bit_orders(n_f)
    part = rows // len(orders)

    def slot(offset):
        return flip(f, offset, bits) * 2 + c

    def piece(turn, offset):
        return out_ref.at[slot(offset), pl.ds(turn * part, part)]

    def link(turn, offset, bit):
        source = x_ref.at[pl.ds(turn * part, part)] if offset == 0 else piece(turn, offset)
        sem = turn * n_f + (offset ^ (1 << bit))
        return remote(
            source,
            piece(turn, offset),
            send.at[sem],
            recv.at[sem],
            {"fsdp": flip(f, 1 << bit, bits)},
        )

    def arrival(turn, offset):
        sem = turn * n_f + offset
        return remote(
            piece(turn, offset), piece(turn, offset), send.at[sem], recv.at[sem], {"core": 1 - c}
        )

    def across(turn, offset):
        source = x_ref.at[pl.ds(turn * part, part)] if offset == 0 else piece(turn, offset)
        sem = turn * n_f + offset
        return remote(
            source, piece(turn, offset), core_send.at[sem], core_recv.at[sem], {"core": 1 - c}
        )

    def crossing(turn, offset):
        where = out_ref.at[flip(f, offset, bits) * 2 + 1 - c, pl.ds(turn * part, part)]
        sem = turn * n_f + offset
        return remote(where, where, core_send.at[sem], core_recv.at[sem], {"core": 1 - c})

    started = []

    def go(copy):
        copy.start()
        started.append(copy)

    for step in range(bits):
        for turn, order in enumerate(orders):
            go(link(turn, 0, order[step]))
    for turn in range(len(orders)):
        go(across(turn, 0))
    own = pltpu.make_async_copy(x_ref, out_ref.at[slot(0)], local_sem)
    own.start()
    pause(1)
    have = [[0] for _ in orders]
    for step in range(bits):
        for at in range(1 << step):
            for turn, order in enumerate(orders):
                offset = have[turn][at] ^ (1 << order[step])
                arrival(turn, offset).wait_recv()
                for later in range(step + 1, bits):
                    go(link(turn, offset, order[later]))
                go(across(turn, offset))
                have[turn].append(offset)
                pause(1)
    for copy in started:
        copy.wait_send()
    for turn in range(len(orders)):
        for offset in have[turn]:
            crossing(turn, offset).wait_recv()
    own.wait()


def gather_body(n_f, x_ref, out_ref, *sems):
    f, c = lax.axis_index("fsdp"), lax.axis_index("core")
    greet(near(n_f, f, c))
    gather_stage(n_f, x_ref, out_ref, *sems, no_pause)


def plane_gather(x, n_f, ident):
    rows, width = x.shape
    count = len(bit_orders(n_f)[1]) * n_f
    out = pl.pallas_call(
        functools.partial(gather_body, n_f),
        out_shape=jax.ShapeDtypeStruct((n_f * 2, rows, width), x.dtype),
        in_specs=[ON_CHIP],
        out_specs=ON_CHIP,
        scratch_shapes=[DMA((count,))] * 4 + [DMA],
        compiler_params=pltpu.CompilerParams(
            collective_id=ident, has_side_effects=True, vmem_limit_bytes=40 << 20
        ),
        name="plane_gather",
    )(x)
    return out.reshape(n_f * 2 * rows, width)


def scatter_stage(
    n_f, part_ref, out_ref, acc, core_in, link_in, send, recv, core_send, core_recv, pause
):
    f, c = lax.axis_index("fsdp"), lax.axis_index("core")
    rows = out_ref.shape[0]
    bits, orders = bit_orders(n_f)
    part = rows // len(orders)
    started = []

    def go(copy):
        copy.start()
        started.append(copy)

    def held(offset, where):
        if acc is None:
            return part_ref.at[flip(f, offset, bits) * 2 + c, where]
        return acc.at[offset, where]

    def across(turn, offset):
        where = pl.ds(turn * part, part)
        sem = turn * n_f + offset
        return remote(
            part_ref.at[flip(f, offset, bits) * 2 + 1 - c, where],
            core_in.at[offset, where],
            core_send.at[sem],
            core_recv.at[sem],
            {"core": 1 - c},
        )

    def link(turn, offset, bit):
        where = pl.ds(turn * part, part)
        sem = turn * n_f + offset
        return remote(
            held(offset, where),
            link_in.at[offset, where],
            send.at[sem],
            recv.at[sem],
            {"fsdp": flip(f, 1 << bit, bits)},
        )

    plan = [[] for _ in range(bits)] + [[(turn, 0) for turn in range(len(orders))]]
    for step in range(bits):
        for offset in range(n_f):
            for turn, order in enumerate(orders):
                if offset >> order[step] & 1 and not any(offset >> b & 1 for b in order[:step]):
                    plan[step].append((turn, offset))
    for todo in plan:
        for turn, offset in todo:
            go(across(turn, offset))
    for step, todo in enumerate(plan):
        pause(1)
        for turn, offset in todo:
            where = pl.ds(turn * part, part)
            across(turn, offset).wait_recv()
            total = part_ref[flip(f, offset, bits) * 2 + c, where].astype(F32)
            total = total + core_in[offset, where].astype(F32)
            for bit in orders[turn][:step]:
                link(turn, offset | (1 << bit), bit).wait_recv()
                total = total + link_in[offset | (1 << bit), where].astype(F32)
            if offset:
                held(offset, where)[...] = total.astype(BF16)
                go(link(turn, offset, orders[turn][step]))
                if offset == n_f - 1:
                    pause(1)
            else:
                out_ref[where] = total
    for copy in started:
        copy.wait_send()


def scatter_body(n_f, *refs):
    f, c = lax.axis_index("fsdp"), lax.axis_index("core")
    greet(near(n_f, f, c))
    scatter_stage(n_f, *refs, no_pause)


def plane_scatter(partial, n_f, ident):
    width = partial.shape[1]
    rows = partial.shape[0] // (n_f * 2)
    count = len(bit_orders(n_f)[1]) * n_f
    return pl.pallas_call(
        functools.partial(scatter_body, n_f),
        out_shape=jax.ShapeDtypeStruct((rows, width), F32),
        in_specs=[ON_CHIP],
        out_specs=ON_CHIP,
        scratch_shapes=[VMEM((n_f, rows, width), BF16)] * 3 + [DMA((count,))] * 4,
        compiler_params=pltpu.CompilerParams(
            collective_id=ident, has_side_effects=True, vmem_limit_bytes=40 << 20
        ),
        name="plane_scatter",
    )(partial.astype(BF16).reshape(n_f * 2, rows, width))


def exchange_stage(n_f, n_z, plane_in, column_in, plane_out, column_out, sems, whole, pause):
    f, z, c = lax.axis_index("fsdp"), lax.axis_index("zz"), lax.axis_index("core")
    peers = plane_peers(n_f, f, c)
    others = column_peers(n_z, z, c) if column_in is not None else []
    copies = []
    local = []
    if column_in is not None:
        mine = z * 2 + c
        for sem, device in others:
            to = device["zz"] * 2 + device["core"]
            source = column_in if whole else column_in.at[to]
            copies.append(
                remote(source, column_out.at[mine], sems[2].at[sem], sems[3].at[sem], device)
            )
        source = column_in if whole else column_in.at[mine]
        local.append(pltpu.make_async_copy(source, column_out.at[mine], sems[5]))
    mine = f * 2 + c
    for sem, device in peers:
        to = device["fsdp"] * 2 + device["core"]
        copies.append(
            remote(plane_in.at[to], plane_out.at[mine], sems[0].at[sem], sems[1].at[sem], device)
        )
    local.append(pltpu.make_async_copy(plane_in.at[mine], plane_out.at[mine], sems[4]))
    for copy in copies + local:
        copy.start()
    pause(1)
    for copy in copies:
        copy.wait_send()
    for sem, device in peers:
        frm = device["fsdp"] * 2 + device["core"]
        remote(
            plane_out.at[frm], plane_out.at[frm], sems[0].at[sem], sems[1].at[sem], device
        ).wait_recv()
    if column_in is not None:
        for offset in range(n_z):
            for other in range(2):
                if offset or other:
                    frm = ((z + n_z - offset) % n_z) * 2 + c + other * (1 - 2 * c)
                    sem = offset * 2 + other
                    remote(
                        column_out.at[frm],
                        column_out.at[frm],
                        sems[2].at[sem],
                        sems[3].at[sem],
                        {"core": 1 - c},
                    ).wait_recv()
    for copy in local:
        copy.wait()


def exchange_body(n_f, n_z, plane_in, column_in, plane_out, column_out, sems, whole):
    f, z, c = lax.axis_index("fsdp"), lax.axis_index("zz"), lax.axis_index("core")
    peers = plane_peers(n_f, f, c)
    others = column_peers(n_z, z, c) if column_in is not None else []
    greet([device for _, device in peers + others])
    exchange_stage(
        n_f, n_z, plane_in, column_in, plane_out, column_out, sems, whole, no_pause
    )


def exchange(plane_in, column_in, n_f, n_z, ident, whole=False):
    outs = [jax.ShapeDtypeStruct(plane_in.shape, plane_in.dtype)]
    ins = [plane_in]
    if column_in is not None:
        block = column_in.shape if whole else column_in.shape[1:]
        outs.append(jax.ShapeDtypeStruct((n_z * 2,) + block, column_in.dtype))
        ins.append(column_in)

    def body(*refs):
        if column_in is None:
            plane_ref, plane_out = refs[:2]
            exchange_body(n_f, n_z, plane_ref, None, plane_out, None, refs[2:], whole)
        else:
            plane_ref, column_ref, plane_out, column_out = refs[:4]
            exchange_body(
                n_f, n_z, plane_ref, column_ref, plane_out, column_out, refs[4:], whole
            )

    result = pl.pallas_call(
        body,
        out_shape=outs,
        in_specs=[ON_CHIP] * len(ins),
        out_specs=[ON_CHIP] * len(outs),
        scratch_shapes=[DMA((n_f * 2,))] * 2 + [DMA((n_z * 2,))] * 2 + [DMA] * 2,
        compiler_params=pltpu.CompilerParams(
            collective_id=ident, has_side_effects=True, vmem_limit_bytes=24 << 20
        ),
        name="exchange",
    )(*ins)
    return result if column_in is not None else result[0]


class Line:
    def __init__(self, n_z, chunks, sems):
        self.n_z, self.chunks = n_z, chunks
        self.red_send, self.red_recv, self.fin_send, self.fin_recv, self.own_sem = sems
        self.z = lax.axis_index("zz")
        self.done = 0

    def toward(self, k, source):
        return remote(
            source,
            self.chunks[k][1],
            self.red_send.at[k],
            self.red_recv.at[k],
            {"zz": jnp.maximum(self.z - 1, 0)},
        )

    def outward(self, k, source):
        return remote(
            source,
            self.chunks[k][2],
            self.fin_send.at[k],
            self.fin_recv.at[k],
            {"zz": jnp.minimum(self.z + 1, self.n_z - 1)},
        )

    def keep(self, k):
        return pltpu.make_async_copy(self.chunks[k][1], self.chunks[k][2], self.own_sem.at[k])

    def reduce(self, k):
        own, landing, _ = self.chunks[k]

        @pl.when(self.z == self.n_z - 1)
        def _():
            self.toward(k, own).start()

        @pl.when(self.z < self.n_z - 1)
        def _():
            self.toward(k, own).wait_recv()
            height = min(16, own.shape[0])

            @pl.loop(0, own.shape[0] // height)
            def _(at):
                where = pl.ds(pl.multiple_of(at * height, height), height)
                landing[where] = (own[where].astype(F32) + landing[where].astype(F32)).astype(BF16)

        @pl.when((self.z < self.n_z - 1) & (self.z > 0))
        def _():
            self.toward(k, landing).start()

        @pl.when(self.z == 0)
        def _():
            self.outward(k, landing).start()
            self.keep(k).start()

    def spread(self, k):
        @pl.when(self.z > 0)
        def _():
            self.outward(k, self.chunks[k][2]).wait_recv()

        @pl.when((self.z > 0) & (self.z < self.n_z - 1))
        def _():
            self.outward(k, self.chunks[k][2]).start()

        @pl.when(self.z == 0)
        def _():
            self.keep(k).wait()

    def tick(self, then=None):
        t = self.done
        self.done += 1
        total = len(self.chunks)
        if t < total:
            self.reduce(t)
        for z in range(self.n_z):
            k = t - self.lag(z)
            if 0 <= k < total:

                @pl.when(self.z == z)
                def _():
                    self.spread(k)
                    if then is not None:
                        then(k)

    def lag(self, z):
        return 2 * z + 1 if z < self.n_z - 1 else 2 * z + 4

    def ticks(self):
        return len(self.chunks) + self.lag(self.n_z - 1)

    def left(self):
        return self.ticks() - self.done

    def finish(self):
        for k in range(len(self.chunks)):

            @pl.when(self.z > 0)
            def _():
                self.toward(k, self.chunks[k][0]).wait_send()

            @pl.when(self.z < self.n_z - 1)
            def _():
                self.outward(k, self.chunks[k][2]).wait_send()


def vector_stage(n_f, n_z, in_ref, out_ref, plane_in, part, line_in, sems, pause):
    f, z, c = lax.axis_index("fsdp"), lax.axis_index("zz"), lax.axis_index("core")
    send, recv, line_send, line_recv, local = sems
    peers = plane_peers(n_f, f, c)
    others = [(offset, {"zz": (z + offset) % n_z}) for offset in range(1, n_z)]
    mine = f * 2 + c
    copies = [
        remote(in_ref.at[device["fsdp"]], plane_in.at[mine], send.at[sem], recv.at[sem], device)
        for sem, device in peers
    ]
    for copy in copies:
        copy.start()
    own = pltpu.make_async_copy(in_ref.at[f], plane_in.at[mine], local)
    own.start()
    own.wait()
    pause(1)
    for sem, device in peers:
        where = plane_in.at[device["fsdp"] * 2 + device["core"]]
        remote(where, where, send.at[sem], recv.at[sem], device).wait_recv()
    total = plane_in[0]
    for at in range(1, n_f * 2):
        total = total + plane_in[at]
    part[...] = total
    line = [
        remote(part, line_in.at[z], line_send.at[sem], line_recv.at[sem], device)
        for sem, device in others
    ]
    for copy in line:
        copy.start()
    pause(1)
    for offset in range(1, n_z):
        where = line_in.at[(z + n_z - offset) % n_z]
        remote(
            where, where, line_send.at[offset], line_recv.at[offset], {"core": 1 - c}
        ).wait_recv()
    line_in[z] = total
    total = line_in[0]
    for at in range(1, n_z):
        total = total + line_in[at]
    out_ref[...] = total
    for copy in copies + line:
        copy.wait_send()


def front_body(n_f, small, w_query, w_kv, small_o, query_o, kv_o, sems):
    f, c = lax.axis_index("fsdp"), lax.axis_index("core")
    bits = n_f.bit_length() - 1
    send, recv, local = sems
    greet([{"fsdp": flip(f, offset, bits)} for offset in range(1, n_f)])
    size = query_o.shape[2]

    def block(to):
        return w_query.at[:, pl.ds(pl.multiple_of((to * 2 + c) * size, LANES), size)]

    copies, locals_ = [], []
    for at, (source, target) in enumerate(((small, small_o), (None, query_o), (w_kv, kv_o))):
        for offset in range(1, n_f):
            to = flip(f, offset, bits)
            sem = at * n_f + offset
            copies.append(
                remote(
                    block(to) if source is None else source,
                    target.at[f],
                    send.at[sem],
                    recv.at[sem],
                    {"fsdp": to},
                )
            )
        locals_.append(
            pltpu.make_async_copy(
                block(f) if source is None else source, target.at[f], local.at[at]
            )
        )
    for copy in copies + locals_:
        copy.start()
    for copy in copies:
        copy.wait_send()
    for at, target in enumerate((small_o, query_o, kv_o)):
        for offset in range(1, n_f):
            where = target.at[flip(f, offset, bits)]
            sem = at * n_f + offset
            remote(where, where, send.at[sem], recv.at[sem], {"core": 1 - c}).wait_recv()
    for copy in locals_:
        copy.wait()


def front(small, w_query, w_kv, own_q, n_f, ident):
    def body(*refs):
        front_body(n_f, *refs[:6], refs[6:])

    return pl.pallas_call(
        body,
        out_shape=[
            jax.ShapeDtypeStruct((n_f,) + small.shape, BF16),
            jax.ShapeDtypeStruct((n_f, w_query.shape[0], own_q), BF16),
            jax.ShapeDtypeStruct((n_f,) + w_kv.shape, BF16),
        ],
        in_specs=[ON_CHIP, ANYWHERE, ON_CHIP],
        out_specs=[ON_CHIP] * 3,
        scratch_shapes=[DMA((3 * n_f,))] * 2 + [DMA((3,))],
        compiler_params=pltpu.CompilerParams(
            collective_id=ident, has_side_effects=True, vmem_limit_bytes=24 << 20
        ),
        name="front",
    )(small, w_query, w_kv)


def heads_side_by_side(block, head):
    count = block.shape[1] // head
    return jnp.concatenate([block[:, at * head : (at + 1) * head] for at in range(count)], axis=0)


def heads_apart(block, count):
    rows = block.shape[0] // count
    return jnp.concatenate([block[at * rows : (at + 1) * rows] for at in range(count)], axis=1)


def attend_body(head, scale, query_ref, kv_ref, mask_ref, mixed_ref, lse_ref):
    query = heads_side_by_side(query_ref[0], head)
    count = query_ref.shape[2] // head
    keys, values = kv_ref[:, :head], kv_ref[:, head:]
    mask = jnp.concatenate([mask_ref[...]] * count, axis=1)
    scores = dot_nt(keys, query) * scale + mask
    peak = jnp.max(scores, axis=0, keepdims=True)
    weights = jnp.exp(scores - peak)
    total = jnp.sum(weights, axis=0, keepdims=True)
    probs = (weights / total).astype(BF16)
    mixed_ref[0] = heads_apart(dot_tn(probs, values).astype(BF16), count)
    lse_ref[0] = peak + jnp.log(total)


def attend(query, kv, mask, head):
    n_p, rows, width = query.shape
    span = kv.shape[0]
    count = width // head
    return pl.pallas_call(
        functools.partial(attend_body, head, 1.0 / math.sqrt(head)),
        out_shape=[
            jax.ShapeDtypeStruct(query.shape, BF16),
            jax.ShapeDtypeStruct((n_p, 1, count * rows), F32),
        ],
        grid=(n_p,),
        in_specs=[
            pl.BlockSpec((1, rows, width), lambda p: (p, 0, 0)),
            pl.BlockSpec((span, 2 * head), lambda p: (0, 0)),
            pl.BlockSpec((span, rows), lambda p: (0, 0)),
        ],
        out_specs=[
            pl.BlockSpec((1, rows, width), lambda p: (p, 0, 0)),
            pl.BlockSpec((1, 1, count * rows), lambda p: (p, 0, 0)),
        ],
        name="attend",
    )(query, kv, mask)


def attend_back_block(head, query_in, grad_in, kv_ref, mask_ref, lse):
    scale = 1.0 / math.sqrt(head)
    query = heads_side_by_side(query_in, head)
    grad = heads_side_by_side(grad_in, head)
    count = query_in.shape[1] // head
    keys, values = kv_ref[:, :head], kv_ref[:, head:]
    mask = jnp.concatenate([mask_ref[...]] * count, axis=1)
    scores = dot_nt(keys, query) * scale + mask
    probs = jnp.exp(scores - lse)
    d_probs = dot_nt(values, grad)
    delta = jnp.sum(probs * d_probs, axis=0, keepdims=True)
    d_scores = (probs * (d_probs - delta)).astype(BF16)
    d_query = heads_apart((dot_tn(d_scores, keys) * scale).astype(BF16), count)
    d_keys = dot(d_scores, query) * scale
    d_values = dot(probs.astype(BF16), grad)
    return d_query, d_keys, d_values


class Box:
    pass


def rows_of(ref, at, height=16):
    return pl.ds(pl.multiple_of(at * height, height), height)


def norm_back_tiles(grad_ref, extra_ref, normal_ref, inverse_ref, gain_ref, base_ref, sums, store):
    rows = normal_ref.shape[0]

    @pl.loop(0, rows // 16)
    def _(at):
        where = rows_of(normal_ref, at)
        grad = grad_ref[where]
        if extra_ref is not None:
            grad = grad + extra_ref[where]
        normal = normal_ref[where].astype(F32)
        scaled = grad * gain_ref[...]
        first = jnp.mean(scaled, axis=-1, keepdims=True)
        second = jnp.mean(scaled * normal, axis=-1, keepdims=True)
        result = base_ref[where].astype(F32) + inverse_ref[where] * (
            scaled - first - normal * second
        )
        store(where, result)
        sums[0:1] += jnp.sum(grad * normal, axis=0, keepdims=True)
        sums[1:2] += jnp.sum(grad, axis=0, keepdims=True)
        sums[2:3] += jnp.sum(result.astype(BF16).astype(F32), axis=0, keepdims=True)


def backward_body(n_f, n_z, head, names, *refs):
    r = Box()
    for name, ref in zip(names, refs, strict=True):
        setattr(r, name, ref)
    f, z, c = lax.axis_index("fsdp"), lax.axis_index("zz"), lax.axis_index("core")
    bits = n_f.bit_length() - 1
    n_p = n_f * 2
    me = f * 2 + c
    rows, width = r.grad_out.shape
    own_q = r.w_out.shape[0]

    loads = {}
    for at, (name, source, target) in enumerate(
        (
            ("part", r.e_part, r.part),
            ("down", r.g_down_in, r.g_down),
            ("up", r.g_up_in, r.g_up),
        )
    ):
        loads[name] = pltpu.make_async_copy(source, target, r.load_sem.at[at])
        loads[name].start()
    greet([device for _, device in plane_peers(n_f, f, c) + column_peers(n_z, z, c)])

    kinds = []
    chunks = []
    for kind, own, landing, final in (
        ("down", r.g_down, r.land_down, r.h_down.at[c]),
        ("up", r.g_up, r.land_up, r.fin_up),
        ("out", r.g_out, r.land_out, r.h_out.at[c]),
        ("q", r.g_q, r.land_q, r.fin_q),
        ("kv", r.g_kv, r.land_kv, r.h_kv.at[c]),
    ):
        for k in range(own.shape[0]):
            kinds.append((kind, k))
            chunks.append((own.at[k], landing.at[k], final.at[k]))
    line = Line(n_z, chunks, (r.red_send, r.red_recv, r.fin_send, r.fin_recv, r.keep_sem))
    home = {"down": r.h_down, "out": r.h_out, "kv": r.h_kv, "up": r.h_up, "q": r.h_q}

    def swap(at, side):
        kind, k = kinds[at]
        where = home[kind].at[side, k]
        return remote(where, where, r.swap_send.at[at], r.swap_recv.at[at], {"core": 1 - c})

    def block(kind, k, source):
        target = home[kind]
        height, size = chunks[kinds.index((kind, k))][2].shape
        per = target.shape[0] // height
        cols = pl.ds(pl.multiple_of(source * size, LANES), size)
        return target.at[pl.ds((k % per) * height, height), cols], k // per, k % per

    def move(at, side):
        kind, k = kinds[at]
        where, owner, turn = block(kind, k, me)
        recv = (r.up_recv if kind == "up" else r.q_recv).at[turn * n_p + me]
        send = r.home_send.at[at * 2 + side]
        return owner, recv, send, where

    def deliver(at):
        kind, k = kinds[at]
        if kind in ("down", "out", "kv"):
            swap(at, c).start()
            return
        for side in range(2):
            owner, recv, send, where = move(at, side)
            here = (f == owner) & (c == side)

            @pl.when(here)
            def _():
                pltpu.make_async_copy(chunks[at][2], where, send).start()

            @pl.when(jnp.logical_not(here))
            def _():
                remote(
                    chunks[at][2], where, send, recv, {"fsdp": owner, "core": side}
                ).start()

    def delivered():
        for at, (kind, k) in enumerate(kinds):
            if kind in ("down", "out", "kv"):
                swap(at, c).wait_send()
                swap(at, 1 - c).wait_recv()
                continue
            for side in range(2):
                owner, recv, send, where = move(at, side)
                here = (f == owner) & (c == side)

                @pl.when(here)
                def _():
                    pltpu.make_async_copy(chunks[at][2], where, send).wait()

                @pl.when(jnp.logical_not(here))
                def _():
                    remote(
                        chunks[at][2], where, send, recv, {"fsdp": owner, "core": side}
                    ).wait_send()

            if k < home[kind].shape[0] // chunks[at][2].shape[0]:
                for sem, device in plane_peers(n_f, f, c):
                    source = device["fsdp"] * 2 + device["core"]
                    where, _, turn = block(kind, k, source)
                    recv = (r.up_recv if kind == "up" else r.q_recv).at[turn * n_p + source]
                    remote(
                        where, where, r.home_send.at[at * 2], recv, {"core": 1 - c}
                    ).wait_recv()

    ready = [False]
    limit = [r.g_down.shape[0] + r.g_up.shape[0]]

    def pause(count):
        if not ready[0]:
            loads["down"].wait()
            loads["up"].wait()
            ready[0] = True
        for _ in range(count):
            if line.left() and line.done < limit[0]:
                line.tick(deliver)

    for ref in (r.sums_two, r.sums_one):
        ref[...] = jnp.zeros_like(ref)
    loads["part"].wait()
    scatter_stage(
        n_f, r.part, r.e_sum, None, r.core_in, r.link_in, *(r.scatter_one.at[at] for at in range(4)), pause
    )

    def store_two(where, result):
        r.d_residual[where] = result
        r.d_branch[where] = result.astype(BF16)

    norm_back_tiles(
        r.e_sum, None, r.normal_two, r.inverse_two, r.gain_two, r.grad_out, r.sums_two, store_two
    )
    loads["normed"] = pltpu.make_async_copy(r.normed_in, r.part, r.load_sem.at[3])
    loads["normed"].start()
    gather_stage(
        n_f, r.d_branch, r.branch_pl, *(r.gather_one.at[at] for at in range(4)), r.local_sem.at[0], pause
    )

    @pl.loop(0, n_p)
    def _(p):
        r.mixed_send[p] = dot_nt(r.branch_pl[p], r.w_out[...]).astype(BF16)

    exchange_stage(
        n_f,
        n_z,
        r.mixed_send,
        None,
        r.d_mixed,
        None,
        [r.swap_one.at[0], r.swap_one.at[1], None, None, r.local_sem.at[1], None],
        False,
        pause,
    )
    tile = min(512, width)
    high = r.g_out.shape[1]
    for j in range(own_q // LANES):
        for n in range(width // tile):
            cols = pl.ds(n * tile, tile)
            result = dot_tn(
                r.mixed_own[:, j * LANES : (j + 1) * LANES],
                r.branch_pl[:, :, cols].reshape(n_p * rows, tile),
            ).astype(BF16)
            for k in range(LANES // high):
                r.g_out[j * (LANES // high) + k, :, cols] = result[k * high : (k + 1) * high]
    limit[0] += r.g_out.shape[0]

    r.d_kv_span[...] = jnp.zeros_like(r.d_kv_span)
    step = max(1, n_p // 4)
    for first in range(0, n_p, step):

        @pl.loop(first, first + step)
        def _(p):
            d_query, d_keys, d_values = attend_back_block(
                head, r.query[p], r.d_mixed[p], r.kv, r.mask, r.lse[p]
            )
            r.dq_send[p] = d_query
            r.d_kv_span[:, :head] += d_keys
            r.d_kv_span[:, head:] += d_values

        pause(1)
    span = r.d_kv_span.shape[0]
    stream = n_z * 2 * rows
    first = jnp.maximum((z * 2 + c + 1) * rows - span, 0)
    r.dkv_send[...] = jnp.zeros_like(r.dkv_send)

    @pl.loop(0, span // rows)
    def _(at):
        block_at = (jnp.maximum((z * 2 + c + 1) * rows - span, 0)) // rows + at
        r.dkv_send[block_at] = r.d_kv_span[pl.ds(pl.multiple_of(at * rows, rows), rows)].astype(BF16)

    exchange_stage(
        n_f,
        n_z,
        r.dq_send,
        r.dkv_send,
        r.dq_own,
        r.dkv_recv,
        [
            r.swap_two.at[0],
            r.swap_two.at[1],
            r.column_sem.at[0],
            r.column_sem.at[1],
            r.local_sem.at[2],
            r.local_sem.at[3],
        ],
        False,
        pause,
    )
    total = r.dkv_recv[0].astype(F32)
    for s in range(1, n_z * 2):
        total = total + r.dkv_recv[s].astype(F32)
    r.d_kv[...] = total.astype(BF16)

    @pl.loop(0, n_p)
    def _(p):
        for n in range(width // tile):
            cols = pl.ds(n * tile, tile)
            r.branch_pl[p, :, cols] = dot_nt(r.dq_own[p], r.w_q[cols]).astype(BF16)

    scatter_stage(
        n_f, r.branch_pl, r.e_sum, None, r.core_in, r.link_in, *(r.scatter_two.at[at] for at in range(4)), pause
    )
    for n in range(width // tile):
        cols = pl.ds(n * tile, tile)
        r.e_extra[:, cols] = dot_nt(r.d_kv[...], r.w_kv[cols])

    def store_one(where, result):
        r.grad_tokens[where] = result.astype(BF16)

    norm_back_tiles(
        r.e_sum, r.e_extra, r.normal_one, r.inverse_one, r.gain_one, r.d_residual, r.sums_one, store_one
    )
    gather_stage(
        n_f, r.d_kv, r.dkv_pl, *(r.gather_two.at[at] for at in range(4)), r.local_sem.at[4], pause
    )

    loads["normed"].wait()
    dq_all = r.dq_own[...].reshape(n_p * rows, own_q)
    step = min(256, r.g_q.shape[1])
    for k in range(r.g_q.shape[0]):
        for at in range(r.g_q.shape[1] // step):
            base = k * r.g_q.shape[1] + at * step
            r.g_q[k, at * step : (at + 1) * step] = dot_tn(
                r.part[:, :, base : base + step].reshape(n_p * rows, step), dq_all
            ).astype(BF16)
    cols = pl.ds(pl.multiple_of(me * own_q, LANES), own_q)
    r.g_kv[0] = dot_tn(
        r.part[:, :, cols].reshape(n_p * rows, own_q), r.dkv_pl[...].reshape(n_p * rows, 2 * head)
    ).astype(BF16)
    loads["out"] = pltpu.make_async_copy(r.out_part, r.part, r.load_sem.at[4])
    loads["out"].start()
    limit[0] = line.ticks()
    pause(2)

    seg = r.vec_in.shape[2]
    r.vec_in[...] = jnp.zeros_like(r.vec_in)
    up_rows = r.up_sum.shape[0]
    d_value = jnp.sum(r.d_kv[:, head:].astype(F32), axis=0, keepdims=True)
    for o in range(n_f):
        cols = slice(o * seg, (o + 1) * seg)
        r.vec_in[o, 0:1] = r.sums_one[0:1, cols]
        r.vec_in[o, 1:2] = r.sums_one[1:2, cols]
        r.vec_in[o, 3:4] = r.sums_two[2:3, cols]
        r.vec_in[o, 4:5] = r.sums_two[0:1, cols]
        r.vec_in[o, 5:6] = r.sums_two[1:2, cols]
        r.vec_in[o, 6:7] = r.down_sum[0:1, cols]
        r.vec_in[o, 7:8, :head] = d_value
        for side in range(2):
            part = jnp.sum(r.dq_send[o * 2 + side].astype(F32), axis=0, keepdims=True)
            r.vec_in[o, 2:3, side * own_q : (side + 1) * own_q] = part

        for side in range(2):

            @pl.when((f == o) & (c == side))
            def _():
                r.vec_in[o, 8 + side * up_rows : 8 + (side + 1) * up_rows] = r.up_sum[...]

    vector_stage(
        n_f,
        n_z,
        r.vec_in,
        r.vectors,
        r.vec_plane,
        r.vec_part,
        r.vec_line,
        [r.vec_sem.at[0], r.vec_sem.at[1], r.vec_line_sem.at[0], r.vec_line_sem.at[1], r.local_sem.at[5]],
        pause,
    )

    loads["out"].wait()
    scatter_stage(
        n_f, r.part, r.out_sum, None, r.core_in, r.link_in, *(r.scatter_three.at[at] for at in range(4)), pause
    )
    pause(line.left())
    line.finish()
    delivered()


def backward(inputs, n_f, n_z, head, own_h, ident):
    rows, width = inputs["grad_out"].shape
    n_p = n_f * 2
    n_s = n_z * 2
    own_q = width // n_p
    seg = width // n_f
    count = len(bit_orders(n_f)[1]) * n_f
    span = inputs["kv"].shape[0]
    high = max(16, (1 << 17) // width)
    down = inputs["g_down_in"].shape
    up = inputs["g_up_in"].shape
    out = (own_q // high, high, width)
    query = (n_f, width // n_f, own_q)
    keyval = (1, own_q, 2 * head)
    chunks = down[0] + up[0] + out[0] + query[0] + 1
    per = seg // up[1]
    in_hbm = ("e_part", "g_down_in", "g_up_in", "normed_in", "out_part")
    outs = {
        "grad_tokens": ((rows, width), BF16, ON_CHIP),
        "out_sum": ((rows, width), F32, ON_CHIP),
        "vectors": ((16, seg), F32, ON_CHIP),
        "h_down": ((2,) + down, BF16, ANYWHERE),
        "h_up": ((seg, own_h * n_p), BF16, ANYWHERE),
        "h_out": ((2,) + out, BF16, ANYWHERE),
        "h_q": ((seg, width), BF16, ANYWHERE),
        "h_kv": ((2,) + keyval, BF16, ANYWHERE),
    }
    plane = (n_p, rows, width)
    blocks = (n_p, rows, own_q)
    scratch = {
        "part": VMEM(plane, BF16),
        "g_down": VMEM(down, BF16),
        "g_up": VMEM(up, BF16),
        "g_out": VMEM(out, BF16),
        "g_q": VMEM(query, BF16),
        "g_kv": VMEM(keyval, BF16),
        "land_down": VMEM(down, BF16),
        "land_up": VMEM(up, BF16),
        "land_out": VMEM(out, BF16),
        "land_q": VMEM(query, BF16),
        "land_kv": VMEM(keyval, BF16),
        "fin_up": VMEM(up, BF16),
        "fin_q": VMEM(query, BF16),
        "core_in": VMEM((n_f, rows, width), BF16),
        "link_in": VMEM((n_f, rows, width), BF16),
        "e_sum": VMEM((rows, width), F32),
        "e_extra": VMEM((rows, width), F32),
        "d_residual": VMEM((rows, width), F32),
        "d_branch": VMEM((rows, width), BF16),
        "branch_pl": VMEM(plane, BF16),
        "mixed_send": VMEM(blocks, BF16),
        "d_mixed": VMEM(blocks, BF16),
        "dq_send": VMEM(blocks, BF16),
        "dq_own": VMEM(blocks, BF16),
        "d_kv_span": VMEM((span, 2 * head), F32),
        "dkv_send": VMEM((n_s, rows, 2 * head), BF16),
        "dkv_recv": VMEM((n_s, rows, 2 * head), BF16),
        "d_kv": VMEM((rows, 2 * head), BF16),
        "dkv_pl": VMEM((n_p, rows, 2 * head), BF16),
        "sums_one": VMEM((8, width), F32),
        "sums_two": VMEM((8, width), F32),
        "vec_in": VMEM((n_f, 16, seg), F32),
        "vec_plane": VMEM((n_p, 16, seg), F32),
        "vec_part": VMEM((16, seg), F32),
        "vec_line": VMEM((n_z, 16, seg), F32),
        "load_sem": DMA((5,)),
        "local_sem": DMA((6,)),
        "red_send": DMA((chunks,)),
        "red_recv": DMA((chunks,)),
        "fin_send": DMA((chunks,)),
        "fin_recv": DMA((chunks,)),
        "keep_sem": DMA((chunks,)),
        "swap_send": DMA((chunks,)),
        "swap_recv": DMA((chunks,)),
        "home_send": DMA((chunks * 2,)),
        "up_recv": DMA((per * n_p,)),
        "q_recv": DMA((n_p,)),
        "scatter_one": DMA((4, count)),
        "scatter_two": DMA((4, count)),
        "scatter_three": DMA((4, count)),
        "gather_one": DMA((4, count)),
        "gather_two": DMA((4, count)),
        "swap_one": DMA((2, n_p)),
        "swap_two": DMA((2, n_p)),
        "column_sem": DMA((2, n_s)),
        "vec_sem": DMA((2, n_p)),
        "vec_line_sem": DMA((2, n_z)),
    }
    names = list(inputs) + list(outs) + list(scratch)
    result = pl.pallas_call(
        functools.partial(backward_body, n_f, n_z, head, names),
        out_shape=[jax.ShapeDtypeStruct(shape, kind) for shape, kind, _ in outs.values()],
        in_specs=[ANYWHERE if name in in_hbm else ON_CHIP for name in inputs],
        out_specs=[place for _, _, place in outs.values()],
        scratch_shapes=list(scratch.values()),
        compiler_params=pltpu.CompilerParams(
            collective_id=ident, has_side_effects=True, vmem_limit_bytes=67043328
        ),
        name="backward",
    )(*inputs.values())
    return dict(zip(outs, result))


def norm_parts(values_in):
    row_mean = jnp.mean(values_in, axis=-1, keepdims=True)
    centered = values_in - row_mean
    variance = jnp.mean(centered * centered, axis=-1, keepdims=True)
    inverse = lax.rsqrt(variance + EPSILON)
    return centered * inverse, inverse


def norm_back(grad, normal, inverse, gain):
    scaled = grad * gain
    first = jnp.mean(scaled, axis=-1, keepdims=True)
    second = jnp.mean(scaled * normal, axis=-1, keepdims=True)
    return inverse * (scaled - first - normal * second)


def row_docs(positions, lengths):
    doc_ends = jnp.cumsum(lengths)
    return jnp.sum((positions[:, None] >= doc_ends[None, :]).astype(jnp.int32), axis=1)


def dot(left, right):
    return jnp.dot(left, right, preferred_element_type=F32)


def dot_tn(left, right):
    return lax.dot_general(left, right, (((0,), (0,)), ((), ())), preferred_element_type=F32)


def dot_nt(left, right):
    return lax.dot_general(left, right, (((1,), (1,)), ((), ())), preferred_element_type=F32)


def shards(
    tokens,
    doc_lengths,
    attn_gain,
    attn_shift,
    qkv_weight,
    query_bias,
    value_bias,
    out_weight,
    out_bias,
    mlp_gain,
    mlp_shift,
    up_weight,
    up_bias,
    down_weight,
    down_bias,
    cotangent,
):
    n_f, n_z, n_c = lax.axis_size("fsdp"), lax.axis_size("zz"), lax.axis_size("core")
    f, z, c = lax.axis_index("fsdp"), lax.axis_index("zz"), lax.axis_index("core")
    n_p = n_f * n_c
    tokens_in = tokens[0].astype(F32)
    lengths = doc_lengths[0]
    grad_out = cotangent[0]
    rows, width = tokens_in.shape
    head = value_bias.shape[0] * n_f
    hidden = up_weight.shape[1]
    own_q = width // n_p
    own_h = hidden // n_p

    smalls = (attn_gain, attn_shift, query_bias, out_bias, mlp_gain, mlp_shift, down_bias, up_bias, value_bias)
    packed = jnp.concatenate(smalls)
    length = packed.shape[0]
    packed = jnp.pad(packed, (0, -length % (16 * LANES))).reshape(-1, LANES)
    packed, w_q, w_kv = front(packed, qkv_weight, qkv_weight[:, width:], own_q, n_f, 15)
    w_q = w_q.reshape(width, own_q)
    w_kv = w_kv.reshape(width, 2 * head)
    packed = packed.reshape(n_f, -1)
    wide, at = [], 0
    for item in smalls:
        size = item.shape[0]
        wide.append(packed[:, at : at + size].reshape(-1).astype(F32))
        at += size
    gain_one, shift_one, bias_q, bias_out, gain_two, shift_two, bias_down, bias_up, bias_v = wide
    plane_at = f * n_c + c
    bias_q_own = lax.dynamic_slice_in_dim(bias_q, plane_at * own_q, own_q)
    bias_up_own = lax.dynamic_slice_in_dim(bias_up, plane_at * own_h, own_h)

    def own_columns(weight, size):
        pieces = []
        for offset in range(n_f):
            to = flip(f, offset, n_f.bit_length() - 1)
            block = lax.dynamic_slice_in_dim(weight, (to * n_c + c) * size, size, axis=1)
            if offset:
                block = lax.ppermute(block, "fsdp", [(i, i ^ offset) for i in range(n_f)])
            pieces.append(block)
        stacked = jnp.zeros((n_f, weight.shape[0], size), BF16)
        for offset in range(n_f):
            stacked = lax.dynamic_update_slice_in_dim(
                stacked, pieces[offset][None], flip(f, offset, n_f.bit_length() - 1), axis=0
            )
        return stacked.reshape(width, size)

    w_up = own_columns(up_weight, own_h)
    w_out = lax.dynamic_slice_in_dim(out_weight, c * own_q, own_q, axis=0)
    w_down = lax.dynamic_slice_in_dim(down_weight, c * own_h, own_h, axis=0)

    normal_one, inverse_one = norm_parts(tokens_in)
    normed = (normal_one * gain_one + shift_one).astype(BF16)
    normed_pl = plane_gather(normed, n_f, 0)
    query_own = (dot(normed_pl, w_q) + bias_q_own).astype(BF16)
    keyval = dot(normed, w_kv)
    keyval = jnp.concatenate([keyval[:, :head], keyval[:, head:] + bias_v], axis=1).astype(BF16)
    query, keyval_all = exchange(
        query_own.reshape(n_p, rows, own_q), keyval, n_f, n_z, 1, whole=True
    )
    stream = n_z * n_c * rows
    span = min(stream, stream // 2 + rows)
    key_first = jnp.clip((z * n_c + c + 1) * rows - span, 0, stream - span)
    kv = lax.dynamic_slice_in_dim(keyval_all.reshape(stream, 2 * head), key_first, span, axis=0)
    key_pos = key_first + jnp.arange(span, dtype=jnp.int32)
    positions = (z * n_c + c) * rows + jnp.arange(rows, dtype=jnp.int32)
    allowed = (row_docs(key_pos, lengths)[:, None] == row_docs(positions, lengths)[None, :]) & (
        positions[None, :] >= key_pos[:, None]
    )
    mask = jnp.where(allowed, 0.0, -1e30).astype(F32)
    mixed, lse = attend(query, kv, mask, head)
    mixed_own = exchange(mixed, None, n_f, n_z, 2).reshape(n_p * rows, own_q)
    branch = plane_scatter(dot(mixed_own, w_out), n_f, 3) + bias_out
    residual = tokens_in + branch

    normal_two, inverse_two = norm_parts(residual)
    normed_mlp = (normal_two * gain_two + shift_two).astype(BF16)
    normed_mlp_pl = plane_gather(normed_mlp, n_f, 4)
    grad_pl = plane_gather(grad_out, n_f, 5)
    inner = dot(normed_mlp_pl, w_up) + bias_up_own
    activated, gelu_back = jax.vjp(lambda v: jax.nn.gelu(v, approximate=True), inner)
    activated = activated.astype(BF16)
    out_part = dot(activated, w_down).astype(BF16).reshape(n_p, rows, width)
    d_act = dot_nt(grad_pl, w_down)
    d_inner = gelu_back(d_act)[0].astype(BF16)
    e_part = dot_nt(d_inner, w_up).astype(BF16).reshape(n_p, rows, width)
    g_down = dot_tn(activated, grad_pl).astype(BF16)
    g_up = dot_tn(normed_mlp_pl, d_inner).astype(BF16)
    seg = width // n_f

    def chunked(block, most):
        height = min(max(16, (1 << 17) // block.shape[1]), most)
        return block.reshape(block.shape[0] // height, height, block.shape[1])

    done = backward(
        {
            "e_part": e_part,
            "out_part": out_part,
            "g_down_in": chunked(g_down, own_h),
            "g_up_in": chunked(g_up, seg),
            "normed_in": normed_pl.reshape(n_p, rows, width),
            "grad_out": grad_out,
            "normal_two": normal_two,
            "inverse_two": inverse_two,
            "gain_two": gain_two[None],
            "normal_one": normal_one,
            "inverse_one": inverse_one,
            "gain_one": gain_one[None],
            "w_out": w_out,
            "w_q": w_q,
            "w_kv": w_kv,
            "query": query,
            "kv": kv,
            "mask": mask,
            "lse": lse,
            "mixed_own": mixed_own,
            "down_sum": jnp.sum(grad_out.astype(F32), axis=0, keepdims=True),
            "up_sum": jnp.sum(d_inner.astype(F32), axis=0).reshape(own_h // seg, seg),
        },
        n_f,
        n_z,
        head,
        own_h,
        9,
    )
    layer_out = residual + done["out_sum"] + bias_down
    vectors = done["vectors"]
    grad_qkv = jnp.concatenate(
        [done["h_q"], done["h_kv"].reshape(n_c * own_q, 2 * head)], axis=1
    ).astype(F32)
    size = value_bias.shape[0]
    grad_value_bias = lax.dynamic_slice_in_dim(vectors[7], f * size, size)
    return (
        layer_out.astype(BF16)[None],
        done["grad_tokens"][None],
        vectors[0],
        vectors[1],
        grad_qkv,
        vectors[2],
        grad_value_bias,
        done["h_out"].reshape(n_c * own_q, width).astype(F32),
        vectors[3],
        vectors[4],
        vectors[5],
        done["h_up"].astype(F32),
        vectors[8 : 8 + hidden // width].reshape(-1),
        done["h_down"].reshape(n_c * own_h, width).astype(F32),
        vectors[6],
    )


def solution(mesh):
    n_f, n_s = mesh.shape["fsdp"], mesh.shape["seq"]
    split = Mesh(mesh.devices.reshape(n_f, n_s // 2, 2), ("fsdp", "zz", "core"))
    act = P("fsdp", ("zz", "core"), None)
    vec = P("fsdp")
    mat = P("fsdp", None)
    return jax.shard_map(
        shards,
        mesh=split,
        in_specs=(act, mat, vec, vec, mat, vec, vec, mat, vec, vec, vec, mat, vec, mat, vec, act),
        out_specs=(act, act, vec, vec, mat, vec, vec, mat, vec, vec, vec, mat, vec, mat, vec),
        check_vma=False,
    )
```

```python
import functools
import math

import jax
import jax.numpy as jnp
from jax import lax
from jax.experimental import pallas as pl
from jax.experimental.pallas import tpu as pltpu
from jax.sharding import Mesh
from jax.sharding import PartitionSpec as P

EPSILON = 1e-05
F32 = jnp.float32
BF16 = jnp.bfloat16
MESH = pl.DeviceIdType.MESH
VMEM = pltpu.VMEM
DMA = pltpu.SemaphoreType.DMA
ON_CHIP = pl.BlockSpec(memory_space=pltpu.VMEM)
ANYWHERE = pl.BlockSpec(memory_space=pl.ANY)
LANES = 128
CHUNK = 1 << 16


def flip(index, offset, bits):
    for bit in range(bits):
        if offset >> bit & 1:
            index = index + (1 << bit) * (1 - 2 * ((index // (1 << bit)) % 2))
    return index


def bit_orders(n_f):
    bits = n_f.bit_length() - 1
    assert 1 << bits == n_f
    turns = min(bits, 2)
    return bits, [[(turn + at) % bits for at in range(bits)] for turn in range(turns)]


def greet(targets):
    barrier = pltpu.get_barrier_semaphore()
    for target in targets:
        pl.semaphore_signal(barrier, inc=1, device_id=target, device_id_type=MESH)
    pl.semaphore_wait(barrier, len(targets))


def plane_peers(n_f, f, c):
    bits = n_f.bit_length() - 1
    peers = []
    for offset in range(n_f):
        for other in range(2):
            if offset or other:
                peers.append(
                    (offset * 2 + other, {"fsdp": flip(f, offset, bits), "core": c + other * (1 - 2 * c)})
                )
    return peers


def column_peers(n_z, z, c):
    peers = []
    for offset in range(n_z):
        for other in range(2):
            if offset or other:
                peers.append(
                    (offset * 2 + other, {"zz": (z + offset) % n_z, "core": c + other * (1 - 2 * c)})
                )
    return peers


def remote(source, target, send, recv, device):
    return pltpu.make_async_remote_copy(
        src_ref=source,
        dst_ref=target,
        send_sem=send,
        recv_sem=recv,
        device_id=device,
        device_id_type=MESH,
    )


def no_pause(count):
    pass


def near(n_f, f, c):
    bits = n_f.bit_length() - 1
    return [{"fsdp": flip(f, 1 << bit, bits)} for bit in range(bits)] + [{"core": 1 - c}]


def gather_stage(n_f, x_ref, out_ref, send, recv, core_send, core_recv, local_sem, pause):
    f, c = lax.axis_index("fsdp"), lax.axis_index("core")
    rows = x_ref.shape[0]
    bits, orders = bit_orders(n_f)
    part = rows // len(orders)

    def slot(offset):
        return flip(f, offset, bits) * 2 + c

    def piece(turn, offset):
        return out_ref.at[slot(offset), pl.ds(turn * part, part)]

    def link(turn, offset, bit):
        source = x_ref.at[pl.ds(turn * part, part)] if offset == 0 else piece(turn, offset)
        sem = turn * n_f + (offset ^ (1 << bit))
        return remote(
            source,
            piece(turn, offset),
            send.at[sem],
            recv.at[sem],
            {"fsdp": flip(f, 1 << bit, bits)},
        )

    def arrival(turn, offset):
        sem = turn * n_f + offset
        return remote(
            piece(turn, offset), piece(turn, offset), send.at[sem], recv.at[sem], {"core": 1 - c}
        )

    def across(turn, offset):
        source = x_ref.at[pl.ds(turn * part, part)] if offset == 0 else piece(turn, offset)
        sem = turn * n_f + offset
        return remote(
            source, piece(turn, offset), core_send.at[sem], core_recv.at[sem], {"core": 1 - c}
        )

    def crossing(turn, offset):
        where = out_ref.at[flip(f, offset, bits) * 2 + 1 - c, pl.ds(turn * part, part)]
        sem = turn * n_f + offset
        return remote(where, where, core_send.at[sem], core_recv.at[sem], {"core": 1 - c})

    started = []

    def go(copy):
        copy.start()
        started.append(copy)

    for step in range(bits):
        for turn, order in enumerate(orders):
            go(link(turn, 0, order[step]))
    for turn in range(len(orders)):
        go(across(turn, 0))
    own = pltpu.make_async_copy(x_ref, out_ref.at[slot(0)], local_sem)
    own.start()
    pause(1)
    have = [[0] for _ in orders]
    for step in range(bits):
        for at in range(1 << step):
            for turn, order in enumerate(orders):
                offset = have[turn][at] ^ (1 << order[step])
                arrival(turn, offset).wait_recv()
                for later in range(step + 1, bits):
                    go(link(turn, offset, order[later]))
                go(across(turn, offset))
                have[turn].append(offset)
                pause(1)
    for copy in started:
        copy.wait_send()
    for turn in range(len(orders)):
        for offset in have[turn]:
            crossing(turn, offset).wait_recv()
    own.wait()


def gather_body(n_f, x_ref, out_ref, *sems):
    f, c = lax.axis_index("fsdp"), lax.axis_index("core")
    greet(near(n_f, f, c))
    gather_stage(n_f, x_ref, out_ref, *sems, no_pause)


def plane_gather(x, n_f, ident):
    rows, width = x.shape
    count = len(bit_orders(n_f)[1]) * n_f
    out = pl.pallas_call(
        functools.partial(gather_body, n_f),
        out_shape=jax.ShapeDtypeStruct((n_f * 2, rows, width), x.dtype),
        in_specs=[ON_CHIP],
        out_specs=ON_CHIP,
        scratch_shapes=[DMA((count,))] * 4 + [DMA],
        compiler_params=pltpu.CompilerParams(
            collective_id=ident, has_side_effects=True, vmem_limit_bytes=40 << 20
        ),
        name="plane_gather",
    )(x)
    return out.reshape(n_f * 2 * rows, width)


def scatter_stage(
    n_f, part_ref, out_ref, acc, core_in, link_in, send, recv, core_send, core_recv, pause
):
    f, c = lax.axis_index("fsdp"), lax.axis_index("core")
    rows = out_ref.shape[0]
    bits, orders = bit_orders(n_f)
    part = rows // len(orders)
    started = []

    def go(copy):
        copy.start()
        started.append(copy)

    def held(offset, where):
        if acc is None:
            return part_ref.at[flip(f, offset, bits) * 2 + c, where]
        return acc.at[offset, where]

    def across(turn, offset):
        where = pl.ds(turn * part, part)
        sem = turn * n_f + offset
        return remote(
            part_ref.at[flip(f, offset, bits) * 2 + 1 - c, where],
            core_in.at[offset, where],
            core_send.at[sem],
            core_recv.at[sem],
            {"core": 1 - c},
        )

    def link(turn, offset, bit):
        where = pl.ds(turn * part, part)
        sem = turn * n_f + offset
        return remote(
            held(offset, where),
            link_in.at[offset, where],
            send.at[sem],
            recv.at[sem],
            {"fsdp": flip(f, 1 << bit, bits)},
        )

    plan = [[] for _ in range(bits)] + [[(turn, 0) for turn in range(len(orders))]]
    for step in range(bits):
        for offset in range(n_f):
            for turn, order in enumerate(orders):
                if offset >> order[step] & 1 and not any(offset >> b & 1 for b in order[:step]):
                    plan[step].append((turn, offset))
    for todo in plan:
        for turn, offset in todo:
            go(across(turn, offset))
    for step, todo in enumerate(plan):
        pause(1)
        for turn, offset in todo:
            where = pl.ds(turn * part, part)
            across(turn, offset).wait_recv()
            total = part_ref[flip(f, offset, bits) * 2 + c, where].astype(F32)
            total = total + core_in[offset, where].astype(F32)
            for bit in orders[turn][:step]:
                link(turn, offset | (1 << bit), bit).wait_recv()
                total = total + link_in[offset | (1 << bit), where].astype(F32)
            if offset:
                held(offset, where)[...] = total.astype(BF16)
                go(link(turn, offset, orders[turn][step]))
                if offset == n_f - 1:
                    pause(1)
            else:
                out_ref[where] = total
    for copy in started:
        copy.wait_send()


def scatter_body(n_f, *refs):
    f, c = lax.axis_index("fsdp"), lax.axis_index("core")
    greet(near(n_f, f, c))
    scatter_stage(n_f, *refs, no_pause)


def plane_scatter(partial, n_f, ident):
    width = partial.shape[1]
    rows = partial.shape[0] // (n_f * 2)
    count = len(bit_orders(n_f)[1]) * n_f
    return pl.pallas_call(
        functools.partial(scatter_body, n_f),
        out_shape=jax.ShapeDtypeStruct((rows, width), F32),
        in_specs=[ON_CHIP],
        out_specs=ON_CHIP,
        scratch_shapes=[VMEM((n_f, rows, width), BF16)] * 3 + [DMA((count,))] * 4,
        compiler_params=pltpu.CompilerParams(
            collective_id=ident, has_side_effects=True, vmem_limit_bytes=40 << 20
        ),
        name="plane_scatter",
    )(partial.astype(BF16).reshape(n_f * 2, rows, width))


def exchange_stage(n_f, n_z, plane_in, column_in, plane_out, column_out, sems, whole, pause):
    f, z, c = lax.axis_index("fsdp"), lax.axis_index("zz"), lax.axis_index("core")
    peers = plane_peers(n_f, f, c)
    others = column_peers(n_z, z, c) if column_in is not None else []
    copies = []
    local = []
    if column_in is not None:
        mine = z * 2 + c
        for sem, device in others:
            to = device["zz"] * 2 + device["core"]
            source = column_in if whole else column_in.at[to]
            copies.append(
                remote(source, column_out.at[mine], sems[2].at[sem], sems[3].at[sem], device)
            )
        source = column_in if whole else column_in.at[mine]
        local.append(pltpu.make_async_copy(source, column_out.at[mine], sems[5]))
    mine = f * 2 + c
    for sem, device in peers:
        to = device["fsdp"] * 2 + device["core"]
        copies.append(
            remote(plane_in.at[to], plane_out.at[mine], sems[0].at[sem], sems[1].at[sem], device)
        )
    local.append(pltpu.make_async_copy(plane_in.at[mine], plane_out.at[mine], sems[4]))
    for copy in copies + local:
        copy.start()
    pause(1)
    for copy in copies:
        copy.wait_send()
    for sem, device in peers:
        frm = device["fsdp"] * 2 + device["core"]
        remote(
            plane_out.at[frm], plane_out.at[frm], sems[0].at[sem], sems[1].at[sem], device
        ).wait_recv()
    if column_in is not None:
        for offset in range(n_z):
            for other in range(2):
                if offset or other:
                    frm = ((z + n_z - offset) % n_z) * 2 + c + other * (1 - 2 * c)
                    sem = offset * 2 + other
                    remote(
                        column_out.at[frm],
                        column_out.at[frm],
                        sems[2].at[sem],
                        sems[3].at[sem],
                        {"core": 1 - c},
                    ).wait_recv()
    for copy in local:
        copy.wait()


def exchange_body(n_f, n_z, plane_in, column_in, plane_out, column_out, sems, whole):
    f, z, c = lax.axis_index("fsdp"), lax.axis_index("zz"), lax.axis_index("core")
    peers = plane_peers(n_f, f, c)
    others = column_peers(n_z, z, c) if column_in is not None else []
    greet([device for _, device in peers + others])
    exchange_stage(
        n_f, n_z, plane_in, column_in, plane_out, column_out, sems, whole, no_pause
    )


def exchange(plane_in, column_in, n_f, n_z, ident, whole=False):
    outs = [jax.ShapeDtypeStruct(plane_in.shape, plane_in.dtype)]
    ins = [plane_in]
    if column_in is not None:
        block = column_in.shape if whole else column_in.shape[1:]
        outs.append(jax.ShapeDtypeStruct((n_z * 2,) + block, column_in.dtype))
        ins.append(column_in)

    def body(*refs):
        if column_in is None:
            plane_ref, plane_out = refs[:2]
            exchange_body(n_f, n_z, plane_ref, None, plane_out, None, refs[2:], whole)
        else:
            plane_ref, column_ref, plane_out, column_out = refs[:4]
            exchange_body(
                n_f, n_z, plane_ref, column_ref, plane_out, column_out, refs[4:], whole
            )

    result = pl.pallas_call(
        body,
        out_shape=outs,
        in_specs=[ON_CHIP] * len(ins),
        out_specs=[ON_CHIP] * len(outs),
        scratch_shapes=[DMA((n_f * 2,))] * 2 + [DMA((n_z * 2,))] * 2 + [DMA] * 2,
        compiler_params=pltpu.CompilerParams(
            collective_id=ident, has_side_effects=True, vmem_limit_bytes=24 << 20
        ),
        name="exchange",
    )(*ins)
    return result if column_in is not None else result[0]


class Line:
    def __init__(self, n_z, chunks, sems):
        self.n_z, self.chunks = n_z, chunks
        self.red_send, self.red_recv, self.fin_send, self.fin_recv, self.own_sem = sems
        self.z = lax.axis_index("zz")
        self.done = 0

    def toward(self, k, source):
        return remote(
            source,
            self.chunks[k][1],
            self.red_send.at[k],
            self.red_recv.at[k],
            {"zz": jnp.maximum(self.z - 1, 0)},
        )

    def outward(self, k, source):
        return remote(
            source,
            self.chunks[k][2],
            self.fin_send.at[k],
            self.fin_recv.at[k],
            {"zz": jnp.minimum(self.z + 1, self.n_z - 1)},
        )

    def keep(self, k):
        return pltpu.make_async_copy(self.chunks[k][1], self.chunks[k][2], self.own_sem.at[k])

    def reduce(self, k, z):
        own, landing, _ = self.chunks[k]
        if z == self.n_z - 1:
            self.toward(k, own).start()
            return
        self.toward(k, own).wait_recv()
        height = min(16, own.shape[0])

        @pl.loop(0, own.shape[0] // height)
        def _(at):
            where = pl.ds(pl.multiple_of(at * height, height), height)
            landing[where] = (own[where].astype(F32) + landing[where].astype(F32)).astype(BF16)

        if z > 0:
            self.toward(k, landing).start()
        else:
            self.outward(k, landing).start()
            self.keep(k).start()

    def spread(self, k, z):
        if z == 0:
            self.keep(k).wait()
            return
        self.outward(k, self.chunks[k][2]).wait_recv()
        if z < self.n_z - 1:
            self.outward(k, self.chunks[k][2]).start()

    def tick(self, then=None):
        t = self.done
        self.done += 1
        total = len(self.chunks)
        for z in range(self.n_z):
            k = t - (self.n_z - 1 - z)
            if 0 <= k < total:

                @pl.when(self.z == z)
                def _():
                    self.reduce(k, z)

            k = t - self.lag(z)
            if 0 <= k < total:

                @pl.when(self.z == z)
                def _():
                    self.spread(k, z)
                    if then is not None:
                        then(k)

    def lag(self, z):
        return self.n_z + 2 * z if z < self.n_z - 1 else self.n_z + 2 * z + 2

    def ticks(self):
        return len(self.chunks) + self.lag(self.n_z - 1)

    def left(self):
        return self.ticks() - self.done

    def finish(self):
        for k in range(len(self.chunks)):

            @pl.when(self.z > 0)
            def _():
                self.toward(k, self.chunks[k][0]).wait_send()

            @pl.when(self.z < self.n_z - 1)
            def _():
                self.outward(k, self.chunks[k][2]).wait_send()


def vector_stage(n_f, n_z, in_ref, out_ref, plane_in, part, line_in, sems, pause):
    f, z, c = lax.axis_index("fsdp"), lax.axis_index("zz"), lax.axis_index("core")
    send, recv, line_send, line_recv, local = sems
    peers = plane_peers(n_f, f, c)
    others = [(offset, {"zz": (z + offset) % n_z}) for offset in range(1, n_z)]
    mine = f * 2 + c
    copies = [
        remote(in_ref.at[device["fsdp"]], plane_in.at[mine], send.at[sem], recv.at[sem], device)
        for sem, device in peers
    ]
    for copy in copies:
        copy.start()
    own = pltpu.make_async_copy(in_ref.at[f], plane_in.at[mine], local)
    own.start()
    own.wait()
    pause(1)
    for sem, device in peers:
        where = plane_in.at[device["fsdp"] * 2 + device["core"]]
        remote(where, where, send.at[sem], recv.at[sem], device).wait_recv()
    total = plane_in[0]
    for at in range(1, n_f * 2):
        total = total + plane_in[at]
    part[...] = total
    line = [
        remote(part, line_in.at[z], line_send.at[sem], line_recv.at[sem], device)
        for sem, device in others
    ]
    for copy in line:
        copy.start()
    pause(1)
    for offset in range(1, n_z):
        where = line_in.at[(z + n_z - offset) % n_z]
        remote(
            where, where, line_send.at[offset], line_recv.at[offset], {"core": 1 - c}
        ).wait_recv()
    line_in[z] = total
    total = line_in[0]
    for at in range(1, n_z):
        total = total + line_in[at]
    out_ref[...] = total
    for copy in copies + line:
        copy.wait_send()


def front_body(n_f, small, w_query, w_kv, small_o, query_o, kv_o, sems):
    f, c = lax.axis_index("fsdp"), lax.axis_index("core")
    bits = n_f.bit_length() - 1
    send, recv, local = sems
    greet([{"fsdp": flip(f, offset, bits)} for offset in range(1, n_f)])
    size = query_o.shape[2]

    def block(to):
        return w_query.at[:, pl.ds(pl.multiple_of((to * 2 + c) * size, LANES), size)]

    copies, locals_ = [], []
    for at, (source, target) in enumerate(((small, small_o), (None, query_o), (w_kv, kv_o))):
        for offset in range(1, n_f):
            to = flip(f, offset, bits)
            sem = at * n_f + offset
            copies.append(
                remote(
                    block(to) if source is None else source,
                    target.at[f],
                    send.at[sem],
                    recv.at[sem],
                    {"fsdp": to},
                )
            )
        locals_.append(
            pltpu.make_async_copy(
                block(f) if source is None else source, target.at[f], local.at[at]
            )
        )
    for copy in copies + locals_:
        copy.start()
    for copy in copies:
        copy.wait_send()
    for at, target in enumerate((small_o, query_o, kv_o)):
        for offset in range(1, n_f):
            where = target.at[flip(f, offset, bits)]
            sem = at * n_f + offset
            remote(where, where, send.at[sem], recv.at[sem], {"core": 1 - c}).wait_recv()
    for copy in locals_:
        copy.wait()


def front(small, w_query, w_kv, own_q, n_f, ident):
    def body(*refs):
        front_body(n_f, *refs[:6], refs[6:])

    return pl.pallas_call(
        body,
        out_shape=[
            jax.ShapeDtypeStruct((n_f,) + small.shape, BF16),
            jax.ShapeDtypeStruct((n_f, w_query.shape[0], own_q), BF16),
            jax.ShapeDtypeStruct((n_f,) + w_kv.shape, BF16),
        ],
        in_specs=[ON_CHIP, ANYWHERE, ON_CHIP],
        out_specs=[ON_CHIP] * 3,
        scratch_shapes=[DMA((3 * n_f,))] * 2 + [DMA((3,))],
        compiler_params=pltpu.CompilerParams(
            collective_id=ident, has_side_effects=True, vmem_limit_bytes=24 << 20
        ),
        name="front",
    )(small, w_query, w_kv)


def heads_side_by_side(block, head):
    count = block.shape[1] // head
    return jnp.concatenate([block[:, at * head : (at + 1) * head] for at in range(count)], axis=0)


def heads_apart(block, count):
    rows = block.shape[0] // count
    return jnp.concatenate([block[at * rows : (at + 1) * rows] for at in range(count)], axis=1)


def attend_body(head, scale, query_ref, kv_ref, mask_ref, mixed_ref, lse_ref):
    query = heads_side_by_side(query_ref[0], head)
    count = query_ref.shape[2] // head
    keys, values = kv_ref[:, :head], kv_ref[:, head:]
    mask = jnp.concatenate([mask_ref[...]] * count, axis=1)
    scores = dot_nt(keys, query) * scale + mask
    peak = jnp.max(scores, axis=0, keepdims=True)
    weights = jnp.exp(scores - peak)
    total = jnp.sum(weights, axis=0, keepdims=True)
    probs = (weights / total).astype(BF16)
    mixed_ref[0] = heads_apart(dot_tn(probs, values).astype(BF16), count)
    lse_ref[0] = peak + jnp.log(total)


def attend(query, kv, mask, head):
    n_p, rows, width = query.shape
    span = kv.shape[0]
    count = width // head
    return pl.pallas_call(
        functools.partial(attend_body, head, 1.0 / math.sqrt(head)),
        out_shape=[
            jax.ShapeDtypeStruct(query.shape, BF16),
            jax.ShapeDtypeStruct((n_p, 1, count * rows), F32),
        ],
        grid=(n_p,),
        in_specs=[
            pl.BlockSpec((1, rows, width), lambda p: (p, 0, 0)),
            pl.BlockSpec((span, 2 * head), lambda p: (0, 0)),
            pl.BlockSpec((span, rows), lambda p: (0, 0)),
        ],
        out_specs=[
            pl.BlockSpec((1, rows, width), lambda p: (p, 0, 0)),
            pl.BlockSpec((1, 1, count * rows), lambda p: (p, 0, 0)),
        ],
        name="attend",
    )(query, kv, mask)


def attend_back_block(head, query_in, grad_in, kv_ref, mask_ref, lse):
    scale = 1.0 / math.sqrt(head)
    query = heads_side_by_side(query_in, head)
    grad = heads_side_by_side(grad_in, head)
    count = query_in.shape[1] // head
    keys, values = kv_ref[:, :head], kv_ref[:, head:]
    mask = jnp.concatenate([mask_ref[...]] * count, axis=1)
    scores = dot_nt(keys, query) * scale + mask
    probs = jnp.exp(scores - lse)
    d_probs = dot_nt(values, grad)
    delta = jnp.sum(probs * d_probs, axis=0, keepdims=True)
    d_scores = (probs * (d_probs - delta)).astype(BF16)
    d_query = heads_apart((dot_tn(d_scores, keys) * scale).astype(BF16), count)
    d_keys = dot(d_scores, query) * scale
    d_values = dot(probs.astype(BF16), grad)
    return d_query, d_keys, d_values


PACE = 2


class Box:
    pass


def rows_of(ref, at, height=16):
    return pl.ds(pl.multiple_of(at * height, height), height)


def norm_back_tiles(grad_ref, extra_ref, normal_ref, inverse_ref, gain_ref, base_ref, sums, store):
    rows = normal_ref.shape[0]

    @pl.loop(0, rows // 16)
    def _(at):
        where = rows_of(normal_ref, at)
        grad = grad_ref[where]
        if extra_ref is not None:
            grad = grad + extra_ref[where]
        normal = normal_ref[where].astype(F32)
        scaled = grad * gain_ref[...]
        first = jnp.mean(scaled, axis=-1, keepdims=True)
        second = jnp.mean(scaled * normal, axis=-1, keepdims=True)
        result = base_ref[where].astype(F32) + inverse_ref[where] * (
            scaled - first - normal * second
        )
        store(where, result)
        sums[0:1] += jnp.sum(grad * normal, axis=0, keepdims=True)
        sums[1:2] += jnp.sum(grad, axis=0, keepdims=True)
        sums[2:3] += jnp.sum(result.astype(BF16).astype(F32), axis=0, keepdims=True)


def backward_body(n_f, n_z, head, names, *refs):
    r = Box()
    for name, ref in zip(names, refs, strict=True):
        setattr(r, name, ref)
    f, z, c = lax.axis_index("fsdp"), lax.axis_index("zz"), lax.axis_index("core")
    bits = n_f.bit_length() - 1
    n_p = n_f * 2
    me = f * 2 + c
    rows, width = r.grad_out.shape
    own_q = r.w_out.shape[0]

    loads = {}
    for at, (name, source, target) in enumerate(
        (
            ("part", r.e_part, r.part),
            ("down", r.g_down_in, r.g_down),
            ("up", r.g_up_in, r.g_up),
        )
    ):
        loads[name] = pltpu.make_async_copy(source, target, r.load_sem.at[at])
        loads[name].start()
    greet([device for _, device in plane_peers(n_f, f, c) + column_peers(n_z, z, c)])

    kinds = []
    chunks = []
    for kind, own, landing, final in (
        ("up", r.g_up, r.land_up, r.fin_up),
        ("down", r.g_down, r.land_down, r.h_down.at[c]),
        ("out", r.g_out, r.land_out, r.h_out.at[c]),
        ("q", r.g_q, r.land_q, r.fin_q),
        ("kv", r.g_kv, r.land_kv, r.h_kv.at[c]),
    ):
        for k in range(own.shape[0]):
            kinds.append((kind, k))
            chunks.append((own.at[k], landing.at[k], final.at[k]))
    line = Line(n_z, chunks, (r.red_send, r.red_recv, r.fin_send, r.fin_recv, r.keep_sem))
    home = {"down": r.h_down, "out": r.h_out, "kv": r.h_kv, "up": r.h_up, "q": r.h_q}

    def swap(at, side):
        kind, k = kinds[at]
        where = home[kind].at[side, k]
        return remote(where, where, r.swap_send.at[at], r.swap_recv.at[at], {"core": 1 - c})

    def block(kind, turn, source):
        target = home[kind]
        height, size = finals[kind].shape[1:]
        cols = pl.ds(pl.multiple_of(source * size, LANES), size)
        return target.at[pl.ds(pl.multiple_of(turn * height, height), height), cols]

    finals = {"up": r.fin_up, "q": r.fin_q}
    home_sem = {
        "up": (r.up_send, r.up_mate, r.up_recv, r.up_relay, r.up_cross),
        "q": (r.q_send, r.q_mate, r.q_recv, r.q_relay, r.q_cross),
    }

    def turns(kind):
        return finals[kind].shape[0] // n_f

    def moves(kind, k):
        send, mate, recv, _, cross = home_sem[kind]
        owner, turn = k // turns(kind), k % turns(kind)
        where = block(kind, turn, me)
        sem = turn * n_f + f
        source = finals[kind].at[k]
        return (
            f == owner,
            lambda: pltpu.make_async_copy(source, where, send.at[k]),
            lambda: remote(source, where, mate.at[k], cross.at[sem], {"core": 1 - c}),
            lambda: remote(source, where, send.at[k], recv.at[sem], {"fsdp": owner}),
        )

    def deliver_split(kind, k):
        here, own, other, away = moves(kind, k)

        @pl.when(here)
        def _():
            own().start()
            other().start()

        @pl.when(jnp.logical_not(here))
        def _():
            away().start()

    def relay(kind, turn, offset):
        _, _, recv, send, cross = home_sem[kind]
        source = flip(f, offset, bits)
        where = block(kind, turn, source * 2 + c)
        sem = turn * n_f + source
        return (
            lambda: remote(where, where, send.at[sem], recv.at[sem], {"core": 1 - c}),
            lambda: remote(where, where, send.at[sem], cross.at[sem], {"core": 1 - c}),
        )

    def relay_all(kind):
        @pl.loop(0, turns(kind))
        def _(turn):
            for offset in range(1, n_f):
                arrival, onward = relay(kind, turn, offset)
                arrival().wait_recv()
                onward().start()

    def deliver(at):
        kind, k = kinds[at]
        if kind in ("down", "out", "kv"):
            swap(at, c).start()
        elif kind == "q":
            deliver_split(kind, k)

    def delivered():
        for at, (kind, k) in enumerate(kinds):
            if kind in ("down", "out", "kv"):
                swap(at, c).wait_send()
                swap(at, 1 - c).wait_recv()
        for kind in ("up", "q"):

            @pl.loop(0, finals[kind].shape[0])
            def _(k):
                here, own, other, away = moves(kind, k)

                @pl.when(here)
                def _():
                    own().wait()
                    other().wait_send()

                @pl.when(jnp.logical_not(here))
                def _():
                    away().wait_send()

            @pl.loop(0, turns(kind))
            def _(turn):
                for offset in range(n_f):
                    if offset:
                        relay(kind, turn, offset)[1]().wait_send()
                    source = flip(f, offset, bits)
                    where = block(kind, turn, source * 2 + 1 - c)
                    cross = home_sem[kind][4].at[turn * n_f + source]
                    remote(where, where, r.swap_send.at[0], cross, {"core": 1 - c}).wait_recv()

    ready = [False]
    limit = [r.g_down.shape[0] + r.g_up.shape[0]]

    def pause(count):
        if not ready[0]:
            loads["down"].wait()
            loads["up"].wait()
            ready[0] = True
        for _ in range(count * PACE):
            if line.left() and line.done < limit[0]:
                line.tick(deliver)

    for ref in (r.sums_two, r.sums_one):
        ref[...] = jnp.zeros_like(ref)
    loads["part"].wait()
    scatter_stage(
        n_f, r.part, r.e_sum, None, r.core_in, r.link_in, *(r.scatter_one.at[at] for at in range(4)), pause
    )

    def store_two(where, result):
        r.d_residual[where] = result
        r.d_branch[where] = result.astype(BF16)

    norm_back_tiles(
        r.e_sum, None, r.normal_two, r.inverse_two, r.gain_two, r.grad_out, r.sums_two, store_two
    )
    loads["normed"] = pltpu.make_async_copy(r.normed_in, r.part, r.load_sem.at[3])
    loads["normed"].start()
    gather_stage(
        n_f, r.d_branch, r.branch_pl, *(r.gather_one.at[at] for at in range(4)), r.local_sem.at[0], pause
    )

    @pl.loop(0, n_p)
    def _(p):
        r.mixed_send[p] = dot_nt(r.branch_pl[p], r.w_out[...]).astype(BF16)

    exchange_stage(
        n_f,
        n_z,
        r.mixed_send,
        None,
        r.d_mixed,
        None,
        [r.swap_one.at[0], r.swap_one.at[1], None, None, r.local_sem.at[1], None],
        False,
        pause,
    )
    tile = min(512, width)
    high = r.g_out.shape[1]
    for j in range(own_q // LANES):
        for n in range(width // tile):
            cols = pl.ds(n * tile, tile)
            result = dot_tn(
                r.mixed_own[:, j * LANES : (j + 1) * LANES],
                r.branch_pl[:, :, cols].reshape(n_p * rows, tile),
            ).astype(BF16)
            for k in range(LANES // high):
                r.g_out[j * (LANES // high) + k, :, cols] = result[k * high : (k + 1) * high]
    limit[0] += r.g_out.shape[0]

    r.d_kv_span[...] = jnp.zeros_like(r.d_kv_span)
    step = max(1, n_p // 4)
    for first in range(0, n_p, step):

        @pl.loop(first, first + step)
        def _(p):
            d_query, d_keys, d_values = attend_back_block(
                head, r.query[p], r.d_mixed[p], r.kv, r.mask, r.lse[p]
            )
            r.dq_send[p] = d_query
            r.d_kv_span[:, :head] += d_keys
            r.d_kv_span[:, head:] += d_values

        pause(1)
    span = r.d_kv_span.shape[0]
    stream = n_z * 2 * rows
    first = jnp.maximum((z * 2 + c + 1) * rows - span, 0)
    r.dkv_send[...] = jnp.zeros_like(r.dkv_send)

    @pl.loop(0, span // rows)
    def _(at):
        block_at = (jnp.maximum((z * 2 + c + 1) * rows - span, 0)) // rows + at
        r.dkv_send[block_at] = r.d_kv_span[pl.ds(pl.multiple_of(at * rows, rows), rows)].astype(BF16)

    exchange_stage(
        n_f,
        n_z,
        r.dq_send,
        r.dkv_send,
        r.dq_own,
        r.dkv_recv,
        [
            r.swap_two.at[0],
            r.swap_two.at[1],
            r.column_sem.at[0],
            r.column_sem.at[1],
            r.local_sem.at[2],
            r.local_sem.at[3],
        ],
        False,
        pause,
    )
    total = r.dkv_recv[0].astype(F32)
    for s in range(1, n_z * 2):
        total = total + r.dkv_recv[s].astype(F32)
    r.d_kv[...] = total.astype(BF16)

    @pl.loop(0, n_p)
    def _(p):
        for n in range(width // tile):
            cols = pl.ds(n * tile, tile)
            r.branch_pl[p, :, cols] = dot_nt(r.dq_own[p], r.w_q[cols]).astype(BF16)

    scatter_stage(
        n_f, r.branch_pl, r.e_sum, None, r.core_in, r.link_in, *(r.scatter_two.at[at] for at in range(4)), pause
    )
    for n in range(width // tile):
        cols = pl.ds(n * tile, tile)
        r.e_extra[:, cols] = dot_nt(r.d_kv[...], r.w_kv[cols])

    def store_one(where, result):
        r.grad_tokens[where] = result.astype(BF16)

    norm_back_tiles(
        r.e_sum, r.e_extra, r.normal_one, r.inverse_one, r.gain_one, r.d_residual, r.sums_one, store_one
    )
    gather_stage(
        n_f, r.d_kv, r.dkv_pl, *(r.gather_two.at[at] for at in range(4)), r.local_sem.at[4], pause
    )

    loads["normed"].wait()
    dq_all = r.dq_own[...].reshape(n_p * rows, own_q)
    step = min(256, r.g_q.shape[1])
    for k in range(r.g_q.shape[0]):
        for at in range(r.g_q.shape[1] // step):
            base = k * r.g_q.shape[1] + at * step
            r.g_q[k, at * step : (at + 1) * step] = dot_tn(
                r.part[:, :, base : base + step].reshape(n_p * rows, step), dq_all
            ).astype(BF16)
    cols = pl.ds(pl.multiple_of(me * own_q, LANES), own_q)
    r.g_kv[0] = dot_tn(
        r.part[:, :, cols].reshape(n_p * rows, own_q), r.dkv_pl[...].reshape(n_p * rows, 2 * head)
    ).astype(BF16)
    loads["out"] = pltpu.make_async_copy(r.out_part, r.part, r.load_sem.at[4])
    loads["out"].start()
    limit[0] = line.ticks()
    pause(2)

    while line.done < r.g_up.shape[0] + line.lag(n_z - 1):
        pause(1)

    @pl.loop(0, r.g_up.shape[0])
    def _(k):
        deliver_split("up", k)

    seg = r.vec_in.shape[2]
    r.vec_in[...] = jnp.zeros_like(r.vec_in)
    up_rows = r.up_sum.shape[0]
    d_value = jnp.sum(r.d_kv[:, head:].astype(F32), axis=0, keepdims=True)
    for o in range(n_f):
        cols = slice(o * seg, (o + 1) * seg)
        r.vec_in[o, 0:1] = r.sums_one[0:1, cols]
        r.vec_in[o, 1:2] = r.sums_one[1:2, cols]
        r.vec_in[o, 3:4] = r.sums_two[2:3, cols]
        r.vec_in[o, 4:5] = r.sums_two[0:1, cols]
        r.vec_in[o, 5:6] = r.sums_two[1:2, cols]
        r.vec_in[o, 6:7] = r.down_sum[0:1, cols]
        r.vec_in[o, 7:8, :head] = d_value
        for side in range(2):
            part = jnp.sum(r.dq_send[o * 2 + side].astype(F32), axis=0, keepdims=True)
            r.vec_in[o, 2:3, side * own_q : (side + 1) * own_q] = part

        for side in range(2):

            @pl.when((f == o) & (c == side))
            def _():
                r.vec_in[o, 8 + side * up_rows : 8 + (side + 1) * up_rows] = r.up_sum[...]

    vector_stage(
        n_f,
        n_z,
        r.vec_in,
        r.vectors,
        r.vec_plane,
        r.vec_part,
        r.vec_line,
        [r.vec_sem.at[0], r.vec_sem.at[1], r.vec_line_sem.at[0], r.vec_line_sem.at[1], r.local_sem.at[5]],
        pause,
    )

    loads["out"].wait()
    scatter_stage(
        n_f, r.part, r.out_sum, None, r.core_in, r.link_in, *(r.scatter_three.at[at] for at in range(4)), pause
    )
    while line.left() > 4 * PACE:
        pause(1)
    relay_all("up")
    while line.left():
        pause(1)
    relay_all("q")
    line.finish()
    delivered()


def backward(inputs, n_f, n_z, head, own_h, ident):
    rows, width = inputs["grad_out"].shape
    n_p = n_f * 2
    n_s = n_z * 2
    own_q = width // n_p
    seg = width // n_f
    count = len(bit_orders(n_f)[1]) * n_f
    span = inputs["kv"].shape[0]
    high = max(16, CHUNK // width)
    tall = min(seg, CHUNK // own_q)
    down = inputs["g_down_in"].shape
    up = inputs["g_up_in"].shape
    out = (own_q // high, high, width)
    query = (width // tall, tall, own_q)
    keyval = (1, own_q, 2 * head)
    chunks = down[0] + up[0] + out[0] + query[0] + 1
    in_hbm = ("e_part", "g_down_in", "g_up_in", "normed_in", "out_part")
    outs = {
        "grad_tokens": ((rows, width), BF16, ON_CHIP),
        "out_sum": ((rows, width), F32, ON_CHIP),
        "vectors": ((16, seg), F32, ON_CHIP),
        "h_down": ((2,) + down, BF16, ANYWHERE),
        "h_up": ((seg, own_h * n_p), BF16, ANYWHERE),
        "h_out": ((2,) + out, BF16, ANYWHERE),
        "h_q": ((seg, width), BF16, ANYWHERE),
        "h_kv": ((2,) + keyval, BF16, ANYWHERE),
    }
    plane = (n_p, rows, width)
    blocks = (n_p, rows, own_q)
    scratch = {
        "part": VMEM(plane, BF16),
        "g_down": VMEM(down, BF16),
        "g_up": VMEM(up, BF16),
        "g_out": VMEM(out, BF16),
        "g_q": VMEM(query, BF16),
        "g_kv": VMEM(keyval, BF16),
        "land_down": VMEM(down, BF16),
        "land_up": VMEM(up, BF16),
        "land_out": VMEM(out, BF16),
        "land_q": VMEM(query, BF16),
        "land_kv": VMEM(keyval, BF16),
        "fin_up": VMEM(up, BF16),
        "fin_q": VMEM(query, BF16),
        "core_in": VMEM((n_f, rows, width), BF16),
        "link_in": VMEM((n_f, rows, width), BF16),
        "e_sum": VMEM((rows, width), F32),
        "e_extra": VMEM((rows, width), F32),
        "d_residual": VMEM((rows, width), F32),
        "d_branch": VMEM((rows, width), BF16),
        "branch_pl": VMEM(plane, BF16),
        "mixed_send": VMEM(blocks, BF16),
        "d_mixed": VMEM(blocks, BF16),
        "dq_send": VMEM(blocks, BF16),
        "dq_own": VMEM(blocks, BF16),
        "d_kv_span": VMEM((span, 2 * head), F32),
        "dkv_send": VMEM((n_s, rows, 2 * head), BF16),
        "dkv_recv": VMEM((n_s, rows, 2 * head), BF16),
        "d_kv": VMEM((rows, 2 * head), BF16),
        "dkv_pl": VMEM((n_p, rows, 2 * head), BF16),
        "sums_one": VMEM((8, width), F32),
        "sums_two": VMEM((8, width), F32),
        "vec_in": VMEM((n_f, 16, seg), F32),
        "vec_plane": VMEM((n_p, 16, seg), F32),
        "vec_part": VMEM((16, seg), F32),
        "vec_line": VMEM((n_z, 16, seg), F32),
        "load_sem": DMA((5,)),
        "local_sem": DMA((6,)),
        "red_send": DMA((chunks,)),
        "red_recv": DMA((chunks,)),
        "fin_send": DMA((chunks,)),
        "fin_recv": DMA((chunks,)),
        "keep_sem": DMA((chunks,)),
        "swap_send": DMA((chunks,)),
        "swap_recv": DMA((chunks,)),
        "up_send": DMA((up[0],)),
        "up_mate": DMA((up[0],)),
        "up_recv": DMA((up[0],)),
        "up_relay": DMA((up[0],)),
        "up_cross": DMA((up[0],)),
        "q_send": DMA((query[0],)),
        "q_mate": DMA((query[0],)),
        "q_recv": DMA((query[0],)),
        "q_relay": DMA((query[0],)),
        "q_cross": DMA((query[0],)),
        "scatter_one": DMA((4, count)),
        "scatter_two": DMA((4, count)),
        "scatter_three": DMA((4, count)),
        "gather_one": DMA((4, count)),
        "gather_two": DMA((4, count)),
        "swap_one": DMA((2, n_p)),
        "swap_two": DMA((2, n_p)),
        "column_sem": DMA((2, n_s)),
        "vec_sem": DMA((2, n_p)),
        "vec_line_sem": DMA((2, n_z)),
    }
    names = list(inputs) + list(outs) + list(scratch)
    result = pl.pallas_call(
        functools.partial(backward_body, n_f, n_z, head, names),
        out_shape=[jax.ShapeDtypeStruct(shape, kind) for shape, kind, _ in outs.values()],
        in_specs=[ANYWHERE if name in in_hbm else ON_CHIP for name in inputs],
        out_specs=[place for _, _, place in outs.values()],
        scratch_shapes=list(scratch.values()),
        compiler_params=pltpu.CompilerParams(
            collective_id=ident, has_side_effects=True, vmem_limit_bytes=67043328
        ),
        name="backward",
    )(*inputs.values())
    return dict(zip(outs, result))


def norm_parts(values_in):
    row_mean = jnp.mean(values_in, axis=-1, keepdims=True)
    centered = values_in - row_mean
    variance = jnp.mean(centered * centered, axis=-1, keepdims=True)
    inverse = lax.rsqrt(variance + EPSILON)
    return centered * inverse, inverse


def norm_back(grad, normal, inverse, gain):
    scaled = grad * gain
    first = jnp.mean(scaled, axis=-1, keepdims=True)
    second = jnp.mean(scaled * normal, axis=-1, keepdims=True)
    return inverse * (scaled - first - normal * second)


def row_docs(positions, lengths):
    doc_ends = jnp.cumsum(lengths)
    return jnp.sum((positions[:, None] >= doc_ends[None, :]).astype(jnp.int32), axis=1)


def dot(left, right):
    return jnp.dot(left, right, preferred_element_type=F32)


def dot_tn(left, right):
    return lax.dot_general(left, right, (((0,), (0,)), ((), ())), preferred_element_type=F32)


def dot_nt(left, right):
    return lax.dot_general(left, right, (((1,), (1,)), ((), ())), preferred_element_type=F32)


def shards(
    tokens,
    doc_lengths,
    attn_gain,
    attn_shift,
    qkv_weight,
    query_bias,
    value_bias,
    out_weight,
    out_bias,
    mlp_gain,
    mlp_shift,
    up_weight,
    up_bias,
    down_weight,
    down_bias,
    cotangent,
):
    n_f, n_z, n_c = lax.axis_size("fsdp"), lax.axis_size("zz"), lax.axis_size("core")
    f, z, c = lax.axis_index("fsdp"), lax.axis_index("zz"), lax.axis_index("core")
    n_p = n_f * n_c
    tokens_in = tokens[0].astype(F32)
    lengths = doc_lengths[0]
    grad_out = cotangent[0]
    rows, width = tokens_in.shape
    head = value_bias.shape[0] * n_f
    hidden = up_weight.shape[1]
    own_q = width // n_p
    own_h = hidden // n_p

    smalls = (attn_gain, attn_shift, query_bias, out_bias, mlp_gain, mlp_shift, down_bias, up_bias, value_bias)
    packed = jnp.concatenate(smalls)
    length = packed.shape[0]
    packed = jnp.pad(packed, (0, -length % (16 * LANES))).reshape(-1, LANES)
    packed, w_q, w_kv = front(packed, qkv_weight, qkv_weight[:, width:], own_q, n_f, 15)
    w_q = w_q.reshape(width, own_q)
    w_kv = w_kv.reshape(width, 2 * head)
    packed = packed.reshape(n_f, -1)
    wide, at = [], 0
    for item in smalls:
        size = item.shape[0]
        wide.append(packed[:, at : at + size].reshape(-1).astype(F32))
        at += size
    gain_one, shift_one, bias_q, bias_out, gain_two, shift_two, bias_down, bias_up, bias_v = wide
    plane_at = f * n_c + c
    bias_q_own = lax.dynamic_slice_in_dim(bias_q, plane_at * own_q, own_q)
    bias_up_own = lax.dynamic_slice_in_dim(bias_up, plane_at * own_h, own_h)

    def own_columns(weight, size):
        pieces = []
        for offset in range(n_f):
            to = flip(f, offset, n_f.bit_length() - 1)
            block = lax.dynamic_slice_in_dim(weight, (to * n_c + c) * size, size, axis=1)
            if offset:
                block = lax.ppermute(block, "fsdp", [(i, i ^ offset) for i in range(n_f)])
            pieces.append(block)
        stacked = jnp.zeros((n_f, weight.shape[0], size), BF16)
        for offset in range(n_f):
            stacked = lax.dynamic_update_slice_in_dim(
                stacked, pieces[offset][None], flip(f, offset, n_f.bit_length() - 1), axis=0
            )
        return stacked.reshape(width, size)

    w_up = own_columns(up_weight, own_h)
    w_out = lax.dynamic_slice_in_dim(out_weight, c * own_q, own_q, axis=0)
    w_down = lax.dynamic_slice_in_dim(down_weight, c * own_h, own_h, axis=0)

    normal_one, inverse_one = norm_parts(tokens_in)
    normed = (normal_one * gain_one + shift_one).astype(BF16)
    normed_pl = plane_gather(normed, n_f, 0)
    query_own = (dot(normed_pl, w_q) + bias_q_own).astype(BF16)
    keyval = dot(normed, w_kv)
    keyval = jnp.concatenate([keyval[:, :head], keyval[:, head:] + bias_v], axis=1).astype(BF16)
    query, keyval_all = exchange(
        query_own.reshape(n_p, rows, own_q), keyval, n_f, n_z, 1, whole=True
    )
    stream = n_z * n_c * rows
    span = min(stream, stream // 2 + rows)
    key_first = jnp.clip((z * n_c + c + 1) * rows - span, 0, stream - span)
    kv = lax.dynamic_slice_in_dim(keyval_all.reshape(stream, 2 * head), key_first, span, axis=0)
    key_pos = key_first + jnp.arange(span, dtype=jnp.int32)
    positions = (z * n_c + c) * rows + jnp.arange(rows, dtype=jnp.int32)
    allowed = (row_docs(key_pos, lengths)[:, None] == row_docs(positions, lengths)[None, :]) & (
        positions[None, :] >= key_pos[:, None]
    )
    mask = jnp.where(allowed, 0.0, -1e30).astype(F32)
    mixed, lse = attend(query, kv, mask, head)
    mixed_own = exchange(mixed, None, n_f, n_z, 2).reshape(n_p * rows, own_q)
    branch = plane_scatter(dot(mixed_own, w_out), n_f, 3) + bias_out
    residual = tokens_in + branch

    normal_two, inverse_two = norm_parts(residual)
    normed_mlp = (normal_two * gain_two + shift_two).astype(BF16)
    normed_mlp_pl = plane_gather(normed_mlp, n_f, 4)
    grad_pl = plane_gather(grad_out, n_f, 5)
    inner = dot(normed_mlp_pl, w_up) + bias_up_own
    activated, gelu_back = jax.vjp(lambda v: jax.nn.gelu(v, approximate=True), inner)
    activated = activated.astype(BF16)
    out_part = dot(activated, w_down).astype(BF16).reshape(n_p, rows, width)
    d_act = dot_nt(grad_pl, w_down)
    d_inner = gelu_back(d_act)[0].astype(BF16)
    e_part = dot_nt(d_inner, w_up).astype(BF16).reshape(n_p, rows, width)
    g_down = dot_tn(activated, grad_pl).astype(BF16)
    g_up = dot_tn(normed_mlp_pl, d_inner).astype(BF16)
    seg = width // n_f

    def chunked(block, most):
        height = min(max(16, CHUNK // block.shape[1]), most)
        return block.reshape(block.shape[0] // height, height, block.shape[1])

    done = backward(
        {
            "e_part": e_part,
            "out_part": out_part,
            "g_down_in": chunked(g_down, own_h),
            "g_up_in": chunked(g_up, seg),
            "normed_in": normed_pl.reshape(n_p, rows, width),
            "grad_out": grad_out,
            "normal_two": normal_two,
            "inverse_two": inverse_two,
            "gain_two": gain_two[None],
            "normal_one": normal_one,
            "inverse_one": inverse_one,
            "gain_one": gain_one[None],
            "w_out": w_out,
            "w_q": w_q,
            "w_kv": w_kv,
            "query": query,
            "kv": kv,
            "mask": mask,
            "lse": lse,
            "mixed_own": mixed_own,
            "down_sum": jnp.sum(grad_out.astype(F32), axis=0, keepdims=True),
            "up_sum": jnp.sum(d_inner.astype(F32), axis=0).reshape(own_h // seg, seg),
        },
        n_f,
        n_z,
        head,
        own_h,
        9,
    )
    layer_out = residual + done["out_sum"] + bias_down
    vectors = done["vectors"]
    grad_qkv = jnp.concatenate(
        [done["h_q"], done["h_kv"].reshape(n_c * own_q, 2 * head)], axis=1
    ).astype(F32)
    size = value_bias.shape[0]
    grad_value_bias = lax.dynamic_slice_in_dim(vectors[7], f * size, size)
    return (
        layer_out.astype(BF16)[None],
        done["grad_tokens"][None],
        vectors[0],
        vectors[1],
        grad_qkv,
        vectors[2],
        grad_value_bias,
        done["h_out"].reshape(n_c * own_q, width).astype(F32),
        vectors[3],
        vectors[4],
        vectors[5],
        done["h_up"].astype(F32),
        vectors[8 : 8 + hidden // width].reshape(-1),
        done["h_down"].reshape(n_c * own_h, width).astype(F32),
        vectors[6],
    )


def solution(mesh):
    n_f, n_s = mesh.shape["fsdp"], mesh.shape["seq"]
    split = Mesh(mesh.devices.reshape(n_f, n_s // 2, 2), ("fsdp", "zz", "core"))
    act = P("fsdp", ("zz", "core"), None)
    vec = P("fsdp")
    mat = P("fsdp", None)
    return jax.shard_map(
        shards,
        mesh=split,
        in_specs=(act, mat, vec, vec, mat, vec, vec, mat, vec, vec, vec, mat, vec, mat, vec, act),
        out_specs=(act, act, vec, vec, mat, vec, vec, mat, vec, vec, vec, mat, vec, mat, vec),
        check_vma=False,
    )
```

```python
import functools
import math

import jax
import jax.numpy as jnp
from jax import lax
from jax.experimental import pallas as pl
from jax.experimental.pallas import tpu as pltpu
from jax.sharding import Mesh
from jax.sharding import PartitionSpec as P

EPSILON = 1e-05
F32 = jnp.float32
BF16 = jnp.bfloat16
MESH = pl.DeviceIdType.MESH
VMEM = pltpu.VMEM
DMA = pltpu.SemaphoreType.DMA
ON_CHIP = pl.BlockSpec(memory_space=pltpu.VMEM)
ANYWHERE = pl.BlockSpec(memory_space=pl.ANY)
LANES = 128
CHUNK = 1 << 16


def flip(index, offset, bits):
    for bit in range(bits):
        if offset >> bit & 1:
            index = index + (1 << bit) * (1 - 2 * ((index // (1 << bit)) % 2))
    return index


def bit_orders(n_f):
    bits = n_f.bit_length() - 1
    assert 1 << bits == n_f
    turns = min(bits, 2)
    return bits, [[(turn + at) % bits for at in range(bits)] for turn in range(turns)]


def greet(targets):
    barrier = pltpu.get_barrier_semaphore()
    for target in targets:
        pl.semaphore_signal(barrier, inc=1, device_id=target, device_id_type=MESH)
    pl.semaphore_wait(barrier, len(targets))


def plane_peers(n_f, f, c):
    bits = n_f.bit_length() - 1
    peers = []
    for offset in range(n_f):
        for other in range(2):
            if offset or other:
                peers.append(
                    (offset * 2 + other, {"fsdp": flip(f, offset, bits), "core": c + other * (1 - 2 * c)})
                )
    return peers


def column_peers(n_z, z, c):
    peers = []
    for offset in range(n_z):
        for other in range(2):
            if offset or other:
                peers.append(
                    (offset * 2 + other, {"zz": (z + offset) % n_z, "core": c + other * (1 - 2 * c)})
                )
    return peers


def remote(source, target, send, recv, device):
    return pltpu.make_async_remote_copy(
        src_ref=source,
        dst_ref=target,
        send_sem=send,
        recv_sem=recv,
        device_id=device,
        device_id_type=MESH,
    )


def no_pause(count):
    pass


class Gather:
    def __init__(self, n_f, x_ref, out_ref, send, recv, core_send, core_recv, local_sem):
        self.f, self.c = lax.axis_index("fsdp"), lax.axis_index("core")
        self.n_f, self.x_ref, self.out_ref = n_f, x_ref, out_ref
        self.send, self.recv, self.core_send, self.core_recv = send, recv, core_send, core_recv
        self.bits, self.orders = bit_orders(n_f)
        self.part = x_ref.shape[0] // len(self.orders)
        self.started = []
        self.have = [[0] for _ in self.orders]
        self.own = lambda: pltpu.make_async_copy(x_ref, out_ref.at[self.slot(0, self.c)], local_sem)

    def slot(self, offset, core):
        return flip(self.f, offset, self.bits) * 2 + core

    def piece(self, turn, offset, core):
        return self.out_ref.at[self.slot(offset, core), pl.ds(turn * self.part, self.part)]

    def source(self, turn, offset):
        if offset:
            return self.piece(turn, offset, self.c)
        return self.x_ref.at[pl.ds(turn * self.part, self.part)]

    def link(self, turn, offset, bit):
        sem = turn * self.n_f + (offset ^ (1 << bit))
        return remote(
            self.source(turn, offset),
            self.piece(turn, offset, self.c),
            self.send.at[sem],
            self.recv.at[sem],
            {"fsdp": flip(self.f, 1 << bit, self.bits)},
        )

    def arrival(self, turn, offset):
        sem = turn * self.n_f + offset
        where = self.piece(turn, offset, self.c)
        return remote(where, where, self.send.at[sem], self.recv.at[sem], {"core": 1 - self.c})

    def across(self, turn, offset):
        sem = turn * self.n_f + offset
        return remote(
            self.source(turn, offset),
            self.piece(turn, offset, self.c),
            self.core_send.at[sem],
            self.core_recv.at[sem],
            {"core": 1 - self.c},
        )

    def crossing(self, turn, offset):
        sem = turn * self.n_f + offset
        where = self.piece(turn, offset, 1 - self.c)
        return remote(
            where, where, self.core_send.at[sem], self.core_recv.at[sem], {"core": 1 - self.c}
        )

    def go(self, copy):
        copy.start()
        self.started.append(copy)

    def start(self):
        for step in range(self.bits):
            for turn, order in enumerate(self.orders):
                self.go(self.link(turn, 0, order[step]))
        for turn in range(len(self.orders)):
            self.go(self.across(turn, 0))
        self.own().start()

    def relay(self, pause):
        for step in range(self.bits):
            for at in range(1 << step):
                for turn, order in enumerate(self.orders):
                    offset = self.have[turn][at] ^ (1 << order[step])
                    self.arrival(turn, offset).wait_recv()
                    for later in range(step + 1, self.bits):
                        self.go(self.link(turn, offset, order[later]))
                    self.go(self.across(turn, offset))
                    self.have[turn].append(offset)
                    pause(1)

    def finish(self):
        for copy in self.started:
            copy.wait_send()
        for turn in range(len(self.orders)):
            for offset in self.have[turn]:
                self.crossing(turn, offset).wait_recv()
        self.own().wait()


def gather_stage(n_f, x_ref, out_ref, *rest):
    gather = Gather(n_f, x_ref, out_ref, *rest[:-1])
    gather.start()
    rest[-1](1)
    gather.relay(rest[-1])
    gather.finish()


def scatter_stage(
    n_f, part_ref, out_ref, acc, core_in, link_in, send, recv, core_send, core_recv, pause
):
    f, c = lax.axis_index("fsdp"), lax.axis_index("core")
    rows = out_ref.shape[0]
    bits, orders = bit_orders(n_f)
    part = rows // len(orders)
    started = []

    def go(copy):
        copy.start()
        started.append(copy)

    def held(offset, where):
        if acc is None:
            return part_ref.at[flip(f, offset, bits) * 2 + c, where]
        return acc.at[offset, where]

    def across(turn, offset):
        where = pl.ds(turn * part, part)
        sem = turn * n_f + offset
        return remote(
            part_ref.at[flip(f, offset, bits) * 2 + 1 - c, where],
            core_in.at[offset, where],
            core_send.at[sem],
            core_recv.at[sem],
            {"core": 1 - c},
        )

    def link(turn, offset, bit):
        where = pl.ds(turn * part, part)
        sem = turn * n_f + offset
        return remote(
            held(offset, where),
            link_in.at[offset, where],
            send.at[sem],
            recv.at[sem],
            {"fsdp": flip(f, 1 << bit, bits)},
        )

    plan = [[] for _ in range(bits)] + [[(turn, 0) for turn in range(len(orders))]]
    for step in range(bits):
        for offset in range(n_f):
            for turn, order in enumerate(orders):
                if offset >> order[step] & 1 and not any(offset >> b & 1 for b in order[:step]):
                    plan[step].append((turn, offset))
    for todo in plan:
        for turn, offset in todo:
            go(across(turn, offset))
    for step, todo in enumerate(plan):
        pause(1)
        for turn, offset in todo:
            where = pl.ds(turn * part, part)
            across(turn, offset).wait_recv()
            total = part_ref[flip(f, offset, bits) * 2 + c, where].astype(F32)
            total = total + core_in[offset, where].astype(F32)
            for bit in orders[turn][:step]:
                link(turn, offset | (1 << bit), bit).wait_recv()
                total = total + link_in[offset | (1 << bit), where].astype(F32)
            if offset:
                held(offset, where)[...] = total.astype(BF16)
                go(link(turn, offset, orders[turn][step]))
                if offset == n_f - 1:
                    pause(1)
            else:
                out_ref[where] = total
    for copy in started:
        copy.wait_send()


def exchange_stage(n_f, n_z, plane_in, column_in, plane_out, column_out, sems, whole, pause):
    f, z, c = lax.axis_index("fsdp"), lax.axis_index("zz"), lax.axis_index("core")
    peers = plane_peers(n_f, f, c)
    others = column_peers(n_z, z, c) if column_in is not None else []
    copies = []
    local = []
    if column_in is not None:
        mine = z * 2 + c
        for sem, device in others:
            to = device["zz"] * 2 + device["core"]
            source = column_in if whole else column_in.at[to]
            copies.append(
                remote(source, column_out.at[mine], sems[2].at[sem], sems[3].at[sem], device)
            )
        source = column_in if whole else column_in.at[mine]
        local.append(pltpu.make_async_copy(source, column_out.at[mine], sems[5]))
    mine = f * 2 + c
    for sem, device in peers:
        to = device["fsdp"] * 2 + device["core"]
        copies.append(
            remote(plane_in.at[to], plane_out.at[mine], sems[0].at[sem], sems[1].at[sem], device)
        )
    local.append(pltpu.make_async_copy(plane_in.at[mine], plane_out.at[mine], sems[4]))
    for copy in copies + local:
        copy.start()
    pause(1)
    for copy in copies:
        copy.wait_send()
    for sem, device in peers:
        frm = device["fsdp"] * 2 + device["core"]
        remote(
            plane_out.at[frm], plane_out.at[frm], sems[0].at[sem], sems[1].at[sem], device
        ).wait_recv()
    if column_in is not None:
        for offset in range(n_z):
            for other in range(2):
                if offset or other:
                    frm = ((z + n_z - offset) % n_z) * 2 + c + other * (1 - 2 * c)
                    sem = offset * 2 + other
                    remote(
                        column_out.at[frm],
                        column_out.at[frm],
                        sems[2].at[sem],
                        sems[3].at[sem],
                        {"core": 1 - c},
                    ).wait_recv()
    for copy in local:
        copy.wait()


class Line:
    def __init__(self, n_z, chunks, sems):
        self.n_z, self.chunks = n_z, chunks
        self.red_send, self.red_recv, self.fin_send, self.fin_recv, self.own_sem = sems
        self.z = lax.axis_index("zz")
        self.done = 0

    def toward(self, k, source):
        return remote(
            source,
            self.chunks[k][1],
            self.red_send.at[k],
            self.red_recv.at[k],
            {"zz": jnp.maximum(self.z - 1, 0)},
        )

    def outward(self, k, source):
        return remote(
            source,
            self.chunks[k][2],
            self.fin_send.at[k],
            self.fin_recv.at[k],
            {"zz": jnp.minimum(self.z + 1, self.n_z - 1)},
        )

    def keep(self, k):
        return pltpu.make_async_copy(self.chunks[k][1], self.chunks[k][2], self.own_sem.at[k])

    def reduce(self, k, z):
        own, landing, _ = self.chunks[k]
        if z == self.n_z - 1:
            self.toward(k, own).start()
            return
        self.toward(k, own).wait_recv()
        height = min(16, own.shape[0])

        @pl.loop(0, own.shape[0] // height)
        def _(at):
            where = pl.ds(pl.multiple_of(at * height, height), height)
            landing[where] = (own[where].astype(F32) + landing[where].astype(F32)).astype(BF16)

        if z > 0:
            self.toward(k, landing).start()
        else:
            self.outward(k, landing).start()
            self.keep(k).start()

    def spread(self, k, z):
        if z == 0:
            self.keep(k).wait()
            return
        self.outward(k, self.chunks[k][2]).wait_recv()
        if z < self.n_z - 1:
            self.outward(k, self.chunks[k][2]).start()

    def tick(self, then=None):
        t = self.done
        self.done += 1
        total = len(self.chunks)
        for z in range(self.n_z):
            k = t - (self.n_z - 1 - z)
            if 0 <= k < total:

                @pl.when(self.z == z)
                def _():
                    self.reduce(k, z)

            k = t - self.lag(z)
            if 0 <= k < total:

                @pl.when(self.z == z)
                def _():
                    self.spread(k, z)
                    if then is not None:
                        then(k)

    def lag(self, z):
        return self.n_z + 2 * z if z < self.n_z - 1 else self.n_z + 2 * z + 2

    def ticks(self):
        return len(self.chunks) + self.lag(self.n_z - 1)

    def left(self):
        return self.ticks() - self.done

    def finish(self):
        for k in range(len(self.chunks)):

            @pl.when(self.z > 0)
            def _():
                self.toward(k, self.chunks[k][0]).wait_send()

            @pl.when(self.z < self.n_z - 1)
            def _():
                self.outward(k, self.chunks[k][2]).wait_send()


def vector_stage(n_f, n_z, in_ref, out_ref, plane_in, part, line_in, sems, pause):
    f, z, c = lax.axis_index("fsdp"), lax.axis_index("zz"), lax.axis_index("core")
    send, recv, line_send, line_recv, local = sems
    peers = plane_peers(n_f, f, c)
    others = [(offset, {"zz": (z + offset) % n_z}) for offset in range(1, n_z)]
    mine = f * 2 + c
    copies = [
        remote(in_ref.at[device["fsdp"]], plane_in.at[mine], send.at[sem], recv.at[sem], device)
        for sem, device in peers
    ]
    for copy in copies:
        copy.start()
    own = pltpu.make_async_copy(in_ref.at[f], plane_in.at[mine], local)
    own.start()
    own.wait()
    pause(1)
    for sem, device in peers:
        where = plane_in.at[device["fsdp"] * 2 + device["core"]]
        remote(where, where, send.at[sem], recv.at[sem], device).wait_recv()
    total = plane_in[0]
    for at in range(1, n_f * 2):
        total = total + plane_in[at]
    part[...] = total
    line = [
        remote(part, line_in.at[z], line_send.at[sem], line_recv.at[sem], device)
        for sem, device in others
    ]
    for copy in line:
        copy.start()
    pause(1)
    for offset in range(1, n_z):
        where = line_in.at[(z + n_z - offset) % n_z]
        remote(
            where, where, line_send.at[offset], line_recv.at[offset], {"core": 1 - c}
        ).wait_recv()
    line_in[z] = total
    total = line_in[0]
    for at in range(1, n_z):
        total = total + line_in[at]
    out_ref[...] = total
    for copy in copies + line:
        copy.wait_send()


def heads_side_by_side(block, head):
    count = block.shape[1] // head
    return jnp.concatenate([block[:, at * head : (at + 1) * head] for at in range(count)], axis=0)


def heads_apart(block, count):
    rows = block.shape[0] // count
    return jnp.concatenate([block[at * rows : (at + 1) * rows] for at in range(count)], axis=1)


def attend_block(head, query_in, kv_ref, mask_ref):
    scale = 1.0 / math.sqrt(head)
    query = heads_side_by_side(query_in, head)
    count = query_in.shape[1] // head
    keys, values = kv_ref[:, :head], kv_ref[:, head:]
    mask = jnp.concatenate([mask_ref[...]] * count, axis=1)
    scores = dot_nt(keys, query) * scale + mask
    peak = jnp.max(scores, axis=0, keepdims=True)
    weights = jnp.exp(scores - peak)
    total = jnp.sum(weights, axis=0, keepdims=True)
    probs = (weights / total).astype(BF16)
    return heads_apart(dot_tn(probs, values).astype(BF16), count), peak + jnp.log(total)


def attend_back_block(head, query_in, grad_in, kv_ref, mask_ref, lse):
    scale = 1.0 / math.sqrt(head)
    query = heads_side_by_side(query_in, head)
    grad = heads_side_by_side(grad_in, head)
    count = query_in.shape[1] // head
    keys, values = kv_ref[:, :head], kv_ref[:, head:]
    mask = jnp.concatenate([mask_ref[...]] * count, axis=1)
    scores = dot_nt(keys, query) * scale + mask
    probs = jnp.exp(scores - lse)
    d_probs = dot_nt(values, grad)
    delta = jnp.sum(probs * d_probs, axis=0, keepdims=True)
    d_scores = (probs * (d_probs - delta)).astype(BF16)
    d_query = heads_apart((dot_tn(d_scores, keys) * scale).astype(BF16), count)
    d_keys = dot(d_scores, query) * scale
    d_values = dot(probs.astype(BF16), grad)
    return d_query, d_keys, d_values


class Box:
    pass


def rows_of(at, height=16):
    return pl.ds(pl.multiple_of(at * height, height), height)


GAIN_ONE, SHIFT_ONE, BIAS_OUT, GAIN_TWO, SHIFT_TWO, BIAS_DOWN, BIAS_VALUE = range(7)


def norm_tiles(load, gain, shift, normal_ref, inverse_ref, normed_ref):
    @pl.loop(0, normal_ref.shape[0] // 16)
    def _(at):
        where = rows_of(at)
        values = load(where)
        row_mean = jnp.mean(values, axis=-1, keepdims=True)
        centered = values - row_mean
        variance = jnp.mean(centered * centered, axis=-1, keepdims=True)
        inverse = lax.rsqrt(variance + EPSILON)
        normal = centered * inverse
        normal_ref[where] = normal
        inverse_ref[where] = inverse
        normed_ref[where] = (normal * gain + shift).astype(BF16)


def forward_body(n_f, n_z, head, names, *refs):
    r = Box()
    for name, ref in zip(names, refs, strict=True):
        setattr(r, name, ref)
    f, z, c = lax.axis_index("fsdp"), lax.axis_index("zz"), lax.axis_index("core")
    bits = n_f.bit_length() - 1
    n_p = n_f * 2
    rows, width = r.tokens.shape
    own_q = r.w_out.shape[0]
    own_h = r.w_up.shape[2]
    seg = width // n_f
    far = [flip(f, offset, bits) for offset in range(n_f)]
    r.small_all[f] = r.small[...]
    greet([device for _, device in plane_peers(n_f, f, c) + column_peers(n_z, z, c)])

    def columns(ref, to, size, where=slice(None)):
        return ref.at[where, pl.ds(pl.multiple_of((to * 2 + c) * size, LANES), size)]

    half = seg // 2
    quarter = seg // n_z

    def kv_piece(source, core):
        return r.w_kv.at[source, pl.ds(pl.multiple_of(core * half, 16), half)]

    def up_piece(source, plane):
        return r.w_up.at[source, pl.ds(pl.multiple_of(plane * quarter, 16), quarter)]

    smalls, early, kv_cross, up_links, up_lines = [], [], [], [], []
    for offset in range(1, n_f):
        device = {"fsdp": far[offset]}
        smalls.append(
            remote(r.small, r.small_all.at[f], r.small_sem.at[0, offset], r.small_sem.at[1, offset], device)
        )
        early.append(
            remote(
                columns(r.qkv_weight, far[offset], own_q),
                r.w_q.at[f],
                r.q_sem.at[0, offset],
                r.q_sem.at[1, offset],
                device,
            )
        )
        early.append(
            remote(
                r.qkv_weight.at[pl.ds(pl.multiple_of(c * half, 16), half), pl.ds(width, 2 * head)],
                kv_piece(f, c),
                r.kv_sem.at[0, offset],
                r.kv_sem.at[1, offset],
                device,
            )
        )
        where = pl.ds(pl.multiple_of(z * quarter, 16), quarter)
        up_links.append(
            remote(
                columns(r.up_weight, far[offset], own_h, where),
                up_piece(f, z),
                r.up_sem.at[0, offset],
                r.up_sem.at[1, offset],
                device,
            )
        )
    locals_ = [
        pltpu.make_async_copy(columns(r.qkv_weight, f, own_q), r.w_q.at[f], r.local_sem.at[0]),
        pltpu.make_async_copy(
            r.qkv_weight.at[:, pl.ds(width, 2 * head)], r.w_kv.at[f], r.local_sem.at[1]
        ),
        pltpu.make_async_copy(columns(r.up_weight, f, own_h), r.up_own, r.local_sem.at[2]),
    ]
    for copy in smalls + early + locals_:
        copy.start()

    for offset in range(1, n_f):
        where = r.small_all.at[far[offset]]
        remote(
            where, where, r.small_sem.at[0, offset], r.small_sem.at[1, offset], {"core": 1 - c}
        ).wait_recv()
    for o in range(n_f):
        r.vecs[:, o * seg : (o + 1) * seg] = r.small_all[o].astype(F32)
    norm_tiles(
        lambda where: r.tokens[where].astype(F32),
        r.vecs[GAIN_ONE : GAIN_ONE + 1],
        r.vecs[SHIFT_ONE : SHIFT_ONE + 1],
        r.normal_one,
        r.inverse_one,
        r.normed,
    )
    normed = Gather(
        n_f, r.normed, r.normed_all, *(r.gather_one.at[at] for at in range(4)), r.local_sem.at[3]
    )
    normed.start()
    for offset in range(1, n_f):
        where = kv_piece(far[offset], c)
        remote(
            where, where, r.kv_sem.at[0, offset], r.kv_sem.at[1, offset], {"core": 1 - c}
        ).wait_recv()
        kv_cross.append(
            remote(where, where, r.kv_sem.at[2, offset], r.kv_sem.at[3, offset], {"core": 1 - c})
        )
        kv_cross[-1].start()
    locals_[2].wait()
    up_home = pltpu.make_async_copy(r.up_own, r.w_up.at[f], r.local_sem.at[4])
    up_home.start()
    normed.relay(no_pause)
    for copy in up_links:
        copy.start()
    for offset in range(1, n_f):
        where = kv_piece(far[offset], 1 - c)
        remote(
            where, where, r.kv_sem.at[2, offset], r.kv_sem.at[3, offset], {"core": 1 - c}
        ).wait_recv()
        where = r.w_q.at[far[offset]]
        remote(
            where, where, r.q_sem.at[0, offset], r.q_sem.at[1, offset], {"core": 1 - c}
        ).wait_recv()
    locals_[0].wait()
    locals_[1].wait()
    bias_v = r.vecs[BIAS_VALUE : BIAS_VALUE + 1, :head]
    for o in range(1, n_f):
        bias_v = bias_v + r.vecs[BIAS_VALUE : BIAS_VALUE + 1, o * seg : o * seg + head]
    keyval = dot(r.normed[...], r.w_kv[...].reshape(width, 2 * head))
    r.keyval[:, :head] = keyval[:, :head].astype(BF16)
    r.keyval[:, head:] = (keyval[:, head:] + bias_v).astype(BF16)
    normed.finish()
    keep = pltpu.make_async_copy(r.normed_all, r.normed_pl, r.local_sem.at[5])
    keep.start()

    @pl.loop(0, n_p)
    def _(p):
        r.query_send[p] = (
            dot(r.normed_all[p], r.w_q[...].reshape(width, own_q)) + r.bias_q[...]
        ).astype(BF16)

    grads = Gather(
        n_f, r.grad_out, r.grad_pl, *(r.gather_two.at[at] for at in range(4)), r.local_sem.at[6]
    )

    def fill(count):
        for offset in range(1, n_f):
            where = up_piece(far[offset], z)
            remote(
                where, where, r.up_sem.at[0, offset], r.up_sem.at[1, offset], {"core": 1 - c}
            ).wait_recv()
            for away in range(1, n_z):
                sem = away * n_f + offset
                up_lines.append(
                    remote(
                        where, where, r.line_sem.at[0, sem], r.line_sem.at[1, sem], {"zz": (z + away) % n_z}
                    )
                )
                up_lines[-1].start()
        grads.start()

    exchange_stage(
        n_f,
        n_z,
        r.query_send,
        r.keyval,
        r.query,
        r.kv_all,
        [
            r.swap_one.at[0],
            r.swap_one.at[1],
            r.column_sem.at[0],
            r.column_sem.at[1],
            r.local_sem.at[7],
            r.local_sem.at[8],
        ],
        True,
        fill,
    )
    span = r.kv.shape[0]
    first = jnp.maximum((z * 2 + c + 1) - span // rows, 0)
    for at in range(span // rows):
        r.kv[at * rows : (at + 1) * rows] = r.kv_all[first + at]

    @pl.loop(0, n_p)
    def _(p):
        mixed, lse = attend_block(head, r.query[p], r.kv, r.mask)
        r.mixed_send[p] = mixed
        r.lse[p] = lse

    exchange_stage(
        n_f,
        n_z,
        r.mixed_send,
        None,
        r.mixed_own,
        None,
        [r.swap_two.at[0], r.swap_two.at[1], None, None, r.local_sem.at[9], None],
        False,
        lambda count: grads.relay(no_pause),
    )
    tile = min(512, width)

    @pl.loop(0, n_p)
    def _(p):
        for n in range(width // tile):
            cols = pl.ds(n * tile, tile)
            r.part[p, :, cols] = dot(r.mixed_own[p], r.w_out[:, cols]).astype(BF16)

    scatter_stage(
        n_f, r.part, r.branch, None, r.core_in, r.link_in, *(r.scatter_one.at[at] for at in range(4)), no_pause
    )

    def second(where):
        values = (
            r.tokens[where].astype(F32) + r.branch[where] + r.vecs[BIAS_OUT : BIAS_OUT + 1]
        )
        r.residual[where] = values
        return values

    norm_tiles(
        second,
        r.vecs[GAIN_TWO : GAIN_TWO + 1],
        r.vecs[SHIFT_TWO : SHIFT_TWO + 1],
        r.normal_two,
        r.inverse_two,
        r.normed_mlp,
    )
    last = Gather(
        n_f, r.normed_mlp, r.normed_mlp_pl, *(r.gather_three.at[at] for at in range(4)), r.local_sem.at[10]
    )
    last.start()
    grads.finish()
    last.relay(no_pause)
    for copy in smalls + early + kv_cross + up_links + up_lines:
        copy.wait_send()
    for offset in range(1, n_f):
        for away in range(1, n_z):
            where = up_piece(far[offset], (z + n_z - away) % n_z)
            sem = away * n_f + offset
            remote(
                where, where, r.line_sem.at[0, sem], r.line_sem.at[1, sem], {"core": 1 - c}
            ).wait_recv()
    up_home.wait()
    keep.wait()
    last.finish()


def forward(inputs, n_f, n_z, head, own_h, ident):
    rows, width = inputs["tokens"].shape
    n_p, n_s = n_f * 2, n_z * 2
    own_q = width // n_p
    seg = width // n_f
    count = len(bit_orders(n_f)[1]) * n_f
    span = inputs["mask"].shape[0]
    in_hbm = ("qkv_weight", "up_weight")
    plane = (n_p, rows, width)
    blocks = (n_p, rows, own_q)
    outs = {
        "normed_pl": (plane, BF16, ANYWHERE),
        "normal_one": ((rows, width), F32, ON_CHIP),
        "inverse_one": ((rows, 1), F32, ON_CHIP),
        "query": (blocks, BF16, ON_CHIP),
        "kv": ((span, 2 * head), BF16, ON_CHIP),
        "lse": ((n_p, 1, own_q // head * rows), F32, ON_CHIP),
        "mixed_own": (blocks, BF16, ON_CHIP),
        "residual": ((rows, width), F32, ON_CHIP),
        "normal_two": ((rows, width), F32, ON_CHIP),
        "inverse_two": ((rows, 1), F32, ON_CHIP),
        "normed_mlp_pl": (plane, BF16, ANYWHERE),
        "grad_pl": (plane, BF16, ANYWHERE),
        "w_q": ((n_f, seg, own_q), BF16, ON_CHIP),
        "w_kv": ((n_f, seg, 2 * head), BF16, ON_CHIP),
        "w_up": ((n_f, seg, own_h), BF16, ANYWHERE),
        "vecs": ((8, width), F32, ON_CHIP),
    }
    scratch = {
        "small_all": VMEM((n_f, 8, seg), BF16),
        "up_own": VMEM((seg, own_h), BF16),
        "normed": VMEM((rows, width), BF16),
        "normed_all": VMEM(plane, BF16),
        "keyval": VMEM((rows, 2 * head), BF16),
        "query_send": VMEM(blocks, BF16),
        "kv_all": VMEM((n_s, rows, 2 * head), BF16),
        "mixed_send": VMEM(blocks, BF16),
        "part": VMEM(plane, BF16),
        "core_in": VMEM((n_f, rows, width), BF16),
        "link_in": VMEM((n_f, rows, width), BF16),
        "branch": VMEM((rows, width), F32),
        "normed_mlp": VMEM((rows, width), BF16),
        "local_sem": DMA((11,)),
        "small_sem": DMA((2, n_f)),
        "q_sem": DMA((2, n_f)),
        "kv_sem": DMA((4, n_f)),
        "up_sem": DMA((2, n_f)),
        "line_sem": DMA((2, n_z * n_f)),
        "gather_one": DMA((4, count)),
        "gather_two": DMA((4, count)),
        "gather_three": DMA((4, count)),
        "scatter_one": DMA((4, count)),
        "swap_one": DMA((2, n_p)),
        "swap_two": DMA((2, n_p)),
        "column_sem": DMA((2, n_s)),
    }
    names = list(inputs) + list(outs) + list(scratch)
    result = pl.pallas_call(
        functools.partial(forward_body, n_f, n_z, head, names),
        out_shape=[jax.ShapeDtypeStruct(shape, kind) for shape, kind, _ in outs.values()],
        in_specs=[ANYWHERE if name in in_hbm else ON_CHIP for name in inputs],
        out_specs=[place for _, _, place in outs.values()],
        scratch_shapes=list(scratch.values()),
        compiler_params=pltpu.CompilerParams(
            collective_id=ident, has_side_effects=True, vmem_limit_bytes=56 << 20
        ),
        name="forward",
    )(*inputs.values())
    return dict(zip(outs, result))


PACE = 2


def norm_back_tiles(grad_ref, extra_ref, normal_ref, inverse_ref, gain_ref, base_ref, sums, store):
    rows = normal_ref.shape[0]

    @pl.loop(0, rows // 16)
    def _(at):
        where = rows_of(at)
        grad = grad_ref[where]
        if extra_ref is not None:
            grad = grad + extra_ref[where]
        normal = normal_ref[where].astype(F32)
        scaled = grad * gain_ref[...]
        first = jnp.mean(scaled, axis=-1, keepdims=True)
        second = jnp.mean(scaled * normal, axis=-1, keepdims=True)
        result = base_ref[where].astype(F32) + inverse_ref[where] * (
            scaled - first - normal * second
        )
        store(where, result)
        sums[0:1] += jnp.sum(grad * normal, axis=0, keepdims=True)
        sums[1:2] += jnp.sum(grad, axis=0, keepdims=True)
        sums[2:3] += jnp.sum(result.astype(BF16).astype(F32), axis=0, keepdims=True)


def backward_body(n_f, n_z, head, names, *refs):
    r = Box()
    for name, ref in zip(names, refs, strict=True):
        setattr(r, name, ref)
    f, z, c = lax.axis_index("fsdp"), lax.axis_index("zz"), lax.axis_index("core")
    bits = n_f.bit_length() - 1
    n_p = n_f * 2
    me = f * 2 + c
    rows, width = r.grad_out.shape
    own_q = r.w_out.shape[0]

    loads = {}
    for at, (name, source, target) in enumerate(
        (
            ("part", r.e_part, r.part),
            ("down", r.g_down_in, r.g_down),
            ("up", r.g_up_in, r.g_up),
        )
    ):
        loads[name] = pltpu.make_async_copy(source, target, r.load_sem.at[at])
        loads[name].start()
    greet([device for _, device in plane_peers(n_f, f, c) + column_peers(n_z, z, c)])

    kinds = []
    chunks = []
    for kind, own, landing, final in (
        ("up", r.g_up, r.land_up, r.fin_up),
        ("down", r.g_down, r.land_down, r.h_down.at[c]),
        ("out", r.g_out, r.land_out, r.h_out.at[c]),
        ("q", r.g_q, r.land_q, r.fin_q),
        ("kv", r.g_kv, r.land_kv, r.h_kv.at[c]),
    ):
        for k in range(own.shape[0]):
            kinds.append((kind, k))
            chunks.append((own.at[k], landing.at[k], final.at[k]))
    line = Line(n_z, chunks, (r.red_send, r.red_recv, r.fin_send, r.fin_recv, r.keep_sem))
    home = {"down": r.h_down, "out": r.h_out, "kv": r.h_kv, "up": r.h_up, "q": r.h_q}

    def swap(at, side):
        kind, k = kinds[at]
        where = home[kind].at[side, k]
        return remote(where, where, r.swap_send.at[at], r.swap_recv.at[at], {"core": 1 - c})

    def block(kind, turn, source):
        target = home[kind]
        height, size = finals[kind].shape[1:]
        cols = pl.ds(pl.multiple_of(source * size, LANES), size)
        return target.at[pl.ds(pl.multiple_of(turn * height, height), height), cols]

    finals = {"up": r.fin_up, "q": r.fin_q}
    home_sem = {
        "up": (r.up_send, r.up_mate, r.up_recv, r.up_relay, r.up_cross),
        "q": (r.q_send, r.q_mate, r.q_recv, r.q_relay, r.q_cross),
    }

    def turns(kind):
        return finals[kind].shape[0] // n_f

    def moves(kind, k):
        send, mate, recv, _, cross = home_sem[kind]
        owner, turn = k // turns(kind), k % turns(kind)
        where = block(kind, turn, me)
        sem = turn * n_f + f
        source = finals[kind].at[k]
        return (
            f == owner,
            lambda: pltpu.make_async_copy(source, where, send.at[k]),
            lambda: remote(source, where, mate.at[k], cross.at[sem], {"core": 1 - c}),
            lambda: remote(source, where, send.at[k], recv.at[sem], {"fsdp": owner}),
        )

    def deliver_split(kind, k):
        here, own, other, away = moves(kind, k)

        @pl.when(here)
        def _():
            own().start()
            other().start()

        @pl.when(jnp.logical_not(here))
        def _():
            away().start()

    def relay(kind, turn, offset):
        _, _, recv, send, cross = home_sem[kind]
        source = flip(f, offset, bits)
        where = block(kind, turn, source * 2 + c)
        sem = turn * n_f + source
        return (
            lambda: remote(where, where, send.at[sem], recv.at[sem], {"core": 1 - c}),
            lambda: remote(where, where, send.at[sem], cross.at[sem], {"core": 1 - c}),
        )

    def relay_all(kind):
        @pl.loop(0, turns(kind))
        def _(turn):
            for offset in range(1, n_f):
                arrival, onward = relay(kind, turn, offset)
                arrival().wait_recv()
                onward().start()

    def deliver(at):
        kind, k = kinds[at]
        if kind in ("down", "out", "kv"):
            swap(at, c).start()
        elif kind == "q":
            deliver_split(kind, k)

    def delivered():
        for at, (kind, k) in enumerate(kinds):
            if kind in ("down", "out", "kv"):
                swap(at, c).wait_send()
                swap(at, 1 - c).wait_recv()
        for kind in ("up", "q"):

            @pl.loop(0, finals[kind].shape[0])
            def _(k):
                here, own, other, away = moves(kind, k)

                @pl.when(here)
                def _():
                    own().wait()
                    other().wait_send()

                @pl.when(jnp.logical_not(here))
                def _():
                    away().wait_send()

            @pl.loop(0, turns(kind))
            def _(turn):
                for offset in range(n_f):
                    if offset:
                        relay(kind, turn, offset)[1]().wait_send()
                    source = flip(f, offset, bits)
                    where = block(kind, turn, source * 2 + 1 - c)
                    cross = home_sem[kind][4].at[turn * n_f + source]
                    remote(where, where, r.swap_send.at[0], cross, {"core": 1 - c}).wait_recv()

    ready = [False]
    limit = [r.g_down.shape[0] + r.g_up.shape[0]]

    def pause(count):
        if not ready[0]:
            loads["down"].wait()
            loads["up"].wait()
            ready[0] = True
        for _ in range(count * PACE):
            if line.left() and line.done < limit[0]:
                line.tick(deliver)

    for ref in (r.sums_two, r.sums_one):
        ref[...] = jnp.zeros_like(ref)
    loads["part"].wait()
    scatter_stage(
        n_f, r.part, r.e_sum, None, r.core_in, r.link_in, *(r.scatter_one.at[at] for at in range(4)), pause
    )

    def store_two(where, result):
        r.d_residual[where] = result
        r.d_branch[where] = result.astype(BF16)

    norm_back_tiles(
        r.e_sum, None, r.normal_two, r.inverse_two, r.gain_two, r.grad_out, r.sums_two, store_two
    )
    loads["normed"] = pltpu.make_async_copy(r.normed_in, r.part, r.load_sem.at[3])
    loads["normed"].start()
    gather_stage(
        n_f, r.d_branch, r.branch_pl, *(r.gather_one.at[at] for at in range(4)), r.local_sem.at[0], pause
    )

    @pl.loop(0, n_p)
    def _(p):
        r.mixed_send[p] = dot_nt(r.branch_pl[p], r.w_out[...]).astype(BF16)

    exchange_stage(
        n_f,
        n_z,
        r.mixed_send,
        None,
        r.d_mixed,
        None,
        [r.swap_one.at[0], r.swap_one.at[1], None, None, r.local_sem.at[1], None],
        False,
        pause,
    )
    tile = min(512, width)
    high = r.g_out.shape[1]
    for j in range(own_q // LANES):
        for n in range(width // tile):
            cols = pl.ds(n * tile, tile)
            result = dot_tn(
                r.mixed_own[:, :, j * LANES : (j + 1) * LANES].reshape(n_p * rows, LANES),
                r.branch_pl[:, :, cols].reshape(n_p * rows, tile),
            ).astype(BF16)
            for k in range(LANES // high):
                r.g_out[j * (LANES // high) + k, :, cols] = result[k * high : (k + 1) * high]
    limit[0] += r.g_out.shape[0]

    r.d_kv_span[...] = jnp.zeros_like(r.d_kv_span)
    step = max(1, n_p // 4)
    for first in range(0, n_p, step):

        @pl.loop(first, first + step)
        def _(p):
            d_query, d_keys, d_values = attend_back_block(
                head, r.query[p], r.d_mixed[p], r.kv, r.mask, r.lse[p]
            )
            r.dq_send[p] = d_query
            r.d_kv_span[:, :head] += d_keys
            r.d_kv_span[:, head:] += d_values

        pause(1)
    span = r.d_kv_span.shape[0]
    stream = n_z * 2 * rows
    first = jnp.maximum((z * 2 + c + 1) * rows - span, 0)
    r.dkv_send[...] = jnp.zeros_like(r.dkv_send)

    @pl.loop(0, span // rows)
    def _(at):
        block_at = (jnp.maximum((z * 2 + c + 1) * rows - span, 0)) // rows + at
        r.dkv_send[block_at] = r.d_kv_span[pl.ds(pl.multiple_of(at * rows, rows), rows)].astype(BF16)

    exchange_stage(
        n_f,
        n_z,
        r.dq_send,
        r.dkv_send,
        r.dq_own,
        r.dkv_recv,
        [
            r.swap_two.at[0],
            r.swap_two.at[1],
            r.column_sem.at[0],
            r.column_sem.at[1],
            r.local_sem.at[2],
            r.local_sem.at[3],
        ],
        False,
        pause,
    )
    total = r.dkv_recv[0].astype(F32)
    for s in range(1, n_z * 2):
        total = total + r.dkv_recv[s].astype(F32)
    r.d_kv[...] = total.astype(BF16)

    @pl.loop(0, n_p)
    def _(p):
        for n in range(width // tile):
            cols = pl.ds(n * tile, tile)
            r.branch_pl[p, :, cols] = dot_nt(r.dq_own[p], r.w_q[cols]).astype(BF16)

    scatter_stage(
        n_f, r.branch_pl, r.e_sum, None, r.core_in, r.link_in, *(r.scatter_two.at[at] for at in range(4)), pause
    )
    for n in range(width // tile):
        cols = pl.ds(n * tile, tile)
        r.e_extra[:, cols] = dot_nt(r.d_kv[...], r.w_kv[cols])

    def store_one(where, result):
        r.grad_tokens[where] = result.astype(BF16)

    norm_back_tiles(
        r.e_sum, r.e_extra, r.normal_one, r.inverse_one, r.gain_one, r.d_residual, r.sums_one, store_one
    )
    gather_stage(
        n_f, r.d_kv, r.dkv_pl, *(r.gather_two.at[at] for at in range(4)), r.local_sem.at[4], pause
    )

    loads["normed"].wait()
    dq_all = r.dq_own[...].reshape(n_p * rows, own_q)
    step = min(256, r.g_q.shape[1])
    for k in range(r.g_q.shape[0]):
        for at in range(r.g_q.shape[1] // step):
            base = k * r.g_q.shape[1] + at * step
            r.g_q[k, at * step : (at + 1) * step] = dot_tn(
                r.part[:, :, base : base + step].reshape(n_p * rows, step), dq_all
            ).astype(BF16)
    cols = pl.ds(pl.multiple_of(me * own_q, LANES), own_q)
    r.g_kv[0] = dot_tn(
        r.part[:, :, cols].reshape(n_p * rows, own_q), r.dkv_pl[...].reshape(n_p * rows, 2 * head)
    ).astype(BF16)
    loads["out"] = pltpu.make_async_copy(r.out_part, r.part, r.load_sem.at[4])
    loads["out"].start()
    limit[0] = line.ticks()
    pause(2)

    while line.done < r.g_up.shape[0] + line.lag(n_z - 1):
        pause(1)

    @pl.loop(0, r.g_up.shape[0])
    def _(k):
        deliver_split("up", k)

    seg = r.vec_in.shape[2]
    r.vec_in[...] = jnp.zeros_like(r.vec_in)
    up_rows = r.up_sum.shape[0]
    d_value = jnp.sum(r.d_kv[:, head:].astype(F32), axis=0, keepdims=True)
    for o in range(n_f):
        cols = slice(o * seg, (o + 1) * seg)
        r.vec_in[o, 0:1] = r.sums_one[0:1, cols]
        r.vec_in[o, 1:2] = r.sums_one[1:2, cols]
        r.vec_in[o, 3:4] = r.sums_two[2:3, cols]
        r.vec_in[o, 4:5] = r.sums_two[0:1, cols]
        r.vec_in[o, 5:6] = r.sums_two[1:2, cols]
        r.vec_in[o, 6:7] = r.down_sum[0:1, cols]
        r.vec_in[o, 7:8, :head] = d_value
        for side in range(2):
            part = jnp.sum(r.dq_send[o * 2 + side].astype(F32), axis=0, keepdims=True)
            r.vec_in[o, 2:3, side * own_q : (side + 1) * own_q] = part

        for side in range(2):

            @pl.when((f == o) & (c == side))
            def _():
                r.vec_in[o, 8 + side * up_rows : 8 + (side + 1) * up_rows] = r.up_sum[...]

    vector_stage(
        n_f,
        n_z,
        r.vec_in,
        r.vectors,
        r.vec_plane,
        r.vec_part,
        r.vec_line,
        [r.vec_sem.at[0], r.vec_sem.at[1], r.vec_line_sem.at[0], r.vec_line_sem.at[1], r.local_sem.at[5]],
        pause,
    )

    loads["out"].wait()
    scatter_stage(
        n_f, r.part, r.out_sum, None, r.core_in, r.link_in, *(r.scatter_three.at[at] for at in range(4)), pause
    )
    while line.left() > 4 * PACE:
        pause(1)
    relay_all("up")
    while line.left():
        pause(1)
    relay_all("q")
    line.finish()
    delivered()


def backward(inputs, n_f, n_z, head, own_h, ident):
    rows, width = inputs["grad_out"].shape
    n_p = n_f * 2
    n_s = n_z * 2
    own_q = width // n_p
    seg = width // n_f
    count = len(bit_orders(n_f)[1]) * n_f
    span = inputs["kv"].shape[0]
    high = max(16, CHUNK // width)
    tall = min(seg, CHUNK // own_q)
    down = inputs["g_down_in"].shape
    up = inputs["g_up_in"].shape
    out = (own_q // high, high, width)
    query = (width // tall, tall, own_q)
    keyval = (1, own_q, 2 * head)
    chunks = down[0] + up[0] + out[0] + query[0] + 1
    in_hbm = ("e_part", "g_down_in", "g_up_in", "normed_in", "out_part")
    outs = {
        "grad_tokens": ((rows, width), BF16, ON_CHIP),
        "out_sum": ((rows, width), F32, ON_CHIP),
        "vectors": ((16, seg), F32, ON_CHIP),
        "h_down": ((2,) + down, BF16, ANYWHERE),
        "h_up": ((seg, own_h * n_p), BF16, ANYWHERE),
        "h_out": ((2,) + out, BF16, ANYWHERE),
        "h_q": ((seg, width), BF16, ANYWHERE),
        "h_kv": ((2,) + keyval, BF16, ANYWHERE),
    }
    plane = (n_p, rows, width)
    blocks = (n_p, rows, own_q)
    scratch = {
        "part": VMEM(plane, BF16),
        "g_down": VMEM(down, BF16),
        "g_up": VMEM(up, BF16),
        "g_out": VMEM(out, BF16),
        "g_q": VMEM(query, BF16),
        "g_kv": VMEM(keyval, BF16),
        "land_down": VMEM(down, BF16),
        "land_up": VMEM(up, BF16),
        "land_out": VMEM(out, BF16),
        "land_q": VMEM(query, BF16),
        "land_kv": VMEM(keyval, BF16),
        "fin_up": VMEM(up, BF16),
        "fin_q": VMEM(query, BF16),
        "core_in": VMEM((n_f, rows, width), BF16),
        "link_in": VMEM((n_f, rows, width), BF16),
        "e_sum": VMEM((rows, width), F32),
        "e_extra": VMEM((rows, width), F32),
        "d_residual": VMEM((rows, width), F32),
        "d_branch": VMEM((rows, width), BF16),
        "branch_pl": VMEM(plane, BF16),
        "mixed_send": VMEM(blocks, BF16),
        "d_mixed": VMEM(blocks, BF16),
        "dq_send": VMEM(blocks, BF16),
        "dq_own": VMEM(blocks, BF16),
        "d_kv_span": VMEM((span, 2 * head), F32),
        "dkv_send": VMEM((n_s, rows, 2 * head), BF16),
        "dkv_recv": VMEM((n_s, rows, 2 * head), BF16),
        "d_kv": VMEM((rows, 2 * head), BF16),
        "dkv_pl": VMEM((n_p, rows, 2 * head), BF16),
        "sums_one": VMEM((8, width), F32),
        "sums_two": VMEM((8, width), F32),
        "vec_in": VMEM((n_f, 16, seg), F32),
        "vec_plane": VMEM((n_p, 16, seg), F32),
        "vec_part": VMEM((16, seg), F32),
        "vec_line": VMEM((n_z, 16, seg), F32),
        "load_sem": DMA((5,)),
        "local_sem": DMA((6,)),
        "red_send": DMA((chunks,)),
        "red_recv": DMA((chunks,)),
        "fin_send": DMA((chunks,)),
        "fin_recv": DMA((chunks,)),
        "keep_sem": DMA((chunks,)),
        "swap_send": DMA((chunks,)),
        "swap_recv": DMA((chunks,)),
        "up_send": DMA((up[0],)),
        "up_mate": DMA((up[0],)),
        "up_recv": DMA((up[0],)),
        "up_relay": DMA((up[0],)),
        "up_cross": DMA((up[0],)),
        "q_send": DMA((query[0],)),
        "q_mate": DMA((query[0],)),
        "q_recv": DMA((query[0],)),
        "q_relay": DMA((query[0],)),
        "q_cross": DMA((query[0],)),
        "scatter_one": DMA((4, count)),
        "scatter_two": DMA((4, count)),
        "scatter_three": DMA((4, count)),
        "gather_one": DMA((4, count)),
        "gather_two": DMA((4, count)),
        "swap_one": DMA((2, n_p)),
        "swap_two": DMA((2, n_p)),
        "column_sem": DMA((2, n_s)),
        "vec_sem": DMA((2, n_p)),
        "vec_line_sem": DMA((2, n_z)),
    }
    names = list(inputs) + list(outs) + list(scratch)
    result = pl.pallas_call(
        functools.partial(backward_body, n_f, n_z, head, names),
        out_shape=[jax.ShapeDtypeStruct(shape, kind) for shape, kind, _ in outs.values()],
        in_specs=[ANYWHERE if name in in_hbm else ON_CHIP for name in inputs],
        out_specs=[place for _, _, place in outs.values()],
        scratch_shapes=list(scratch.values()),
        compiler_params=pltpu.CompilerParams(
            collective_id=ident, has_side_effects=True, vmem_limit_bytes=67043328
        ),
        name="backward",
    )(*inputs.values())
    return dict(zip(outs, result))


def row_docs(positions, lengths):
    doc_ends = jnp.cumsum(lengths)
    return jnp.sum((positions[:, None] >= doc_ends[None, :]).astype(jnp.int32), axis=1)


def dot(left, right):
    return jnp.dot(left, right, preferred_element_type=F32)


def dot_tn(left, right):
    return lax.dot_general(left, right, (((0,), (0,)), ((), ())), preferred_element_type=F32)


def dot_nt(left, right):
    return lax.dot_general(left, right, (((1,), (1,)), ((), ())), preferred_element_type=F32)


def shards(
    tokens,
    doc_lengths,
    attn_gain,
    attn_shift,
    qkv_weight,
    query_bias,
    value_bias,
    out_weight,
    out_bias,
    mlp_gain,
    mlp_shift,
    up_weight,
    up_bias,
    down_weight,
    down_bias,
    cotangent,
):
    n_f, n_z, n_c = lax.axis_size("fsdp"), lax.axis_size("zz"), lax.axis_size("core")
    f, z, c = lax.axis_index("fsdp"), lax.axis_index("zz"), lax.axis_index("core")
    n_p = n_f * n_c
    lengths = doc_lengths[0]
    grad_out = cotangent[0]
    rows, width = grad_out.shape
    head = value_bias.shape[0] * n_f
    hidden = up_weight.shape[1]
    own_q = width // n_p
    own_h = hidden // n_p
    seg = width // n_f

    def own(vector, size):
        return lax.dynamic_slice_in_dim(vector, c * size, size, axis=0)

    value_row = lax.dynamic_update_slice_in_dim(
        jnp.zeros((seg,), BF16), value_bias, f * value_bias.shape[0], axis=0
    )
    small = jnp.stack(
        [attn_gain, attn_shift, out_bias, mlp_gain, mlp_shift, down_bias, value_row, value_row]
    )
    stream = n_z * n_c * rows
    span = min(stream, stream // 2 + rows)
    key_first = jnp.maximum((z * n_c + c + 1) * rows - span, 0)
    key_pos = key_first + jnp.arange(span, dtype=jnp.int32)
    positions = (z * n_c + c) * rows + jnp.arange(rows, dtype=jnp.int32)
    allowed = (row_docs(key_pos, lengths)[:, None] == row_docs(positions, lengths)[None, :]) & (
        positions[None, :] >= key_pos[:, None]
    )
    mask = jnp.where(allowed, 0.0, -1e30).astype(F32)
    w_out = own(out_weight, own_q)
    w_down = own(down_weight, own_h)
    ahead = forward(
        {
            "tokens": tokens[0],
            "grad_out": grad_out,
            "small": small,
            "bias_q": own(query_bias, own_q).astype(F32)[None],
            "mask": mask,
            "w_out": w_out,
            "qkv_weight": qkv_weight,
            "up_weight": up_weight,
        },
        n_f,
        n_z,
        head,
        own_h,
        8,
    )
    vecs = ahead["vecs"]
    w_up = ahead["w_up"].reshape(width, own_h)
    grad_pl = ahead["grad_pl"].reshape(n_p * rows, width)
    normed_mlp_pl = ahead["normed_mlp_pl"].reshape(n_p * rows, width)

    inner = dot(normed_mlp_pl, w_up) + own(up_bias, own_h).astype(F32)
    activated, gelu_back = jax.vjp(lambda v: jax.nn.gelu(v, approximate=True), inner)
    activated = activated.astype(BF16)
    out_part = dot(activated, w_down).astype(BF16).reshape(n_p, rows, width)
    d_act = dot_nt(grad_pl, w_down)
    d_inner = gelu_back(d_act)[0].astype(BF16)
    e_part = dot_nt(d_inner, w_up).astype(BF16).reshape(n_p, rows, width)
    g_down = dot_tn(activated, grad_pl).astype(BF16)
    g_up = dot_tn(normed_mlp_pl, d_inner).astype(BF16)

    def chunked(block, most):
        height = min(max(16, CHUNK // block.shape[1]), most)
        return block.reshape(block.shape[0] // height, height, block.shape[1])

    done = backward(
        {
            "e_part": e_part,
            "out_part": out_part,
            "g_down_in": chunked(g_down, own_h),
            "g_up_in": chunked(g_up, seg),
            "normed_in": ahead["normed_pl"],
            "grad_out": grad_out,
            "normal_two": ahead["normal_two"],
            "inverse_two": ahead["inverse_two"],
            "gain_two": vecs[GAIN_TWO : GAIN_TWO + 1],
            "normal_one": ahead["normal_one"],
            "inverse_one": ahead["inverse_one"],
            "gain_one": vecs[GAIN_ONE : GAIN_ONE + 1],
            "w_out": w_out,
            "w_q": ahead["w_q"].reshape(width, own_q),
            "w_kv": ahead["w_kv"].reshape(width, 2 * head),
            "query": ahead["query"],
            "kv": ahead["kv"],
            "mask": mask,
            "lse": ahead["lse"],
            "mixed_own": ahead["mixed_own"],
            "down_sum": jnp.sum(grad_out.astype(F32), axis=0, keepdims=True),
            "up_sum": jnp.sum(d_inner.astype(F32), axis=0).reshape(own_h // seg, seg),
        },
        n_f,
        n_z,
        head,
        own_h,
        9,
    )
    layer_out = ahead["residual"] + done["out_sum"] + vecs[BIAS_DOWN]
    vectors = done["vectors"]
    grad_qkv = jnp.concatenate(
        [done["h_q"], done["h_kv"].reshape(n_c * own_q, 2 * head)], axis=1
    ).astype(F32)
    size = value_bias.shape[0]
    grad_value_bias = lax.dynamic_slice_in_dim(vectors[7], f * size, size)
    return (
        layer_out.astype(BF16)[None],
        done["grad_tokens"][None],
        vectors[0],
        vectors[1],
        grad_qkv,
        vectors[2],
        grad_value_bias,
        done["h_out"].reshape(n_c * own_q, width).astype(F32),
        vectors[3],
        vectors[4],
        vectors[5],
        done["h_up"].astype(F32),
        vectors[8 : 8 + hidden // width].reshape(-1),
        done["h_down"].reshape(n_c * own_h, width).astype(F32),
        vectors[6],
    )


def solution(mesh):
    n_f, n_s = mesh.shape["fsdp"], mesh.shape["seq"]
    split = Mesh(mesh.devices.reshape(n_f, n_s // 2, 2), ("fsdp", "zz", "core"))
    act = P("fsdp", ("zz", "core"), None)
    vec = P("fsdp")
    mat = P("fsdp", None)
    return jax.shard_map(
        shards,
        mesh=split,
        in_specs=(act, mat, vec, vec, mat, vec, vec, mat, vec, vec, vec, mat, vec, mat, vec, act),
        out_specs=(act, act, vec, vec, mat, vec, vec, mat, vec, vec, vec, mat, vec, mat, vec),
        check_vma=False,
    )
```

```python
import functools
import math

import jax
import jax.numpy as jnp
from jax import lax
from jax.experimental import pallas as pl
from jax.experimental.pallas import tpu as pltpu
from jax.sharding import Mesh
from jax.sharding import PartitionSpec as P

EPSILON = 1e-05
F32 = jnp.float32
BF16 = jnp.bfloat16
MESH = pl.DeviceIdType.MESH
VMEM = pltpu.VMEM
DMA = pltpu.SemaphoreType.DMA
ON_CHIP = pl.BlockSpec(memory_space=pltpu.VMEM)
ANYWHERE = pl.BlockSpec(memory_space=pl.ANY)
LANES = 128
CHUNK = 1 << 16


def flip(index, offset, bits):
    for bit in range(bits):
        if offset >> bit & 1:
            index = index + (1 << bit) * (1 - 2 * ((index // (1 << bit)) % 2))
    return index


def bit_orders(n_f):
    bits = n_f.bit_length() - 1
    assert 1 << bits == n_f
    turns = min(bits, 2)
    return bits, [[(turn + at) % bits for at in range(bits)] for turn in range(turns)]


def greet(targets):
    barrier = pltpu.get_barrier_semaphore()
    for target in targets:
        pl.semaphore_signal(barrier, inc=1, device_id=target, device_id_type=MESH)
    pl.semaphore_wait(barrier, len(targets))


def plane_peers(n_f, f, c):
    bits = n_f.bit_length() - 1
    peers = []
    for offset in range(n_f):
        for other in range(2):
            if offset or other:
                peers.append(
                    (offset * 2 + other, {"fsdp": flip(f, offset, bits), "core": c + other * (1 - 2 * c)})
                )
    return peers


def column_peers(n_z, z, c):
    peers = []
    for offset in range(n_z):
        for other in range(2):
            if offset or other:
                peers.append(
                    (offset * 2 + other, {"zz": (z + offset) % n_z, "core": c + other * (1 - 2 * c)})
                )
    return peers


def remote(source, target, send, recv, device):
    return pltpu.make_async_remote_copy(
        src_ref=source,
        dst_ref=target,
        send_sem=send,
        recv_sem=recv,
        device_id=device,
        device_id_type=MESH,
    )


def no_pause(count):
    pass


class Gather:
    def __init__(self, n_f, x_ref, out_ref, send, recv, core_send, core_recv, local_sem):
        self.f, self.c = lax.axis_index("fsdp"), lax.axis_index("core")
        self.n_f, self.x_ref, self.out_ref = n_f, x_ref, out_ref
        self.send, self.recv, self.core_send, self.core_recv = send, recv, core_send, core_recv
        self.bits, self.orders = bit_orders(n_f)
        self.part = x_ref.shape[0] // len(self.orders)
        self.started = []
        self.have = [[0] for _ in self.orders]
        self.own = lambda: pltpu.make_async_copy(x_ref, out_ref.at[self.slot(0, self.c)], local_sem)

    def slot(self, offset, core):
        return flip(self.f, offset, self.bits) * 2 + core

    def piece(self, turn, offset, core):
        return self.out_ref.at[self.slot(offset, core), pl.ds(turn * self.part, self.part)]

    def source(self, turn, offset):
        if offset:
            return self.piece(turn, offset, self.c)
        return self.x_ref.at[pl.ds(turn * self.part, self.part)]

    def link(self, turn, offset, bit):
        sem = turn * self.n_f + (offset ^ (1 << bit))
        return remote(
            self.source(turn, offset),
            self.piece(turn, offset, self.c),
            self.send.at[sem],
            self.recv.at[sem],
            {"fsdp": flip(self.f, 1 << bit, self.bits)},
        )

    def arrival(self, turn, offset):
        sem = turn * self.n_f + offset
        where = self.piece(turn, offset, self.c)
        return remote(where, where, self.send.at[sem], self.recv.at[sem], {"core": 1 - self.c})

    def across(self, turn, offset):
        sem = turn * self.n_f + offset
        return remote(
            self.source(turn, offset),
            self.piece(turn, offset, self.c),
            self.core_send.at[sem],
            self.core_recv.at[sem],
            {"core": 1 - self.c},
        )

    def crossing(self, turn, offset):
        sem = turn * self.n_f + offset
        where = self.piece(turn, offset, 1 - self.c)
        return remote(
            where, where, self.core_send.at[sem], self.core_recv.at[sem], {"core": 1 - self.c}
        )

    def go(self, copy):
        copy.start()
        self.started.append(copy)

    def start(self):
        for step in range(self.bits):
            for turn, order in enumerate(self.orders):
                self.go(self.link(turn, 0, order[step]))
        for turn in range(len(self.orders)):
            self.go(self.across(turn, 0))
        self.own().start()

    def relay(self, pause):
        for step in range(self.bits):
            for at in range(1 << step):
                for turn, order in enumerate(self.orders):
                    offset = self.have[turn][at] ^ (1 << order[step])
                    self.arrival(turn, offset).wait_recv()
                    for later in range(step + 1, self.bits):
                        self.go(self.link(turn, offset, order[later]))
                    self.go(self.across(turn, offset))
                    self.have[turn].append(offset)
                    pause(1)

    def finish(self):
        for copy in self.started:
            copy.wait_send()
        for turn in range(len(self.orders)):
            for offset in self.have[turn]:
                self.crossing(turn, offset).wait_recv()
        self.own().wait()


def gather_stage(n_f, x_ref, out_ref, *rest):
    gather = Gather(n_f, x_ref, out_ref, *rest[:-1])
    gather.start()
    rest[-1](1)
    gather.relay(rest[-1])
    gather.finish()


def scatter_stage(
    n_f, part_ref, out_ref, acc, core_in, link_in, send, recv, core_send, core_recv, pause
):
    f, c = lax.axis_index("fsdp"), lax.axis_index("core")
    rows = out_ref.shape[0]
    bits, orders = bit_orders(n_f)
    part = rows // len(orders)
    started = []

    def go(copy):
        copy.start()
        started.append(copy)

    def held(offset, where):
        if acc is None:
            return part_ref.at[flip(f, offset, bits) * 2 + c, where]
        return acc.at[offset, where]

    def across(turn, offset):
        where = pl.ds(turn * part, part)
        sem = turn * n_f + offset
        return remote(
            part_ref.at[flip(f, offset, bits) * 2 + 1 - c, where],
            core_in.at[offset, where],
            core_send.at[sem],
            core_recv.at[sem],
            {"core": 1 - c},
        )

    def link(turn, offset, bit):
        where = pl.ds(turn * part, part)
        sem = turn * n_f + offset
        return remote(
            held(offset, where),
            link_in.at[offset, where],
            send.at[sem],
            recv.at[sem],
            {"fsdp": flip(f, 1 << bit, bits)},
        )

    plan = [[] for _ in range(bits)] + [[(turn, 0) for turn in range(len(orders))]]
    for step in range(bits):
        for offset in range(n_f):
            for turn, order in enumerate(orders):
                if offset >> order[step] & 1 and not any(offset >> b & 1 for b in order[:step]):
                    plan[step].append((turn, offset))
    for todo in plan:
        for turn, offset in todo:
            go(across(turn, offset))
    for step, todo in enumerate(plan):
        pause(1)
        for turn, offset in todo:
            where = pl.ds(turn * part, part)
            across(turn, offset).wait_recv()
            total = part_ref[flip(f, offset, bits) * 2 + c, where].astype(F32)
            total = total + core_in[offset, where].astype(F32)
            for bit in orders[turn][:step]:
                link(turn, offset | (1 << bit), bit).wait_recv()
                total = total + link_in[offset | (1 << bit), where].astype(F32)
            if offset:
                held(offset, where)[...] = total.astype(BF16)
                go(link(turn, offset, orders[turn][step]))
                if offset == n_f - 1:
                    pause(1)
            else:
                out_ref[where] = total
    for copy in started:
        copy.wait_send()


def exchange_stage(n_f, n_z, plane_in, column_in, plane_out, column_out, sems, whole, pause):
    f, z, c = lax.axis_index("fsdp"), lax.axis_index("zz"), lax.axis_index("core")
    peers = plane_peers(n_f, f, c)
    others = column_peers(n_z, z, c) if column_in is not None else []
    copies = []
    local = []
    if column_in is not None:
        mine = z * 2 + c
        for sem, device in others:
            to = device["zz"] * 2 + device["core"]
            source = column_in if whole else column_in.at[to]
            copies.append(
                remote(source, column_out.at[mine], sems[2].at[sem], sems[3].at[sem], device)
            )
        source = column_in if whole else column_in.at[mine]
        local.append(pltpu.make_async_copy(source, column_out.at[mine], sems[5]))
    mine = f * 2 + c
    for sem, device in peers:
        to = device["fsdp"] * 2 + device["core"]
        copies.append(
            remote(plane_in.at[to], plane_out.at[mine], sems[0].at[sem], sems[1].at[sem], device)
        )
    local.append(pltpu.make_async_copy(plane_in.at[mine], plane_out.at[mine], sems[4]))
    for copy in copies + local:
        copy.start()
    pause(1)
    for copy in copies:
        copy.wait_send()
    for sem, device in peers:
        frm = device["fsdp"] * 2 + device["core"]
        remote(
            plane_out.at[frm], plane_out.at[frm], sems[0].at[sem], sems[1].at[sem], device
        ).wait_recv()
    if column_in is not None:
        for offset in range(n_z):
            for other in range(2):
                if offset or other:
                    frm = ((z + n_z - offset) % n_z) * 2 + c + other * (1 - 2 * c)
                    sem = offset * 2 + other
                    remote(
                        column_out.at[frm],
                        column_out.at[frm],
                        sems[2].at[sem],
                        sems[3].at[sem],
                        {"core": 1 - c},
                    ).wait_recv()
    for copy in local:
        copy.wait()


class Line:
    def __init__(self, n_z, chunks, sems):
        self.n_z, self.chunks = n_z, chunks
        self.red_send, self.red_recv, self.fin_send, self.fin_recv, self.own_sem = sems
        self.z = lax.axis_index("zz")
        self.done = 0

    def toward(self, k, source):
        return remote(
            source,
            self.chunks[k][1],
            self.red_send.at[k],
            self.red_recv.at[k],
            {"zz": jnp.maximum(self.z - 1, 0)},
        )

    def outward(self, k, source):
        return remote(
            source,
            self.chunks[k][2],
            self.fin_send.at[k],
            self.fin_recv.at[k],
            {"zz": jnp.minimum(self.z + 1, self.n_z - 1)},
        )

    def keep(self, k):
        return pltpu.make_async_copy(self.chunks[k][1], self.chunks[k][2], self.own_sem.at[k])

    def reduce(self, k, z):
        own, landing, _ = self.chunks[k]
        if z == self.n_z - 1:
            self.toward(k, own).start()
            return
        self.toward(k, own).wait_recv()
        height = min(16, own.shape[0])

        @pl.loop(0, own.shape[0] // height)
        def _(at):
            where = pl.ds(pl.multiple_of(at * height, height), height)
            landing[where] = (own[where].astype(F32) + landing[where].astype(F32)).astype(BF16)

        if z > 0:
            self.toward(k, landing).start()
        else:
            self.outward(k, landing).start()
            self.keep(k).start()

    def spread(self, k, z):
        if z == 0:
            self.keep(k).wait()
            return
        self.outward(k, self.chunks[k][2]).wait_recv()
        if z < self.n_z - 1:
            self.outward(k, self.chunks[k][2]).start()

    def tick(self, then=None):
        t = self.done
        self.done += 1
        total = len(self.chunks)
        for z in range(self.n_z):
            k = t - STAGGER * (self.n_z - 1 - z)
            if 0 <= k < total:

                @pl.when(self.z == z)
                def _():
                    self.reduce(k, z)

            k = t - self.lag(z)
            if 0 <= k < total:

                @pl.when(self.z == z)
                def _():
                    self.spread(k, z)
                    if then is not None:
                        then(k)

    def lag(self, z):
        return STAGGER * (self.n_z - 1) + 1 + BEHIND * z

    def ticks(self):
        return len(self.chunks) + self.lag(self.n_z - 1)

    def left(self):
        return self.ticks() - self.done

    def finish(self):
        for k in range(len(self.chunks)):

            @pl.when(self.z > 0)
            def _():
                self.toward(k, self.chunks[k][0]).wait_send()

            @pl.when(self.z < self.n_z - 1)
            def _():
                self.outward(k, self.chunks[k][2]).wait_send()


def vector_stage(n_f, n_z, in_ref, out_ref, plane_in, part, line_in, sems, pause):
    f, z, c = lax.axis_index("fsdp"), lax.axis_index("zz"), lax.axis_index("core")
    send, recv, line_send, line_recv, local = sems
    peers = plane_peers(n_f, f, c)
    others = [(offset, {"zz": (z + offset) % n_z}) for offset in range(1, n_z)]
    mine = f * 2 + c
    copies = [
        remote(in_ref.at[device["fsdp"]], plane_in.at[mine], send.at[sem], recv.at[sem], device)
        for sem, device in peers
    ]
    for copy in copies:
        copy.start()
    own = pltpu.make_async_copy(in_ref.at[f], plane_in.at[mine], local)
    own.start()
    own.wait()
    pause(1)
    for sem, device in peers:
        where = plane_in.at[device["fsdp"] * 2 + device["core"]]
        remote(where, where, send.at[sem], recv.at[sem], device).wait_recv()
    total = plane_in[0]
    for at in range(1, n_f * 2):
        total = total + plane_in[at]
    part[...] = total
    line = [
        remote(part, line_in.at[z], line_send.at[sem], line_recv.at[sem], device)
        for sem, device in others
    ]
    for copy in line:
        copy.start()
    pause(1)
    for offset in range(1, n_z):
        where = line_in.at[(z + n_z - offset) % n_z]
        remote(
            where, where, line_send.at[offset], line_recv.at[offset], {"core": 1 - c}
        ).wait_recv()
    line_in[z] = total
    total = line_in[0]
    for at in range(1, n_z):
        total = total + line_in[at]
    out_ref[...] = total
    for copy in copies + line:
        copy.wait_send()


def heads_side_by_side(block, head):
    count = block.shape[1] // head
    return jnp.concatenate([block[:, at * head : (at + 1) * head] for at in range(count)], axis=0)


def heads_apart(block, count):
    rows = block.shape[0] // count
    return jnp.concatenate([block[at * rows : (at + 1) * rows] for at in range(count)], axis=1)


def attend_block(head, query_in, kv_ref, mask_ref):
    scale = 1.0 / math.sqrt(head)
    query = heads_side_by_side(query_in, head)
    count = query_in.shape[1] // head
    keys, values = kv_ref[:, :head], kv_ref[:, head:]
    mask = jnp.concatenate([mask_ref[...]] * count, axis=1)
    scores = dot_nt(keys, query) * scale + mask
    peak = jnp.max(scores, axis=0, keepdims=True)
    weights = jnp.exp(scores - peak)
    total = jnp.sum(weights, axis=0, keepdims=True)
    probs = (weights / total).astype(BF16)
    return heads_apart(dot_tn(probs, values).astype(BF16), count), peak + jnp.log(total)


def attend_back_block(head, query_in, grad_in, kv_ref, mask_ref, lse):
    scale = 1.0 / math.sqrt(head)
    query = heads_side_by_side(query_in, head)
    grad = heads_side_by_side(grad_in, head)
    count = query_in.shape[1] // head
    keys, values = kv_ref[:, :head], kv_ref[:, head:]
    mask = jnp.concatenate([mask_ref[...]] * count, axis=1)
    scores = dot_nt(keys, query) * scale + mask
    probs = jnp.exp(scores - lse)
    d_probs = dot_nt(values, grad)
    delta = jnp.sum(probs * d_probs, axis=0, keepdims=True)
    d_scores = (probs * (d_probs - delta)).astype(BF16)
    d_query = heads_apart((dot_tn(d_scores, keys) * scale).astype(BF16), count)
    d_keys = dot(d_scores, query) * scale
    d_values = dot(probs.astype(BF16), grad)
    return d_query, d_keys, d_values


class Box:
    pass


def rows_of(at, height=16):
    return pl.ds(pl.multiple_of(at * height, height), height)


GAIN_ONE, SHIFT_ONE, BIAS_OUT, GAIN_TWO, SHIFT_TWO, BIAS_DOWN, BIAS_QUERY = range(7)


def norm_tiles(load, gain, shift, normal_ref, inverse_ref, normed_ref):
    @pl.loop(0, normal_ref.shape[0] // 16)
    def _(at):
        where = rows_of(at)
        values = load(where)
        row_mean = jnp.mean(values, axis=-1, keepdims=True)
        centered = values - row_mean
        variance = jnp.mean(centered * centered, axis=-1, keepdims=True)
        inverse = lax.rsqrt(variance + EPSILON)
        normal = centered * inverse
        normal_ref[where] = normal
        inverse_ref[where] = inverse
        normed_ref[where] = (normal * gain + shift).astype(BF16)


def forward_body(n_f, n_z, head, names, *refs):
    r = Box()
    for name, ref in zip(names, refs, strict=True):
        setattr(r, name, ref)
    f, z, c = lax.axis_index("fsdp"), lax.axis_index("zz"), lax.axis_index("core")
    bits = n_f.bit_length() - 1
    n_p = n_f * 2
    rows, width = r.tokens.shape
    own_q = r.w_q.shape[2]
    own_h = r.w_up.shape[2]
    seg = width // n_f
    far = [flip(f, offset, bits) for offset in range(n_f)]
    r.small_all[f] = r.small[...]
    r.small_f32[...] = r.small[...].astype(F32)
    greet([device for _, device in plane_peers(n_f, f, c) + column_peers(n_z, z, c)])

    def columns(ref, to, size, where=slice(None)):
        return ref.at[where, pl.ds(pl.multiple_of((to * 2 + c) * size, LANES), size)]

    half = seg // 2
    quarter = seg // n_z

    def kv_piece(source, core):
        return r.w_kv.at[source, pl.ds(pl.multiple_of(core * half, 16), half)]

    def up_piece(source, plane):
        return r.w_up.at[source, pl.ds(pl.multiple_of(plane * quarter, 16), quarter)]

    smalls, early, kv_cross, up_links, up_lines = [], [], [], [], []
    for offset in range(1, n_f):
        device = {"fsdp": far[offset]}
        smalls.append(
            remote(r.small, r.small_all.at[f], r.small_sem.at[0, offset], r.small_sem.at[1, offset], device)
        )
        early.append(
            remote(
                columns(r.qkv_weight, far[offset], own_q),
                r.w_q.at[f],
                r.q_sem.at[0, offset],
                r.q_sem.at[1, offset],
                device,
            )
        )
        early.append(
            remote(
                r.qkv_weight.at[pl.ds(pl.multiple_of(c * half, 16), half), pl.ds(width, 2 * head)],
                kv_piece(f, c),
                r.kv_sem.at[0, offset],
                r.kv_sem.at[1, offset],
                device,
            )
        )
        where = pl.ds(pl.multiple_of(z * quarter, 16), quarter)
        up_links.append(
            remote(
                columns(r.up_weight, far[offset], own_h, where),
                up_piece(f, z),
                r.up_sem.at[0, offset],
                r.up_sem.at[1, offset],
                device,
            )
        )
    locals_ = [
        pltpu.make_async_copy(columns(r.qkv_weight, f, own_q), r.w_q.at[f], r.local_sem.at[0]),
        pltpu.make_async_copy(
            r.qkv_weight.at[:, pl.ds(width, 2 * head)], r.w_kv.at[f], r.local_sem.at[1]
        ),
        pltpu.make_async_copy(columns(r.up_weight, f, own_h), r.up_own, r.local_sem.at[2]),
        pltpu.make_async_copy(
            r.out_weight.at[pl.ds(pl.multiple_of(c * own_q, 16), own_q)], r.w_out, r.local_sem.at[11]
        ),
    ]
    for copy in smalls + early + locals_:
        copy.start()

    for offset in range(1, n_f):
        where = r.small_all.at[far[offset]]
        remote(
            where, where, r.small_sem.at[0, offset], r.small_sem.at[1, offset], {"core": 1 - c}
        ).wait_recv()
    bias_v = jnp.zeros((8, LANES), F32)
    for o in range(n_f):
        block = r.small_all[o].astype(F32)
        r.vecs[:, o * seg : (o + 1) * seg] = block
        shift = o * (head // n_f)
        block = block[:, :LANES]
        bias_v = bias_v + (pltpu.roll(block, shift, axis=1) if shift else block)
    norm_tiles(
        lambda where: r.tokens[where].astype(F32),
        r.vecs[GAIN_ONE : GAIN_ONE + 1],
        r.vecs[SHIFT_ONE : SHIFT_ONE + 1],
        r.normal_one,
        r.inverse_one,
        r.normed,
    )
    bias_q = r.small_f32[BIAS_QUERY : BIAS_QUERY + 1, pl.ds(pl.multiple_of(c * own_q, LANES), own_q)]
    normed = Gather(
        n_f, r.normed, r.normed_all, *(r.gather_one.at[at] for at in range(4)), r.local_sem.at[3]
    )
    normed.start()
    for offset in range(1, n_f):
        where = kv_piece(far[offset], c)
        remote(
            where, where, r.kv_sem.at[0, offset], r.kv_sem.at[1, offset], {"core": 1 - c}
        ).wait_recv()
        kv_cross.append(
            remote(where, where, r.kv_sem.at[2, offset], r.kv_sem.at[3, offset], {"core": 1 - c})
        )
        kv_cross[-1].start()
    locals_[2].wait()
    up_home = pltpu.make_async_copy(r.up_own, r.w_up.at[f], r.local_sem.at[4])
    up_home.start()
    normed.relay(no_pause)
    for copy in up_links:
        copy.start()
    span = r.kv.shape[0]
    first = jnp.maximum((z * 2 + c + 1) - span // rows, 0)
    key_pos = first * rows + lax.broadcasted_iota(jnp.int32, (span, rows), 0)
    row_pos = (z * 2 + c) * rows + lax.broadcasted_iota(jnp.int32, (span, rows), 1)
    same = jnp.zeros((span, rows), jnp.int32)
    doc_end = jnp.zeros((1, 1), jnp.int32)
    for at in range(r.lengths.shape[1]):
        doc_end = doc_end + r.lengths[:, at : at + 1]
        edge = (key_pos >= doc_end) != (row_pos >= doc_end)
        same = same + edge.astype(jnp.int32)
    r.mask[...] = jnp.where((same == 0) & (row_pos >= key_pos), 0.0, -1e30).astype(F32)
    for offset in range(1, n_f):
        where = kv_piece(far[offset], 1 - c)
        remote(
            where, where, r.kv_sem.at[2, offset], r.kv_sem.at[3, offset], {"core": 1 - c}
        ).wait_recv()
        where = r.w_q.at[far[offset]]
        remote(
            where, where, r.q_sem.at[0, offset], r.q_sem.at[1, offset], {"core": 1 - c}
        ).wait_recv()
    locals_[0].wait()
    locals_[1].wait()
    keyval = dot(r.normed[...], r.w_kv[...].reshape(width, 2 * head))
    r.keyval[:, :head] = keyval[:, :head].astype(BF16)
    r.keyval[:, head:] = (keyval[:, head:] + bias_v[7:8, :head]).astype(BF16)
    normed.finish()
    keep = pltpu.make_async_copy(r.normed_all, r.normed_pl, r.local_sem.at[5])
    keep.start()

    @pl.loop(0, n_p)
    def _(p):
        r.query_send[p] = (
            dot(r.normed_all[p], r.w_q[...].reshape(width, own_q)) + bias_q
        ).astype(BF16)

    grads = Gather(
        n_f, r.grad_out, r.grad_pl, *(r.gather_two.at[at] for at in range(4)), r.local_sem.at[6]
    )

    def fill(count):
        for offset in range(1, n_f):
            where = up_piece(far[offset], z)
            remote(
                where, where, r.up_sem.at[0, offset], r.up_sem.at[1, offset], {"core": 1 - c}
            ).wait_recv()
            for away in range(1, n_z):
                sem = away * n_f + offset
                up_lines.append(
                    remote(
                        where, where, r.line_sem.at[0, sem], r.line_sem.at[1, sem], {"zz": (z + away) % n_z}
                    )
                )
                up_lines[-1].start()
        grads.start()

    exchange_stage(
        n_f,
        n_z,
        r.query_send,
        r.keyval,
        r.query,
        r.kv_all,
        [
            r.swap_one.at[0],
            r.swap_one.at[1],
            r.column_sem.at[0],
            r.column_sem.at[1],
            r.local_sem.at[7],
            r.local_sem.at[8],
        ],
        True,
        fill,
    )
    for at in range(span // rows):
        r.kv[at * rows : (at + 1) * rows] = r.kv_all[first + at]

    @pl.loop(0, n_p)
    def _(p):
        mixed, lse = attend_block(head, r.query[p], r.kv, r.mask)
        r.mixed_send[p] = mixed
        r.lse[p] = lse

    exchange_stage(
        n_f,
        n_z,
        r.mixed_send,
        None,
        r.mixed_own,
        None,
        [r.swap_two.at[0], r.swap_two.at[1], None, None, r.local_sem.at[9], None],
        False,
        lambda count: grads.relay(no_pause),
    )
    tile = min(512, width)
    locals_[3].wait()

    @pl.loop(0, n_p)
    def _(p):
        for n in range(width // tile):
            cols = pl.ds(n * tile, tile)
            r.part[p, :, cols] = dot(r.mixed_own[p], r.w_out[:, cols]).astype(BF16)

    scatter_stage(
        n_f, r.part, r.branch, None, r.core_in, r.link_in, *(r.scatter_one.at[at] for at in range(4)), no_pause
    )

    def second(where):
        values = (
            r.tokens[where].astype(F32) + r.branch[where] + r.vecs[BIAS_OUT : BIAS_OUT + 1]
        )
        r.residual[where] = values
        return values

    norm_tiles(
        second,
        r.vecs[GAIN_TWO : GAIN_TWO + 1],
        r.vecs[SHIFT_TWO : SHIFT_TWO + 1],
        r.normal_two,
        r.inverse_two,
        r.normed_mlp,
    )
    last = Gather(
        n_f, r.normed_mlp, r.normed_mlp_pl, *(r.gather_three.at[at] for at in range(4)), r.local_sem.at[10]
    )
    last.start()
    grads.finish()
    last.relay(no_pause)
    for copy in smalls + early + kv_cross + up_links + up_lines:
        copy.wait_send()
    for offset in range(1, n_f):
        for away in range(1, n_z):
            where = up_piece(far[offset], (z + n_z - away) % n_z)
            sem = away * n_f + offset
            remote(
                where, where, r.line_sem.at[0, sem], r.line_sem.at[1, sem], {"core": 1 - c}
            ).wait_recv()
    up_home.wait()
    keep.wait()
    last.finish()


def forward(inputs, n_f, n_z, head, own_h, ident):
    rows, width = inputs["tokens"].shape
    n_p, n_s = n_f * 2, n_z * 2
    own_q = width // n_p
    seg = width // n_f
    count = len(bit_orders(n_f)[1]) * n_f
    stream = n_s * rows
    span = min(stream, stream // 2 + rows)
    in_hbm = ("qkv_weight", "up_weight", "out_weight")
    plane = (n_p, rows, width)
    blocks = (n_p, rows, own_q)
    outs = {
        "normed_pl": (plane, BF16, ANYWHERE),
        "normal_one": ((rows, width), F32, ON_CHIP),
        "inverse_one": ((rows, 1), F32, ON_CHIP),
        "query": (blocks, BF16, ON_CHIP),
        "kv": ((span, 2 * head), BF16, ON_CHIP),
        "lse": ((n_p, 1, own_q // head * rows), F32, ON_CHIP),
        "mixed_own": (blocks, BF16, ON_CHIP),
        "residual": ((rows, width), F32, ON_CHIP),
        "normal_two": ((rows, width), F32, ON_CHIP),
        "inverse_two": ((rows, 1), F32, ON_CHIP),
        "normed_mlp_pl": (plane, BF16, ANYWHERE),
        "grad_pl": (plane, BF16, ANYWHERE),
        "w_q": ((n_f, seg, own_q), BF16, ON_CHIP),
        "w_kv": ((n_f, seg, 2 * head), BF16, ON_CHIP),
        "w_up": ((n_f, seg, own_h), BF16, ANYWHERE),
        "vecs": ((8, width), F32, ON_CHIP),
        "mask": ((span, rows), F32, ON_CHIP),
        "w_out": ((own_q, width), BF16, ON_CHIP),
    }
    scratch = {
        "small_all": VMEM((n_f,) + inputs["small"].shape, BF16),
        "small_f32": VMEM(inputs["small"].shape, F32),

        "up_own": VMEM((seg, own_h), BF16),
        "normed": VMEM((rows, width), BF16),
        "normed_all": VMEM(plane, BF16),
        "keyval": VMEM((rows, 2 * head), BF16),
        "query_send": VMEM(blocks, BF16),
        "kv_all": VMEM((n_s, rows, 2 * head), BF16),
        "mixed_send": VMEM(blocks, BF16),
        "part": VMEM(plane, BF16),
        "core_in": VMEM((n_f, rows, width), BF16),
        "link_in": VMEM((n_f, rows, width), BF16),
        "branch": VMEM((rows, width), F32),
        "normed_mlp": VMEM((rows, width), BF16),
        "local_sem": DMA((12,)),
        "small_sem": DMA((2, n_f)),
        "q_sem": DMA((2, n_f)),
        "kv_sem": DMA((4, n_f)),
        "up_sem": DMA((2, n_f)),
        "line_sem": DMA((2, n_z * n_f)),
        "gather_one": DMA((4, count)),
        "gather_two": DMA((4, count)),
        "gather_three": DMA((4, count)),
        "scatter_one": DMA((4, count)),
        "swap_one": DMA((2, n_p)),
        "swap_two": DMA((2, n_p)),
        "column_sem": DMA((2, n_s)),
    }
    names = list(inputs) + list(outs) + list(scratch)
    result = pl.pallas_call(
        functools.partial(forward_body, n_f, n_z, head, names),
        out_shape=[jax.ShapeDtypeStruct(shape, kind) for shape, kind, _ in outs.values()],
        in_specs=[ANYWHERE if name in in_hbm else ON_CHIP for name in inputs],
        out_specs=[place for _, _, place in outs.values()],
        scratch_shapes=list(scratch.values()),
        compiler_params=pltpu.CompilerParams(
            collective_id=ident, has_side_effects=True, vmem_limit_bytes=56 << 20
        ),
        name="forward",
    )(*inputs.values())
    return dict(zip(outs, result))


PACE = 2
STAGGER = 3
BEHIND = 3


def norm_back_tiles(grad_ref, extra_ref, normal_ref, inverse_ref, gain_ref, base_ref, sums, store):
    rows = normal_ref.shape[0]

    @pl.loop(0, rows // 16)
    def _(at):
        where = rows_of(at)
        grad = grad_ref[where]
        if extra_ref is not None:
            grad = grad + extra_ref[where]
        normal = normal_ref[where].astype(F32)
        scaled = grad * gain_ref[...]
        first = jnp.mean(scaled, axis=-1, keepdims=True)
        second = jnp.mean(scaled * normal, axis=-1, keepdims=True)
        base = base_ref[where].astype(F32)
        result = base + inverse_ref[where] * (
            scaled - first - normal * second
        )
        store(where, result)
        sums[0:1] += jnp.sum(grad * normal, axis=0, keepdims=True)
        sums[1:2] += jnp.sum(grad, axis=0, keepdims=True)
        sums[2:3] += jnp.sum(result.astype(BF16).astype(F32), axis=0, keepdims=True)
        sums[3:4] += jnp.sum(base, axis=0, keepdims=True)


def backward_body(n_f, n_z, head, names, *refs):
    r = Box()
    for name, ref in zip(names, refs, strict=True):
        setattr(r, name, ref)
    f, z, c = lax.axis_index("fsdp"), lax.axis_index("zz"), lax.axis_index("core")
    bits = n_f.bit_length() - 1
    n_p = n_f * 2
    me = f * 2 + c
    rows, width = r.grad_out.shape
    own_q = r.w_out.shape[0]

    loads = {}
    for at, (name, source, target) in enumerate(
        (
            ("part", r.e_part, r.part),
            ("down", r.g_down_in, r.g_down),
            ("up", r.g_up_in, r.g_up),
        )
    ):
        loads[name] = pltpu.make_async_copy(source, target, r.load_sem.at[at])
        loads[name].start()
    greet([device for _, device in plane_peers(n_f, f, c) + column_peers(n_z, z, c)])

    kinds = []
    chunks = []
    for kind, own, landing, final in (
        ("up", r.g_up, r.land_up, r.fin_up),
        ("down", r.g_down, r.land_down, r.h_down.at[c]),
        ("out", r.g_out, r.land_out, r.h_out.at[c]),
        ("q", r.g_q, r.land_q, r.fin_q),
        ("kv", r.g_kv, r.land_kv, r.h_kv.at[c]),
    ):
        for k in range(own.shape[0]):
            kinds.append((kind, k))
            chunks.append((own.at[k], landing.at[k], final.at[k]))
    line = Line(n_z, chunks, (r.red_send, r.red_recv, r.fin_send, r.fin_recv, r.keep_sem))
    home = {"down": r.h_down, "out": r.h_out, "kv": r.h_kv, "up": r.h_up, "q": r.h_q}

    def swap(at, side):
        kind, k = kinds[at]
        where = home[kind].at[side, k]
        return remote(where, where, r.swap_send.at[at], r.swap_recv.at[at], {"core": 1 - c})

    def block(kind, turn, source):
        target = home[kind]
        height, size = finals[kind].shape[1:]
        cols = pl.ds(pl.multiple_of(source * size, LANES), size)
        return target.at[pl.ds(pl.multiple_of(turn * height, height), height), cols]

    finals = {"up": r.fin_up, "q": r.fin_q}
    home_sem = {
        "up": (r.up_send, r.up_mate, r.up_recv, r.up_relay, r.up_cross),
        "q": (r.q_send, r.q_mate, r.q_recv, r.q_relay, r.q_cross),
    }

    def turns(kind):
        return finals[kind].shape[0] // n_f

    def moves(kind, k):
        send, mate, recv, _, cross = home_sem[kind]
        owner, turn = k // turns(kind), k % turns(kind)
        where = block(kind, turn, me)
        sem = turn * n_f + f
        source = finals[kind].at[k]
        return (
            f == owner,
            lambda: pltpu.make_async_copy(source, where, send.at[k]),
            lambda: remote(source, where, mate.at[k], cross.at[sem], {"core": 1 - c}),
            lambda: remote(source, where, send.at[k], recv.at[sem], {"fsdp": owner}),
        )

    def deliver_split(kind, k):
        here, own, other, away = moves(kind, k)

        @pl.when(here)
        def _():
            own().start()
            other().start()

        @pl.when(jnp.logical_not(here))
        def _():
            away().start()

    def relay(kind, turn, offset):
        _, _, recv, send, cross = home_sem[kind]
        source = flip(f, offset, bits)
        where = block(kind, turn, source * 2 + c)
        sem = turn * n_f + source
        return (
            lambda: remote(where, where, send.at[sem], recv.at[sem], {"core": 1 - c}),
            lambda: remote(where, where, send.at[sem], cross.at[sem], {"core": 1 - c}),
        )

    def relay_all(kind):
        @pl.loop(0, turns(kind))
        def _(turn):
            for offset in range(1, n_f):
                arrival, onward = relay(kind, turn, offset)
                arrival().wait_recv()
                onward().start()

    def deliver(at):
        kind, k = kinds[at]
        if kind in ("down", "out", "kv"):
            swap(at, c).start()
        elif kind == "q":
            deliver_split(kind, k)

    def delivered():
        for at, (kind, k) in enumerate(kinds):
            if kind in ("down", "out", "kv"):
                swap(at, c).wait_send()
                swap(at, 1 - c).wait_recv()
        for kind in ("up", "q"):

            @pl.loop(0, finals[kind].shape[0])
            def _(k):
                here, own, other, away = moves(kind, k)

                @pl.when(here)
                def _():
                    own().wait()
                    other().wait_send()

                @pl.when(jnp.logical_not(here))
                def _():
                    away().wait_send()

            @pl.loop(0, turns(kind))
            def _(turn):
                for offset in range(n_f):
                    if offset:
                        relay(kind, turn, offset)[1]().wait_send()
                    source = flip(f, offset, bits)
                    where = block(kind, turn, source * 2 + 1 - c)
                    cross = home_sem[kind][4].at[turn * n_f + source]
                    remote(where, where, r.swap_send.at[0], cross, {"core": 1 - c}).wait_recv()

    ready = [False]
    limit = [r.g_down.shape[0] + r.g_up.shape[0]]

    def pause(count):
        if not ready[0]:
            loads["down"].wait()
            loads["up"].wait()
            ready[0] = True
        for _ in range(count * PACE):
            if line.left() and line.done < limit[0]:
                line.tick(deliver)

    for ref in (r.sums_two, r.sums_one):
        ref[...] = jnp.zeros_like(ref)
    loads["part"].wait()
    scatter_stage(
        n_f, r.part, r.e_sum, None, r.core_in, r.link_in, *(r.scatter_one.at[at] for at in range(4)), pause
    )

    def store_two(where, result):
        r.d_residual[where] = result
        r.d_branch[where] = result.astype(BF16)

    norm_back_tiles(
        r.e_sum, None, r.normal_two, r.inverse_two, r.gain_two, r.grad_out, r.sums_two, store_two
    )
    loads["normed"] = pltpu.make_async_copy(r.normed_in, r.part, r.load_sem.at[3])
    loads["normed"].start()
    gather_stage(
        n_f, r.d_branch, r.branch_pl, *(r.gather_one.at[at] for at in range(4)), r.local_sem.at[0], pause
    )

    @pl.loop(0, n_p)
    def _(p):
        r.mixed_send[p] = dot_nt(r.branch_pl[p], r.w_out[...]).astype(BF16)

    exchange_stage(
        n_f,
        n_z,
        r.mixed_send,
        None,
        r.d_mixed,
        None,
        [r.swap_one.at[0], r.swap_one.at[1], None, None, r.local_sem.at[1], None],
        False,
        pause,
    )
    tile = min(512, width)
    high = r.g_out.shape[1]
    for j in range(own_q // LANES):
        for n in range(width // tile):
            cols = pl.ds(n * tile, tile)
            result = dot_tn(
                r.mixed_own[:, :, j * LANES : (j + 1) * LANES].reshape(n_p * rows, LANES),
                r.branch_pl[:, :, cols].reshape(n_p * rows, tile),
            ).astype(BF16)
            for k in range(LANES // high):
                r.g_out[j * (LANES // high) + k, :, cols] = result[k * high : (k + 1) * high]
    limit[0] += r.g_out.shape[0]

    r.d_kv_span[...] = jnp.zeros_like(r.d_kv_span)
    step = max(1, n_p // 4)
    for first in range(0, n_p, step):

        @pl.loop(first, first + step)
        def _(p):
            d_query, d_keys, d_values = attend_back_block(
                head, r.query[p], r.d_mixed[p], r.kv, r.mask, r.lse[p]
            )
            r.dq_send[p] = d_query
            r.d_kv_span[:, :head] += d_keys
            r.d_kv_span[:, head:] += d_values

        pause(1)
    span = r.d_kv_span.shape[0]
    stream = n_z * 2 * rows
    first = jnp.maximum((z * 2 + c + 1) * rows - span, 0)
    r.dkv_send[...] = jnp.zeros_like(r.dkv_send)

    @pl.loop(0, span // rows)
    def _(at):
        block_at = (jnp.maximum((z * 2 + c + 1) * rows - span, 0)) // rows + at
        r.dkv_send[block_at] = r.d_kv_span[pl.ds(pl.multiple_of(at * rows, rows), rows)].astype(BF16)

    exchange_stage(
        n_f,
        n_z,
        r.dq_send,
        r.dkv_send,
        r.dq_own,
        r.dkv_recv,
        [
            r.swap_two.at[0],
            r.swap_two.at[1],
            r.column_sem.at[0],
            r.column_sem.at[1],
            r.local_sem.at[2],
            r.local_sem.at[3],
        ],
        False,
        pause,
    )
    total = r.dkv_recv[0].astype(F32)
    for s in range(1, n_z * 2):
        total = total + r.dkv_recv[s].astype(F32)
    r.d_kv[...] = total.astype(BF16)

    @pl.loop(0, n_p)
    def _(p):
        for n in range(width // tile):
            cols = pl.ds(n * tile, tile)
            r.branch_pl[p, :, cols] = dot_nt(r.dq_own[p], r.w_q[cols]).astype(BF16)

    scatter_stage(
        n_f, r.branch_pl, r.e_sum, None, r.core_in, r.link_in, *(r.scatter_two.at[at] for at in range(4)), pause
    )
    for n in range(width // tile):
        cols = pl.ds(n * tile, tile)
        r.e_extra[:, cols] = dot_nt(r.d_kv[...], r.w_kv[cols])

    def store_one(where, result):
        r.grad_tokens[where] = result.astype(BF16)

    norm_back_tiles(
        r.e_sum, r.e_extra, r.normal_one, r.inverse_one, r.gain_one, r.d_residual, r.sums_one, store_one
    )
    gather_stage(
        n_f, r.d_kv, r.dkv_pl, *(r.gather_two.at[at] for at in range(4)), r.local_sem.at[4], pause
    )

    loads["normed"].wait()
    dq_all = r.dq_own[...].reshape(n_p * rows, own_q)
    step = min(256, r.g_q.shape[1])
    for k in range(r.g_q.shape[0]):
        for at in range(r.g_q.shape[1] // step):
            base = k * r.g_q.shape[1] + at * step
            r.g_q[k, at * step : (at + 1) * step] = dot_tn(
                r.part[:, :, base : base + step].reshape(n_p * rows, step), dq_all
            ).astype(BF16)
    cols = pl.ds(pl.multiple_of(me * own_q, LANES), own_q)
    r.g_kv[0] = dot_tn(
        r.part[:, :, cols].reshape(n_p * rows, own_q), r.dkv_pl[...].reshape(n_p * rows, 2 * head)
    ).astype(BF16)
    loads["out"] = pltpu.make_async_copy(r.out_part, r.part, r.load_sem.at[4])
    loads["out"].start()
    limit[0] = line.ticks()
    pause(2)

    seg = r.vec_in.shape[2]
    r.vec_in[...] = jnp.zeros_like(r.vec_in)
    up_rows = r.up_sum.shape[0]
    d_value = jnp.sum(r.d_kv[:, head:].astype(F32), axis=0, keepdims=True)
    for o in range(n_f):
        cols = slice(o * seg, (o + 1) * seg)
        r.vec_in[o, 0:1] = r.sums_one[0:1, cols]
        r.vec_in[o, 1:2] = r.sums_one[1:2, cols]
        r.vec_in[o, 3:4] = r.sums_two[2:3, cols]
        r.vec_in[o, 4:5] = r.sums_two[0:1, cols]
        r.vec_in[o, 5:6] = r.sums_two[1:2, cols]
        r.vec_in[o, 6:7] = r.sums_two[3:4, cols]
        r.vec_in[o, 7:8, :head] = d_value
        for side in range(2):
            part = jnp.sum(r.dq_send[o * 2 + side].astype(F32), axis=0, keepdims=True)
            r.vec_in[o, 2:3, side * own_q : (side + 1) * own_q] = part

        for side in range(2):

            @pl.when((f == o) & (c == side))
            def _():
                r.vec_in[o, 8 + side * up_rows : 8 + (side + 1) * up_rows] = r.up_sum[...]

    vector_stage(
        n_f,
        n_z,
        r.vec_in,
        r.vectors,
        r.vec_plane,
        r.vec_part,
        r.vec_line,
        [r.vec_sem.at[0], r.vec_sem.at[1], r.vec_line_sem.at[0], r.vec_line_sem.at[1], r.local_sem.at[5]],
        pause,
    )

    loads["out"].wait()
    scatter_stage(
        n_f, r.part, r.out_sum, None, r.core_in, r.link_in, *(r.scatter_three.at[at] for at in range(4)), pause
    )
    while line.done < r.g_up.shape[0] + line.lag(n_z - 1):
        pause(1)

    @pl.loop(0, r.g_up.shape[0])
    def _(k):
        deliver_split("up", k)

    while line.left() > 4 * PACE:
        pause(1)
    relay_all("up")
    while line.left():
        pause(1)
    relay_all("q")
    line.finish()
    delivered()


def backward(inputs, n_f, n_z, head, own_h, ident):
    rows, width = inputs["grad_out"].shape
    n_p = n_f * 2
    n_s = n_z * 2
    own_q = width // n_p
    seg = width // n_f
    count = len(bit_orders(n_f)[1]) * n_f
    span = inputs["kv"].shape[0]
    high = max(16, CHUNK // width)
    tall = min(seg, CHUNK // own_q)
    down = inputs["g_down_in"].shape
    up = inputs["g_up_in"].shape
    out = (own_q // high, high, width)
    query = (width // tall, tall, own_q)
    keyval = (1, own_q, 2 * head)
    chunks = down[0] + up[0] + out[0] + query[0] + 1
    in_hbm = ("e_part", "g_down_in", "g_up_in", "normed_in", "out_part")
    outs = {
        "grad_tokens": ((rows, width), BF16, ON_CHIP),
        "out_sum": ((rows, width), F32, ON_CHIP),
        "vectors": ((16, seg), F32, ON_CHIP),
        "h_down": ((2,) + down, BF16, ANYWHERE),
        "h_up": ((seg, own_h * n_p), BF16, ANYWHERE),
        "h_out": ((2,) + out, BF16, ANYWHERE),
        "h_q": ((seg, width), BF16, ANYWHERE),
        "h_kv": ((2,) + keyval, BF16, ANYWHERE),
    }
    plane = (n_p, rows, width)
    blocks = (n_p, rows, own_q)
    scratch = {
        "part": VMEM(plane, BF16),
        "g_down": VMEM(down, BF16),
        "g_up": VMEM(up, BF16),
        "g_out": VMEM(out, BF16),
        "g_q": VMEM(query, BF16),
        "g_kv": VMEM(keyval, BF16),
        "land_down": VMEM(down, BF16),
        "land_up": VMEM(up, BF16),
        "land_out": VMEM(out, BF16),
        "land_q": VMEM(query, BF16),
        "land_kv": VMEM(keyval, BF16),
        "fin_up": VMEM(up, BF16),
        "fin_q": VMEM(query, BF16),
        "core_in": VMEM((n_f, rows, width), BF16),
        "link_in": VMEM((n_f, rows, width), BF16),
        "e_sum": VMEM((rows, width), F32),
        "e_extra": VMEM((rows, width), F32),
        "d_residual": VMEM((rows, width), F32),
        "d_branch": VMEM((rows, width), BF16),
        "branch_pl": VMEM(plane, BF16),
        "mixed_send": VMEM(blocks, BF16),
        "d_mixed": VMEM(blocks, BF16),
        "dq_send": VMEM(blocks, BF16),
        "dq_own": VMEM(blocks, BF16),
        "d_kv_span": VMEM((span, 2 * head), F32),
        "dkv_send": VMEM((n_s, rows, 2 * head), BF16),
        "dkv_recv": VMEM((n_s, rows, 2 * head), BF16),
        "d_kv": VMEM((rows, 2 * head), BF16),
        "dkv_pl": VMEM((n_p, rows, 2 * head), BF16),
        "sums_one": VMEM((8, width), F32),
        "sums_two": VMEM((8, width), F32),
        "vec_in": VMEM((n_f, 16, seg), F32),
        "vec_plane": VMEM((n_p, 16, seg), F32),
        "vec_part": VMEM((16, seg), F32),
        "vec_line": VMEM((n_z, 16, seg), F32),
        "load_sem": DMA((5,)),
        "local_sem": DMA((6,)),
        "red_send": DMA((chunks,)),
        "red_recv": DMA((chunks,)),
        "fin_send": DMA((chunks,)),
        "fin_recv": DMA((chunks,)),
        "keep_sem": DMA((chunks,)),
        "swap_send": DMA((chunks,)),
        "swap_recv": DMA((chunks,)),
        "up_send": DMA((up[0],)),
        "up_mate": DMA((up[0],)),
        "up_recv": DMA((up[0],)),
        "up_relay": DMA((up[0],)),
        "up_cross": DMA((up[0],)),
        "q_send": DMA((query[0],)),
        "q_mate": DMA((query[0],)),
        "q_recv": DMA((query[0],)),
        "q_relay": DMA((query[0],)),
        "q_cross": DMA((query[0],)),
        "scatter_one": DMA((4, count)),
        "scatter_two": DMA((4, count)),
        "scatter_three": DMA((4, count)),
        "gather_one": DMA((4, count)),
        "gather_two": DMA((4, count)),
        "swap_one": DMA((2, n_p)),
        "swap_two": DMA((2, n_p)),
        "column_sem": DMA((2, n_s)),
        "vec_sem": DMA((2, n_p)),
        "vec_line_sem": DMA((2, n_z)),
    }
    names = list(inputs) + list(outs) + list(scratch)
    result = pl.pallas_call(
        functools.partial(backward_body, n_f, n_z, head, names),
        out_shape=[jax.ShapeDtypeStruct(shape, kind) for shape, kind, _ in outs.values()],
        in_specs=[ANYWHERE if name in in_hbm else ON_CHIP for name in inputs],
        out_specs=[place for _, _, place in outs.values()],
        scratch_shapes=list(scratch.values()),
        compiler_params=pltpu.CompilerParams(
            collective_id=ident, has_side_effects=True, vmem_limit_bytes=67043328
        ),
        name="backward",
    )(*inputs.values())
    return dict(zip(outs, result))


def dot(left, right):
    return jnp.dot(left, right, preferred_element_type=F32)


def dot_tn(left, right):
    return lax.dot_general(left, right, (((0,), (0,)), ((), ())), preferred_element_type=F32)


def dot_nt(left, right):
    return lax.dot_general(left, right, (((1,), (1,)), ((), ())), preferred_element_type=F32)


def widen_body(count, *refs):
    at = 0
    for ref in refs[:count]:
        refs[count][:, at : at + ref.shape[1]] = ref[...].astype(F32)
        at += ref.shape[1]


def widen(*pieces):
    height = pieces[0].shape[0]
    width = sum(item.shape[1] for item in pieces)
    block = min(height, 1 << ((1 << 20) // width).bit_length() - 1)
    specs = [pl.BlockSpec((block, item.shape[1]), lambda i: (i, 0)) for item in pieces]
    return pl.pallas_call(
        functools.partial(widen_body, len(pieces)),
        out_shape=jax.ShapeDtypeStruct((height, width), F32),
        grid=(pl.cdiv(height, block),),
        in_specs=specs,
        out_specs=pl.BlockSpec((block, width), lambda i: (i, 0)),
        compiler_params=pltpu.CompilerParams(vmem_limit_bytes=40 << 20),
        name="widen",
    )(*pieces)


def shards(
    tokens,
    doc_lengths,
    attn_gain,
    attn_shift,
    qkv_weight,
    query_bias,
    value_bias,
    out_weight,
    out_bias,
    mlp_gain,
    mlp_shift,
    up_weight,
    up_bias,
    down_weight,
    down_bias,
    cotangent,
):
    n_f, n_z, n_c = lax.axis_size("fsdp"), lax.axis_size("zz"), lax.axis_size("core")
    f, z, c = lax.axis_index("fsdp"), lax.axis_index("zz"), lax.axis_index("core")
    n_p = n_f * n_c
    grad_out = cotangent[0]
    rows, width = grad_out.shape
    head = value_bias.shape[0] * n_f
    hidden = up_weight.shape[1]
    own_q = width // n_p
    own_h = hidden // n_p
    seg = width // n_f

    def own(vector, size):
        return lax.dynamic_slice_in_dim(vector, c * size, size, axis=0)

    row = lax.broadcasted_iota(jnp.int32, (8, seg), 0)
    small = jnp.broadcast_to(jnp.pad(value_bias, (0, seg - value_bias.shape[0]))[None], (8, seg))
    vectors = (attn_gain, attn_shift, out_bias, mlp_gain, mlp_shift, down_bias, query_bias)
    for at, item in enumerate(vectors):
        small = jnp.where(row == at, item[None], small)
    w_down = own(down_weight, own_h)
    ahead = forward(
        {
            "tokens": tokens[0],
            "grad_out": grad_out,
            "small": small,
            "lengths": doc_lengths,
            "out_weight": out_weight,
            "qkv_weight": qkv_weight,
            "up_weight": up_weight,
        },
        n_f,
        n_z,
        head,
        own_h,
        8,
    )
    vecs = ahead["vecs"]
    w_up = ahead["w_up"].reshape(width, own_h)
    grad_pl = ahead["grad_pl"].reshape(n_p * rows, width)
    normed_mlp_pl = ahead["normed_mlp_pl"].reshape(n_p * rows, width)

    inner = dot(normed_mlp_pl, w_up) + own(up_bias, own_h).astype(F32)
    activated, gelu_back = jax.vjp(lambda v: jax.nn.gelu(v, approximate=True), inner)
    activated = activated.astype(BF16)
    out_part = dot(activated, w_down).astype(BF16).reshape(n_p, rows, width)
    d_act = dot_nt(grad_pl, w_down)
    d_inner = gelu_back(d_act)[0].astype(BF16)
    e_part = dot_nt(d_inner, w_up).astype(BF16).reshape(n_p, rows, width)
    g_down = dot_tn(activated, grad_pl).astype(BF16)
    g_up = dot_tn(normed_mlp_pl, d_inner).astype(BF16)

    def chunked(block, most):
        height = min(max(16, CHUNK // block.shape[1]), most)
        return block.reshape(block.shape[0] // height, height, block.shape[1])

    done = backward(
        {
            "e_part": e_part,
            "out_part": out_part,
            "g_down_in": chunked(g_down, own_h),
            "g_up_in": chunked(g_up, seg),
            "normed_in": ahead["normed_pl"],
            "grad_out": grad_out,
            "normal_two": ahead["normal_two"],
            "inverse_two": ahead["inverse_two"],
            "gain_two": vecs[GAIN_TWO : GAIN_TWO + 1],
            "normal_one": ahead["normal_one"],
            "inverse_one": ahead["inverse_one"],
            "gain_one": vecs[GAIN_ONE : GAIN_ONE + 1],
            "w_out": ahead["w_out"],
            "w_q": ahead["w_q"].reshape(width, own_q),
            "w_kv": ahead["w_kv"].reshape(width, 2 * head),
            "query": ahead["query"],
            "kv": ahead["kv"],
            "mask": ahead["mask"],
            "lse": ahead["lse"],
            "mixed_own": ahead["mixed_own"],
            "up_sum": jnp.sum(d_inner.astype(F32), axis=0).reshape(own_h // seg, seg),
        },
        n_f,
        n_z,
        head,
        own_h,
        9,
    )
    layer_out = ahead["residual"] + done["out_sum"] + vecs[BIAS_DOWN]
    vectors = done["vectors"]
    grad_qkv = widen(done["h_q"], done["h_kv"].reshape(n_c * own_q, 2 * head))
    size = value_bias.shape[0]
    grad_value_bias = lax.dynamic_slice_in_dim(vectors[7], f * size, size)
    return (
        layer_out.astype(BF16)[None],
        done["grad_tokens"][None],
        vectors[0],
        vectors[1],
        grad_qkv,
        vectors[2],
        grad_value_bias,
        widen(done["h_out"].reshape(n_c * own_q, width)),
        vectors[3],
        vectors[4],
        vectors[5],
        widen(done["h_up"]),
        vectors[8 : 8 + hidden // width].reshape(-1),
        widen(done["h_down"].reshape(n_c * own_h, width)),
        vectors[6],
    )


def solution(mesh):
    n_f, n_s = mesh.shape["fsdp"], mesh.shape["seq"]
    split = Mesh(mesh.devices.reshape(n_f, n_s // 2, 2), ("fsdp", "zz", "core"))
    act = P("fsdp", ("zz", "core"), None)
    vec = P("fsdp")
    mat = P("fsdp", None)
    return jax.shard_map(
        shards,
        mesh=split,
        in_specs=(act, mat, vec, vec, mat, vec, vec, mat, vec, vec, vec, mat, vec, mat, vec, act),
        out_specs=(act, act, vec, vec, mat, vec, vec, mat, vec, vec, vec, mat, vec, mat, vec),
        check_vma=False,
    )
```

```python
import functools
import math

import jax
import jax.numpy as jnp
from jax import lax
from jax.experimental import pallas as pl
from jax.experimental.pallas import tpu as pltpu
from jax.sharding import Mesh
from jax.sharding import PartitionSpec as P

EPSILON = 1e-05
F32 = jnp.float32
BF16 = jnp.bfloat16
MESH = pl.DeviceIdType.MESH
VMEM = pltpu.VMEM
DMA = pltpu.SemaphoreType.DMA
ON_CHIP = pl.BlockSpec(memory_space=pltpu.VMEM)
ANYWHERE = pl.BlockSpec(memory_space=pl.ANY)
LANES = 128
CHUNK = 1 << 16


def flip(index, offset, bits):
    for bit in range(bits):
        if offset >> bit & 1:
            index = index + (1 << bit) * (1 - 2 * ((index // (1 << bit)) % 2))
    return index


def bit_orders(n_f):
    bits = n_f.bit_length() - 1
    assert 1 << bits == n_f
    turns = min(bits, 2)
    return bits, [[(turn + at) % bits for at in range(bits)] for turn in range(turns)]


def greet(targets):
    barrier = pltpu.get_barrier_semaphore()
    for target in targets:
        pl.semaphore_signal(barrier, inc=1, device_id=target, device_id_type=MESH)
    pl.semaphore_wait(barrier, len(targets))


def plane_peers(n_f, f, c):
    bits = n_f.bit_length() - 1
    peers = []
    for offset in range(n_f):
        for other in range(2):
            if offset or other:
                peers.append(
                    (offset * 2 + other, {"fsdp": flip(f, offset, bits), "core": c + other * (1 - 2 * c)})
                )
    return peers


def column_peers(n_z, z, c):
    peers = []
    for offset in range(n_z):
        for other in range(2):
            if offset or other:
                peers.append(
                    (offset * 2 + other, {"zz": (z + offset) % n_z, "core": c + other * (1 - 2 * c)})
                )
    return peers


def remote(source, target, send, recv, device):
    return pltpu.make_async_remote_copy(
        src_ref=source,
        dst_ref=target,
        send_sem=send,
        recv_sem=recv,
        device_id=device,
        device_id_type=MESH,
    )


def no_pause(count):
    pass


class Gather:
    def __init__(self, n_f, x_ref, out_ref, send, recv, core_send, core_recv, local_sem):
        self.f, self.c = lax.axis_index("fsdp"), lax.axis_index("core")
        self.n_f, self.x_ref, self.out_ref = n_f, x_ref, out_ref
        self.send, self.recv, self.core_send, self.core_recv = send, recv, core_send, core_recv
        self.bits, self.orders = bit_orders(n_f)
        self.part = x_ref.shape[0] // len(self.orders)
        self.started = []
        self.have = [[0] for _ in self.orders]
        self.own = lambda: pltpu.make_async_copy(x_ref, out_ref.at[self.slot(0, self.c)], local_sem)

    def slot(self, offset, core):
        return flip(self.f, offset, self.bits) * 2 + core

    def piece(self, turn, offset, core):
        return self.out_ref.at[self.slot(offset, core), pl.ds(turn * self.part, self.part)]

    def source(self, turn, offset):
        if offset:
            return self.piece(turn, offset, self.c)
        return self.x_ref.at[pl.ds(turn * self.part, self.part)]

    def link(self, turn, offset, bit):
        sem = turn * self.n_f + (offset ^ (1 << bit))
        return remote(
            self.source(turn, offset),
            self.piece(turn, offset, self.c),
            self.send.at[sem],
            self.recv.at[sem],
            {"fsdp": flip(self.f, 1 << bit, self.bits)},
        )

    def arrival(self, turn, offset):
        sem = turn * self.n_f + offset
        where = self.piece(turn, offset, self.c)
        return remote(where, where, self.send.at[sem], self.recv.at[sem], {"core": 1 - self.c})

    def across(self, turn, offset):
        sem = turn * self.n_f + offset
        return remote(
            self.source(turn, offset),
            self.piece(turn, offset, self.c),
            self.core_send.at[sem],
            self.core_recv.at[sem],
            {"core": 1 - self.c},
        )

    def crossing(self, turn, offset):
        sem = turn * self.n_f + offset
        where = self.piece(turn, offset, 1 - self.c)
        return remote(
            where, where, self.core_send.at[sem], self.core_recv.at[sem], {"core": 1 - self.c}
        )

    def go(self, copy):
        copy.start()
        self.started.append(copy)

    def start(self):
        for step in range(self.bits):
            for turn, order in enumerate(self.orders):
                self.go(self.link(turn, 0, order[step]))
        for turn in range(len(self.orders)):
            self.go(self.across(turn, 0))
        self.own().start()

    def relay(self, pause):
        for step in range(self.bits):
            for at in range(1 << step):
                for turn, order in enumerate(self.orders):
                    offset = self.have[turn][at] ^ (1 << order[step])
                    self.arrival(turn, offset).wait_recv()
                    for later in range(step + 1, self.bits):
                        self.go(self.link(turn, offset, order[later]))
                    self.go(self.across(turn, offset))
                    self.have[turn].append(offset)
                    pause(1)

    def finish(self):
        for copy in self.started:
            copy.wait_send()
        for turn in range(len(self.orders)):
            for offset in self.have[turn]:
                self.crossing(turn, offset).wait_recv()
        self.own().wait()


def gather_stage(n_f, x_ref, out_ref, *rest):
    gather = Gather(n_f, x_ref, out_ref, *rest[:-1])
    gather.start()
    rest[-1](1)
    gather.relay(rest[-1])
    gather.finish()


def scatter_stage(
    n_f, part_ref, out_ref, acc, core_in, link_in, send, recv, core_send, core_recv, pause
):
    f, c = lax.axis_index("fsdp"), lax.axis_index("core")
    rows = out_ref.shape[0]
    bits, orders = bit_orders(n_f)
    part = rows // len(orders)
    started = []

    def go(copy):
        copy.start()
        started.append(copy)

    def held(offset, where):
        if acc is None:
            return part_ref.at[flip(f, offset, bits) * 2 + c, where]
        return acc.at[offset, where]

    def across(turn, offset):
        where = pl.ds(turn * part, part)
        sem = turn * n_f + offset
        return remote(
            part_ref.at[flip(f, offset, bits) * 2 + 1 - c, where],
            core_in.at[offset, where],
            core_send.at[sem],
            core_recv.at[sem],
            {"core": 1 - c},
        )

    def link(turn, offset, bit):
        where = pl.ds(turn * part, part)
        sem = turn * n_f + offset
        return remote(
            held(offset, where),
            link_in.at[offset, where],
            send.at[sem],
            recv.at[sem],
            {"fsdp": flip(f, 1 << bit, bits)},
        )

    plan = [[] for _ in range(bits)] + [[(turn, 0) for turn in range(len(orders))]]
    for step in range(bits):
        for offset in range(n_f):
            for turn, order in enumerate(orders):
                if offset >> order[step] & 1 and not any(offset >> b & 1 for b in order[:step]):
                    plan[step].append((turn, offset))
    for todo in plan:
        for turn, offset in todo:
            go(across(turn, offset))
    for step, todo in enumerate(plan):
        pause(1)
        for turn, offset in todo:
            where = pl.ds(turn * part, part)
            across(turn, offset).wait_recv()
            total = part_ref[flip(f, offset, bits) * 2 + c, where].astype(F32)
            total = total + core_in[offset, where].astype(F32)
            for bit in orders[turn][:step]:
                link(turn, offset | (1 << bit), bit).wait_recv()
                total = total + link_in[offset | (1 << bit), where].astype(F32)
            if offset:
                held(offset, where)[...] = total.astype(BF16)
                go(link(turn, offset, orders[turn][step]))
                if offset == n_f - 1:
                    pause(1)
            else:
                out_ref[where] = total
    for copy in started:
        copy.wait_send()


def exchange_stage(n_f, n_z, plane_in, column_in, plane_out, column_out, sems, whole, pause):
    f, z, c = lax.axis_index("fsdp"), lax.axis_index("zz"), lax.axis_index("core")
    peers = plane_peers(n_f, f, c)
    others = column_peers(n_z, z, c) if column_in is not None else []
    copies = []
    local = []
    if column_in is not None:
        mine = z * 2 + c
        for sem, device in others:
            to = device["zz"] * 2 + device["core"]
            source = column_in if whole else column_in.at[to]
            copies.append(
                remote(source, column_out.at[mine], sems[2].at[sem], sems[3].at[sem], device)
            )
        source = column_in if whole else column_in.at[mine]
        local.append(pltpu.make_async_copy(source, column_out.at[mine], sems[5]))
    mine = f * 2 + c
    for sem, device in peers:
        to = device["fsdp"] * 2 + device["core"]
        copies.append(
            remote(plane_in.at[to], plane_out.at[mine], sems[0].at[sem], sems[1].at[sem], device)
        )
    local.append(pltpu.make_async_copy(plane_in.at[mine], plane_out.at[mine], sems[4]))
    for copy in copies + local:
        copy.start()
    pause(1)
    for copy in copies:
        copy.wait_send()
    for sem, device in peers:
        frm = device["fsdp"] * 2 + device["core"]
        remote(
            plane_out.at[frm], plane_out.at[frm], sems[0].at[sem], sems[1].at[sem], device
        ).wait_recv()
    if column_in is not None:
        for offset in range(n_z):
            for other in range(2):
                if offset or other:
                    frm = ((z + n_z - offset) % n_z) * 2 + c + other * (1 - 2 * c)
                    sem = offset * 2 + other
                    remote(
                        column_out.at[frm],
                        column_out.at[frm],
                        sems[2].at[sem],
                        sems[3].at[sem],
                        {"core": 1 - c},
                    ).wait_recv()
    for copy in local:
        copy.wait()


class Line:
    def __init__(self, n_z, chunks, sems):
        self.n_z, self.chunks = n_z, chunks
        self.red_send, self.red_recv, self.fin_send, self.fin_recv, self.own_sem = sems
        place, self.turn = lax.axis_index("zz"), 1 - 2 * lax.axis_index("core")
        self.place = place
        self.z = place + lax.axis_index("core") * (n_z - 1 - 2 * place)
        self.done = 0

    def toward(self, k, source):
        return remote(
            source,
            self.chunks[k][1],
            self.red_send.at[k],
            self.red_recv.at[k],
            {"zz": jnp.clip(self.place - self.turn, 0, self.n_z - 1)},
        )

    def outward(self, k, source):
        return remote(
            source,
            self.chunks[k][2],
            self.fin_send.at[k],
            self.fin_recv.at[k],
            {"zz": jnp.clip(self.place + self.turn, 0, self.n_z - 1)},
        )

    def keep(self, k):
        return pltpu.make_async_copy(self.chunks[k][1], self.chunks[k][2], self.own_sem.at[k])

    def reduce(self, k, z):
        own, landing, _ = self.chunks[k]
        if z == self.n_z - 1:
            self.toward(k, own).start()
            return
        self.toward(k, own).wait_recv()
        height = min(16, own.shape[0])

        @pl.loop(0, own.shape[0] // height)
        def _(at):
            where = pl.ds(pl.multiple_of(at * height, height), height)
            landing[where] = (own[where].astype(F32) + landing[where].astype(F32)).astype(BF16)

        if z > 0:
            self.toward(k, landing).start()
        else:
            self.outward(k, landing).start()
            self.keep(k).start()

    def spread(self, k, z):
        if z == 0:
            self.keep(k).wait()
            return
        self.outward(k, self.chunks[k][2]).wait_recv()
        if z < self.n_z - 1:
            self.outward(k, self.chunks[k][2]).start()

    def tick(self, then=None):
        t = self.done
        self.done += 1
        total = len(self.chunks)
        for z in range(self.n_z):
            k = t - STAGGER * (self.n_z - 1 - z)
            if 0 <= k < total:

                @pl.when(self.z == z)
                def _():
                    self.reduce(k, z)

            k = t - self.lag(z)
            if 0 <= k < total:

                @pl.when(self.z == z)
                def _():
                    self.spread(k, z)
                    if then is not None:
                        then(k)

    def lag(self, z):
        return STAGGER * (self.n_z - 1) + 1 + BEHIND * z

    def ticks(self):
        return len(self.chunks) + self.lag(self.n_z - 1)

    def left(self):
        return self.ticks() - self.done

    def finish(self):
        for k in range(len(self.chunks)):

            @pl.when(self.z > 0)
            def _():
                self.toward(k, self.chunks[k][0]).wait_send()

            @pl.when(self.z < self.n_z - 1)
            def _():
                self.outward(k, self.chunks[k][2]).wait_send()


def vector_stage(n_f, n_z, in_ref, out_ref, plane_in, part, line_in, sems, pause):
    f, z, c = lax.axis_index("fsdp"), lax.axis_index("zz"), lax.axis_index("core")
    send, recv, line_send, line_recv, local = sems
    peers = plane_peers(n_f, f, c)
    others = [(offset, {"zz": (z + offset) % n_z}) for offset in range(1, n_z)]
    mine = f * 2 + c
    copies = [
        remote(in_ref.at[device["fsdp"]], plane_in.at[mine], send.at[sem], recv.at[sem], device)
        for sem, device in peers
    ]
    for copy in copies:
        copy.start()
    own = pltpu.make_async_copy(in_ref.at[f], plane_in.at[mine], local)
    own.start()
    own.wait()
    pause(1)
    for sem, device in peers:
        where = plane_in.at[device["fsdp"] * 2 + device["core"]]
        remote(where, where, send.at[sem], recv.at[sem], device).wait_recv()
    total = plane_in[0]
    for at in range(1, n_f * 2):
        total = total + plane_in[at]
    part[...] = total
    line = [
        remote(part, line_in.at[z], line_send.at[sem], line_recv.at[sem], device)
        for sem, device in others
    ]
    for copy in line:
        copy.start()
    pause(1)
    for offset in range(1, n_z):
        where = line_in.at[(z + n_z - offset) % n_z]
        remote(
            where, where, line_send.at[offset], line_recv.at[offset], {"core": 1 - c}
        ).wait_recv()
    line_in[z] = total
    total = line_in[0]
    for at in range(1, n_z):
        total = total + line_in[at]
    out_ref[...] = total
    for copy in copies + line:
        copy.wait_send()


def heads_side_by_side(block, head):
    count = block.shape[1] // head
    return jnp.concatenate([block[:, at * head : (at + 1) * head] for at in range(count)], axis=0)


def heads_apart(block, count):
    rows = block.shape[0] // count
    return jnp.concatenate([block[at * rows : (at + 1) * rows] for at in range(count)], axis=1)


def attend_block(head, query_in, kv_ref, mask_ref):
    scale = 1.0 / math.sqrt(head)
    query = heads_side_by_side(query_in, head)
    count = query_in.shape[1] // head
    keys, values = kv_ref[:, :head], kv_ref[:, head:]
    mask = jnp.concatenate([mask_ref[...]] * count, axis=1)
    scores = dot_nt(keys, query) * scale + mask
    peak = jnp.max(scores, axis=0, keepdims=True)
    weights = jnp.exp(scores - peak)
    total = jnp.sum(weights, axis=0, keepdims=True)
    probs = (weights / total).astype(BF16)
    return heads_apart(dot_tn(probs, values).astype(BF16), count), peak + jnp.log(total)


def attend_back_block(head, query_in, grad_in, kv_ref, mask_ref, lse):
    scale = 1.0 / math.sqrt(head)
    query = heads_side_by_side(query_in, head)
    grad = heads_side_by_side(grad_in, head)
    count = query_in.shape[1] // head
    keys, values = kv_ref[:, :head], kv_ref[:, head:]
    mask = jnp.concatenate([mask_ref[...]] * count, axis=1)
    scores = dot_nt(keys, query) * scale + mask
    probs = jnp.exp(scores - lse)
    d_probs = dot_nt(values, grad)
    delta = jnp.sum(probs * d_probs, axis=0, keepdims=True)
    d_scores = (probs * (d_probs - delta)).astype(BF16)
    d_query = heads_apart((dot_tn(d_scores, keys) * scale).astype(BF16), count)
    d_keys = dot(d_scores, query) * scale
    d_values = dot(probs.astype(BF16), grad)
    return d_query, d_keys, d_values


class Box:
    pass


def rows_of(at, height=16):
    return pl.ds(pl.multiple_of(at * height, height), height)


GAIN_ONE, SHIFT_ONE, BIAS_OUT, GAIN_TWO, SHIFT_TWO, BIAS_DOWN, BIAS_QUERY = range(7)


def norm_tiles(load, gain, shift, normal_ref, inverse_ref, normed_ref):
    @pl.loop(0, normal_ref.shape[0] // 16)
    def _(at):
        where = rows_of(at)
        values = load(where)
        row_mean = jnp.mean(values, axis=-1, keepdims=True)
        centered = values - row_mean
        variance = jnp.mean(centered * centered, axis=-1, keepdims=True)
        inverse = lax.rsqrt(variance + EPSILON)
        normal = centered * inverse
        normal_ref[where] = normal
        inverse_ref[where] = inverse
        normed_ref[where] = (normal * gain + shift).astype(BF16)


def forward_body(n_f, n_z, head, names, *refs):
    r = Box()
    for name, ref in zip(names, refs, strict=True):
        setattr(r, name, ref)
    f, z, c = lax.axis_index("fsdp"), lax.axis_index("zz"), lax.axis_index("core")
    bits = n_f.bit_length() - 1
    n_p = n_f * 2
    rows, width = r.tokens.shape
    own_q = r.w_q.shape[2]
    own_h = r.w_up.shape[2]
    seg = width // n_f
    far = [flip(f, offset, bits) for offset in range(n_f)]
    r.small_all[f] = r.small[...]
    r.small_f32[...] = r.small[...].astype(F32)
    greet([device for _, device in plane_peers(n_f, f, c) + column_peers(n_z, z, c)])

    def columns(ref, to, size, where=slice(None)):
        return ref.at[where, pl.ds(pl.multiple_of((to * 2 + c) * size, LANES), size)]

    half = seg // 2
    quarter = seg // n_z

    def kv_piece(source, core):
        return r.w_kv.at[source, pl.ds(pl.multiple_of(core * half, 16), half)]

    def up_piece(source, plane):
        return r.w_up.at[source, pl.ds(pl.multiple_of(plane * quarter, 16), quarter)]

    smalls, early, kv_cross, up_links, up_lines = [], [], [], [], []
    for offset in range(1, n_f):
        device = {"fsdp": far[offset]}
        smalls.append(
            remote(r.small, r.small_all.at[f], r.small_sem.at[0, offset], r.small_sem.at[1, offset], device)
        )
        early.append(
            remote(
                columns(r.qkv_weight, far[offset], own_q),
                r.w_q.at[f],
                r.q_sem.at[0, offset],
                r.q_sem.at[1, offset],
                device,
            )
        )
        early.append(
            remote(
                r.qkv_weight.at[pl.ds(pl.multiple_of(c * half, 16), half), pl.ds(width, 2 * head)],
                kv_piece(f, c),
                r.kv_sem.at[0, offset],
                r.kv_sem.at[1, offset],
                device,
            )
        )
        where = pl.ds(pl.multiple_of(z * quarter, 16), quarter)
        up_links.append(
            remote(
                columns(r.up_weight, far[offset], own_h, where),
                up_piece(f, z),
                r.up_sem.at[0, offset],
                r.up_sem.at[1, offset],
                device,
            )
        )
    locals_ = [
        pltpu.make_async_copy(columns(r.qkv_weight, f, own_q), r.w_q.at[f], r.local_sem.at[0]),
        pltpu.make_async_copy(
            r.qkv_weight.at[:, pl.ds(width, 2 * head)], r.w_kv.at[f], r.local_sem.at[1]
        ),
        pltpu.make_async_copy(columns(r.up_weight, f, own_h), r.up_own, r.local_sem.at[2]),
        pltpu.make_async_copy(
            r.out_weight.at[pl.ds(pl.multiple_of(c * own_q, 16), own_q)], r.w_out, r.local_sem.at[11]
        ),
    ]
    for copy in smalls + early + locals_:
        copy.start()

    for offset in range(1, n_f):
        where = r.small_all.at[far[offset]]
        remote(
            where, where, r.small_sem.at[0, offset], r.small_sem.at[1, offset], {"core": 1 - c}
        ).wait_recv()
    bias_v = jnp.zeros((8, LANES), F32)
    for o in range(n_f):
        block = r.small_all[o].astype(F32)
        r.vecs[:, o * seg : (o + 1) * seg] = block
        shift = o * (head // n_f)
        block = block[:, :LANES]
        bias_v = bias_v + (pltpu.roll(block, shift, axis=1) if shift else block)
    norm_tiles(
        lambda where: r.tokens[where].astype(F32),
        r.vecs[GAIN_ONE : GAIN_ONE + 1],
        r.vecs[SHIFT_ONE : SHIFT_ONE + 1],
        r.normal_one,
        r.inverse_one,
        r.normed,
    )
    bias_q = r.small_f32[BIAS_QUERY : BIAS_QUERY + 1, pl.ds(pl.multiple_of(c * own_q, LANES), own_q)]
    normed = Gather(
        n_f, r.normed, r.normed_all, *(r.gather_one.at[at] for at in range(4)), r.local_sem.at[3]
    )
    normed.start()
    for offset in range(1, n_f):
        where = kv_piece(far[offset], c)
        remote(
            where, where, r.kv_sem.at[0, offset], r.kv_sem.at[1, offset], {"core": 1 - c}
        ).wait_recv()
        kv_cross.append(
            remote(where, where, r.kv_sem.at[2, offset], r.kv_sem.at[3, offset], {"core": 1 - c})
        )
        kv_cross[-1].start()
    locals_[2].wait()
    up_home = pltpu.make_async_copy(r.up_own, r.w_up.at[f], r.local_sem.at[4])
    up_home.start()
    normed.relay(no_pause)
    for copy in up_links:
        copy.start()
    span = r.kv.shape[0]
    first = jnp.maximum((z * 2 + c + 1) - span // rows, 0)
    key_pos = first * rows + lax.broadcasted_iota(jnp.int32, (span, rows), 0)
    row_pos = (z * 2 + c) * rows + lax.broadcasted_iota(jnp.int32, (span, rows), 1)
    same = jnp.zeros((span, rows), jnp.int32)
    doc_end = jnp.zeros((1, 1), jnp.int32)
    for at in range(r.lengths.shape[1]):
        doc_end = doc_end + r.lengths[:, at : at + 1]
        edge = (key_pos >= doc_end) != (row_pos >= doc_end)
        same = same + edge.astype(jnp.int32)
    r.mask[...] = jnp.where((same == 0) & (row_pos >= key_pos), 0.0, -1e30).astype(F32)
    for offset in range(1, n_f):
        where = kv_piece(far[offset], 1 - c)
        remote(
            where, where, r.kv_sem.at[2, offset], r.kv_sem.at[3, offset], {"core": 1 - c}
        ).wait_recv()
        where = r.w_q.at[far[offset]]
        remote(
            where, where, r.q_sem.at[0, offset], r.q_sem.at[1, offset], {"core": 1 - c}
        ).wait_recv()
    locals_[0].wait()
    locals_[1].wait()
    keyval = dot(r.normed[...], r.w_kv[...].reshape(width, 2 * head))
    r.keyval[:, :head] = keyval[:, :head].astype(BF16)
    r.keyval[:, head:] = (keyval[:, head:] + bias_v[7:8, :head]).astype(BF16)
    normed.finish()
    keep = pltpu.make_async_copy(r.normed_all, r.normed_pl, r.local_sem.at[5])
    keep.start()

    @pl.loop(0, n_p)
    def _(p):
        r.query_send[p] = (
            dot(r.normed_all[p], r.w_q[...].reshape(width, own_q)) + bias_q
        ).astype(BF16)

    grads = Gather(
        n_f, r.grad_out, r.grad_pl, *(r.gather_two.at[at] for at in range(4)), r.local_sem.at[6]
    )

    def fill(count):
        for offset in range(1, n_f):
            where = up_piece(far[offset], z)
            remote(
                where, where, r.up_sem.at[0, offset], r.up_sem.at[1, offset], {"core": 1 - c}
            ).wait_recv()
            for away in range(1, n_z):
                sem = away * n_f + offset
                up_lines.append(
                    remote(
                        where, where, r.line_sem.at[0, sem], r.line_sem.at[1, sem], {"zz": (z + away) % n_z}
                    )
                )
                up_lines[-1].start()
        grads.start()

    exchange_stage(
        n_f,
        n_z,
        r.query_send,
        r.keyval,
        r.query,
        r.kv_all,
        [
            r.swap_one.at[0],
            r.swap_one.at[1],
            r.column_sem.at[0],
            r.column_sem.at[1],
            r.local_sem.at[7],
            r.local_sem.at[8],
        ],
        True,
        fill,
    )
    for at in range(span // rows):
        r.kv[at * rows : (at + 1) * rows] = r.kv_all[first + at]

    @pl.loop(0, n_p)
    def _(p):
        mixed, lse = attend_block(head, r.query[p], r.kv, r.mask)
        r.mixed_send[p] = mixed
        r.lse[p] = lse

    exchange_stage(
        n_f,
        n_z,
        r.mixed_send,
        None,
        r.mixed_own,
        None,
        [r.swap_two.at[0], r.swap_two.at[1], None, None, r.local_sem.at[9], None],
        False,
        lambda count: grads.relay(no_pause),
    )
    tile = min(512, width)
    locals_[3].wait()

    @pl.loop(0, n_p)
    def _(p):
        for n in range(width // tile):
            cols = pl.ds(n * tile, tile)
            r.part[p, :, cols] = dot(r.mixed_own[p], r.w_out[:, cols]).astype(BF16)

    scatter_stage(
        n_f, r.part, r.branch, None, r.core_in, r.link_in, *(r.scatter_one.at[at] for at in range(4)), no_pause
    )

    def second(where):
        values = (
            r.tokens[where].astype(F32) + r.branch[where] + r.vecs[BIAS_OUT : BIAS_OUT + 1]
        )
        r.residual[where] = values
        return values

    norm_tiles(
        second,
        r.vecs[GAIN_TWO : GAIN_TWO + 1],
        r.vecs[SHIFT_TWO : SHIFT_TWO + 1],
        r.normal_two,
        r.inverse_two,
        r.normed_mlp,
    )
    last = Gather(
        n_f, r.normed_mlp, r.normed_mlp_pl, *(r.gather_three.at[at] for at in range(4)), r.local_sem.at[10]
    )
    last.start()
    grads.finish()
    last.relay(no_pause)
    for copy in smalls + early + kv_cross + up_links + up_lines:
        copy.wait_send()
    for offset in range(1, n_f):
        for away in range(1, n_z):
            where = up_piece(far[offset], (z + n_z - away) % n_z)
            sem = away * n_f + offset
            remote(
                where, where, r.line_sem.at[0, sem], r.line_sem.at[1, sem], {"core": 1 - c}
            ).wait_recv()
    up_home.wait()
    keep.wait()
    last.finish()


def forward(inputs, n_f, n_z, head, own_h, ident):
    rows, width = inputs["tokens"].shape
    n_p, n_s = n_f * 2, n_z * 2
    own_q = width // n_p
    seg = width // n_f
    count = len(bit_orders(n_f)[1]) * n_f
    stream = n_s * rows
    span = min(stream, stream // 2 + rows)
    in_hbm = ("qkv_weight", "up_weight", "out_weight")
    plane = (n_p, rows, width)
    blocks = (n_p, rows, own_q)
    outs = {
        "normed_pl": (plane, BF16, ANYWHERE),
        "normal_one": ((rows, width), F32, ON_CHIP),
        "inverse_one": ((rows, 1), F32, ON_CHIP),
        "query": (blocks, BF16, ON_CHIP),
        "kv": ((span, 2 * head), BF16, ON_CHIP),
        "lse": ((n_p, 1, own_q // head * rows), F32, ON_CHIP),
        "mixed_own": (blocks, BF16, ON_CHIP),
        "residual": ((rows, width), F32, ON_CHIP),
        "normal_two": ((rows, width), F32, ON_CHIP),
        "inverse_two": ((rows, 1), F32, ON_CHIP),
        "normed_mlp_pl": (plane, BF16, ANYWHERE),
        "grad_pl": (plane, BF16, ANYWHERE),
        "w_q": ((n_f, seg, own_q), BF16, ON_CHIP),
        "w_kv": ((n_f, seg, 2 * head), BF16, ON_CHIP),
        "w_up": ((n_f, seg, own_h), BF16, ANYWHERE),
        "vecs": ((8, width), F32, ON_CHIP),
        "mask": ((span, rows), F32, ON_CHIP),
        "w_out": ((own_q, width), BF16, ON_CHIP),
    }
    scratch = {
        "small_all": VMEM((n_f,) + inputs["small"].shape, BF16),
        "small_f32": VMEM(inputs["small"].shape, F32),

        "up_own": VMEM((seg, own_h), BF16),
        "normed": VMEM((rows, width), BF16),
        "normed_all": VMEM(plane, BF16),
        "keyval": VMEM((rows, 2 * head), BF16),
        "query_send": VMEM(blocks, BF16),
        "kv_all": VMEM((n_s, rows, 2 * head), BF16),
        "mixed_send": VMEM(blocks, BF16),
        "part": VMEM(plane, BF16),
        "core_in": VMEM((n_f, rows, width), BF16),
        "link_in": VMEM((n_f, rows, width), BF16),
        "branch": VMEM((rows, width), F32),
        "normed_mlp": VMEM((rows, width), BF16),
        "local_sem": DMA((12,)),
        "small_sem": DMA((2, n_f)),
        "q_sem": DMA((2, n_f)),
        "kv_sem": DMA((4, n_f)),
        "up_sem": DMA((2, n_f)),
        "line_sem": DMA((2, n_z * n_f)),
        "gather_one": DMA((4, count)),
        "gather_two": DMA((4, count)),
        "gather_three": DMA((4, count)),
        "scatter_one": DMA((4, count)),
        "swap_one": DMA((2, n_p)),
        "swap_two": DMA((2, n_p)),
        "column_sem": DMA((2, n_s)),
    }
    names = list(inputs) + list(outs) + list(scratch)
    result = pl.pallas_call(
        functools.partial(forward_body, n_f, n_z, head, names),
        out_shape=[jax.ShapeDtypeStruct(shape, kind) for shape, kind, _ in outs.values()],
        in_specs=[ANYWHERE if name in in_hbm else ON_CHIP for name in inputs],
        out_specs=[place for _, _, place in outs.values()],
        scratch_shapes=list(scratch.values()),
        compiler_params=pltpu.CompilerParams(
            collective_id=ident, has_side_effects=True, vmem_limit_bytes=56 << 20
        ),
        name="forward",
    )(*inputs.values())
    return dict(zip(outs, result))


PACE = 2
STAGGER = 3
BEHIND = 3


def norm_back_tiles(grad_ref, extra_ref, normal_ref, inverse_ref, gain_ref, base_ref, sums, store):
    rows = normal_ref.shape[0]

    @pl.loop(0, rows // 16)
    def _(at):
        where = rows_of(at)
        grad = grad_ref[where]
        if extra_ref is not None:
            grad = grad + extra_ref[where]
        normal = normal_ref[where].astype(F32)
        scaled = grad * gain_ref[...]
        first = jnp.mean(scaled, axis=-1, keepdims=True)
        second = jnp.mean(scaled * normal, axis=-1, keepdims=True)
        base = base_ref[where].astype(F32)
        result = base + inverse_ref[where] * (
            scaled - first - normal * second
        )
        store(where, result)
        sums[0:1] += jnp.sum(grad * normal, axis=0, keepdims=True)
        sums[1:2] += jnp.sum(grad, axis=0, keepdims=True)
        sums[2:3] += jnp.sum(result.astype(BF16).astype(F32), axis=0, keepdims=True)
        sums[3:4] += jnp.sum(base, axis=0, keepdims=True)


def backward_body(n_f, n_z, head, names, *refs):
    r = Box()
    for name, ref in zip(names, refs, strict=True):
        setattr(r, name, ref)
    f, z, c = lax.axis_index("fsdp"), lax.axis_index("zz"), lax.axis_index("core")
    bits = n_f.bit_length() - 1
    n_p = n_f * 2
    me = f * 2 + c
    rows, width = r.grad_out.shape
    own_q = r.w_out.shape[0]

    loads = {}
    for at, (name, source, target) in enumerate(
        (
            ("part", r.e_part, r.part),
            ("down", r.g_down_in, r.g_down),
            ("up", r.g_up_in, r.g_up),
        )
    ):
        loads[name] = pltpu.make_async_copy(source, target, r.load_sem.at[at])
        loads[name].start()
    greet([device for _, device in plane_peers(n_f, f, c) + column_peers(n_z, z, c)])

    kinds = []
    chunks = []
    for kind, own, landing, final in (
        ("up", r.g_up, r.land_up, r.fin_up),
        ("down", r.g_down, r.land_down, r.h_down.at[c]),
        ("out", r.g_out, r.land_out, r.h_out.at[c]),
        ("q", r.g_q, r.land_q, r.fin_q),
        ("kv", r.g_kv, r.land_kv, r.h_kv.at[c]),
    ):
        for k in range(own.shape[0]):
            if kind == "q":
                k = flip(f, k % n_f, bits) * (own.shape[0] // n_f) + k // n_f
            kinds.append((kind, k))
            chunks.append((own.at[k], landing.at[k], final.at[k]))
    line = Line(n_z, chunks, (r.red_send, r.red_recv, r.fin_send, r.fin_recv, r.keep_sem))
    home = {"down": r.h_down, "out": r.h_out, "kv": r.h_kv, "up": r.h_up, "q": r.h_q}

    def swap(at, side):
        kind, k = kinds[at]
        where = home[kind].at[side, k]
        return remote(where, where, r.swap_send.at[at], r.swap_recv.at[at], {"core": 1 - c})

    def block(kind, turn, source):
        target = home[kind]
        height, size = finals[kind].shape[1:]
        cols = pl.ds(pl.multiple_of(source * size, LANES), size)
        return target.at[pl.ds(pl.multiple_of(turn * height, height), height), cols]

    finals = {"up": r.fin_up, "q": r.fin_q}
    home_sem = {
        "up": (r.up_send, r.up_mate, r.up_recv, r.up_relay, r.up_cross),
        "q": (r.q_send, r.q_mate, r.q_recv, r.q_relay, r.q_cross),
    }

    def turns(kind):
        return finals[kind].shape[0] // n_f

    def moves(kind, k):
        send, mate, recv, _, cross = home_sem[kind]
        owner, turn = k // turns(kind), k % turns(kind)
        where = block(kind, turn, me)
        sem = turn * n_f + f
        source = finals[kind].at[k]
        return (
            f == owner,
            lambda: pltpu.make_async_copy(source, where, send.at[k]),
            lambda: remote(source, where, mate.at[k], cross.at[sem], {"core": 1 - c}),
            lambda: remote(source, where, send.at[k], recv.at[sem], {"fsdp": owner}),
        )

    def deliver_split(kind, k):
        here, own, other, away = moves(kind, k)

        @pl.when(here)
        def _():
            own().start()
            other().start()

        @pl.when(jnp.logical_not(here))
        def _():
            away().start()

    def relay(kind, turn, offset):
        _, _, recv, send, cross = home_sem[kind]
        source = flip(f, offset, bits)
        where = block(kind, turn, source * 2 + c)
        sem = turn * n_f + source
        return (
            lambda: remote(where, where, send.at[sem], recv.at[sem], {"core": 1 - c}),
            lambda: remote(where, where, send.at[sem], cross.at[sem], {"core": 1 - c}),
        )

    def relay_all(kind):
        @pl.loop(0, turns(kind))
        def _(turn):
            for offset in range(1, n_f):
                arrival, onward = relay(kind, turn, offset)
                arrival().wait_recv()
                onward().start()

    def deliver(at):
        kind, k = kinds[at]
        if kind in ("down", "out", "kv"):
            swap(at, c).start()
        elif kind == "q":
            deliver_split(kind, k)

    def delivered():
        for at, (kind, k) in enumerate(kinds):
            if kind in ("down", "out", "kv"):
                swap(at, c).wait_send()
                swap(at, 1 - c).wait_recv()
        for kind in ("up", "q"):

            @pl.loop(0, finals[kind].shape[0])
            def _(k):
                here, own, other, away = moves(kind, k)

                @pl.when(here)
                def _():
                    own().wait()
                    other().wait_send()

                @pl.when(jnp.logical_not(here))
                def _():
                    away().wait_send()

            @pl.loop(0, turns(kind))
            def _(turn):
                for offset in range(n_f):
                    if offset:
                        relay(kind, turn, offset)[1]().wait_send()
                    source = flip(f, offset, bits)
                    where = block(kind, turn, source * 2 + 1 - c)
                    cross = home_sem[kind][4].at[turn * n_f + source]
                    remote(where, where, r.swap_send.at[0], cross, {"core": 1 - c}).wait_recv()

    ready = [False]
    limit = [r.g_down.shape[0] + r.g_up.shape[0]]

    def pause(count):
        if not ready[0]:
            loads["down"].wait()
            loads["up"].wait()
            ready[0] = True
        for _ in range(count * PACE):
            if line.left() and line.done < limit[0]:
                line.tick(deliver)

    for ref in (r.sums_two, r.sums_one):
        ref[...] = jnp.zeros_like(ref)
    loads["part"].wait()
    scatter_stage(
        n_f, r.part, r.e_sum, None, r.core_in, r.link_in, *(r.scatter_one.at[at] for at in range(4)), pause
    )

    def store_two(where, result):
        r.d_residual[where] = result
        r.d_branch[where] = result.astype(BF16)

    norm_back_tiles(
        r.e_sum, None, r.normal_two, r.inverse_two, r.gain_two, r.grad_out, r.sums_two, store_two
    )
    loads["normed"] = pltpu.make_async_copy(r.normed_in, r.part, r.load_sem.at[3])
    loads["normed"].start()
    gather_stage(
        n_f, r.d_branch, r.branch_pl, *(r.gather_one.at[at] for at in range(4)), r.local_sem.at[0], pause
    )

    @pl.loop(0, n_p)
    def _(p):
        r.mixed_send[p] = dot_nt(r.branch_pl[p], r.w_out[...]).astype(BF16)

    exchange_stage(
        n_f,
        n_z,
        r.mixed_send,
        None,
        r.d_mixed,
        None,
        [r.swap_one.at[0], r.swap_one.at[1], None, None, r.local_sem.at[1], None],
        False,
        pause,
    )
    tile = min(512, width)
    high = r.g_out.shape[1]
    for j in range(own_q // LANES):
        for n in range(width // tile):
            cols = pl.ds(n * tile, tile)
            result = dot_tn(
                r.mixed_own[:, :, j * LANES : (j + 1) * LANES].reshape(n_p * rows, LANES),
                r.branch_pl[:, :, cols].reshape(n_p * rows, tile),
            ).astype(BF16)
            for k in range(LANES // high):
                r.g_out[j * (LANES // high) + k, :, cols] = result[k * high : (k + 1) * high]
    limit[0] += r.g_out.shape[0]

    r.d_kv_span[...] = jnp.zeros_like(r.d_kv_span)
    step = max(1, n_p // 4)
    for first in range(0, n_p, step):

        @pl.loop(first, first + step)
        def _(p):
            d_query, d_keys, d_values = attend_back_block(
                head, r.query[p], r.d_mixed[p], r.kv, r.mask, r.lse[p]
            )
            r.dq_send[p] = d_query
            r.d_kv_span[:, :head] += d_keys
            r.d_kv_span[:, head:] += d_values

        pause(1)
    span = r.d_kv_span.shape[0]
    stream = n_z * 2 * rows
    first = jnp.maximum((z * 2 + c + 1) * rows - span, 0)
    r.dkv_send[...] = jnp.zeros_like(r.dkv_send)

    @pl.loop(0, span // rows)
    def _(at):
        block_at = (jnp.maximum((z * 2 + c + 1) * rows - span, 0)) // rows + at
        r.dkv_send[block_at] = r.d_kv_span[pl.ds(pl.multiple_of(at * rows, rows), rows)].astype(BF16)

    exchange_stage(
        n_f,
        n_z,
        r.dq_send,
        r.dkv_send,
        r.dq_own,
        r.dkv_recv,
        [
            r.swap_two.at[0],
            r.swap_two.at[1],
            r.column_sem.at[0],
            r.column_sem.at[1],
            r.local_sem.at[2],
            r.local_sem.at[3],
        ],
        False,
        pause,
    )
    total = r.dkv_recv[0].astype(F32)
    for s in range(1, n_z * 2):
        total = total + r.dkv_recv[s].astype(F32)
    r.d_kv[...] = total.astype(BF16)

    @pl.loop(0, n_p)
    def _(p):
        for n in range(width // tile):
            cols = pl.ds(n * tile, tile)
            r.branch_pl[p, :, cols] = dot_nt(r.dq_own[p], r.w_q[cols]).astype(BF16)

    scatter_stage(
        n_f, r.branch_pl, r.e_sum, None, r.core_in, r.link_in, *(r.scatter_two.at[at] for at in range(4)), pause
    )
    for n in range(width // tile):
        cols = pl.ds(n * tile, tile)
        r.e_extra[:, cols] = dot_nt(r.d_kv[...], r.w_kv[cols])

    def store_one(where, result):
        r.grad_tokens[where] = result.astype(BF16)

    norm_back_tiles(
        r.e_sum, r.e_extra, r.normal_one, r.inverse_one, r.gain_one, r.d_residual, r.sums_one, store_one
    )
    gather_stage(
        n_f, r.d_kv, r.dkv_pl, *(r.gather_two.at[at] for at in range(4)), r.local_sem.at[4], pause
    )

    loads["normed"].wait()
    dq_all = r.dq_own[...].reshape(n_p * rows, own_q)
    step = min(256, r.g_q.shape[1])
    for k in range(r.g_q.shape[0]):
        for at in range(r.g_q.shape[1] // step):
            base = k * r.g_q.shape[1] + at * step
            r.g_q[k, at * step : (at + 1) * step] = dot_tn(
                r.part[:, :, base : base + step].reshape(n_p * rows, step), dq_all
            ).astype(BF16)
    cols = pl.ds(pl.multiple_of(me * own_q, LANES), own_q)
    r.g_kv[0] = dot_tn(
        r.part[:, :, cols].reshape(n_p * rows, own_q), r.dkv_pl[...].reshape(n_p * rows, 2 * head)
    ).astype(BF16)
    loads["out"] = pltpu.make_async_copy(r.out_part, r.part, r.load_sem.at[4])
    loads["out"].start()
    limit[0] = line.ticks()
    pause(2)

    while line.done < r.g_up.shape[0] + line.lag(n_z - 1):
        pause(1)

    @pl.loop(0, turns("up"))
    def _(turn):
        for offset in range(n_f):
            deliver_split("up", flip(f, (offset + 1) % n_f, bits) * turns("up") + turn)

    pause(6)

    seg = r.vec_in.shape[2]
    r.vec_in[...] = jnp.zeros_like(r.vec_in)
    up_rows = r.up_sum.shape[0]
    d_value = jnp.sum(r.d_kv[:, head:].astype(F32), axis=0, keepdims=True)
    for o in range(n_f):
        cols = slice(o * seg, (o + 1) * seg)
        r.vec_in[o, 0:1] = r.sums_one[0:1, cols]
        r.vec_in[o, 1:2] = r.sums_one[1:2, cols]
        r.vec_in[o, 3:4] = r.sums_two[2:3, cols]
        r.vec_in[o, 4:5] = r.sums_two[0:1, cols]
        r.vec_in[o, 5:6] = r.sums_two[1:2, cols]
        r.vec_in[o, 6:7] = r.sums_two[3:4, cols]
        r.vec_in[o, 7:8, :head] = d_value
        for side in range(2):
            part = jnp.sum(r.dq_send[o * 2 + side].astype(F32), axis=0, keepdims=True)
            r.vec_in[o, 2:3, side * own_q : (side + 1) * own_q] = part

        for side in range(2):

            @pl.when((f == o) & (c == side))
            def _():
                r.vec_in[o, 8 + side * up_rows : 8 + (side + 1) * up_rows] = r.up_sum[...]

    vector_stage(
        n_f,
        n_z,
        r.vec_in,
        r.vectors,
        r.vec_plane,
        r.vec_part,
        r.vec_line,
        [r.vec_sem.at[0], r.vec_sem.at[1], r.vec_line_sem.at[0], r.vec_line_sem.at[1], r.local_sem.at[5]],
        pause,
    )

    loads["out"].wait()
    scatter_stage(
        n_f, r.part, r.out_sum, None, r.core_in, r.link_in, *(r.scatter_three.at[at] for at in range(4)), pause
    )
    while line.left() > 4 * PACE:
        pause(1)
    relay_all("up")
    while line.left():
        pause(1)
    relay_all("q")
    line.finish()
    delivered()


def backward(inputs, n_f, n_z, head, own_h, ident):
    rows, width = inputs["grad_out"].shape
    n_p = n_f * 2
    n_s = n_z * 2
    own_q = width // n_p
    seg = width // n_f
    count = len(bit_orders(n_f)[1]) * n_f
    span = inputs["kv"].shape[0]
    high = max(16, CHUNK // width)
    tall = min(seg, CHUNK // own_q)
    down = inputs["g_down_in"].shape
    up = inputs["g_up_in"].shape
    out = (own_q // high, high, width)
    query = (width // tall, tall, own_q)
    keyval = (1, own_q, 2 * head)
    chunks = down[0] + up[0] + out[0] + query[0] + 1
    in_hbm = ("e_part", "g_down_in", "g_up_in", "normed_in", "out_part")
    outs = {
        "grad_tokens": ((rows, width), BF16, ON_CHIP),
        "out_sum": ((rows, width), F32, ON_CHIP),
        "vectors": ((16, seg), F32, ON_CHIP),
        "h_down": ((2,) + down, BF16, ANYWHERE),
        "h_up": ((seg, own_h * n_p), BF16, ANYWHERE),
        "h_out": ((2,) + out, BF16, ANYWHERE),
        "h_q": ((seg, width), BF16, ANYWHERE),
        "h_kv": ((2,) + keyval, BF16, ANYWHERE),
    }
    plane = (n_p, rows, width)
    blocks = (n_p, rows, own_q)
    scratch = {
        "part": VMEM(plane, BF16),
        "g_down": VMEM(down, BF16),
        "g_up": VMEM(up, BF16),
        "g_out": VMEM(out, BF16),
        "g_q": VMEM(query, BF16),
        "g_kv": VMEM(keyval, BF16),
        "land_down": VMEM(down, BF16),
        "land_up": VMEM(up, BF16),
        "land_out": VMEM(out, BF16),
        "land_q": VMEM(query, BF16),
        "land_kv": VMEM(keyval, BF16),
        "fin_up": VMEM(up, BF16),
        "fin_q": VMEM(query, BF16),
        "core_in": VMEM((n_f, rows, width), BF16),
        "link_in": VMEM((n_f, rows, width), BF16),
        "e_sum": VMEM((rows, width), F32),
        "e_extra": VMEM((rows, width), F32),
        "d_residual": VMEM((rows, width), F32),
        "d_branch": VMEM((rows, width), BF16),
        "branch_pl": VMEM(plane, BF16),
        "mixed_send": VMEM(blocks, BF16),
        "d_mixed": VMEM(blocks, BF16),
        "dq_send": VMEM(blocks, BF16),
        "dq_own": VMEM(blocks, BF16),
        "d_kv_span": VMEM((span, 2 * head), F32),
        "dkv_send": VMEM((n_s, rows, 2 * head), BF16),
        "dkv_recv": VMEM((n_s, rows, 2 * head), BF16),
        "d_kv": VMEM((rows, 2 * head), BF16),
        "dkv_pl": VMEM((n_p, rows, 2 * head), BF16),
        "sums_one": VMEM((8, width), F32),
        "sums_two": VMEM((8, width), F32),
        "vec_in": VMEM((n_f, 16, seg), F32),
        "vec_plane": VMEM((n_p, 16, seg), F32),
        "vec_part": VMEM((16, seg), F32),
        "vec_line": VMEM((n_z, 16, seg), F32),
        "load_sem": DMA((5,)),
        "local_sem": DMA((6,)),
        "red_send": DMA((chunks,)),
        "red_recv": DMA((chunks,)),
        "fin_send": DMA((chunks,)),
        "fin_recv": DMA((chunks,)),
        "keep_sem": DMA((chunks,)),
        "swap_send": DMA((chunks,)),
        "swap_recv": DMA((chunks,)),
        "up_send": DMA((up[0],)),
        "up_mate": DMA((up[0],)),
        "up_recv": DMA((up[0],)),
        "up_relay": DMA((up[0],)),
        "up_cross": DMA((up[0],)),
        "q_send": DMA((query[0],)),
        "q_mate": DMA((query[0],)),
        "q_recv": DMA((query[0],)),
        "q_relay": DMA((query[0],)),
        "q_cross": DMA((query[0],)),
        "scatter_one": DMA((4, count)),
        "scatter_two": DMA((4, count)),
        "scatter_three": DMA((4, count)),
        "gather_one": DMA((4, count)),
        "gather_two": DMA((4, count)),
        "swap_one": DMA((2, n_p)),
        "swap_two": DMA((2, n_p)),
        "column_sem": DMA((2, n_s)),
        "vec_sem": DMA((2, n_p)),
        "vec_line_sem": DMA((2, n_z)),
    }
    names = list(inputs) + list(outs) + list(scratch)
    result = pl.pallas_call(
        functools.partial(backward_body, n_f, n_z, head, names),
        out_shape=[jax.ShapeDtypeStruct(shape, kind) for shape, kind, _ in outs.values()],
        in_specs=[ANYWHERE if name in in_hbm else ON_CHIP for name in inputs],
        out_specs=[place for _, _, place in outs.values()],
        scratch_shapes=list(scratch.values()),
        compiler_params=pltpu.CompilerParams(
            collective_id=ident, has_side_effects=True, vmem_limit_bytes=67043328
        ),
        name="backward",
    )(*inputs.values())
    return dict(zip(outs, result))


def dot(left, right):
    return jnp.dot(left, right, preferred_element_type=F32)


def dot_tn(left, right):
    return lax.dot_general(left, right, (((0,), (0,)), ((), ())), preferred_element_type=F32)


def dot_nt(left, right):
    return lax.dot_general(left, right, (((1,), (1,)), ((), ())), preferred_element_type=F32)


def widen_body(count, *refs):
    at = 0
    for ref in refs[:count]:
        refs[count][:, at : at + ref.shape[1]] = ref[...].astype(F32)
        at += ref.shape[1]


def widen(*pieces):
    height = pieces[0].shape[0]
    width = sum(item.shape[1] for item in pieces)
    block = min(height, 1 << ((1 << 20) // width).bit_length() - 1)
    specs = [pl.BlockSpec((block, item.shape[1]), lambda i: (i, 0)) for item in pieces]
    return pl.pallas_call(
        functools.partial(widen_body, len(pieces)),
        out_shape=jax.ShapeDtypeStruct((height, width), F32),
        grid=(pl.cdiv(height, block),),
        in_specs=specs,
        out_specs=pl.BlockSpec((block, width), lambda i: (i, 0)),
        compiler_params=pltpu.CompilerParams(vmem_limit_bytes=40 << 20),
        name="widen",
    )(*pieces)


def shards(
    tokens,
    doc_lengths,
    attn_gain,
    attn_shift,
    qkv_weight,
    query_bias,
    value_bias,
    out_weight,
    out_bias,
    mlp_gain,
    mlp_shift,
    up_weight,
    up_bias,
    down_weight,
    down_bias,
    cotangent,
):
    n_f, n_z, n_c = lax.axis_size("fsdp"), lax.axis_size("zz"), lax.axis_size("core")
    f, z, c = lax.axis_index("fsdp"), lax.axis_index("zz"), lax.axis_index("core")
    n_p = n_f * n_c
    grad_out = cotangent[0]
    rows, width = grad_out.shape
    head = value_bias.shape[0] * n_f
    hidden = up_weight.shape[1]
    own_q = width // n_p
    own_h = hidden // n_p
    seg = width // n_f

    def own(vector, size):
        return lax.dynamic_slice_in_dim(vector, c * size, size, axis=0)

    row = lax.broadcasted_iota(jnp.int32, (8, seg), 0)
    small = jnp.broadcast_to(jnp.pad(value_bias, (0, seg - value_bias.shape[0]))[None], (8, seg))
    vectors = (attn_gain, attn_shift, out_bias, mlp_gain, mlp_shift, down_bias, query_bias)
    for at, item in enumerate(vectors):
        small = jnp.where(row == at, item[None], small)
    w_down = own(down_weight, own_h)
    ahead = forward(
        {
            "tokens": tokens[0],
            "grad_out": grad_out,
            "small": small,
            "lengths": doc_lengths,
            "out_weight": out_weight,
            "qkv_weight": qkv_weight,
            "up_weight": up_weight,
        },
        n_f,
        n_z,
        head,
        own_h,
        8,
    )
    vecs = ahead["vecs"]
    w_up = ahead["w_up"].reshape(width, own_h)
    grad_pl = ahead["grad_pl"].reshape(n_p * rows, width)
    normed_mlp_pl = ahead["normed_mlp_pl"].reshape(n_p * rows, width)

    inner = dot(normed_mlp_pl, w_up) + own(up_bias, own_h).astype(F32)
    activated, gelu_back = jax.vjp(lambda v: jax.nn.gelu(v, approximate=True), inner)
    activated = activated.astype(BF16)
    out_part = dot(activated, w_down).astype(BF16).reshape(n_p, rows, width)
    d_act = dot_nt(grad_pl, w_down)
    d_inner = gelu_back(d_act)[0].astype(BF16)
    e_part = dot_nt(d_inner, w_up).astype(BF16).reshape(n_p, rows, width)
    g_down = dot_tn(activated, grad_pl).astype(BF16)
    g_up = dot_tn(normed_mlp_pl, d_inner).astype(BF16)

    def chunked(block, most):
        height = min(max(16, CHUNK // block.shape[1]), most)
        return block.reshape(block.shape[0] // height, height, block.shape[1])

    done = backward(
        {
            "e_part": e_part,
            "out_part": out_part,
            "g_down_in": chunked(g_down, own_h),
            "g_up_in": chunked(g_up, seg),
            "normed_in": ahead["normed_pl"],
            "grad_out": grad_out,
            "normal_two": ahead["normal_two"],
            "inverse_two": ahead["inverse_two"],
            "gain_two": vecs[GAIN_TWO : GAIN_TWO + 1],
            "normal_one": ahead["normal_one"],
            "inverse_one": ahead["inverse_one"],
            "gain_one": vecs[GAIN_ONE : GAIN_ONE + 1],
            "w_out": ahead["w_out"],
            "w_q": ahead["w_q"].reshape(width, own_q),
            "w_kv": ahead["w_kv"].reshape(width, 2 * head),
            "query": ahead["query"],
            "kv": ahead["kv"],
            "mask": ahead["mask"],
            "lse": ahead["lse"],
            "mixed_own": ahead["mixed_own"],
            "up_sum": jnp.sum(d_inner.astype(F32), axis=0).reshape(own_h // seg, seg),
        },
        n_f,
        n_z,
        head,
        own_h,
        9,
    )
    layer_out = ahead["residual"] + done["out_sum"] + vecs[BIAS_DOWN]
    vectors = done["vectors"]
    grad_qkv = widen(done["h_q"], done["h_kv"].reshape(n_c * own_q, 2 * head))
    size = value_bias.shape[0]
    grad_value_bias = lax.dynamic_slice_in_dim(vectors[7], f * size, size)
    return (
        layer_out.astype(BF16)[None],
        done["grad_tokens"][None],
        vectors[0],
        vectors[1],
        grad_qkv,
        vectors[2],
        grad_value_bias,
        widen(done["h_out"].reshape(n_c * own_q, width)),
        vectors[3],
        vectors[4],
        vectors[5],
        widen(done["h_up"]),
        vectors[8 : 8 + hidden // width].reshape(-1),
        widen(done["h_down"].reshape(n_c * own_h, width)),
        vectors[6],
    )


def solution(mesh):
    n_f, n_s = mesh.shape["fsdp"], mesh.shape["seq"]
    split = Mesh(mesh.devices.reshape(n_f, n_s // 2, 2), ("fsdp", "zz", "core"))
    act = P("fsdp", ("zz", "core"), None)
    vec = P("fsdp")
    mat = P("fsdp", None)
    return jax.shard_map(
        shards,
        mesh=split,
        in_specs=(act, mat, vec, vec, mat, vec, vec, mat, vec, vec, vec, mat, vec, mat, vec, act),
        out_specs=(act, act, vec, vec, mat, vec, vec, mat, vec, vec, vec, mat, vec, mat, vec),
        check_vma=False,
    )
```

```python
import functools
import math

import jax
import jax.numpy as jnp
from jax import lax
from jax.experimental import pallas as pl
from jax.experimental.pallas import tpu as pltpu
from jax.sharding import Mesh
from jax.sharding import PartitionSpec as P

EPSILON = 1e-05
F32 = jnp.float32
BF16 = jnp.bfloat16
MESH = pl.DeviceIdType.MESH
VMEM = pltpu.VMEM
DMA = pltpu.SemaphoreType.DMA
ON_CHIP = pl.BlockSpec(memory_space=pltpu.VMEM)
ANYWHERE = pl.BlockSpec(memory_space=pl.ANY)
LANES = 128
CHUNK = 1 << 16


def flip(index, offset, bits):
    for bit in range(bits):
        if offset >> bit & 1:
            index = index + (1 << bit) * (1 - 2 * ((index // (1 << bit)) % 2))
    return index


def bit_orders(n_f):
    bits = n_f.bit_length() - 1
    assert 1 << bits == n_f
    turns = min(bits, 2)
    return bits, [[(turn + at) % bits for at in range(bits)] for turn in range(turns)]


def greet(targets):
    barrier = pltpu.get_barrier_semaphore()
    for target in targets:
        pl.semaphore_signal(barrier, inc=1, device_id=target, device_id_type=MESH)
    pl.semaphore_wait(barrier, len(targets))


def plane_peers(n_f, f, c):
    bits = n_f.bit_length() - 1
    peers = []
    for offset in range(n_f):
        for other in range(2):
            if offset or other:
                peers.append(
                    (offset * 2 + other, {"fsdp": flip(f, offset, bits), "core": c + other * (1 - 2 * c)})
                )
    return peers


def column_peers(n_z, z, c):
    peers = []
    for offset in range(n_z):
        for other in range(2):
            if offset or other:
                peers.append(
                    (offset * 2 + other, {"zz": (z + offset) % n_z, "core": c + other * (1 - 2 * c)})
                )
    return peers


def remote(source, target, send, recv, device):
    return pltpu.make_async_remote_copy(
        src_ref=source,
        dst_ref=target,
        send_sem=send,
        recv_sem=recv,
        device_id=device,
        device_id_type=MESH,
    )


def no_pause(count):
    pass


class Gather:
    def __init__(self, n_f, x_ref, out_ref, send, recv, core_send, core_recv, local_sem):
        self.f, self.c = lax.axis_index("fsdp"), lax.axis_index("core")
        self.n_f, self.x_ref, self.out_ref = n_f, x_ref, out_ref
        self.send, self.recv, self.core_send, self.core_recv = send, recv, core_send, core_recv
        self.bits, self.orders = bit_orders(n_f)
        self.part = x_ref.shape[0] // len(self.orders)
        self.started = []
        self.have = [[0] for _ in self.orders]
        self.own = lambda: pltpu.make_async_copy(x_ref, out_ref.at[self.slot(0, self.c)], local_sem)

    def slot(self, offset, core):
        return flip(self.f, offset, self.bits) * 2 + core

    def piece(self, turn, offset, core):
        return self.out_ref.at[self.slot(offset, core), pl.ds(turn * self.part, self.part)]

    def source(self, turn, offset):
        if offset:
            return self.piece(turn, offset, self.c)
        return self.x_ref.at[pl.ds(turn * self.part, self.part)]

    def link(self, turn, offset, bit):
        sem = turn * self.n_f + (offset ^ (1 << bit))
        return remote(
            self.source(turn, offset),
            self.piece(turn, offset, self.c),
            self.send.at[sem],
            self.recv.at[sem],
            {"fsdp": flip(self.f, 1 << bit, self.bits)},
        )

    def arrival(self, turn, offset):
        sem = turn * self.n_f + offset
        where = self.piece(turn, offset, self.c)
        return remote(where, where, self.send.at[sem], self.recv.at[sem], {"core": 1 - self.c})

    def across(self, turn, offset):
        sem = turn * self.n_f + offset
        return remote(
            self.source(turn, offset),
            self.piece(turn, offset, self.c),
            self.core_send.at[sem],
            self.core_recv.at[sem],
            {"core": 1 - self.c},
        )

    def crossing(self, turn, offset):
        sem = turn * self.n_f + offset
        where = self.piece(turn, offset, 1 - self.c)
        return remote(
            where, where, self.core_send.at[sem], self.core_recv.at[sem], {"core": 1 - self.c}
        )

    def go(self, copy):
        copy.start()
        self.started.append(copy)

    def start(self):
        for step in range(self.bits):
            for turn, order in enumerate(self.orders):
                self.go(self.link(turn, 0, order[step]))
        for turn in range(len(self.orders)):
            self.go(self.across(turn, 0))
        self.own().start()

    def relay(self, pause):
        for step in range(self.bits):
            for at in range(1 << step):
                for turn, order in enumerate(self.orders):
                    offset = self.have[turn][at] ^ (1 << order[step])
                    self.arrival(turn, offset).wait_recv()
                    for later in range(step + 1, self.bits):
                        self.go(self.link(turn, offset, order[later]))
                    self.go(self.across(turn, offset))
                    self.have[turn].append(offset)
                    pause(1)

    def finish(self):
        for copy in self.started:
            copy.wait_send()
        for turn in range(len(self.orders)):
            for offset in self.have[turn]:
                self.crossing(turn, offset).wait_recv()
        self.own().wait()


def gather_stage(n_f, x_ref, out_ref, *rest):
    gather = Gather(n_f, x_ref, out_ref, *rest[:-1])
    gather.start()
    rest[-1](1)
    gather.relay(rest[-1])
    gather.finish()


def scatter_stage(
    n_f, part_ref, out_ref, acc, core_in, link_in, send, recv, core_send, core_recv, pause
):
    f, c = lax.axis_index("fsdp"), lax.axis_index("core")
    rows = out_ref.shape[0]
    bits, orders = bit_orders(n_f)
    part = rows // len(orders)
    started = []

    def go(copy):
        copy.start()
        started.append(copy)

    def held(offset, where):
        if acc is None:
            return part_ref.at[flip(f, offset, bits) * 2 + c, where]
        return acc.at[offset, where]

    def across(turn, offset):
        where = pl.ds(turn * part, part)
        sem = turn * n_f + offset
        return remote(
            part_ref.at[flip(f, offset, bits) * 2 + 1 - c, where],
            core_in.at[offset, where],
            core_send.at[sem],
            core_recv.at[sem],
            {"core": 1 - c},
        )

    def link(turn, offset, bit):
        where = pl.ds(turn * part, part)
        sem = turn * n_f + offset
        return remote(
            held(offset, where),
            link_in.at[offset, where],
            send.at[sem],
            recv.at[sem],
            {"fsdp": flip(f, 1 << bit, bits)},
        )

    plan = [[] for _ in range(bits)] + [[(turn, 0) for turn in range(len(orders))]]
    for step in range(bits):
        for offset in range(n_f):
            for turn, order in enumerate(orders):
                if offset >> order[step] & 1 and not any(offset >> b & 1 for b in order[:step]):
                    plan[step].append((turn, offset))
    for todo in plan:
        for turn, offset in todo:
            go(across(turn, offset))
    for step, todo in enumerate(plan):
        pause(1)
        for turn, offset in todo:
            where = pl.ds(turn * part, part)
            across(turn, offset).wait_recv()
            total = part_ref[flip(f, offset, bits) * 2 + c, where].astype(F32)
            total = total + core_in[offset, where].astype(F32)
            for bit in orders[turn][:step]:
                link(turn, offset | (1 << bit), bit).wait_recv()
                total = total + link_in[offset | (1 << bit), where].astype(F32)
            if offset:
                held(offset, where)[...] = total.astype(BF16)
                go(link(turn, offset, orders[turn][step]))
                if offset == n_f - 1:
                    pause(1)
            else:
                out_ref[where] = total
    for copy in started:
        copy.wait_send()


def exchange_stage(n_f, n_z, plane_in, column_in, plane_out, column_out, sems, whole, pause):
    f, z, c = lax.axis_index("fsdp"), lax.axis_index("zz"), lax.axis_index("core")
    peers = plane_peers(n_f, f, c)
    others = column_peers(n_z, z, c) if column_in is not None else []
    copies = []
    local = []
    if column_in is not None:
        mine = z * 2 + c
        for sem, device in others:
            to = device["zz"] * 2 + device["core"]
            source = column_in if whole else column_in.at[to]
            copies.append(
                remote(source, column_out.at[mine], sems[2].at[sem], sems[3].at[sem], device)
            )
        source = column_in if whole else column_in.at[mine]
        local.append(pltpu.make_async_copy(source, column_out.at[mine], sems[5]))
    mine = f * 2 + c
    for sem, device in peers:
        to = device["fsdp"] * 2 + device["core"]
        copies.append(
            remote(plane_in.at[to], plane_out.at[mine], sems[0].at[sem], sems[1].at[sem], device)
        )
    local.append(pltpu.make_async_copy(plane_in.at[mine], plane_out.at[mine], sems[4]))
    for copy in copies + local:
        copy.start()
    pause(1)
    for copy in copies:
        copy.wait_send()
    for sem, device in peers:
        frm = device["fsdp"] * 2 + device["core"]
        remote(
            plane_out.at[frm], plane_out.at[frm], sems[0].at[sem], sems[1].at[sem], device
        ).wait_recv()
    if column_in is not None:
        for offset in range(n_z):
            for other in range(2):
                if offset or other:
                    frm = ((z + n_z - offset) % n_z) * 2 + c + other * (1 - 2 * c)
                    sem = offset * 2 + other
                    remote(
                        column_out.at[frm],
                        column_out.at[frm],
                        sems[2].at[sem],
                        sems[3].at[sem],
                        {"core": 1 - c},
                    ).wait_recv()
    for copy in local:
        copy.wait()


class Line:
    def __init__(self, n_z, kinds, sems):
        self.n_z, self.kinds = n_z, kinds
        self.base = [sum(kind[0] for kind in kinds[:at]) for at in range(len(kinds))]
        self.total = sum(kind[0] for kind in kinds)
        self.red_send, self.red_recv, self.fin_send, self.fin_recv, self.own_sem = sems
        self.place, self.turn = lax.axis_index("zz"), 1 - 2 * lax.axis_index("core")
        self.z = self.place + lax.axis_index("core") * (n_z - 1 - 2 * self.place)
        self.leaf, self.root = self.z == n_z - 1, self.z == 0
        self.inner = (self.z > 0) & (self.z < n_z - 1)
        self.done = 0

    def toward(self, kind, k, source):
        sem = self.base[kind] + k
        return remote(
            source,
            self.kinds[kind][1](k)[1],
            self.red_send.at[sem],
            self.red_recv.at[sem],
            {"zz": jnp.clip(self.place - self.turn, 0, self.n_z - 1)},
        )

    def outward(self, kind, k, source):
        sem = self.base[kind] + k
        return remote(
            source,
            self.kinds[kind][1](k)[2],
            self.fin_send.at[sem],
            self.fin_recv.at[sem],
            {"zz": jnp.clip(self.place + self.turn, 0, self.n_z - 1)},
        )

    def keep(self, kind, k):
        _, landing, final = self.kinds[kind][1](k)
        return pltpu.make_async_copy(landing, final, self.own_sem.at[self.base[kind] + k])

    def reduce(self, kind, k):
        own, landing, _ = self.kinds[kind][1](k)

        @pl.when(self.leaf)
        def _():
            self.toward(kind, k, own).start()

        @pl.when(jnp.logical_not(self.leaf))
        def _():
            self.toward(kind, k, own).wait_recv()
            height = min(16, own.shape[0])

            @pl.loop(0, own.shape[0] // height)
            def _(at):
                where = pl.ds(pl.multiple_of(at * height, height), height)
                landing[where] = (own[where].astype(F32) + landing[where].astype(F32)).astype(BF16)

        @pl.when(self.inner)
        def _():
            self.toward(kind, k, landing).start()

        @pl.when(self.root)
        def _():
            self.outward(kind, k, landing).start()
            self.keep(kind, k).start()

    def spread(self, kind, k):
        final = self.kinds[kind][1](k)[2]

        @pl.when(self.root)
        def _():
            self.keep(kind, k).wait()

        @pl.when(jnp.logical_not(self.root))
        def _():
            self.outward(kind, k, final).wait_recv()

        @pl.when(self.inner)
        def _():
            self.outward(kind, k, final).start()

        self.kinds[kind][2](k)

    def each(self, slope, back, action, at, count):
        low = [self.done - back - slope * z for z in range(self.n_z)]
        here = self.done + at - back - slope * self.z
        for kind, (chunks, _, _) in enumerate(self.kinds):
            base = self.base[kind]
            if base <= min(low) and max(low) + count <= base + chunks:
                action(kind, here - base)
            elif any(k < base + chunks and base < k + count for k in low):

                @pl.when((here >= base) & (here < base + chunks))
                def _():
                    action(kind, here - base)

    def run(self, count):
        count = min(count, self.left())
        if count <= 0:
            return

        @pl.loop(0, count)
        def _(at):
            first = STAGGER * (self.n_z - 1)
            self.each(-STAGGER, first, self.reduce, at, count)
            self.each(BEHIND, first + 1, self.spread, at, count)

        self.done += count

    def lag(self, z):
        return STAGGER * (self.n_z - 1) + 1 + BEHIND * z

    def left(self):
        return self.total + self.lag(self.n_z - 1) - self.done

    def finish(self):
        for kind, (count, refs, _) in enumerate(self.kinds):

            @pl.loop(0, count)
            def _(k):
                @pl.when(jnp.logical_not(self.root))
                def _():
                    self.toward(kind, k, refs(k)[0]).wait_send()

                @pl.when(jnp.logical_not(self.leaf))
                def _():
                    self.outward(kind, k, refs(k)[2]).wait_send()


def vector_stage(n_f, n_z, in_ref, out_ref, plane_in, part, line_in, sems, pause):
    f, z, c = lax.axis_index("fsdp"), lax.axis_index("zz"), lax.axis_index("core")
    send, recv, line_send, line_recv, local = sems
    peers = plane_peers(n_f, f, c)
    others = [(offset, {"zz": (z + offset) % n_z}) for offset in range(1, n_z)]
    mine = f * 2 + c
    copies = [
        remote(in_ref.at[device["fsdp"]], plane_in.at[mine], send.at[sem], recv.at[sem], device)
        for sem, device in peers
    ]
    for copy in copies:
        copy.start()
    own = pltpu.make_async_copy(in_ref.at[f], plane_in.at[mine], local)
    own.start()
    own.wait()
    pause(1)
    for sem, device in peers:
        where = plane_in.at[device["fsdp"] * 2 + device["core"]]
        remote(where, where, send.at[sem], recv.at[sem], device).wait_recv()
    total = plane_in[0]
    for at in range(1, n_f * 2):
        total = total + plane_in[at]
    part[...] = total
    line = [
        remote(part, line_in.at[z], line_send.at[sem], line_recv.at[sem], device)
        for sem, device in others
    ]
    for copy in line:
        copy.start()
    pause(1)
    for offset in range(1, n_z):
        where = line_in.at[(z + n_z - offset) % n_z]
        remote(
            where, where, line_send.at[offset], line_recv.at[offset], {"core": 1 - c}
        ).wait_recv()
    line_in[z] = total
    total = line_in[0]
    for at in range(1, n_z):
        total = total + line_in[at]
    out_ref[...] = total
    for copy in copies + line:
        copy.wait_send()


def heads_side_by_side(block, head):
    count = block.shape[1] // head
    return jnp.concatenate([block[:, at * head : (at + 1) * head] for at in range(count)], axis=0)


def heads_apart(block, count):
    rows = block.shape[0] // count
    return jnp.concatenate([block[at * rows : (at + 1) * rows] for at in range(count)], axis=1)


def attend_block(head, query_in, kv_ref, mask_ref):
    scale = 1.0 / math.sqrt(head)
    query = heads_side_by_side(query_in, head)
    count = query_in.shape[1] // head
    keys, values = kv_ref[:, :head], kv_ref[:, head:]
    mask = jnp.concatenate([mask_ref[...]] * count, axis=1)
    scores = dot_nt(keys, query) * scale + mask
    peak = jnp.max(scores, axis=0, keepdims=True)
    weights = jnp.exp(scores - peak)
    total = jnp.sum(weights, axis=0, keepdims=True)
    probs = (weights / total).astype(BF16)
    return heads_apart(dot_tn(probs, values).astype(BF16), count), peak + jnp.log(total)


def attend_back_block(head, query_in, grad_in, kv_ref, mask_ref, lse):
    scale = 1.0 / math.sqrt(head)
    query = heads_side_by_side(query_in, head)
    grad = heads_side_by_side(grad_in, head)
    count = query_in.shape[1] // head
    keys, values = kv_ref[:, :head], kv_ref[:, head:]
    mask = jnp.concatenate([mask_ref[...]] * count, axis=1)
    scores = dot_nt(keys, query) * scale + mask
    probs = jnp.exp(scores - lse)
    d_probs = dot_nt(values, grad)
    delta = jnp.sum(probs * d_probs, axis=0, keepdims=True)
    d_scores = (probs * (d_probs - delta)).astype(BF16)
    d_query = heads_apart((dot_tn(d_scores, keys) * scale).astype(BF16), count)
    d_keys = dot(d_scores, query) * scale
    d_values = dot(probs.astype(BF16), grad)
    return d_query, d_keys, d_values


class Box:
    pass


def rows_of(at, height=16):
    return pl.ds(pl.multiple_of(at * height, height), height)


GAIN_ONE, SHIFT_ONE, BIAS_OUT, GAIN_TWO, SHIFT_TWO, BIAS_DOWN, BIAS_QUERY = range(7)


def norm_tiles(load, gain, shift, normal_ref, inverse_ref, normed_ref):
    @pl.loop(0, normal_ref.shape[0] // 16)
    def _(at):
        where = rows_of(at)
        values = load(where)
        row_mean = jnp.mean(values, axis=-1, keepdims=True)
        centered = values - row_mean
        variance = jnp.mean(centered * centered, axis=-1, keepdims=True)
        inverse = lax.rsqrt(variance + EPSILON)
        normal = centered * inverse
        normal_ref[where] = normal
        inverse_ref[where] = inverse
        normed_ref[where] = (normal * gain + shift).astype(BF16)


def forward_body(n_f, n_z, head, names, *refs):
    r = Box()
    for name, ref in zip(names, refs, strict=True):
        setattr(r, name, ref)
    f, z, c = lax.axis_index("fsdp"), lax.axis_index("zz"), lax.axis_index("core")
    bits = n_f.bit_length() - 1
    n_p = n_f * 2
    rows, width = r.tokens.shape
    own_q = r.w_q.shape[2]
    own_h = r.w_up.shape[2]
    seg = width // n_f
    far = [flip(f, offset, bits) for offset in range(n_f)]
    r.small_all[f] = r.small[...]
    r.small_f32[...] = r.small[...].astype(F32)
    greet([device for _, device in plane_peers(n_f, f, c) + column_peers(n_z, z, c)])

    def columns(ref, to, size, where=slice(None)):
        return ref.at[where, pl.ds(pl.multiple_of((to * 2 + c) * size, LANES), size)]

    half = seg // 2
    quarter = seg // n_z

    def kv_piece(source, core):
        return r.w_kv.at[source, pl.ds(pl.multiple_of(core * half, 16), half)]

    def up_piece(source, plane):
        return r.w_up.at[source, pl.ds(pl.multiple_of(plane * quarter, 16), quarter)]

    smalls, early, kv_cross, up_links, up_lines = [], [], [], [], []
    for offset in range(1, n_f):
        device = {"fsdp": far[offset]}
        smalls.append(
            remote(r.small, r.small_all.at[f], r.small_sem.at[0, offset], r.small_sem.at[1, offset], device)
        )
        early.append(
            remote(
                columns(r.qkv_weight, far[offset], own_q),
                r.w_q.at[f],
                r.q_sem.at[0, offset],
                r.q_sem.at[1, offset],
                device,
            )
        )
        early.append(
            remote(
                r.qkv_weight.at[pl.ds(pl.multiple_of(c * half, 16), half), pl.ds(width, 2 * head)],
                kv_piece(f, c),
                r.kv_sem.at[0, offset],
                r.kv_sem.at[1, offset],
                device,
            )
        )
        where = pl.ds(pl.multiple_of(z * quarter, 16), quarter)
        up_links.append(
            remote(
                columns(r.up_weight, far[offset], own_h, where),
                up_piece(f, z),
                r.up_sem.at[0, offset],
                r.up_sem.at[1, offset],
                device,
            )
        )
    locals_ = [
        pltpu.make_async_copy(columns(r.qkv_weight, f, own_q), r.w_q.at[f], r.local_sem.at[0]),
        pltpu.make_async_copy(
            r.qkv_weight.at[:, pl.ds(width, 2 * head)], r.w_kv.at[f], r.local_sem.at[1]
        ),
        pltpu.make_async_copy(columns(r.up_weight, f, own_h), r.up_own, r.local_sem.at[2]),
        pltpu.make_async_copy(
            r.out_weight.at[pl.ds(pl.multiple_of(c * own_q, 16), own_q)], r.w_out, r.local_sem.at[11]
        ),
    ]
    for copy in smalls + early + locals_:
        copy.start()

    for offset in range(1, n_f):
        where = r.small_all.at[far[offset]]
        remote(
            where, where, r.small_sem.at[0, offset], r.small_sem.at[1, offset], {"core": 1 - c}
        ).wait_recv()
    bias_v = jnp.zeros((8, LANES), F32)
    for o in range(n_f):
        block = r.small_all[o].astype(F32)
        r.vecs[:, o * seg : (o + 1) * seg] = block
        shift = o * (head // n_f)
        block = block[:, :LANES]
        bias_v = bias_v + (pltpu.roll(block, shift, axis=1) if shift else block)
    norm_tiles(
        lambda where: r.tokens[where].astype(F32),
        r.vecs[GAIN_ONE : GAIN_ONE + 1],
        r.vecs[SHIFT_ONE : SHIFT_ONE + 1],
        r.normal_one,
        r.inverse_one,
        r.normed,
    )
    bias_q = r.small_f32[BIAS_QUERY : BIAS_QUERY + 1, pl.ds(pl.multiple_of(c * own_q, LANES), own_q)]
    normed = Gather(
        n_f, r.normed, r.normed_all, *(r.gather_one.at[at] for at in range(4)), r.local_sem.at[3]
    )
    normed.start()
    for offset in range(1, n_f):
        where = kv_piece(far[offset], c)
        remote(
            where, where, r.kv_sem.at[0, offset], r.kv_sem.at[1, offset], {"core": 1 - c}
        ).wait_recv()
        kv_cross.append(
            remote(where, where, r.kv_sem.at[2, offset], r.kv_sem.at[3, offset], {"core": 1 - c})
        )
        kv_cross[-1].start()
    locals_[2].wait()
    up_home = pltpu.make_async_copy(r.up_own, r.w_up.at[f], r.local_sem.at[4])
    up_home.start()
    normed.relay(no_pause)
    for copy in up_links:
        copy.start()
    span = r.kv.shape[0]
    first = jnp.maximum((z * 2 + c + 1) - span // rows, 0)
    key_pos = first * rows + lax.broadcasted_iota(jnp.int32, (span, rows), 0)
    row_pos = (z * 2 + c) * rows + lax.broadcasted_iota(jnp.int32, (span, rows), 1)
    same = jnp.zeros((span, rows), jnp.int32)
    doc_end = jnp.zeros((1, 1), jnp.int32)
    for at in range(r.lengths.shape[1]):
        doc_end = doc_end + r.lengths[:, at : at + 1]
        edge = (key_pos >= doc_end) != (row_pos >= doc_end)
        same = same + edge.astype(jnp.int32)
    r.mask[...] = jnp.where((same == 0) & (row_pos >= key_pos), 0.0, -1e30).astype(F32)
    for offset in range(1, n_f):
        where = kv_piece(far[offset], 1 - c)
        remote(
            where, where, r.kv_sem.at[2, offset], r.kv_sem.at[3, offset], {"core": 1 - c}
        ).wait_recv()
        where = r.w_q.at[far[offset]]
        remote(
            where, where, r.q_sem.at[0, offset], r.q_sem.at[1, offset], {"core": 1 - c}
        ).wait_recv()
    locals_[0].wait()
    locals_[1].wait()
    keyval = dot(r.normed[...], r.w_kv[...].reshape(width, 2 * head))
    r.keyval[:, :head] = keyval[:, :head].astype(BF16)
    r.keyval[:, head:] = (keyval[:, head:] + bias_v[7:8, :head]).astype(BF16)
    normed.finish()
    keep = pltpu.make_async_copy(r.normed_all, r.normed_pl, r.local_sem.at[5])
    keep.start()

    @pl.loop(0, n_p)
    def _(p):
        r.query_send[p] = (
            dot(r.normed_all[p], r.w_q[...].reshape(width, own_q)) + bias_q
        ).astype(BF16)

    grads = Gather(
        n_f, r.grad_out, r.grad_pl, *(r.gather_two.at[at] for at in range(4)), r.local_sem.at[6]
    )

    def fill(count):
        for offset in range(1, n_f):
            where = up_piece(far[offset], z)
            remote(
                where, where, r.up_sem.at[0, offset], r.up_sem.at[1, offset], {"core": 1 - c}
            ).wait_recv()
            for away in range(1, n_z):
                sem = away * n_f + offset
                up_lines.append(
                    remote(
                        where, where, r.line_sem.at[0, sem], r.line_sem.at[1, sem], {"zz": (z + away) % n_z}
                    )
                )
                up_lines[-1].start()
        grads.start()

    exchange_stage(
        n_f,
        n_z,
        r.query_send,
        r.keyval,
        r.query,
        r.kv_all,
        [
            r.swap_one.at[0],
            r.swap_one.at[1],
            r.column_sem.at[0],
            r.column_sem.at[1],
            r.local_sem.at[7],
            r.local_sem.at[8],
        ],
        True,
        fill,
    )
    for at in range(span // rows):
        r.kv[at * rows : (at + 1) * rows] = r.kv_all[first + at]

    @pl.loop(0, n_p)
    def _(p):
        mixed, lse = attend_block(head, r.query[p], r.kv, r.mask)
        r.mixed_send[p] = mixed
        r.lse[p] = lse

    exchange_stage(
        n_f,
        n_z,
        r.mixed_send,
        None,
        r.mixed_own,
        None,
        [r.swap_two.at[0], r.swap_two.at[1], None, None, r.local_sem.at[9], None],
        False,
        lambda count: grads.relay(no_pause),
    )
    tile = min(512, width)
    locals_[3].wait()

    @pl.loop(0, n_p)
    def _(p):
        for n in range(width // tile):
            cols = pl.ds(n * tile, tile)
            r.part[p, :, cols] = dot(r.mixed_own[p], r.w_out[:, cols]).astype(BF16)

    scatter_stage(
        n_f, r.part, r.branch, None, r.core_in, r.link_in, *(r.scatter_one.at[at] for at in range(4)), no_pause
    )

    def second(where):
        values = (
            r.tokens[where].astype(F32) + r.branch[where] + r.vecs[BIAS_OUT : BIAS_OUT + 1]
        )
        r.residual[where] = values
        return values

    norm_tiles(
        second,
        r.vecs[GAIN_TWO : GAIN_TWO + 1],
        r.vecs[SHIFT_TWO : SHIFT_TWO + 1],
        r.normal_two,
        r.inverse_two,
        r.normed_mlp,
    )
    last = Gather(
        n_f, r.normed_mlp, r.normed_mlp_pl, *(r.gather_three.at[at] for at in range(4)), r.local_sem.at[10]
    )
    last.start()
    grads.finish()
    last.relay(no_pause)
    for copy in smalls + early + kv_cross + up_links + up_lines:
        copy.wait_send()
    for offset in range(1, n_f):
        for away in range(1, n_z):
            where = up_piece(far[offset], (z + n_z - away) % n_z)
            sem = away * n_f + offset
            remote(
                where, where, r.line_sem.at[0, sem], r.line_sem.at[1, sem], {"core": 1 - c}
            ).wait_recv()
    up_home.wait()
    keep.wait()
    last.finish()


def forward(inputs, n_f, n_z, head, own_h, ident):
    rows, width = inputs["tokens"].shape
    n_p, n_s = n_f * 2, n_z * 2
    own_q = width // n_p
    seg = width // n_f
    count = len(bit_orders(n_f)[1]) * n_f
    stream = n_s * rows
    span = min(stream, stream // 2 + rows)
    in_hbm = ("qkv_weight", "up_weight", "out_weight")
    plane = (n_p, rows, width)
    blocks = (n_p, rows, own_q)
    outs = {
        "normed_pl": (plane, BF16, ANYWHERE),
        "normal_one": ((rows, width), F32, ON_CHIP),
        "inverse_one": ((rows, 1), F32, ON_CHIP),
        "query": (blocks, BF16, ON_CHIP),
        "kv": ((span, 2 * head), BF16, ON_CHIP),
        "lse": ((n_p, 1, own_q // head * rows), F32, ON_CHIP),
        "mixed_own": (blocks, BF16, ON_CHIP),
        "residual": ((rows, width), F32, ON_CHIP),
        "normal_two": ((rows, width), F32, ON_CHIP),
        "inverse_two": ((rows, 1), F32, ON_CHIP),
        "normed_mlp_pl": (plane, BF16, ANYWHERE),
        "grad_pl": (plane, BF16, ANYWHERE),
        "w_q": ((n_f, seg, own_q), BF16, ON_CHIP),
        "w_kv": ((n_f, seg, 2 * head), BF16, ON_CHIP),
        "w_up": ((n_f, seg, own_h), BF16, ANYWHERE),
        "vecs": ((8, width), F32, ON_CHIP),
        "mask": ((span, rows), F32, ON_CHIP),
        "w_out": ((own_q, width), BF16, ON_CHIP),
    }
    scratch = {
        "small_all": VMEM((n_f,) + inputs["small"].shape, BF16),
        "small_f32": VMEM(inputs["small"].shape, F32),

        "up_own": VMEM((seg, own_h), BF16),
        "normed": VMEM((rows, width), BF16),
        "normed_all": VMEM(plane, BF16),
        "keyval": VMEM((rows, 2 * head), BF16),
        "query_send": VMEM(blocks, BF16),
        "kv_all": VMEM((n_s, rows, 2 * head), BF16),
        "mixed_send": VMEM(blocks, BF16),
        "part": VMEM(plane, BF16),
        "core_in": VMEM((n_f, rows, width), BF16),
        "link_in": VMEM((n_f, rows, width), BF16),
        "branch": VMEM((rows, width), F32),
        "normed_mlp": VMEM((rows, width), BF16),
        "local_sem": DMA((12,)),
        "small_sem": DMA((2, n_f)),
        "q_sem": DMA((2, n_f)),
        "kv_sem": DMA((4, n_f)),
        "up_sem": DMA((2, n_f)),
        "line_sem": DMA((2, n_z * n_f)),
        "gather_one": DMA((4, count)),
        "gather_two": DMA((4, count)),
        "gather_three": DMA((4, count)),
        "scatter_one": DMA((4, count)),
        "swap_one": DMA((2, n_p)),
        "swap_two": DMA((2, n_p)),
        "column_sem": DMA((2, n_s)),
    }
    names = list(inputs) + list(outs) + list(scratch)
    result = pl.pallas_call(
        functools.partial(forward_body, n_f, n_z, head, names),
        out_shape=[jax.ShapeDtypeStruct(shape, kind) for shape, kind, _ in outs.values()],
        in_specs=[ANYWHERE if name in in_hbm else ON_CHIP for name in inputs],
        out_specs=[place for _, _, place in outs.values()],
        scratch_shapes=list(scratch.values()),
        compiler_params=pltpu.CompilerParams(
            collective_id=ident, has_side_effects=True, vmem_limit_bytes=56 << 20
        ),
        name="forward",
    )(*inputs.values())
    return dict(zip(outs, result))


PACE = 2
STAGGER = 3
BEHIND = 3


def norm_back_tiles(grad_ref, extra_ref, normal_ref, inverse_ref, gain_ref, base_ref, sums, store):
    rows = normal_ref.shape[0]

    @pl.loop(0, rows // 16)
    def _(at):
        where = rows_of(at)
        grad = grad_ref[where]
        if extra_ref is not None:
            grad = grad + extra_ref[where]
        normal = normal_ref[where].astype(F32)
        scaled = grad * gain_ref[...]
        first = jnp.mean(scaled, axis=-1, keepdims=True)
        second = jnp.mean(scaled * normal, axis=-1, keepdims=True)
        base = base_ref[where].astype(F32)
        result = base + inverse_ref[where] * (
            scaled - first - normal * second
        )
        store(where, result)
        sums[0:1] += jnp.sum(grad * normal, axis=0, keepdims=True)
        sums[1:2] += jnp.sum(grad, axis=0, keepdims=True)
        sums[2:3] += jnp.sum(result.astype(BF16).astype(F32), axis=0, keepdims=True)
        sums[3:4] += jnp.sum(base, axis=0, keepdims=True)


def backward_body(n_f, n_z, head, names, *refs):
    r = Box()
    for name, ref in zip(names, refs, strict=True):
        setattr(r, name, ref)
    f, z, c = lax.axis_index("fsdp"), lax.axis_index("zz"), lax.axis_index("core")
    bits = n_f.bit_length() - 1
    n_p = n_f * 2
    me = f * 2 + c
    rows, width = r.grad_out.shape
    own_q = r.w_out.shape[0]

    loads = {}
    for at, (name, source, target) in enumerate(
        (
            ("part", r.e_part, r.part),
            ("down", r.g_down_in, r.g_down),
            ("up", r.g_up_in, r.g_up),
        )
    ):
        loads[name] = pltpu.make_async_copy(source, target, r.load_sem.at[at])
        loads[name].start()
    greet([device for _, device in plane_peers(n_f, f, c) + column_peers(n_z, z, c)])

    home = {"down": r.h_down, "out": r.h_out, "kv": r.h_kv, "up": r.h_up, "q": r.h_q}

    def plain(own, landing, final):
        return lambda k: (own.at[k], landing.at[k], final.at[k])

    def turned(k):
        k = owner_turn(k)
        return r.g_q.at[k], r.land_q.at[k], r.fin_q.at[k]

    def owner_turn(k):
        per = r.g_q.shape[0] // n_f
        offset, turn = k % n_f, k // n_f
        owner = f
        for bit in range(bits):
            crossed = owner + (1 << bit) * (1 - 2 * ((owner // (1 << bit)) % 2))
            flag = (offset // (1 << bit)) % 2
            owner = owner + flag * (crossed - owner)
        return owner * per + turn

    starts = {"down": 0, "out": r.g_down.shape[0], "kv": r.g_down.shape[0] + r.g_out.shape[0]}

    def swap(kind, k, side):
        sem = starts[kind] + k
        where = home[kind].at[side, k]
        return remote(where, where, r.swap_send.at[sem], r.swap_recv.at[sem], {"core": 1 - c})

    def mate(kind):
        return lambda k: swap(kind, k, c).start()

    line = Line(
        n_z,
        [
            (r.g_up.shape[0], plain(r.g_up, r.land_up, r.fin_up), lambda k: None),
            (r.g_down.shape[0], plain(r.g_down, r.land_down, r.h_down.at[c]), mate("down")),
            (r.g_out.shape[0], plain(r.g_out, r.land_out, r.h_out.at[c]), mate("out")),
            (r.g_q.shape[0], turned, lambda k: deliver_split("q", owner_turn(k))),
            (r.g_kv.shape[0], plain(r.g_kv, r.land_kv, r.h_kv.at[c]), mate("kv")),
        ],
        (r.red_send, r.red_recv, r.fin_send, r.fin_recv, r.keep_sem),
    )

    def block(kind, turn, source):
        target = home[kind]
        height, size = finals[kind].shape[1:]
        cols = pl.ds(pl.multiple_of(source * size, LANES), size)
        return target.at[pl.ds(pl.multiple_of(turn * height, height), height), cols]

    finals = {"up": r.fin_up, "q": r.fin_q}
    home_sem = {
        "up": (r.up_send, r.up_mate, r.up_recv, r.up_relay, r.up_cross),
        "q": (r.q_send, r.q_mate, r.q_recv, r.q_relay, r.q_cross),
    }

    def turns(kind):
        return finals[kind].shape[0] // n_f

    def moves(kind, k):
        send, mate, recv, _, cross = home_sem[kind]
        owner, turn = k // turns(kind), k % turns(kind)
        where = block(kind, turn, me)
        sem = turn * n_f + f
        source = finals[kind].at[k]
        return (
            f == owner,
            lambda: pltpu.make_async_copy(source, where, send.at[k]),
            lambda: remote(source, where, mate.at[k], cross.at[sem], {"core": 1 - c}),
            lambda: remote(source, where, send.at[k], recv.at[sem], {"fsdp": owner}),
        )

    def deliver_split(kind, k):
        here, own, other, away = moves(kind, k)

        @pl.when(here)
        def _():
            own().start()
            other().start()

        @pl.when(jnp.logical_not(here))
        def _():
            away().start()

    def relay(kind, turn, offset):
        _, _, recv, send, cross = home_sem[kind]
        source = flip(f, offset, bits)
        where = block(kind, turn, source * 2 + c)
        sem = turn * n_f + source
        return (
            lambda: remote(where, where, send.at[sem], recv.at[sem], {"core": 1 - c}),
            lambda: remote(where, where, send.at[sem], cross.at[sem], {"core": 1 - c}),
        )

    def relay_all(kind):
        @pl.loop(0, turns(kind))
        def _(turn):
            for offset in range(1, n_f):
                arrival, onward = relay(kind, turn, offset)
                arrival().wait_recv()
                onward().start()

    def delivered():
        for kind in starts:

            @pl.loop(0, home[kind].shape[1])
            def _(k):
                swap(kind, k, c).wait_send()
                swap(kind, k, 1 - c).wait_recv()

        for kind in ("up", "q"):

            @pl.loop(0, finals[kind].shape[0])
            def _(k):
                here, own, other, away = moves(kind, k)

                @pl.when(here)
                def _():
                    own().wait()
                    other().wait_send()

                @pl.when(jnp.logical_not(here))
                def _():
                    away().wait_send()

            @pl.loop(0, turns(kind))
            def _(turn):
                for offset in range(n_f):
                    if offset:
                        relay(kind, turn, offset)[1]().wait_send()
                    source = flip(f, offset, bits)
                    where = block(kind, turn, source * 2 + 1 - c)
                    cross = home_sem[kind][4].at[turn * n_f + source]
                    remote(where, where, r.swap_send.at[0], cross, {"core": 1 - c}).wait_recv()

    ready = [False]
    limit = [r.g_down.shape[0] + r.g_up.shape[0]]

    def pause(count):
        if not ready[0]:
            loads["down"].wait()
            loads["up"].wait()
            ready[0] = True
        line.run(min(count * PACE, limit[0] - line.done))

    for ref in (r.sums_two, r.sums_one):
        ref[...] = jnp.zeros_like(ref)
    loads["part"].wait()
    scatter_stage(
        n_f, r.part, r.e_sum, None, r.core_in, r.link_in, *(r.scatter_one.at[at] for at in range(4)), pause
    )

    def store_two(where, result):
        r.d_residual[where] = result
        r.d_branch[where] = result.astype(BF16)

    norm_back_tiles(
        r.e_sum, None, r.normal_two, r.inverse_two, r.gain_two, r.grad_out, r.sums_two, store_two
    )
    loads["normed"] = pltpu.make_async_copy(r.normed_in, r.part, r.load_sem.at[3])
    loads["normed"].start()
    gather_stage(
        n_f, r.d_branch, r.branch_pl, *(r.gather_one.at[at] for at in range(4)), r.local_sem.at[0], pause
    )

    @pl.loop(0, n_p)
    def _(p):
        r.mixed_send[p] = dot_nt(r.branch_pl[p], r.w_out[...]).astype(BF16)

    exchange_stage(
        n_f,
        n_z,
        r.mixed_send,
        None,
        r.d_mixed,
        None,
        [r.swap_one.at[0], r.swap_one.at[1], None, None, r.local_sem.at[1], None],
        False,
        pause,
    )
    tile = min(512, width)
    high = r.g_out.shape[1]
    for j in range(own_q // LANES):
        for n in range(width // tile):
            cols = pl.ds(n * tile, tile)
            result = dot_tn(
                r.mixed_own[:, :, j * LANES : (j + 1) * LANES].reshape(n_p * rows, LANES),
                r.branch_pl[:, :, cols].reshape(n_p * rows, tile),
            ).astype(BF16)
            for k in range(LANES // high):
                r.g_out[j * (LANES // high) + k, :, cols] = result[k * high : (k + 1) * high]
    limit[0] += r.g_out.shape[0]

    r.d_kv_span[...] = jnp.zeros_like(r.d_kv_span)
    step = max(1, n_p // 2)
    for first in range(0, n_p, step):

        @pl.loop(first, first + step)
        def _(p):
            d_query, d_keys, d_values = attend_back_block(
                head, r.query[p], r.d_mixed[p], r.kv, r.mask, r.lse[p]
            )
            r.dq_send[p] = d_query
            r.d_kv_span[:, :head] += d_keys
            r.d_kv_span[:, head:] += d_values

        pause(2)
    span = r.d_kv_span.shape[0]
    stream = n_z * 2 * rows
    first = jnp.maximum((z * 2 + c + 1) * rows - span, 0)
    r.dkv_send[...] = jnp.zeros_like(r.dkv_send)

    @pl.loop(0, span // rows)
    def _(at):
        block_at = (jnp.maximum((z * 2 + c + 1) * rows - span, 0)) // rows + at
        r.dkv_send[block_at] = r.d_kv_span[pl.ds(pl.multiple_of(at * rows, rows), rows)].astype(BF16)

    exchange_stage(
        n_f,
        n_z,
        r.dq_send,
        r.dkv_send,
        r.dq_own,
        r.dkv_recv,
        [
            r.swap_two.at[0],
            r.swap_two.at[1],
            r.column_sem.at[0],
            r.column_sem.at[1],
            r.local_sem.at[2],
            r.local_sem.at[3],
        ],
        False,
        pause,
    )
    total = r.dkv_recv[0].astype(F32)
    for s in range(1, n_z * 2):
        total = total + r.dkv_recv[s].astype(F32)
    r.d_kv[...] = total.astype(BF16)

    @pl.loop(0, n_p)
    def _(p):
        for n in range(width // tile):
            cols = pl.ds(n * tile, tile)
            r.branch_pl[p, :, cols] = dot_nt(r.dq_own[p], r.w_q[cols]).astype(BF16)

    scatter_stage(
        n_f, r.branch_pl, r.e_sum, None, r.core_in, r.link_in, *(r.scatter_two.at[at] for at in range(4)), pause
    )
    for n in range(width // tile):
        cols = pl.ds(n * tile, tile)
        r.e_extra[:, cols] = dot_nt(r.d_kv[...], r.w_kv[cols])

    def store_one(where, result):
        r.grad_tokens[where] = result.astype(BF16)

    norm_back_tiles(
        r.e_sum, r.e_extra, r.normal_one, r.inverse_one, r.gain_one, r.d_residual, r.sums_one, store_one
    )
    gather_stage(
        n_f, r.d_kv, r.dkv_pl, *(r.gather_two.at[at] for at in range(4)), r.local_sem.at[4], pause
    )

    loads["normed"].wait()
    dq_all = r.dq_own[...].reshape(n_p * rows, own_q)
    tall = r.g_q.shape[1]

    @pl.loop(0, r.g_q.shape[0])
    def _(k):
        own = pl.ds(pl.multiple_of(k * tall, LANES), tall)
        r.g_q[k] = dot_tn(r.part[:, :, own].reshape(n_p * rows, tall), dq_all).astype(BF16)

    cols = pl.ds(pl.multiple_of(me * own_q, LANES), own_q)
    r.g_kv[0] = dot_tn(
        r.part[:, :, cols].reshape(n_p * rows, own_q), r.dkv_pl[...].reshape(n_p * rows, 2 * head)
    ).astype(BF16)
    loads["out"] = pltpu.make_async_copy(r.out_part, r.part, r.load_sem.at[4])
    loads["out"].start()
    limit[0] = line.total + line.lag(n_z - 1)
    pause(2)

    line.run(r.g_up.shape[0] + line.lag(n_z - 1) - line.done)

    @pl.loop(0, turns("up"))
    def _(turn):
        for offset in range(n_f):
            deliver_split("up", flip(f, (offset + 1) % n_f, bits) * turns("up") + turn)

    pause(6)

    seg = r.vec_in.shape[2]
    r.vec_in[...] = jnp.zeros_like(r.vec_in)
    up_rows = r.up_sum.shape[0]
    d_value = jnp.sum(r.d_kv[:, head:].astype(F32), axis=0, keepdims=True)
    for o in range(n_f):
        cols = slice(o * seg, (o + 1) * seg)
        r.vec_in[o, 0:1] = r.sums_one[0:1, cols]
        r.vec_in[o, 1:2] = r.sums_one[1:2, cols]
        r.vec_in[o, 3:4] = r.sums_two[2:3, cols]
        r.vec_in[o, 4:5] = r.sums_two[0:1, cols]
        r.vec_in[o, 5:6] = r.sums_two[1:2, cols]
        r.vec_in[o, 6:7] = r.sums_two[3:4, cols]
        r.vec_in[o, 7:8, :head] = d_value
        for side in range(2):
            part = jnp.sum(r.dq_send[o * 2 + side].astype(F32), axis=0, keepdims=True)
            r.vec_in[o, 2:3, side * own_q : (side + 1) * own_q] = part

        for side in range(2):

            @pl.when((f == o) & (c == side))
            def _():
                r.vec_in[o, 8 + side * up_rows : 8 + (side + 1) * up_rows] = r.up_sum[...]

    vector_stage(
        n_f,
        n_z,
        r.vec_in,
        r.vectors,
        r.vec_plane,
        r.vec_part,
        r.vec_line,
        [r.vec_sem.at[0], r.vec_sem.at[1], r.vec_line_sem.at[0], r.vec_line_sem.at[1], r.local_sem.at[5]],
        pause,
    )

    loads["out"].wait()
    scatter_stage(
        n_f, r.part, r.out_sum, None, r.core_in, r.link_in, *(r.scatter_three.at[at] for at in range(4)), pause
    )
    line.run(line.left() - 4 * PACE)
    relay_all("up")
    line.run(line.left())
    relay_all("q")
    line.finish()
    delivered()


def backward(inputs, n_f, n_z, head, own_h, ident):
    rows, width = inputs["grad_out"].shape
    n_p = n_f * 2
    n_s = n_z * 2
    own_q = width // n_p
    seg = width // n_f
    count = len(bit_orders(n_f)[1]) * n_f
    span = inputs["kv"].shape[0]
    high = max(16, CHUNK // width)
    tall = min(seg, CHUNK // own_q)
    down = inputs["g_down_in"].shape
    up = inputs["g_up_in"].shape
    out = (own_q // high, high, width)
    query = (width // tall, tall, own_q)
    keyval = (1, own_q, 2 * head)
    chunks = down[0] + up[0] + out[0] + query[0] + 1
    in_hbm = ("e_part", "g_down_in", "g_up_in", "normed_in", "out_part")
    outs = {
        "grad_tokens": ((rows, width), BF16, ON_CHIP),
        "out_sum": ((rows, width), F32, ON_CHIP),
        "vectors": ((16, seg), F32, ON_CHIP),
        "h_down": ((2,) + down, BF16, ANYWHERE),
        "h_up": ((seg, own_h * n_p), BF16, ANYWHERE),
        "h_out": ((2,) + out, BF16, ANYWHERE),
        "h_q": ((seg, width), BF16, ANYWHERE),
        "h_kv": ((2,) + keyval, BF16, ANYWHERE),
    }
    plane = (n_p, rows, width)
    blocks = (n_p, rows, own_q)
    scratch = {
        "part": VMEM(plane, BF16),
        "g_down": VMEM(down, BF16),
        "g_up": VMEM(up, BF16),
        "g_out": VMEM(out, BF16),
        "g_q": VMEM(query, BF16),
        "g_kv": VMEM(keyval, BF16),
        "land_down": VMEM(down, BF16),
        "land_up": VMEM(up, BF16),
        "land_out": VMEM(out, BF16),
        "land_q": VMEM(query, BF16),
        "land_kv": VMEM(keyval, BF16),
        "fin_up": VMEM(up, BF16),
        "fin_q": VMEM(query, BF16),
        "core_in": VMEM((n_f, rows, width), BF16),
        "link_in": VMEM((n_f, rows, width), BF16),
        "e_sum": VMEM((rows, width), F32),
        "e_extra": VMEM((rows, width), F32),
        "d_residual": VMEM((rows, width), F32),
        "d_branch": VMEM((rows, width), BF16),
        "branch_pl": VMEM(plane, BF16),
        "mixed_send": VMEM(blocks, BF16),
        "d_mixed": VMEM(blocks, BF16),
        "dq_send": VMEM(blocks, BF16),
        "dq_own": VMEM(blocks, BF16),
        "d_kv_span": VMEM((span, 2 * head), F32),
        "dkv_send": VMEM((n_s, rows, 2 * head), BF16),
        "dkv_recv": VMEM((n_s, rows, 2 * head), BF16),
        "d_kv": VMEM((rows, 2 * head), BF16),
        "dkv_pl": VMEM((n_p, rows, 2 * head), BF16),
        "sums_one": VMEM((8, width), F32),
        "sums_two": VMEM((8, width), F32),
        "vec_in": VMEM((n_f, 16, seg), F32),
        "vec_plane": VMEM((n_p, 16, seg), F32),
        "vec_part": VMEM((16, seg), F32),
        "vec_line": VMEM((n_z, 16, seg), F32),
        "load_sem": DMA((5,)),
        "local_sem": DMA((6,)),
        "red_send": DMA((chunks,)),
        "red_recv": DMA((chunks,)),
        "fin_send": DMA((chunks,)),
        "fin_recv": DMA((chunks,)),
        "keep_sem": DMA((chunks,)),
        "swap_send": DMA((chunks,)),
        "swap_recv": DMA((chunks,)),
        "up_send": DMA((up[0],)),
        "up_mate": DMA((up[0],)),
        "up_recv": DMA((up[0],)),
        "up_relay": DMA((up[0],)),
        "up_cross": DMA((up[0],)),
        "q_send": DMA((query[0],)),
        "q_mate": DMA((query[0],)),
        "q_recv": DMA((query[0],)),
        "q_relay": DMA((query[0],)),
        "q_cross": DMA((query[0],)),
        "scatter_one": DMA((4, count)),
        "scatter_two": DMA((4, count)),
        "scatter_three": DMA((4, count)),
        "gather_one": DMA((4, count)),
        "gather_two": DMA((4, count)),
        "swap_one": DMA((2, n_p)),
        "swap_two": DMA((2, n_p)),
        "column_sem": DMA((2, n_s)),
        "vec_sem": DMA((2, n_p)),
        "vec_line_sem": DMA((2, n_z)),
    }
    names = list(inputs) + list(outs) + list(scratch)
    result = pl.pallas_call(
        functools.partial(backward_body, n_f, n_z, head, names),
        out_shape=[jax.ShapeDtypeStruct(shape, kind) for shape, kind, _ in outs.values()],
        in_specs=[ANYWHERE if name in in_hbm else ON_CHIP for name in inputs],
        out_specs=[place for _, _, place in outs.values()],
        scratch_shapes=list(scratch.values()),
        compiler_params=pltpu.CompilerParams(
            collective_id=ident, has_side_effects=True, vmem_limit_bytes=67043328
        ),
        name="backward",
    )(*inputs.values())
    return dict(zip(outs, result))


def dot(left, right):
    return jnp.dot(left, right, preferred_element_type=F32)


def dot_tn(left, right):
    return lax.dot_general(left, right, (((0,), (0,)), ((), ())), preferred_element_type=F32)


def dot_nt(left, right):
    return lax.dot_general(left, right, (((1,), (1,)), ((), ())), preferred_element_type=F32)


def widen_body(count, *refs):
    at = 0
    for ref in refs[:count]:
        refs[count][:, at : at + ref.shape[1]] = ref[...].astype(F32)
        at += ref.shape[1]


def widen(*pieces):
    height = pieces[0].shape[0]
    width = sum(item.shape[1] for item in pieces)
    block = min(height, 1 << ((1 << 20) // width).bit_length() - 1)
    specs = [pl.BlockSpec((block, item.shape[1]), lambda i: (i, 0)) for item in pieces]
    return pl.pallas_call(
        functools.partial(widen_body, len(pieces)),
        out_shape=jax.ShapeDtypeStruct((height, width), F32),
        grid=(pl.cdiv(height, block),),
        in_specs=specs,
        out_specs=pl.BlockSpec((block, width), lambda i: (i, 0)),
        compiler_params=pltpu.CompilerParams(vmem_limit_bytes=40 << 20),
        name="widen",
    )(*pieces)


def shards(
    tokens,
    doc_lengths,
    attn_gain,
    attn_shift,
    qkv_weight,
    query_bias,
    value_bias,
    out_weight,
    out_bias,
    mlp_gain,
    mlp_shift,
    up_weight,
    up_bias,
    down_weight,
    down_bias,
    cotangent,
):
    n_f, n_z, n_c = lax.axis_size("fsdp"), lax.axis_size("zz"), lax.axis_size("core")
    f, z, c = lax.axis_index("fsdp"), lax.axis_index("zz"), lax.axis_index("core")
    n_p = n_f * n_c
    grad_out = cotangent[0]
    rows, width = grad_out.shape
    head = value_bias.shape[0] * n_f
    hidden = up_weight.shape[1]
    own_q = width // n_p
    own_h = hidden // n_p
    seg = width // n_f

    def own(vector, size):
        return lax.dynamic_slice_in_dim(vector, c * size, size, axis=0)

    row = lax.broadcasted_iota(jnp.int32, (8, seg), 0)
    small = jnp.broadcast_to(jnp.pad(value_bias, (0, seg - value_bias.shape[0]))[None], (8, seg))
    vectors = (attn_gain, attn_shift, out_bias, mlp_gain, mlp_shift, down_bias, query_bias)
    for at, item in enumerate(vectors):
        small = jnp.where(row == at, item[None], small)
    w_down = own(down_weight, own_h)
    ahead = forward(
        {
            "tokens": tokens[0],
            "grad_out": grad_out,
            "small": small,
            "lengths": doc_lengths,
            "out_weight": out_weight,
            "qkv_weight": qkv_weight,
            "up_weight": up_weight,
        },
        n_f,
        n_z,
        head,
        own_h,
        8,
    )
    vecs = ahead["vecs"]
    w_up = ahead["w_up"].reshape(width, own_h)
    grad_pl = ahead["grad_pl"].reshape(n_p * rows, width)
    normed_mlp_pl = ahead["normed_mlp_pl"].reshape(n_p * rows, width)

    inner = dot(normed_mlp_pl, w_up) + own(up_bias, own_h).astype(F32)
    activated, gelu_back = jax.vjp(lambda v: jax.nn.gelu(v, approximate=True), inner)
    activated = activated.astype(BF16)
    out_part = dot(activated, w_down).astype(BF16).reshape(n_p, rows, width)
    d_act = dot_nt(grad_pl, w_down)
    d_inner = gelu_back(d_act)[0].astype(BF16)
    e_part = dot_nt(d_inner, w_up).astype(BF16).reshape(n_p, rows, width)
    g_down = dot_tn(activated, grad_pl).astype(BF16)
    g_up = dot_tn(normed_mlp_pl, d_inner).astype(BF16)

    def chunked(block, most):
        height = min(max(16, CHUNK // block.shape[1]), most)
        return block.reshape(block.shape[0] // height, height, block.shape[1])

    done = backward(
        {
            "e_part": e_part,
            "out_part": out_part,
            "g_down_in": chunked(g_down, own_h),
            "g_up_in": chunked(g_up, seg),
            "normed_in": ahead["normed_pl"],
            "grad_out": grad_out,
            "normal_two": ahead["normal_two"],
            "inverse_two": ahead["inverse_two"],
            "gain_two": vecs[GAIN_TWO : GAIN_TWO + 1],
            "normal_one": ahead["normal_one"],
            "inverse_one": ahead["inverse_one"],
            "gain_one": vecs[GAIN_ONE : GAIN_ONE + 1],
            "w_out": ahead["w_out"],
            "w_q": ahead["w_q"].reshape(width, own_q),
            "w_kv": ahead["w_kv"].reshape(width, 2 * head),
            "query": ahead["query"],
            "kv": ahead["kv"],
            "mask": ahead["mask"],
            "lse": ahead["lse"],
            "mixed_own": ahead["mixed_own"],
            "up_sum": jnp.sum(d_inner.astype(F32), axis=0).reshape(own_h // seg, seg),
        },
        n_f,
        n_z,
        head,
        own_h,
        9,
    )
    layer_out = ahead["residual"] + done["out_sum"] + vecs[BIAS_DOWN]
    vectors = done["vectors"]
    grad_qkv = widen(done["h_q"], done["h_kv"].reshape(n_c * own_q, 2 * head))
    size = value_bias.shape[0]
    grad_value_bias = lax.dynamic_slice_in_dim(vectors[7], f * size, size)
    return (
        layer_out.astype(BF16)[None],
        done["grad_tokens"][None],
        vectors[0],
        vectors[1],
        grad_qkv,
        vectors[2],
        grad_value_bias,
        widen(done["h_out"].reshape(n_c * own_q, width)),
        vectors[3],
        vectors[4],
        vectors[5],
        widen(done["h_up"]),
        vectors[8 : 8 + hidden // width].reshape(-1),
        widen(done["h_down"].reshape(n_c * own_h, width)),
        vectors[6],
    )


def solution(mesh):
    n_f, n_s = mesh.shape["fsdp"], mesh.shape["seq"]
    split = Mesh(mesh.devices.reshape(n_f, n_s // 2, 2), ("fsdp", "zz", "core"))
    act = P("fsdp", ("zz", "core"), None)
    vec = P("fsdp")
    mat = P("fsdp", None)
    return jax.shard_map(
        shards,
        mesh=split,
        in_specs=(act, mat, vec, vec, mat, vec, vec, mat, vec, vec, vec, mat, vec, mat, vec, act),
        out_specs=(act, act, vec, vec, mat, vec, vec, mat, vec, vec, vec, mat, vec, mat, vec),
        check_vma=False,
    )
```

```python
import functools
import math

import jax
import jax.numpy as jnp
from jax import lax
from jax.experimental import pallas as pl
from jax.experimental.pallas import tpu as pltpu
from jax.sharding import Mesh
from jax.sharding import PartitionSpec as P

EPSILON = 1e-05
F32 = jnp.float32
BF16 = jnp.bfloat16
MESH = pl.DeviceIdType.MESH
VMEM = pltpu.VMEM
DMA = pltpu.SemaphoreType.DMA
ON_CHIP = pl.BlockSpec(memory_space=pltpu.VMEM)
ANYWHERE = pl.BlockSpec(memory_space=pl.ANY)
LANES = 128
CHUNK = 1 << 16


def flip(index, offset, bits):
    for bit in range(bits):
        if offset >> bit & 1:
            index = index + (1 << bit) * (1 - 2 * ((index // (1 << bit)) % 2))
    return index


def bit_orders(n_f):
    bits = n_f.bit_length() - 1
    assert 1 << bits == n_f
    turns = min(bits, 2)
    return bits, [[(turn + at) % bits for at in range(bits)] for turn in range(turns)]


def greet(targets):
    barrier = pltpu.get_barrier_semaphore()
    for target in targets:
        pl.semaphore_signal(barrier, inc=1, device_id=target, device_id_type=MESH)
    pl.semaphore_wait(barrier, len(targets))


def plane_peers(n_f, f, c):
    bits = n_f.bit_length() - 1
    peers = []
    for offset in range(n_f):
        for other in range(2):
            if offset or other:
                peers.append(
                    (offset * 2 + other, {"fsdp": flip(f, offset, bits), "core": c + other * (1 - 2 * c)})
                )
    return peers


def column_peers(n_z, z, c):
    peers = []
    for offset in range(n_z):
        for other in range(2):
            if offset or other:
                peers.append(
                    (offset * 2 + other, {"zz": (z + offset) % n_z, "core": c + other * (1 - 2 * c)})
                )
    return peers


def remote(source, target, send, recv, device):
    return pltpu.make_async_remote_copy(
        src_ref=source,
        dst_ref=target,
        send_sem=send,
        recv_sem=recv,
        device_id=device,
        device_id_type=MESH,
    )


def no_pause(count):
    pass


class Gather:
    def __init__(self, n_f, x_ref, out_ref, send, recv, core_send, core_recv, local_sem):
        self.f, self.c = lax.axis_index("fsdp"), lax.axis_index("core")
        self.n_f, self.x_ref, self.out_ref = n_f, x_ref, out_ref
        self.send, self.recv, self.core_send, self.core_recv = send, recv, core_send, core_recv
        self.bits, self.orders = bit_orders(n_f)
        self.part = x_ref.shape[0] // len(self.orders)
        self.started = []
        self.have = [[0] for _ in self.orders]
        self.own = lambda: pltpu.make_async_copy(x_ref, out_ref.at[self.slot(0, self.c)], local_sem)

    def slot(self, offset, core):
        return flip(self.f, offset, self.bits) * 2 + core

    def piece(self, turn, offset, core):
        return self.out_ref.at[self.slot(offset, core), pl.ds(turn * self.part, self.part)]

    def source(self, turn, offset):
        if offset:
            return self.piece(turn, offset, self.c)
        return self.x_ref.at[pl.ds(turn * self.part, self.part)]

    def link(self, turn, offset, bit):
        sem = turn * self.n_f + (offset ^ (1 << bit))
        return remote(
            self.source(turn, offset),
            self.piece(turn, offset, self.c),
            self.send.at[sem],
            self.recv.at[sem],
            {"fsdp": flip(self.f, 1 << bit, self.bits)},
        )

    def arrival(self, turn, offset):
        sem = turn * self.n_f + offset
        where = self.piece(turn, offset, self.c)
        return remote(where, where, self.send.at[sem], self.recv.at[sem], {"core": 1 - self.c})

    def across(self, turn, offset):
        sem = turn * self.n_f + offset
        return remote(
            self.source(turn, offset),
            self.piece(turn, offset, self.c),
            self.core_send.at[sem],
            self.core_recv.at[sem],
            {"core": 1 - self.c},
        )

    def crossing(self, turn, offset):
        sem = turn * self.n_f + offset
        where = self.piece(turn, offset, 1 - self.c)
        return remote(
            where, where, self.core_send.at[sem], self.core_recv.at[sem], {"core": 1 - self.c}
        )

    def go(self, copy):
        copy.start()
        self.started.append(copy)

    def start(self):
        for step in range(self.bits):
            for turn, order in enumerate(self.orders):
                self.go(self.link(turn, 0, order[step]))
        for turn in range(len(self.orders)):
            self.go(self.across(turn, 0))
        self.own().start()

    def relay(self, pause):
        for step in range(self.bits):
            for at in range(1 << step):
                for turn, order in enumerate(self.orders):
                    offset = self.have[turn][at] ^ (1 << order[step])
                    self.arrival(turn, offset).wait_recv()
                    for later in range(step + 1, self.bits):
                        self.go(self.link(turn, offset, order[later]))
                    self.go(self.across(turn, offset))
                    self.have[turn].append(offset)
                    pause(1)

    def finish(self):
        for copy in self.started:
            copy.wait_send()
        for turn in range(len(self.orders)):
            for offset in self.have[turn]:
                self.crossing(turn, offset).wait_recv()
        self.own().wait()


def gather_stage(n_f, x_ref, out_ref, *rest):
    gather = Gather(n_f, x_ref, out_ref, *rest[:-1])
    gather.start()
    rest[-1](1)
    gather.relay(rest[-1])
    gather.finish()


def scatter_stage(
    n_f, part_ref, out_ref, acc, core_in, link_in, send, recv, core_send, core_recv, pause
):
    f, c = lax.axis_index("fsdp"), lax.axis_index("core")
    rows = out_ref.shape[0]
    bits, orders = bit_orders(n_f)
    part = rows // len(orders)
    started = []

    def go(copy):
        copy.start()
        started.append(copy)

    def held(offset, where):
        if acc is None:
            return part_ref.at[flip(f, offset, bits) * 2 + c, where]
        return acc.at[offset, where]

    def across(turn, offset):
        where = pl.ds(turn * part, part)
        sem = turn * n_f + offset
        return remote(
            part_ref.at[flip(f, offset, bits) * 2 + 1 - c, where],
            core_in.at[offset, where],
            core_send.at[sem],
            core_recv.at[sem],
            {"core": 1 - c},
        )

    def link(turn, offset, bit):
        where = pl.ds(turn * part, part)
        sem = turn * n_f + offset
        return remote(
            held(offset, where),
            link_in.at[offset, where],
            send.at[sem],
            recv.at[sem],
            {"fsdp": flip(f, 1 << bit, bits)},
        )

    plan = [[] for _ in range(bits)] + [[(turn, 0) for turn in range(len(orders))]]
    for step in range(bits):
        for offset in range(n_f):
            for turn, order in enumerate(orders):
                if offset >> order[step] & 1 and not any(offset >> b & 1 for b in order[:step]):
                    plan[step].append((turn, offset))
    for todo in plan:
        for turn, offset in todo:
            go(across(turn, offset))
    for step, todo in enumerate(plan):
        pause(1)
        for turn, offset in todo:
            where = pl.ds(turn * part, part)
            across(turn, offset).wait_recv()
            total = part_ref[flip(f, offset, bits) * 2 + c, where].astype(F32)
            total = total + core_in[offset, where].astype(F32)
            for bit in orders[turn][:step]:
                link(turn, offset | (1 << bit), bit).wait_recv()
                total = total + link_in[offset | (1 << bit), where].astype(F32)
            if offset:
                held(offset, where)[...] = total.astype(BF16)
                go(link(turn, offset, orders[turn][step]))
                if offset == n_f - 1:
                    pause(1)
            else:
                out_ref[where] = total
    for copy in started:
        copy.wait_send()


def exchange_stage(n_f, n_z, plane_in, column_in, plane_out, column_out, sems, whole, pause):
    f, z, c = lax.axis_index("fsdp"), lax.axis_index("zz"), lax.axis_index("core")
    peers = plane_peers(n_f, f, c)
    others = column_peers(n_z, z, c) if column_in is not None else []
    copies = []
    local = []
    if column_in is not None:
        mine = z * 2 + c
        for sem, device in others:
            to = device["zz"] * 2 + device["core"]
            source = column_in if whole else column_in.at[to]
            copies.append(
                remote(source, column_out.at[mine], sems[2].at[sem], sems[3].at[sem], device)
            )
        source = column_in if whole else column_in.at[mine]
        local.append(pltpu.make_async_copy(source, column_out.at[mine], sems[5]))
    mine = f * 2 + c
    for sem, device in peers:
        to = device["fsdp"] * 2 + device["core"]
        copies.append(
            remote(plane_in.at[to], plane_out.at[mine], sems[0].at[sem], sems[1].at[sem], device)
        )
    local.append(pltpu.make_async_copy(plane_in.at[mine], plane_out.at[mine], sems[4]))
    for copy in copies + local:
        copy.start()
    pause(1)
    for copy in copies:
        copy.wait_send()
    for sem, device in peers:
        frm = device["fsdp"] * 2 + device["core"]
        remote(
            plane_out.at[frm], plane_out.at[frm], sems[0].at[sem], sems[1].at[sem], device
        ).wait_recv()
    if column_in is not None:
        for offset in range(n_z):
            for other in range(2):
                if offset or other:
                    frm = ((z + n_z - offset) % n_z) * 2 + c + other * (1 - 2 * c)
                    sem = offset * 2 + other
                    remote(
                        column_out.at[frm],
                        column_out.at[frm],
                        sems[2].at[sem],
                        sems[3].at[sem],
                        {"core": 1 - c},
                    ).wait_recv()
    for copy in local:
        copy.wait()


class Line:
    def __init__(self, n_z, kinds, sems):
        self.n_z, self.kinds = n_z, kinds
        self.base = [sum(kind[0] for kind in kinds[:at]) for at in range(len(kinds))]
        self.total = sum(kind[0] for kind in kinds)
        self.red_send, self.red_recv, self.fin_send, self.fin_recv, self.own_sem = sems
        self.place, self.turn = lax.axis_index("zz"), 1 - 2 * lax.axis_index("core")
        self.z = self.place + lax.axis_index("core") * (n_z - 1 - 2 * self.place)
        self.leaf, self.root = self.z == n_z - 1, self.z == 0
        self.inner = (self.z > 0) & (self.z < n_z - 1)
        self.done = 0

    def toward(self, kind, k, source):
        sem = self.base[kind] + k
        return remote(
            source,
            self.kinds[kind][1](k)[1],
            self.red_send.at[sem],
            self.red_recv.at[sem],
            {"zz": jnp.clip(self.place - self.turn, 0, self.n_z - 1)},
        )

    def outward(self, kind, k, source):
        sem = self.base[kind] + k
        return remote(
            source,
            self.kinds[kind][1](k)[2],
            self.fin_send.at[sem],
            self.fin_recv.at[sem],
            {"zz": jnp.clip(self.place + self.turn, 0, self.n_z - 1)},
        )

    def keep(self, kind, k):
        _, landing, final = self.kinds[kind][1](k)
        return pltpu.make_async_copy(landing, final, self.own_sem.at[self.base[kind] + k])

    def reduce(self, kind, k):
        own, landing, _ = self.kinds[kind][1](k)

        @pl.when(self.leaf)
        def _():
            self.toward(kind, k, own).start()

        @pl.when(jnp.logical_not(self.leaf))
        def _():
            self.toward(kind, k, own).wait_recv()
            height = min(16, own.shape[0])

            @pl.loop(0, own.shape[0] // height)
            def _(at):
                where = pl.ds(pl.multiple_of(at * height, height), height)
                landing[where] = (own[where].astype(F32) + landing[where].astype(F32)).astype(BF16)

        @pl.when(self.inner)
        def _():
            self.toward(kind, k, landing).start()

        @pl.when(self.root)
        def _():
            self.outward(kind, k, landing).start()
            self.keep(kind, k).start()

    def spread(self, kind, k):
        final = self.kinds[kind][1](k)[2]

        @pl.when(self.root)
        def _():
            self.keep(kind, k).wait()

        @pl.when(jnp.logical_not(self.root))
        def _():
            self.outward(kind, k, final).wait_recv()

        @pl.when(self.inner)
        def _():
            self.outward(kind, k, final).start()

        self.kinds[kind][2](k)

    def each(self, slope, back, action, at, count):
        low = [self.done - back - slope * z for z in range(self.n_z)]
        here = self.done + at - back - slope * self.z
        for kind, (chunks, _, _) in enumerate(self.kinds):
            base = self.base[kind]
            if base <= min(low) and max(low) + count <= base + chunks:
                action(kind, here - base)
            elif any(k < base + chunks and base < k + count for k in low):

                @pl.when((here >= base) & (here < base + chunks))
                def _():
                    action(kind, here - base)

    def run(self, count):
        count = min(count, self.left())
        if count <= 0:
            return

        @pl.loop(0, count)
        def _(at):
            first = STAGGER * (self.n_z - 1)
            self.each(-STAGGER, first, self.reduce, at, count)
            self.each(BEHIND, first + 1, self.spread, at, count)

        self.done += count

    def lag(self, z):
        return STAGGER * (self.n_z - 1) + 1 + BEHIND * z

    def left(self):
        return self.total + self.lag(self.n_z - 1) - self.done

    def finish(self):
        for kind, (count, refs, _) in enumerate(self.kinds):

            @pl.loop(0, count)
            def _(k):
                @pl.when(jnp.logical_not(self.root))
                def _():
                    self.toward(kind, k, refs(k)[0]).wait_send()

                @pl.when(jnp.logical_not(self.leaf))
                def _():
                    self.outward(kind, k, refs(k)[2]).wait_send()


def vector_stage(n_f, n_z, in_ref, out_ref, plane_in, part, line_in, sems, pause):
    f, z, c = lax.axis_index("fsdp"), lax.axis_index("zz"), lax.axis_index("core")
    send, recv, line_send, line_recv, local = sems
    peers = plane_peers(n_f, f, c)
    others = [(offset, {"zz": (z + offset) % n_z}) for offset in range(1, n_z)]
    mine = f * 2 + c
    copies = [
        remote(in_ref.at[device["fsdp"]], plane_in.at[mine], send.at[sem], recv.at[sem], device)
        for sem, device in peers
    ]
    for copy in copies:
        copy.start()
    own = pltpu.make_async_copy(in_ref.at[f], plane_in.at[mine], local)
    own.start()
    own.wait()
    pause(1)
    for sem, device in peers:
        where = plane_in.at[device["fsdp"] * 2 + device["core"]]
        remote(where, where, send.at[sem], recv.at[sem], device).wait_recv()
    total = plane_in[0]
    for at in range(1, n_f * 2):
        total = total + plane_in[at]
    part[...] = total
    line = [
        remote(part, line_in.at[z], line_send.at[sem], line_recv.at[sem], device)
        for sem, device in others
    ]
    for copy in line:
        copy.start()
    pause(1)
    for offset in range(1, n_z):
        where = line_in.at[(z + n_z - offset) % n_z]
        remote(
            where, where, line_send.at[offset], line_recv.at[offset], {"core": 1 - c}
        ).wait_recv()
    line_in[z] = total
    total = line_in[0]
    for at in range(1, n_z):
        total = total + line_in[at]
    out_ref[...] = total
    for copy in copies + line:
        copy.wait_send()


def heads_side_by_side(block, head):
    count = block.shape[1] // head
    return jnp.concatenate([block[:, at * head : (at + 1) * head] for at in range(count)], axis=0)


def heads_apart(block, count):
    rows = block.shape[0] // count
    return jnp.concatenate([block[at * rows : (at + 1) * rows] for at in range(count)], axis=1)


def attend_block(head, query_in, kv_ref, mask_ref):
    scale = 1.0 / math.sqrt(head)
    query = heads_side_by_side(query_in, head)
    count = query_in.shape[1] // head
    keys, values = kv_ref[:, :head], kv_ref[:, head:]
    mask = jnp.concatenate([mask_ref[...]] * count, axis=1)
    scores = dot_nt(keys, query) * scale + mask
    peak = jnp.max(scores, axis=0, keepdims=True)
    weights = jnp.exp(scores - peak)
    total = jnp.sum(weights, axis=0, keepdims=True)
    probs = (weights / total).astype(BF16)
    return heads_apart(dot_tn(probs, values).astype(BF16), count), peak + jnp.log(total)


def attend_back_block(head, query_in, grad_in, kv_ref, mask_ref, lse):
    scale = 1.0 / math.sqrt(head)
    query = heads_side_by_side(query_in, head)
    grad = heads_side_by_side(grad_in, head)
    count = query_in.shape[1] // head
    keys, values = kv_ref[:, :head], kv_ref[:, head:]
    mask = jnp.concatenate([mask_ref[...]] * count, axis=1)
    scores = dot_nt(keys, query) * scale + mask
    probs = jnp.exp(scores - lse)
    d_probs = dot_nt(values, grad)
    delta = jnp.sum(probs * d_probs, axis=0, keepdims=True)
    d_scores = (probs * (d_probs - delta)).astype(BF16)
    d_query = heads_apart((dot_tn(d_scores, keys) * scale).astype(BF16), count)
    d_keys = dot(d_scores, query) * scale
    d_values = dot(probs.astype(BF16), grad)
    return d_query, d_keys, d_values


class Box:
    pass


def rows_of(at, height=16):
    return pl.ds(pl.multiple_of(at * height, height), height)


GAIN_ONE, SHIFT_ONE, BIAS_OUT, GAIN_TWO, SHIFT_TWO, BIAS_DOWN, BIAS_QUERY = range(7)


def norm_tiles(load, gain, shift, normal_ref, inverse_ref, normed_ref):
    @pl.loop(0, normal_ref.shape[0] // 16)
    def _(at):
        where = rows_of(at)
        values = load(where)
        row_mean = jnp.mean(values, axis=-1, keepdims=True)
        centered = values - row_mean
        variance = jnp.mean(centered * centered, axis=-1, keepdims=True)
        inverse = lax.rsqrt(variance + EPSILON)
        normal = centered * inverse
        normal_ref[where] = normal
        inverse_ref[where] = inverse
        normed_ref[where] = (normal * gain + shift).astype(BF16)


def forward_body(n_f, n_z, head, names, *refs):
    r = Box()
    for name, ref in zip(names, refs, strict=True):
        setattr(r, name, ref)
    f, z, c = lax.axis_index("fsdp"), lax.axis_index("zz"), lax.axis_index("core")
    bits = n_f.bit_length() - 1
    n_p = n_f * 2
    rows, width = r.tokens.shape
    own_q = r.w_q.shape[2]
    own_h = r.w_up.shape[2]
    seg = width // n_f
    far = [flip(f, offset, bits) for offset in range(n_f)]
    r.small_all[f] = r.small[...]
    r.small_f32[...] = r.small[...].astype(F32)
    greet([device for _, device in plane_peers(n_f, f, c) + column_peers(n_z, z, c)])

    def columns(ref, to, size, where=slice(None)):
        return ref.at[where, pl.ds(pl.multiple_of((to * 2 + c) * size, LANES), size)]

    half = seg // 2
    quarter = seg // n_z

    def kv_piece(source, core):
        return r.w_kv.at[source, pl.ds(pl.multiple_of(core * half, 16), half)]

    def up_piece(source, plane):
        return r.w_up.at[source, pl.ds(pl.multiple_of(plane * quarter, 16), quarter)]

    smalls, early, kv_cross, up_links, up_lines = [], [], [], [], []
    for offset in range(1, n_f):
        device = {"fsdp": far[offset]}
        smalls.append(
            remote(r.small, r.small_all.at[f], r.small_sem.at[0, offset], r.small_sem.at[1, offset], device)
        )
        early.append(
            remote(
                columns(r.qkv_weight, far[offset], own_q),
                r.w_q.at[f],
                r.q_sem.at[0, offset],
                r.q_sem.at[1, offset],
                device,
            )
        )
        early.append(
            remote(
                r.qkv_weight.at[pl.ds(pl.multiple_of(c * half, 16), half), pl.ds(width, 2 * head)],
                kv_piece(f, c),
                r.kv_sem.at[0, offset],
                r.kv_sem.at[1, offset],
                device,
            )
        )
        where = pl.ds(pl.multiple_of(z * quarter, 16), quarter)
        up_links.append(
            remote(
                columns(r.up_weight, far[offset], own_h, where),
                up_piece(f, z),
                r.up_sem.at[0, offset],
                r.up_sem.at[1, offset],
                device,
            )
        )
    locals_ = [
        pltpu.make_async_copy(columns(r.qkv_weight, f, own_q), r.w_q.at[f], r.local_sem.at[0]),
        pltpu.make_async_copy(
            r.qkv_weight.at[:, pl.ds(width, 2 * head)], r.w_kv.at[f], r.local_sem.at[1]
        ),
        pltpu.make_async_copy(columns(r.up_weight, f, own_h), r.up_own, r.local_sem.at[2]),
        pltpu.make_async_copy(
            r.out_weight.at[pl.ds(pl.multiple_of(c * own_q, 16), own_q)], r.w_out, r.local_sem.at[11]
        ),
    ]
    for copy in smalls + early + locals_:
        copy.start()

    for offset in range(1, n_f):
        where = r.small_all.at[far[offset]]
        remote(
            where, where, r.small_sem.at[0, offset], r.small_sem.at[1, offset], {"core": 1 - c}
        ).wait_recv()
    bias_v = jnp.zeros((8, LANES), F32)
    for o in range(n_f):
        block = r.small_all[o].astype(F32)
        r.vecs[:, o * seg : (o + 1) * seg] = block
        shift = o * (head // n_f)
        block = block[:, :LANES]
        bias_v = bias_v + (pltpu.roll(block, shift, axis=1) if shift else block)
    norm_tiles(
        lambda where: r.tokens[where].astype(F32),
        r.vecs[GAIN_ONE : GAIN_ONE + 1],
        r.vecs[SHIFT_ONE : SHIFT_ONE + 1],
        r.normal_one,
        r.inverse_one,
        r.normed,
    )
    bias_q = r.small_f32[BIAS_QUERY : BIAS_QUERY + 1, pl.ds(pl.multiple_of(c * own_q, LANES), own_q)]
    normed = Gather(
        n_f, r.normed, r.normed_all, *(r.gather_one.at[at] for at in range(4)), r.local_sem.at[3]
    )
    normed.start()
    for offset in range(1, n_f):
        where = kv_piece(far[offset], c)
        remote(
            where, where, r.kv_sem.at[0, offset], r.kv_sem.at[1, offset], {"core": 1 - c}
        ).wait_recv()
        kv_cross.append(
            remote(where, where, r.kv_sem.at[2, offset], r.kv_sem.at[3, offset], {"core": 1 - c})
        )
        kv_cross[-1].start()
    locals_[2].wait()
    up_home = pltpu.make_async_copy(r.up_own, r.w_up.at[f], r.local_sem.at[4])
    up_home.start()
    normed.relay(no_pause)
    for copy in up_links:
        copy.start()
    span = r.kv.shape[0]
    first = jnp.maximum((z * 2 + c + 1) - span // rows, 0)
    key_pos = first * rows + lax.broadcasted_iota(jnp.int32, (span, rows), 0)
    row_pos = (z * 2 + c) * rows + lax.broadcasted_iota(jnp.int32, (span, rows), 1)
    same = jnp.zeros((span, rows), jnp.int32)
    doc_end = jnp.zeros((1, 1), jnp.int32)
    for at in range(r.lengths.shape[1]):
        doc_end = doc_end + r.lengths[:, at : at + 1]
        edge = (key_pos >= doc_end) != (row_pos >= doc_end)
        same = same + edge.astype(jnp.int32)
    r.mask[...] = jnp.where((same == 0) & (row_pos >= key_pos), 0.0, -1e30).astype(F32)
    for offset in range(1, n_f):
        where = kv_piece(far[offset], 1 - c)
        remote(
            where, where, r.kv_sem.at[2, offset], r.kv_sem.at[3, offset], {"core": 1 - c}
        ).wait_recv()
        where = r.w_q.at[far[offset]]
        remote(
            where, where, r.q_sem.at[0, offset], r.q_sem.at[1, offset], {"core": 1 - c}
        ).wait_recv()
    locals_[0].wait()
    locals_[1].wait()
    keyval = dot(r.normed[...], r.w_kv[...].reshape(width, 2 * head))
    r.keyval[:, :head] = keyval[:, :head].astype(BF16)
    r.keyval[:, head:] = (keyval[:, head:] + bias_v[7:8, :head]).astype(BF16)
    normed.finish()
    keep = pltpu.make_async_copy(r.normed_all, r.normed_pl, r.local_sem.at[5])
    keep.start()

    @pl.loop(0, n_p)
    def _(p):
        r.query_send[p] = (
            dot(r.normed_all[p], r.w_q[...].reshape(width, own_q)) + bias_q
        ).astype(BF16)

    grads = Gather(
        n_f, r.grad_out, r.grad_pl, *(r.gather_two.at[at] for at in range(4)), r.local_sem.at[6]
    )

    def fill(count):
        for offset in range(1, n_f):
            where = up_piece(far[offset], z)
            remote(
                where, where, r.up_sem.at[0, offset], r.up_sem.at[1, offset], {"core": 1 - c}
            ).wait_recv()
            for away in range(1, n_z):
                sem = away * n_f + offset
                up_lines.append(
                    remote(
                        where, where, r.line_sem.at[0, sem], r.line_sem.at[1, sem], {"zz": (z + away) % n_z}
                    )
                )
                up_lines[-1].start()
        grads.start()

    exchange_stage(
        n_f,
        n_z,
        r.query_send,
        r.keyval,
        r.query,
        r.kv_all,
        [
            r.swap_one.at[0],
            r.swap_one.at[1],
            r.column_sem.at[0],
            r.column_sem.at[1],
            r.local_sem.at[7],
            r.local_sem.at[8],
        ],
        True,
        fill,
    )
    for at in range(span // rows):
        r.kv[at * rows : (at + 1) * rows] = r.kv_all[first + at]

    @pl.loop(0, n_p)
    def _(p):
        mixed, lse = attend_block(head, r.query[p], r.kv, r.mask)
        r.mixed_send[p] = mixed
        r.lse[p] = lse

    exchange_stage(
        n_f,
        n_z,
        r.mixed_send,
        None,
        r.mixed_own,
        None,
        [r.swap_two.at[0], r.swap_two.at[1], None, None, r.local_sem.at[9], None],
        False,
        lambda count: grads.relay(no_pause),
    )
    tile = min(512, width)
    locals_[3].wait()

    @pl.loop(0, n_p)
    def _(p):
        for n in range(width // tile):
            cols = pl.ds(n * tile, tile)
            r.part[p, :, cols] = dot(r.mixed_own[p], r.w_out[:, cols]).astype(BF16)

    scatter_stage(
        n_f, r.part, r.branch, None, r.core_in, r.link_in, *(r.scatter_one.at[at] for at in range(4)), no_pause
    )

    def second(where):
        values = (
            r.tokens[where].astype(F32) + r.branch[where] + r.vecs[BIAS_OUT : BIAS_OUT + 1]
        )
        r.residual[where] = values
        return values

    norm_tiles(
        second,
        r.vecs[GAIN_TWO : GAIN_TWO + 1],
        r.vecs[SHIFT_TWO : SHIFT_TWO + 1],
        r.normal_two,
        r.inverse_two,
        r.normed_mlp,
    )
    last = Gather(
        n_f, r.normed_mlp, r.normed_mlp_pl, *(r.gather_three.at[at] for at in range(4)), r.local_sem.at[10]
    )
    last.start()
    grads.finish()
    last.relay(no_pause)
    for copy in smalls + early + kv_cross + up_links + up_lines:
        copy.wait_send()
    for offset in range(1, n_f):
        for away in range(1, n_z):
            where = up_piece(far[offset], (z + n_z - away) % n_z)
            sem = away * n_f + offset
            remote(
                where, where, r.line_sem.at[0, sem], r.line_sem.at[1, sem], {"core": 1 - c}
            ).wait_recv()
    up_home.wait()
    keep.wait()
    last.finish()


def forward(inputs, n_f, n_z, head, own_h, ident):
    rows, width = inputs["tokens"].shape
    n_p, n_s = n_f * 2, n_z * 2
    own_q = width // n_p
    seg = width // n_f
    count = len(bit_orders(n_f)[1]) * n_f
    stream = n_s * rows
    span = min(stream, stream // 2 + rows)
    in_hbm = ("qkv_weight", "up_weight", "out_weight")
    plane = (n_p, rows, width)
    blocks = (n_p, rows, own_q)
    outs = {
        "normed_pl": (plane, BF16, ANYWHERE),
        "normal_one": ((rows, width), F32, ON_CHIP),
        "inverse_one": ((rows, 1), F32, ON_CHIP),
        "query": (blocks, BF16, ON_CHIP),
        "kv": ((span, 2 * head), BF16, ON_CHIP),
        "lse": ((n_p, 1, own_q // head * rows), F32, ON_CHIP),
        "mixed_own": (blocks, BF16, ON_CHIP),
        "residual": ((rows, width), F32, ON_CHIP),
        "normal_two": ((rows, width), F32, ON_CHIP),
        "inverse_two": ((rows, 1), F32, ON_CHIP),
        "normed_mlp_pl": (plane, BF16, ANYWHERE),
        "grad_pl": (plane, BF16, ANYWHERE),
        "w_q": ((n_f, seg, own_q), BF16, ON_CHIP),
        "w_kv": ((n_f, seg, 2 * head), BF16, ON_CHIP),
        "w_up": ((n_f, seg, own_h), BF16, ANYWHERE),
        "vecs": ((8, width), F32, ON_CHIP),
        "mask": ((span, rows), F32, ON_CHIP),
        "w_out": ((own_q, width), BF16, ON_CHIP),
    }
    scratch = {
        "small_all": VMEM((n_f,) + inputs["small"].shape, BF16),
        "small_f32": VMEM(inputs["small"].shape, F32),

        "up_own": VMEM((seg, own_h), BF16),
        "normed": VMEM((rows, width), BF16),
        "normed_all": VMEM(plane, BF16),
        "keyval": VMEM((rows, 2 * head), BF16),
        "query_send": VMEM(blocks, BF16),
        "kv_all": VMEM((n_s, rows, 2 * head), BF16),
        "mixed_send": VMEM(blocks, BF16),
        "part": VMEM(plane, BF16),
        "core_in": VMEM((n_f, rows, width), BF16),
        "link_in": VMEM((n_f, rows, width), BF16),
        "branch": VMEM((rows, width), F32),
        "normed_mlp": VMEM((rows, width), BF16),
        "local_sem": DMA((12,)),
        "small_sem": DMA((2, n_f)),
        "q_sem": DMA((2, n_f)),
        "kv_sem": DMA((4, n_f)),
        "up_sem": DMA((2, n_f)),
        "line_sem": DMA((2, n_z * n_f)),
        "gather_one": DMA((4, count)),
        "gather_two": DMA((4, count)),
        "gather_three": DMA((4, count)),
        "scatter_one": DMA((4, count)),
        "swap_one": DMA((2, n_p)),
        "swap_two": DMA((2, n_p)),
        "column_sem": DMA((2, n_s)),
    }
    names = list(inputs) + list(outs) + list(scratch)
    result = pl.pallas_call(
        functools.partial(forward_body, n_f, n_z, head, names),
        out_shape=[jax.ShapeDtypeStruct(shape, kind) for shape, kind, _ in outs.values()],
        in_specs=[ANYWHERE if name in in_hbm else ON_CHIP for name in inputs],
        out_specs=[place for _, _, place in outs.values()],
        scratch_shapes=list(scratch.values()),
        compiler_params=pltpu.CompilerParams(
            collective_id=ident, has_side_effects=True, vmem_limit_bytes=56 << 20
        ),
        name="forward",
    )(*inputs.values())
    return dict(zip(outs, result))


PACE = 2
STAGGER = 3
BEHIND = 2


def norm_back_tiles(grad_ref, extra_ref, normal_ref, inverse_ref, gain_ref, base_ref, sums, store):
    rows = normal_ref.shape[0]

    @pl.loop(0, rows // 16)
    def _(at):
        where = rows_of(at)
        grad = grad_ref[where]
        if extra_ref is not None:
            grad = grad + extra_ref[where]
        normal = normal_ref[where].astype(F32)
        scaled = grad * gain_ref[...]
        first = jnp.mean(scaled, axis=-1, keepdims=True)
        second = jnp.mean(scaled * normal, axis=-1, keepdims=True)
        base = base_ref[where].astype(F32)
        result = base + inverse_ref[where] * (
            scaled - first - normal * second
        )
        store(where, result)
        sums[0:1] += jnp.sum(grad * normal, axis=0, keepdims=True)
        sums[1:2] += jnp.sum(grad, axis=0, keepdims=True)
        sums[2:3] += jnp.sum(result.astype(BF16).astype(F32), axis=0, keepdims=True)
        sums[3:4] += jnp.sum(base, axis=0, keepdims=True)


def backward_body(n_f, n_z, head, names, *refs):
    r = Box()
    for name, ref in zip(names, refs, strict=True):
        setattr(r, name, ref)
    f, z, c = lax.axis_index("fsdp"), lax.axis_index("zz"), lax.axis_index("core")
    bits = n_f.bit_length() - 1
    n_p = n_f * 2
    me = f * 2 + c
    rows, width = r.grad_out.shape
    own_q = r.w_out.shape[0]

    loads = {}
    for at, (name, source, target) in enumerate(
        (
            ("part", r.e_part, r.part),
            ("down", r.g_down_in, r.g_down),
            ("up", r.g_up_in, r.g_up),
        )
    ):
        loads[name] = pltpu.make_async_copy(source, target, r.load_sem.at[at])
        loads[name].start()
    greet([device for _, device in plane_peers(n_f, f, c) + column_peers(n_z, z, c)])

    home = {"down": r.h_down, "out": r.h_out, "kv": r.h_kv, "up": r.h_up, "q": r.h_q}

    def plain(own, landing, final):
        return lambda k: (own.at[k], landing.at[k], final.at[k])

    def turned(k):
        k = owner_turn(k)
        return r.g_q.at[k], r.land_q.at[k], r.fin_q.at[k]

    def owner_turn(k):
        per = r.g_q.shape[0] // n_f
        offset, turn = k % n_f, k // n_f
        owner = f
        for bit in range(bits):
            crossed = owner + (1 << bit) * (1 - 2 * ((owner // (1 << bit)) % 2))
            flag = (offset // (1 << bit)) % 2
            owner = owner + flag * (crossed - owner)
        return owner * per + turn

    starts = {"down": 0, "out": r.g_down.shape[0], "kv": r.g_down.shape[0] + r.g_out.shape[0]}

    def swap(kind, k, side):
        sem = starts[kind] + k
        where = home[kind].at[side, k]
        return remote(where, where, r.swap_send.at[sem], r.swap_recv.at[sem], {"core": 1 - c})

    def mate(kind):
        return lambda k: swap(kind, k, c).start()

    line = Line(
        n_z,
        [
            (r.g_up.shape[0], plain(r.g_up, r.land_up, r.fin_up), lambda k: None),
            (r.g_down.shape[0], plain(r.g_down, r.land_down, r.h_down.at[c]), mate("down")),
            (r.g_out.shape[0], plain(r.g_out, r.land_out, r.h_out.at[c]), mate("out")),
            (r.g_q.shape[0], turned, lambda k: deliver_split("q", owner_turn(k))),
            (r.g_kv.shape[0], plain(r.g_kv, r.land_kv, r.h_kv.at[c]), mate("kv")),
        ],
        (r.red_send, r.red_recv, r.fin_send, r.fin_recv, r.keep_sem),
    )

    def block(kind, turn, source):
        target = home[kind]
        height, size = finals[kind].shape[1:]
        cols = pl.ds(pl.multiple_of(source * size, LANES), size)
        return target.at[pl.ds(pl.multiple_of(turn * height, height), height), cols]

    finals = {"up": r.fin_up, "q": r.fin_q}
    home_sem = {
        "up": (r.up_send, r.up_mate, r.up_recv, r.up_relay, r.up_cross),
        "q": (r.q_send, r.q_mate, r.q_recv, r.q_relay, r.q_cross),
    }

    def turns(kind):
        return finals[kind].shape[0] // n_f

    def moves(kind, k):
        send, mate, recv, _, cross = home_sem[kind]
        owner, turn = k // turns(kind), k % turns(kind)
        where = block(kind, turn, me)
        sem = turn * n_f + f
        source = finals[kind].at[k]
        return (
            f == owner,
            lambda: pltpu.make_async_copy(source, where, send.at[k]),
            lambda: remote(source, where, mate.at[k], cross.at[sem], {"core": 1 - c}),
            lambda: remote(source, where, send.at[k], recv.at[sem], {"fsdp": owner}),
        )

    def deliver_split(kind, k):
        here, own, other, away = moves(kind, k)

        @pl.when(here)
        def _():
            own().start()
            other().start()

        @pl.when(jnp.logical_not(here))
        def _():
            away().start()

    def relay(kind, turn, offset):
        _, _, recv, send, cross = home_sem[kind]
        source = flip(f, offset, bits)
        where = block(kind, turn, source * 2 + c)
        sem = turn * n_f + source
        return (
            lambda: remote(where, where, send.at[sem], recv.at[sem], {"core": 1 - c}),
            lambda: remote(where, where, send.at[sem], cross.at[sem], {"core": 1 - c}),
        )

    def relay_all(kind):
        @pl.loop(0, turns(kind))
        def _(turn):
            for offset in range(1, n_f):
                arrival, onward = relay(kind, turn, offset)
                arrival().wait_recv()
                onward().start()

    def delivered():
        for kind in starts:

            @pl.loop(0, home[kind].shape[1])
            def _(k):
                swap(kind, k, c).wait_send()
                swap(kind, k, 1 - c).wait_recv()

        for kind in ("up", "q"):

            @pl.loop(0, finals[kind].shape[0])
            def _(k):
                here, own, other, away = moves(kind, k)

                @pl.when(here)
                def _():
                    own().wait()
                    other().wait_send()

                @pl.when(jnp.logical_not(here))
                def _():
                    away().wait_send()

            @pl.loop(0, turns(kind))
            def _(turn):
                for offset in range(n_f):
                    if offset:
                        relay(kind, turn, offset)[1]().wait_send()
                    source = flip(f, offset, bits)
                    where = block(kind, turn, source * 2 + 1 - c)
                    cross = home_sem[kind][4].at[turn * n_f + source]
                    remote(where, where, r.swap_send.at[0], cross, {"core": 1 - c}).wait_recv()

    ready = [False]
    limit = [r.g_down.shape[0] + r.g_up.shape[0]]

    def pause(count):
        if not ready[0]:
            loads["down"].wait()
            loads["up"].wait()
            ready[0] = True
        line.run(min(count * PACE, limit[0] - line.done))

    for ref in (r.sums_two, r.sums_one):
        ref[...] = jnp.zeros_like(ref)
    loads["part"].wait()
    scatter_stage(
        n_f, r.part, r.e_sum, None, r.core_in, r.link_in, *(r.scatter_one.at[at] for at in range(4)), pause
    )

    def store_two(where, result):
        r.d_residual[where] = result
        r.d_branch[where] = result.astype(BF16)

    norm_back_tiles(
        r.e_sum, None, r.normal_two, r.inverse_two, r.gain_two, r.grad_out, r.sums_two, store_two
    )
    loads["normed"] = pltpu.make_async_copy(r.normed_in, r.part, r.load_sem.at[3])
    loads["normed"].start()
    gather_stage(
        n_f, r.d_branch, r.branch_pl, *(r.gather_one.at[at] for at in range(4)), r.local_sem.at[0], pause
    )

    @pl.loop(0, n_p)
    def _(p):
        r.mixed_send[p] = dot_nt(r.branch_pl[p], r.w_out[...]).astype(BF16)

    exchange_stage(
        n_f,
        n_z,
        r.mixed_send,
        None,
        r.d_mixed,
        None,
        [r.swap_one.at[0], r.swap_one.at[1], None, None, r.local_sem.at[1], None],
        False,
        pause,
    )
    tile = min(512, width)
    high = r.g_out.shape[1]
    for j in range(own_q // LANES):
        for n in range(width // tile):
            cols = pl.ds(n * tile, tile)
            result = dot_tn(
                r.mixed_own[:, :, j * LANES : (j + 1) * LANES].reshape(n_p * rows, LANES),
                r.branch_pl[:, :, cols].reshape(n_p * rows, tile),
            ).astype(BF16)
            for k in range(LANES // high):
                r.g_out[j * (LANES // high) + k, :, cols] = result[k * high : (k + 1) * high]
    limit[0] += r.g_out.shape[0]

    r.d_kv_span[...] = jnp.zeros_like(r.d_kv_span)
    step = max(1, n_p // 2)
    for first in range(0, n_p, step):

        @pl.loop(first, first + step)
        def _(p):
            d_query, d_keys, d_values = attend_back_block(
                head, r.query[p], r.d_mixed[p], r.kv, r.mask, r.lse[p]
            )
            r.dq_send[p] = d_query
            r.d_kv_span[:, :head] += d_keys
            r.d_kv_span[:, head:] += d_values

        pause(2)
    span = r.d_kv_span.shape[0]
    stream = n_z * 2 * rows
    first = jnp.maximum((z * 2 + c + 1) * rows - span, 0)
    r.dkv_send[...] = jnp.zeros_like(r.dkv_send)

    @pl.loop(0, span // rows)
    def _(at):
        block_at = (jnp.maximum((z * 2 + c + 1) * rows - span, 0)) // rows + at
        r.dkv_send[block_at] = r.d_kv_span[pl.ds(pl.multiple_of(at * rows, rows), rows)].astype(BF16)

    exchange_stage(
        n_f,
        n_z,
        r.dq_send,
        r.dkv_send,
        r.dq_own,
        r.dkv_recv,
        [
            r.swap_two.at[0],
            r.swap_two.at[1],
            r.column_sem.at[0],
            r.column_sem.at[1],
            r.local_sem.at[2],
            r.local_sem.at[3],
        ],
        False,
        pause,
    )
    total = r.dkv_recv[0].astype(F32)
    for s in range(1, n_z * 2):
        total = total + r.dkv_recv[s].astype(F32)
    r.d_kv[...] = total.astype(BF16)

    @pl.loop(0, n_p)
    def _(p):
        for n in range(width // tile):
            cols = pl.ds(n * tile, tile)
            r.branch_pl[p, :, cols] = dot_nt(r.dq_own[p], r.w_q[cols]).astype(BF16)

    scatter_stage(
        n_f, r.branch_pl, r.e_sum, None, r.core_in, r.link_in, *(r.scatter_two.at[at] for at in range(4)), pause
    )
    for n in range(width // tile):
        cols = pl.ds(n * tile, tile)
        r.e_extra[:, cols] = dot_nt(r.d_kv[...], r.w_kv[cols])

    def store_one(where, result):
        r.grad_tokens[where] = result.astype(BF16)

    norm_back_tiles(
        r.e_sum, r.e_extra, r.normal_one, r.inverse_one, r.gain_one, r.d_residual, r.sums_one, store_one
    )
    gather_stage(
        n_f, r.d_kv, r.dkv_pl, *(r.gather_two.at[at] for at in range(4)), r.local_sem.at[4], pause
    )

    loads["normed"].wait()
    dq_all = r.dq_own[...].reshape(n_p * rows, own_q)
    tall = r.g_q.shape[1]

    @pl.loop(0, r.g_q.shape[0])
    def _(k):
        own = pl.ds(pl.multiple_of(k * tall, LANES), tall)
        r.g_q[k] = dot_tn(r.part[:, :, own].reshape(n_p * rows, tall), dq_all).astype(BF16)

    cols = pl.ds(pl.multiple_of(me * own_q, LANES), own_q)
    r.g_kv[0] = dot_tn(
        r.part[:, :, cols].reshape(n_p * rows, own_q), r.dkv_pl[...].reshape(n_p * rows, 2 * head)
    ).astype(BF16)
    loads["out"] = pltpu.make_async_copy(r.out_part, r.part, r.load_sem.at[4])
    loads["out"].start()
    limit[0] = line.total + line.lag(n_z - 1)
    pause(2)

    line.run(r.g_up.shape[0] + line.lag(n_z - 1) - line.done)

    @pl.loop(0, turns("up"))
    def _(turn):
        for offset in range(n_f):
            deliver_split("up", flip(f, (offset + 1) % n_f, bits) * turns("up") + turn)

    pause(6)

    seg = r.vec_in.shape[2]
    r.vec_in[...] = jnp.zeros_like(r.vec_in)
    up_rows = r.up_sum.shape[0]
    d_value = jnp.sum(r.d_kv[:, head:].astype(F32), axis=0, keepdims=True)
    for o in range(n_f):
        cols = slice(o * seg, (o + 1) * seg)
        r.vec_in[o, 0:1] = r.sums_one[0:1, cols]
        r.vec_in[o, 1:2] = r.sums_one[1:2, cols]
        r.vec_in[o, 3:4] = r.sums_two[2:3, cols]
        r.vec_in[o, 4:5] = r.sums_two[0:1, cols]
        r.vec_in[o, 5:6] = r.sums_two[1:2, cols]
        r.vec_in[o, 6:7] = r.sums_two[3:4, cols]
        r.vec_in[o, 7:8, :head] = d_value
        for side in range(2):
            part = jnp.sum(r.dq_send[o * 2 + side].astype(F32), axis=0, keepdims=True)
            r.vec_in[o, 2:3, side * own_q : (side + 1) * own_q] = part

        for side in range(2):

            @pl.when((f == o) & (c == side))
            def _():
                r.vec_in[o, 8 + side * up_rows : 8 + (side + 1) * up_rows] = r.up_sum[...]

    vector_stage(
        n_f,
        n_z,
        r.vec_in,
        r.vectors,
        r.vec_plane,
        r.vec_part,
        r.vec_line,
        [r.vec_sem.at[0], r.vec_sem.at[1], r.vec_line_sem.at[0], r.vec_line_sem.at[1], r.local_sem.at[5]],
        pause,
    )

    loads["out"].wait()
    scatter_stage(
        n_f, r.part, r.out_sum, None, r.core_in, r.link_in, *(r.scatter_three.at[at] for at in range(4)), pause
    )
    line.run(line.left() - 4 * PACE)
    relay_all("up")
    line.run(line.left())
    relay_all("q")
    line.finish()
    delivered()


def backward(inputs, n_f, n_z, head, own_h, ident):
    rows, width = inputs["grad_out"].shape
    n_p = n_f * 2
    n_s = n_z * 2
    own_q = width // n_p
    seg = width // n_f
    count = len(bit_orders(n_f)[1]) * n_f
    span = inputs["kv"].shape[0]
    high = max(16, CHUNK // width)
    tall = min(seg, CHUNK // own_q)
    down = inputs["g_down_in"].shape
    up = inputs["g_up_in"].shape
    out = (own_q // high, high, width)
    query = (width // tall, tall, own_q)
    keyval = (1, own_q, 2 * head)
    chunks = down[0] + up[0] + out[0] + query[0] + 1
    in_hbm = ("e_part", "g_down_in", "g_up_in", "normed_in", "out_part")
    outs = {
        "grad_tokens": ((rows, width), BF16, ON_CHIP),
        "out_sum": ((rows, width), F32, ON_CHIP),
        "vectors": ((16, seg), F32, ON_CHIP),
        "h_down": ((2,) + down, BF16, ANYWHERE),
        "h_up": ((seg, own_h * n_p), BF16, ANYWHERE),
        "h_out": ((2,) + out, BF16, ANYWHERE),
        "h_q": ((seg, width), BF16, ANYWHERE),
        "h_kv": ((2,) + keyval, BF16, ANYWHERE),
    }
    plane = (n_p, rows, width)
    blocks = (n_p, rows, own_q)
    scratch = {
        "part": VMEM(plane, BF16),
        "g_down": VMEM(down, BF16),
        "g_up": VMEM(up, BF16),
        "g_out": VMEM(out, BF16),
        "g_q": VMEM(query, BF16),
        "g_kv": VMEM(keyval, BF16),
        "land_down": VMEM(down, BF16),
        "land_up": VMEM(up, BF16),
        "land_out": VMEM(out, BF16),
        "land_q": VMEM(query, BF16),
        "land_kv": VMEM(keyval, BF16),
        "fin_up": VMEM(up, BF16),
        "fin_q": VMEM(query, BF16),
        "core_in": VMEM((n_f, rows, width), BF16),
        "link_in": VMEM((n_f, rows, width), BF16),
        "e_sum": VMEM((rows, width), F32),
        "e_extra": VMEM((rows, width), F32),
        "d_residual": VMEM((rows, width), F32),
        "d_branch": VMEM((rows, width), BF16),
        "branch_pl": VMEM(plane, BF16),
        "mixed_send": VMEM(blocks, BF16),
        "d_mixed": VMEM(blocks, BF16),
        "dq_send": VMEM(blocks, BF16),
        "dq_own": VMEM(blocks, BF16),
        "d_kv_span": VMEM((span, 2 * head), F32),
        "dkv_send": VMEM((n_s, rows, 2 * head), BF16),
        "dkv_recv": VMEM((n_s, rows, 2 * head), BF16),
        "d_kv": VMEM((rows, 2 * head), BF16),
        "dkv_pl": VMEM((n_p, rows, 2 * head), BF16),
        "sums_one": VMEM((8, width), F32),
        "sums_two": VMEM((8, width), F32),
        "vec_in": VMEM((n_f, 16, seg), F32),
        "vec_plane": VMEM((n_p, 16, seg), F32),
        "vec_part": VMEM((16, seg), F32),
        "vec_line": VMEM((n_z, 16, seg), F32),
        "load_sem": DMA((5,)),
        "local_sem": DMA((6,)),
        "red_send": DMA((chunks,)),
        "red_recv": DMA((chunks,)),
        "fin_send": DMA((chunks,)),
        "fin_recv": DMA((chunks,)),
        "keep_sem": DMA((chunks,)),
        "swap_send": DMA((chunks,)),
        "swap_recv": DMA((chunks,)),
        "up_send": DMA((up[0],)),
        "up_mate": DMA((up[0],)),
        "up_recv": DMA((up[0],)),
        "up_relay": DMA((up[0],)),
        "up_cross": DMA((up[0],)),
        "q_send": DMA((query[0],)),
        "q_mate": DMA((query[0],)),
        "q_recv": DMA((query[0],)),
        "q_relay": DMA((query[0],)),
        "q_cross": DMA((query[0],)),
        "scatter_one": DMA((4, count)),
        "scatter_two": DMA((4, count)),
        "scatter_three": DMA((4, count)),
        "gather_one": DMA((4, count)),
        "gather_two": DMA((4, count)),
        "swap_one": DMA((2, n_p)),
        "swap_two": DMA((2, n_p)),
        "column_sem": DMA((2, n_s)),
        "vec_sem": DMA((2, n_p)),
        "vec_line_sem": DMA((2, n_z)),
    }
    names = list(inputs) + list(outs) + list(scratch)
    result = pl.pallas_call(
        functools.partial(backward_body, n_f, n_z, head, names),
        out_shape=[jax.ShapeDtypeStruct(shape, kind) for shape, kind, _ in outs.values()],
        in_specs=[ANYWHERE if name in in_hbm else ON_CHIP for name in inputs],
        out_specs=[place for _, _, place in outs.values()],
        scratch_shapes=list(scratch.values()),
        compiler_params=pltpu.CompilerParams(
            collective_id=ident, has_side_effects=True, vmem_limit_bytes=67043328
        ),
        name="backward",
    )(*inputs.values())
    return dict(zip(outs, result))


def dot(left, right):
    return jnp.dot(left, right, preferred_element_type=F32)


def dot_tn(left, right):
    return lax.dot_general(left, right, (((0,), (0,)), ((), ())), preferred_element_type=F32)


def dot_nt(left, right):
    return lax.dot_general(left, right, (((1,), (1,)), ((), ())), preferred_element_type=F32)


def widen_body(count, *refs):
    at = 0
    for ref in refs[:count]:
        refs[count][:, at : at + ref.shape[1]] = ref[...].astype(F32)
        at += ref.shape[1]


def widen(*pieces):
    height = pieces[0].shape[0]
    width = sum(item.shape[1] for item in pieces)
    block = min(height, 1 << ((1 << 20) // width).bit_length() - 1)
    specs = [pl.BlockSpec((block, item.shape[1]), lambda i: (i, 0)) for item in pieces]
    return pl.pallas_call(
        functools.partial(widen_body, len(pieces)),
        out_shape=jax.ShapeDtypeStruct((height, width), F32),
        grid=(pl.cdiv(height, block),),
        in_specs=specs,
        out_specs=pl.BlockSpec((block, width), lambda i: (i, 0)),
        compiler_params=pltpu.CompilerParams(vmem_limit_bytes=40 << 20),
        name="widen",
    )(*pieces)


def shards(
    tokens,
    doc_lengths,
    attn_gain,
    attn_shift,
    qkv_weight,
    query_bias,
    value_bias,
    out_weight,
    out_bias,
    mlp_gain,
    mlp_shift,
    up_weight,
    up_bias,
    down_weight,
    down_bias,
    cotangent,
):
    n_f, n_z, n_c = lax.axis_size("fsdp"), lax.axis_size("zz"), lax.axis_size("core")
    f, z, c = lax.axis_index("fsdp"), lax.axis_index("zz"), lax.axis_index("core")
    n_p = n_f * n_c
    grad_out = cotangent[0]
    rows, width = grad_out.shape
    head = value_bias.shape[0] * n_f
    hidden = up_weight.shape[1]
    own_q = width // n_p
    own_h = hidden // n_p
    seg = width // n_f

    def own(vector, size):
        return lax.dynamic_slice_in_dim(vector, c * size, size, axis=0)

    row = lax.broadcasted_iota(jnp.int32, (8, seg), 0)
    small = jnp.broadcast_to(jnp.pad(value_bias, (0, seg - value_bias.shape[0]))[None], (8, seg))
    vectors = (attn_gain, attn_shift, out_bias, mlp_gain, mlp_shift, down_bias, query_bias)
    for at, item in enumerate(vectors):
        small = jnp.where(row == at, item[None], small)
    w_down = own(down_weight, own_h)
    ahead = forward(
        {
            "tokens": tokens[0],
            "grad_out": grad_out,
            "small": small,
            "lengths": doc_lengths,
            "out_weight": out_weight,
            "qkv_weight": qkv_weight,
            "up_weight": up_weight,
        },
        n_f,
        n_z,
        head,
        own_h,
        8,
    )
    vecs = ahead["vecs"]
    w_up = ahead["w_up"].reshape(width, own_h)
    grad_pl = ahead["grad_pl"].reshape(n_p * rows, width)
    normed_mlp_pl = ahead["normed_mlp_pl"].reshape(n_p * rows, width)

    inner = dot(normed_mlp_pl, w_up) + own(up_bias, own_h).astype(F32)
    activated, gelu_back = jax.vjp(lambda v: jax.nn.gelu(v, approximate=True), inner)
    activated = activated.astype(BF16)
    out_part = dot(activated, w_down).astype(BF16).reshape(n_p, rows, width)
    d_act = dot_nt(grad_pl, w_down)
    d_inner = gelu_back(d_act)[0].astype(BF16)
    e_part = dot_nt(d_inner, w_up).astype(BF16).reshape(n_p, rows, width)
    g_down = dot_tn(activated, grad_pl).astype(BF16)
    g_up = dot_tn(normed_mlp_pl, d_inner).astype(BF16)

    def chunked(block, most):
        height = min(max(16, CHUNK // block.shape[1]), most)
        return block.reshape(block.shape[0] // height, height, block.shape[1])

    done = backward(
        {
            "e_part": e_part,
            "out_part": out_part,
            "g_down_in": chunked(g_down, own_h),
            "g_up_in": chunked(g_up, seg),
            "normed_in": ahead["normed_pl"],
            "grad_out": grad_out,
            "normal_two": ahead["normal_two"],
            "inverse_two": ahead["inverse_two"],
            "gain_two": vecs[GAIN_TWO : GAIN_TWO + 1],
            "normal_one": ahead["normal_one"],
            "inverse_one": ahead["inverse_one"],
            "gain_one": vecs[GAIN_ONE : GAIN_ONE + 1],
            "w_out": ahead["w_out"],
            "w_q": ahead["w_q"].reshape(width, own_q),
            "w_kv": ahead["w_kv"].reshape(width, 2 * head),
            "query": ahead["query"],
            "kv": ahead["kv"],
            "mask": ahead["mask"],
            "lse": ahead["lse"],
            "mixed_own": ahead["mixed_own"],
            "up_sum": jnp.sum(d_inner.astype(F32), axis=0).reshape(own_h // seg, seg),
        },
        n_f,
        n_z,
        head,
        own_h,
        9,
    )
    layer_out = ahead["residual"] + done["out_sum"] + vecs[BIAS_DOWN]
    vectors = done["vectors"]
    grad_qkv = widen(done["h_q"], done["h_kv"].reshape(n_c * own_q, 2 * head))
    size = value_bias.shape[0]
    grad_value_bias = lax.dynamic_slice_in_dim(vectors[7], f * size, size)
    return (
        layer_out.astype(BF16)[None],
        done["grad_tokens"][None],
        vectors[0],
        vectors[1],
        grad_qkv,
        vectors[2],
        grad_value_bias,
        widen(done["h_out"].reshape(n_c * own_q, width)),
        vectors[3],
        vectors[4],
        vectors[5],
        widen(done["h_up"]),
        vectors[8 : 8 + hidden // width].reshape(-1),
        widen(done["h_down"].reshape(n_c * own_h, width)),
        vectors[6],
    )


def solution(mesh):
    n_f, n_s = mesh.shape["fsdp"], mesh.shape["seq"]
    split = Mesh(mesh.devices.reshape(n_f, n_s // 2, 2), ("fsdp", "zz", "core"))
    act = P("fsdp", ("zz", "core"), None)
    vec = P("fsdp")
    mat = P("fsdp", None)
    return jax.shard_map(
        shards,
        mesh=split,
        in_specs=(act, mat, vec, vec, mat, vec, vec, mat, vec, vec, vec, mat, vec, mat, vec, act),
        out_specs=(act, act, vec, vec, mat, vec, vec, mat, vec, vec, vec, mat, vec, mat, vec),
        check_vma=False,
    )
```
